32 devices in a mesh: ctx: 16 (over z, x, core), fs: 2 (over y).
Axes of the slice: x: 2, y: 2, z: 4, core: 2. Of those that a mesh axis runs over, the one named last changes fastest.
Arguments:
- tokens: bfloat16 [2, 4096, 1280], P('fs', 'ctx'), may hold values from -6 to 6
- query_weight: bfloat16 [1280, 1280], P('fs'), may hold values from -0.15625 to 0.15625
- key_weight: bfloat16 [1280, 1280], P('fs'), may hold values from -0.15625 to 0.15625
- value_weight: bfloat16 [1280, 1280], P('fs'), may hold values from -0.15625 to 0.15625
- out_weight: bfloat16 [1280, 1280], P('fs'), may hold values from -0.625 to 0.625
- inner_weight: bfloat16 [1280, 1280], P('fs'), may hold values from -0.15625 to 0.15625
- outer_weight: bfloat16 [1280, 1280], P('fs'), may hold values from -0.15625 to 0.15625
- attn_gain: bfloat16 [1280], P('fs'), may hold values from 0.099609375 to 1.8984375
- mlp_gain: bfloat16 [1280], P('fs'), may hold values from 0.099609375 to 1.8984375
- query_scale: float32 [80], replicated, may hold values from 0.5 to 2
- doc_starts: int32 [2, 8], P('fs'), may hold values from 0 to 4095, as said below
- cotangent: bfloat16 [2, 4096, 1280], P('fs', 'ctx'), may hold values from -6 to 6
Outputs:
- output: bfloat16 [2, 4096, 1280], P('fs', 'ctx')
- tokens_grad: bfloat16 [2, 4096, 1280], P('fs', 'ctx')
- query_grad: float32 [1280, 1280], P('fs')
- key_grad: float32 [1280, 1280], P('fs')
- value_grad: float32 [1280, 1280], P('fs')
- out_grad: float32 [1280, 1280], P('fs')
- inner_grad: float32 [1280, 1280], P('fs')
- outer_grad: float32 [1280, 1280], P('fs')
- attn_gain_grad: float32 [1280], P('fs')
- mlp_gain_grad: float32 [1280], P('fs')
- query_scale_grad: float32 [80], replicated
The draws below stay inside these ranges and needn't reach their ends.
Inputs may be any that keep to these rules, and one draw needn't show every extreme that they name: `doc_starts`: within a stream the starts rise strictly, the first is 0 and the last is 4095. In every stream one document begins in the first 256 positions and ends in the last 256.
All inputs are finite; a program needn't handle non-finite values.
Results may differ from the reference program's by a relative error of at most 0.024.
Values may be sent and summed in bfloat16 or wider, within the bound.
A program may use at most 128 MiB of HBM per device.

```python
import math
import jax
import jax.numpy as jnp
from jax import lax

D = 1280
H = 16
HD = 80
FF = 1280
TOK_DEV = 256
NDOC = 8
SEQ = 4096
STREAMS = 2


def draw_doc_starts(key, part):
    key_a, key_b, key_c, key_d = jax.random.split(jax.random.fold_in(key, 17), 4)
    quarter = TOK_DEV // 4
    eighth = TOK_DEV // 8
    first = 1 + jax.random.randint(key_a, (STREAMS,), 0, quarter)
    second = first + 1 + jax.random.randint(key_b, (STREAMS,), 0, quarter)
    third = SEQ - TOK_DEV + quarter + jax.random.randint(key_c, (STREAMS,), 0, quarter)
    gaps = 1 + jax.random.randint(key_d, (STREAMS, NDOC - 5), 0, eighth)
    later = third[:, None] + jnp.cumsum(gaps, axis=1)
    zeros_col = jnp.zeros((STREAMS, 1), jnp.int32)
    last_col = jnp.full((STREAMS, 1), SEQ - 1, jnp.int32)
    return jnp.concatenate([zeros_col, first[:, None], second[:, None], third[:, None], later, last_col], axis=1).astype(jnp.int32)


def block_scale(stream_key, extent, cuts, low, top_value):
    gain, own = 1.0, jax.random.fold_in(stream_key, 6)
    for axis_at, shards_of in cuts:
        heights = jnp.exp(jax.random.uniform(jax.random.fold_in(own, axis_at), (shards_of,), jnp.float32, low / len(cuts), top_value / len(cuts)))
        gain = gain * jnp.repeat(heights, extent[axis_at] // shards_of).reshape([-1 if axis == axis_at else 1 for axis in range(len(extent))])
    return gain


def gaussian(rng, shape, deviation, reach, cuts=(), held_as=jnp.bfloat16):
    entries = deviation * jax.random.normal(rng, shape, jnp.float32)
    if cuts:
        entries = entries * block_scale(rng, shape, cuts, -0.22, 0.18)
    return jnp.clip(entries, -reach, reach).astype(held_as)


def setup_inputs(seed: int = 0) -> dict:
    arg_keys = jax.random.split(jax.random.key(seed), 13)
    return {
        "tokens": gaussian(arg_keys[0], (STREAMS, SEQ, D), 1.0, 6.0, ((0, 2), (1, 16))),
        "query_weight": gaussian(arg_keys[1], (D, D), D ** -0.5, 0.15625, ((0, 2),)),
        "key_weight": gaussian(arg_keys[2], (D, D), D ** -0.5, 0.15625, ((0, 2),)),
        "value_weight": gaussian(arg_keys[3], (D, D), D ** -0.5, 0.15625, ((0, 2),)),
        "out_weight": gaussian(arg_keys[4], (D, D), (D // 16) ** -0.5, 0.625, ((0, 2),)),
        "inner_weight": gaussian(arg_keys[5], (D, FF), D ** -0.5, 0.15625, ((0, 2),)),
        "outer_weight": gaussian(arg_keys[6], (FF, D), FF ** -0.5, 0.15625, ((0, 2),)),
        "attn_gain": jnp.clip(1.0 + 0.18 * jax.random.normal(arg_keys[7], (D,), jnp.float32), 0.099609375, 1.8984375).astype(jnp.bfloat16),
        "mlp_gain": jnp.clip(1.0 + 0.18 * jax.random.normal(arg_keys[8], (D,), jnp.float32), 0.099609375, 1.8984375).astype(jnp.bfloat16),
        "query_scale": jnp.clip(jnp.exp(jax.random.uniform(arg_keys[9], (HD,), jnp.float32, math.log(0.5), math.log(2.0))), 0.5, 2.0),
        "doc_starts": draw_doc_starts(jax.random.fold_in(arg_keys[12], 71), 0),
        "cotangent": gaussian(arg_keys[11], (STREAMS, SEQ, D), 1.0, 6.0, ((0, 2), (1, 16))),
    }


@jax.custom_vjp
def low(v):
    return lax.optimization_barrier(v.astype(jnp.bfloat16)).astype(jnp.float32)

@jax.custom_vjp
def low_back(v):
    return v

def low_keep(v):
    return (low(v), None)

def low_pass(kept, grad):
    return (grad,)

def back_keep(v):
    return (v, None)

def back_low(kept, grad):
    return (low(grad),)
low.defvjp(low_keep, low_pass)
low_back.defvjp(back_keep, back_low)
epsilon = 1e-06
neg_big = -1e+30

def product(left, right):
    return jnp.dot(left, right, precision=lax.Precision.HIGHEST)

def rms_norm(values_in, gain_vec):
    return values_in * lax.rsqrt(lax.optimization_barrier(jnp.mean(values_in * values_in, axis=-1, keepdims=True)) + epsilon) * gain_vec

def layer_forward(tokens_all, segments, query_weight, key_weight, value_weight, out_weight, inner_weight, outer_weight, attn_gain, mlp_gain, query_scale):
    block_rows = math.gcd(SEQ, 512)
    scale_vec = jnp.tile(query_scale, H) / math.sqrt(HD)
    positions = jnp.arange(SEQ, dtype=jnp.int32)

    def stream_forward(pair):
        rows_in, seg_row = pair
        hidden_one = low(rms_norm(rows_in, attn_gain))
        queries = low(low_back(product(hidden_one, query_weight)) * scale_vec).reshape(SEQ, H, HD)
        key_rows = low(low_back(product(hidden_one, key_weight))).reshape(SEQ, H, HD)
        value_rows = low(low_back(product(hidden_one, value_weight))).reshape(SEQ, H, HD)

        def attend(block):
            query_block, query_pos, query_seg = block
            scores = low_back(jnp.einsum('qhd,khd->hqk', query_block, key_rows, precision=lax.Precision.HIGHEST))
            allowed = (positions[None, :] <= query_pos[:, None]) & (seg_row[None, :] == query_seg[:, None])
            masked = jnp.where(allowed[None], scores, neg_big)
            weights = jax.nn.softmax(masked, axis=-1)
            return jnp.einsum('hqk,khd->qhd', low(weights), value_rows, precision=lax.Precision.HIGHEST)
        blocks = (queries.reshape(SEQ // block_rows, block_rows, H, HD), positions.reshape(SEQ // block_rows, block_rows), seg_row.reshape(SEQ // block_rows, block_rows))
        attended = lax.map(jax.checkpoint(attend), blocks).reshape(SEQ, D)
        attn_low = low(low_back(attended))
        resid = low_back(rows_in + product(attn_low, out_weight))
        hidden_two = low(rms_norm(resid, mlp_gain))
        inner_pre = low_back(product(hidden_two, inner_weight))
        active = low(jax.nn.silu(inner_pre))
        return resid + product(active, outer_weight)
    return lax.map(stream_forward, (tokens_all, segments))

def reference(tokens, query_weight, key_weight, value_weight, out_weight, inner_weight, outer_weight, attn_gain, mlp_gain, query_scale, doc_starts, cotangent):
    positions = jnp.arange(SEQ, dtype=jnp.int32)
    segments = lax.optimization_barrier(jnp.sum((doc_starts[:, None, :] <= positions[None, :, None]).astype(jnp.int32), axis=-1)) - 1
    segments = segments.astype(jnp.int32)
    primals = (tokens.astype(jnp.float32), query_weight.astype(jnp.float32), key_weight.astype(jnp.float32), value_weight.astype(jnp.float32), out_weight.astype(jnp.float32), inner_weight.astype(jnp.float32), outer_weight.astype(jnp.float32), attn_gain.astype(jnp.float32), mlp_gain.astype(jnp.float32), query_scale.astype(jnp.float32))

    def forward_fn(tok, qw, kw, vw, ow, iw, uw, ga, gm, qs):
        return layer_forward(tok, segments, qw, kw, vw, ow, iw, uw, ga, gm, qs)
    result, pullback = jax.vjp(forward_fn, *primals)
    grads = pullback(cotangent.astype(jnp.float32))
    return (result.astype(jnp.bfloat16), grads[0].astype(jnp.bfloat16), grads[1].astype(jnp.float32), grads[2].astype(jnp.float32), grads[3].astype(jnp.float32), grads[4].astype(jnp.float32), grads[5].astype(jnp.float32), grads[6].astype(jnp.float32), grads[7].astype(jnp.float32), grads[8].astype(jnp.float32), grads[9].astype(jnp.float32))
```

```python
import functools
import math

import jax
import jax.numpy as jnp
from jax import lax
from jax.experimental import pallas as pl
from jax.experimental.pallas import tpu as pltpu
from jax.sharding import PartitionSpec as P

H = 16
HD = 80


epsilon = 1e-06
neg_big = -1e30


def passed_along(block, axis, distance):
    devices = range(lax.axis_size(axis))
    route = [((i - distance) % len(devices), i) for i in devices]
    return lax.ppermute(block, axis, route)


def shifted(value, axis, steps):
    count = lax.axis_size(axis)
    leading, last = (max(0, -steps), min(count, count - steps))
    return lax.ppermute(value, axis, [(source, source + steps) for source in range(leading, last)])


def rms_scale(values_in):
    return lax.rsqrt(jnp.mean(values_in * values_in, axis=-1, keepdims=True) + epsilon)


def norm_back(grad_normed, normed, scale_rows):
    inner_mean = jnp.mean(grad_normed * normed, axis=-1, keepdims=True)
    return scale_rows * (grad_normed - normed * inner_mean)


def segment_of(positions, starts_row):
    return jnp.sum((starts_row[None, :] <= positions[:, None]).astype(jnp.int32), axis=1) - 1


def block_mask(query_pos, query_seg, key_pos, key_seg):
    return (key_pos[None, :] <= query_pos[:, None]) & (key_seg[None, :] == query_seg[:, None])


def scores_of(query_block, key_block):
    return jnp.einsum("qhd,khd->hqk", query_block, key_block, preferred_element_type=jnp.float32)


def pass_grads(grad_key_acc, grad_value_acc):
    return (
        passed_along(grad_key_acc.astype(jnp.bfloat16), "ctx", 1).astype(grad_key_acc.dtype),
        passed_along(grad_value_acc.astype(jnp.bfloat16), "ctx", 1).astype(grad_value_acc.dtype),
    )


def general_local(
    tokens,
    query_weight,
    key_weight,
    value_weight,
    out_weight,
    inner_weight,
    outer_weight,
    attn_gain,
    mlp_gain,
    query_scale,
    doc_starts,
    cotangent,
):
    row_count = tokens.shape[1]
    model_width = tokens.shape[2]
    ctx_count = lax.axis_size("ctx")
    ctx_place = lax.axis_index("ctx")
    (
        query_full,
        key_full,
        value_full,
        out_full,
        inner_full,
        outer_full,
        attn_gain_full,
        mlp_gain_full,
    ) = (
        lax.all_gather(query_weight, "fs", axis=0, tiled=True),
        lax.all_gather(key_weight, "fs", axis=0, tiled=True),
        lax.all_gather(value_weight, "fs", axis=0, tiled=True),
        lax.all_gather(out_weight, "fs", axis=0, tiled=True),
        lax.all_gather(inner_weight, "fs", axis=0, tiled=True),
        lax.all_gather(outer_weight, "fs", axis=0, tiled=True),
        lax.all_gather(attn_gain, "fs", axis=0, tiled=True),
        lax.all_gather(mlp_gain, "fs", axis=0, tiled=True),
    )
    starts_row = doc_starts[0]
    local_pos = ctx_place * row_count + jnp.arange(row_count, dtype=jnp.int32)
    local_seg = segment_of(local_pos, starts_row)

    def heads_of(flat_block):
        return flat_block.reshape(row_count, H, HD)

    token_rows = tokens[0].astype(jnp.float32)
    scale_one = rms_scale(token_rows)
    normed_one = token_rows * scale_one
    gain_one = attn_gain_full.astype(jnp.float32)
    hidden_one = (normed_one * gain_one).astype(jnp.bfloat16)
    query_raw = jnp.dot(hidden_one, query_full, preferred_element_type=jnp.float32)
    scale_vec = jnp.tile(query_scale, H) / math.sqrt(HD)
    queries = heads_of((query_raw * scale_vec).astype(jnp.bfloat16))
    key_rows = jnp.dot(hidden_one, key_full, preferred_element_type=jnp.float32).astype(
        jnp.bfloat16
    )
    value_rows = jnp.dot(hidden_one, value_full, preferred_element_type=jnp.float32).astype(
        jnp.bfloat16
    )

    def key_info(turn_index):
        source = (ctx_place - turn_index) % ctx_count
        key_pos = source * row_count + jnp.arange(row_count, dtype=jnp.int32)
        return (source, key_pos, segment_of(key_pos, starts_row))

    def keep_state(state_in):
        return state_in

    def attend(softmax_state, key_flat, value_flat, turn_index):
        source, key_pos, key_seg = key_info(turn_index)

        def compute(state_in):
            run_max, run_sum, run_acc = state_in
            key_block = heads_of(key_flat)
            value_block = heads_of(value_flat)
            allowed = block_mask(local_pos, local_seg, key_pos, key_seg)
            scores = jnp.where(allowed[None], scores_of(queries, key_block), neg_big)
            new_max = jnp.maximum(run_max, jnp.max(scores, axis=-1))
            weights = jnp.where(allowed[None], jnp.exp(scores - new_max[..., None]), 0.0)
            factor = jnp.exp(run_max - new_max)
            run_sum = run_sum * factor + jnp.sum(weights, axis=-1)
            run_acc = run_acc * factor[..., None] + jnp.einsum(
                "hqk,khd->hqd",
                weights.astype(jnp.bfloat16),
                value_block,
                preferred_element_type=jnp.float32,
            )
            return (new_max, run_sum, run_acc)

        return lax.cond(source <= ctx_place, compute, keep_state, softmax_state)

    start_state = (
        jnp.full((H, row_count), neg_big, jnp.float32),
        jnp.zeros((H, row_count), jnp.float32),
        jnp.zeros((H, row_count, HD), jnp.float32),
    )
    start_state = attend(start_state, key_rows, value_rows, jnp.int32(0))
    stores = ()

    def forward_turn(turn_index, loop_state):
        key_block, value_block, softmax_state, kept = loop_state
        key_block, value_block = shifted((key_block, value_block), "ctx", 1)
        softmax_state = attend(softmax_state, key_block, value_block, turn_index)
        return (key_block, value_block, softmax_state, kept)

    loop_out = lax.fori_loop(
        1, ctx_count, forward_turn, (key_rows, value_rows, start_state, stores)
    )
    run_max, run_sum, run_acc = loop_out[2]
    stores = loop_out[3]
    log_total = run_max + jnp.log(run_sum)
    attn_heads = run_acc / run_sum[..., None]
    attn_low = (
        jnp.transpose(attn_heads, (1, 0, 2)).reshape(row_count, model_width).astype(jnp.bfloat16)
    )
    resid = token_rows + jnp.dot(attn_low, out_full, preferred_element_type=jnp.float32)
    scale_two = rms_scale(resid)
    normed_two = resid * scale_two
    gain_two = mlp_gain_full.astype(jnp.float32)
    hidden_two = (normed_two * gain_two).astype(jnp.bfloat16)
    inner_pre = jnp.dot(hidden_two, inner_full, preferred_element_type=jnp.float32)
    active = jax.nn.silu(inner_pre).astype(jnp.bfloat16)
    result = resid + jnp.dot(active, outer_full, preferred_element_type=jnp.float32)
    grad_out = cotangent[0]
    grad_active = jnp.dot(grad_out, outer_full.T, preferred_element_type=jnp.float32)
    grad_outer = jnp.dot(active.T, grad_out, preferred_element_type=jnp.float32)
    sigmoid_in = jax.nn.sigmoid(inner_pre)
    grad_inner_pre = (grad_active * sigmoid_in * (1.0 + inner_pre * (1.0 - sigmoid_in))).astype(
        jnp.bfloat16
    )
    grad_inner = jnp.dot(hidden_two.T, grad_inner_pre, preferred_element_type=jnp.float32)
    grad_hidden_two = jnp.dot(grad_inner_pre, inner_full.T, preferred_element_type=jnp.float32)
    grad_gain_two = jnp.sum(grad_hidden_two * normed_two, axis=0)
    grad_resid = grad_out.astype(jnp.float32) + norm_back(
        grad_hidden_two * gain_two, normed_two, scale_two
    )
    grad_resid_low = grad_resid.astype(jnp.bfloat16)
    grad_outw = jnp.dot(attn_low.T, grad_resid_low, preferred_element_type=jnp.float32)
    grad_attended = heads_of(
        jnp.dot(grad_resid_low, out_full.T, preferred_element_type=jnp.float32).astype(jnp.bfloat16)
    )
    row_delta = jnp.einsum("qhd,hqd->hq", grad_attended.astype(jnp.float32), attn_heads)

    def attend_back(grad_parts, key_flat, value_flat, turn_index):
        source, key_pos, key_seg = key_info(turn_index)

        def compute(parts_in):
            grad_query_acc, grad_key_acc, grad_value_acc = parts_in
            key_block = heads_of(key_flat)
            value_block = heads_of(value_flat)
            allowed = block_mask(local_pos, local_seg, key_pos, key_seg)
            scores = scores_of(queries, key_block)
            probabilities = jnp.where(allowed[None], jnp.exp(scores - log_total[..., None]), 0.0)
            grad_value_acc = grad_value_acc + jnp.einsum(
                "hqk,qhd->khd",
                probabilities.astype(jnp.bfloat16),
                grad_attended,
                preferred_element_type=jnp.float32,
            ).reshape(row_count, model_width)
            grad_probs = jnp.einsum(
                "qhd,khd->hqk", grad_attended, value_block, preferred_element_type=jnp.float32
            )
            grad_scores = (probabilities * (grad_probs - row_delta[..., None])).astype(jnp.bfloat16)
            grad_query_acc = grad_query_acc + jnp.einsum(
                "hqk,khd->qhd", grad_scores, key_block, preferred_element_type=jnp.float32
            )
            grad_key_acc = grad_key_acc + jnp.einsum(
                "hqk,qhd->khd", grad_scores, queries, preferred_element_type=jnp.float32
            ).reshape(row_count, model_width)
            return (grad_query_acc, grad_key_acc, grad_value_acc)

        return lax.cond(source <= ctx_place, compute, keep_state, grad_parts)

    def back_compute(turn_index, loop_state):
        key_block, value_block, grad_parts = loop_state
        grad_parts = attend_back(grad_parts, key_block, value_block, turn_index)
        grad_key_acc, grad_value_acc = pass_grads(grad_parts[1], grad_parts[2])
        return (key_block, value_block, (grad_parts[0], grad_key_acc, grad_value_acc))

    def back_turn(turn_index, loop_state):
        key_block, value_block, grad_parts = back_compute(turn_index, loop_state)
        key_block, value_block = shifted((key_block, value_block), "ctx", 1)
        return (key_block, value_block, grad_parts)

    zero_heads = jnp.zeros((row_count, H, HD), jnp.float32)
    zero_flat = jnp.zeros((row_count, model_width), jnp.float32)
    back_state = lax.fori_loop(
        0, ctx_count - 1, back_turn, (key_rows, value_rows, (zero_heads, zero_flat, zero_flat))
    )
    back_state = back_compute(jnp.int32(ctx_count - 1), back_state)
    grad_query_acc, grad_key_acc, grad_value_acc = back_state[2]
    grad_query_flat = grad_query_acc.reshape(row_count, model_width)
    grad_key_low = grad_key_acc.astype(jnp.bfloat16)
    grad_value_low = grad_value_acc.astype(jnp.bfloat16)
    grad_query_raw = (grad_query_flat * scale_vec).astype(jnp.bfloat16)
    grad_scale = jnp.sum(
        (grad_query_flat * query_raw).reshape(row_count, H, HD), axis=(0, 1)
    ) / math.sqrt(HD)
    grad_qw = jnp.dot(hidden_one.T, grad_query_raw, preferred_element_type=jnp.float32)
    grad_kw = jnp.dot(hidden_one.T, grad_key_low, preferred_element_type=jnp.float32)
    grad_vw = jnp.dot(hidden_one.T, grad_value_low, preferred_element_type=jnp.float32)
    grad_hidden_one = (
        jnp.dot(grad_query_raw, query_full.T, preferred_element_type=jnp.float32)
        + jnp.dot(grad_key_low, key_full.T, preferred_element_type=jnp.float32)
        + jnp.dot(grad_value_low, value_full.T, preferred_element_type=jnp.float32)
    )
    grad_gain_one = jnp.sum(grad_hidden_one * normed_one, axis=0)
    grad_tokens = grad_resid_low.astype(jnp.float32) + norm_back(
        grad_hidden_one * gain_one, normed_one, scale_one
    )
    shard_count = lax.axis_size("fs")
    scale_rows = jnp.broadcast_to(grad_scale[None, :], (shard_count, grad_scale.shape[0]))
    shares = (
        lax.psum_scatter(
            grad_qw.astype(jnp.bfloat16), "fs", scatter_dimension=0, tiled=True
        ).astype(jnp.float32),
        lax.psum_scatter(
            grad_kw.astype(jnp.bfloat16), "fs", scatter_dimension=0, tiled=True
        ).astype(jnp.float32),
        lax.psum_scatter(
            grad_vw.astype(jnp.bfloat16), "fs", scatter_dimension=0, tiled=True
        ).astype(jnp.float32),
        lax.psum_scatter(
            grad_outw.astype(jnp.bfloat16), "fs", scatter_dimension=0, tiled=True
        ).astype(jnp.float32),
        lax.psum_scatter(
            grad_inner.astype(jnp.bfloat16), "fs", scatter_dimension=0, tiled=True
        ).astype(jnp.float32),
        lax.psum_scatter(
            grad_outer.astype(jnp.bfloat16), "fs", scatter_dimension=0, tiled=True
        ).astype(jnp.float32),
        lax.psum_scatter(
            grad_gain_one.astype(jnp.bfloat16), "fs", scatter_dimension=0, tiled=True
        ).astype(jnp.float32),
        lax.psum_scatter(
            grad_gain_two.astype(jnp.bfloat16), "fs", scatter_dimension=0, tiled=True
        ).astype(jnp.float32),
        lax.psum_scatter(
            scale_rows.astype(jnp.bfloat16), "fs", scatter_dimension=0, tiled=True
        ).astype(jnp.float32),
    )
    totals = (
        lax.psum(shares[0].astype(jnp.bfloat16), "ctx").astype(jnp.float32),
        lax.psum(shares[1].astype(jnp.bfloat16), "ctx").astype(jnp.float32),
        lax.psum(shares[2].astype(jnp.bfloat16), "ctx").astype(jnp.float32),
        lax.psum(shares[3].astype(jnp.bfloat16), "ctx").astype(jnp.float32),
        lax.psum(shares[4].astype(jnp.bfloat16), "ctx").astype(jnp.float32),
        lax.psum(shares[5].astype(jnp.bfloat16), "ctx").astype(jnp.float32),
        lax.psum(shares[6].astype(jnp.bfloat16), "ctx").astype(jnp.float32),
        lax.psum(shares[7].astype(jnp.bfloat16), "ctx").astype(jnp.float32),
        lax.psum(shares[8].astype(jnp.bfloat16), "ctx").astype(jnp.float32),
    )
    return (
        result[None].astype(jnp.bfloat16),
        grad_tokens[None].astype(jnp.bfloat16),
        totals[0],
        totals[1],
        totals[2],
        totals[3],
        totals[4],
        totals[5],
        totals[6],
        totals[7],
        totals[8][0],
    )


MESH = pl.DeviceIdType.MESH
ANY = pl.BlockSpec(memory_space=pl.ANY)
VMEM = pl.BlockSpec(memory_space=pltpu.VMEM)
BF = jnp.bfloat16
F32 = jnp.float32


def fast_fits(mesh):
    return mesh.shape["ctx"] == H and mesh.shape["fs"] == 2


def remote(src, dst, ssem, rsem, target):
    return pltpu.make_async_remote_copy(
        src_ref=src, dst_ref=dst, send_sem=ssem, recv_sem=rsem, device_id=target, device_id_type=MESH
    )


def signal(target):
    pl.semaphore_signal(
        pltpu.get_barrier_semaphore(), inc=1, device_id=target, device_id_type=MESH
    )


def place():
    me = lax.axis_index("ctx")
    return me, lax.axis_index("fs"), me // 4, lax.rem(me // 2, 2), lax.rem(me, 2)


def dot(a, b, dims=((1,), (0,))):
    return lax.dot_general(a, b, (dims, ((), ())), preferred_element_type=F32)


NT = ((1,), (1,))
TN = ((0,), (0,))


def weight_pull(own, other, k, fs, me, ssem, rsem):
    half = own[0].shape[0] // 2
    rows = pl.ds(pl.multiple_of(k * half, 64), half)
    yn = (me, 1 - fs)
    sib = (me + 1 - 2 * k, fs)
    n = len(own)
    first = [remote(own[i].at[rows], other[i].at[rows], ssem.at[i], rsem.at[i], yn) for i in range(n)]
    second = [
        remote(other[i].at[rows], other[i].at[rows], ssem.at[n + i], rsem.at[n + i], sib)
        for i in range(n)
    ]
    return first, second


def gather_kernel(n_w, tok_ref, gain_ref, wt_ref, *rest):
    own = rest[:n_w]
    h_all, wt_all, gain_full = rest[n_w : n_w + 3]
    other = rest[n_w + 3 : 2 * n_w + 3]
    h_own, gain_other, gain_own, ssem, rsem, wssem, wrsem, ysem, lsem = rest[2 * n_w + 3 :]
    me, fs, z, x, k = place()
    sib, xn, yn = (me + 1 - 2 * k, fs), (me + 2 - 4 * x, fs), (me, 1 - fs)
    up, dn = (me + 4, fs), (me - 4, fs)
    bar = pltpu.get_barrier_semaphore()
    signal(sib)
    signal(xn)
    signal(yn)

    @pl.when(z < 3)
    def _():
        signal(up)

    @pl.when(z > 0)
    def _():
        signal(dn)

    gain_own[...] = gain_ref[...]
    rows = tok_ref[...].astype(F32)
    normed = rows * lax.rsqrt(jnp.mean(rows * rows, axis=-1, keepdims=True) + epsilon)
    pl.semaphore_wait(bar, 3 + (z + 2) // 3 + (5 - z) // 3)

    gain_copy = remote(gain_own, gain_other, ysem.at[0], ysem.at[1], yn)
    gain_copy.start()
    half = wt_ref.shape[1]
    columns = pl.ds(pl.multiple_of(fs * half, 128), half)
    wt_copy = remote(wt_ref, wt_all.at[:, columns], ysem.at[2], ysem.at[3], yn)
    wt_copy.start()
    wt_here = pltpu.make_async_copy(wt_ref, wt_all.at[:, columns], lsem.at[0])
    wt_here.start()
    first, second = weight_pull(own, other, k, fs, me, wssem, wrsem)
    gain_copy.wait()
    for c in first:
        c.start()
    g_here = gain_own[...].astype(F32)
    g_there = gain_other[...].astype(F32)
    gains = jnp.where(
        fs == 0,
        jnp.concatenate([g_here, g_there], axis=1),
        jnp.concatenate([g_there, g_here], axis=1),
    )
    gain_full[...] = gains
    h_own[...] = (normed * gains[0:1]).astype(BF)

    def cp(slot, t, si, mine=False):
        return remote(h_own if mine else h_all.at[slot], h_all.at[slot], ssem.at[si], rsem.at[slot], t)

    here = pltpu.make_async_copy(h_own, h_all.at[me], lsem.at[1])
    cp(me, xn, 0, True).start()

    @pl.when(z < 3)
    def _():
        cp(me, up, 1, True).start()

    @pl.when(z > 0)
    def _():
        cp(me, dn, 2, True).start()

    cp(me, sib, 3, True).start()
    here.start()
    for d in range(1, 4):
        a = 4 + (d - 1) * 6

        @pl.when(z >= d)
        def _(a=a, d=d):
            s = me - 4 * d
            cp(s, dn, a).wait_recv()

            @pl.when(z < 3)
            def _():
                cp(s, up, a).start()

            cp(s, xn, a + 1).start()
            cp(s, sib, a + 2).start()

        @pl.when(z + d <= 3)
        def _(a=a, d=d):
            s = me + 4 * d
            cp(s, up, a + 3).wait_recv()

            @pl.when(z > 0)
            def _():
                cp(s, dn, a + 3).start()

            cp(s, xn, a + 4).start()
            cp(s, sib, a + 5).start()

        if d <= n_w:
            first[d - 1].wait_recv()
            second[d - 1].start()

    xo = me + 2 - 4 * x
    for zz in range(4):
        s = xo + 4 * (zz - z)
        cp(s, xn, 22 + zz).wait_recv()
        cp(s, sib, 22 + zz).start()
    for i in range(3, n_w):
        first[i].wait_recv()
        second[i].start()
    for zz in range(4):
        for xx in range(2):
            cp(zz * 4 + xx * 2 + 1 - k, sib, 0).wait_recv()
    cp(me, xn, 0, True).wait_send()

    @pl.when(z < 3)
    def _():
        cp(me, up, 1, True).wait_send()

    @pl.when(z > 0)
    def _():
        cp(me, dn, 2, True).wait_send()

    cp(me, sib, 3, True).wait_send()
    for d in range(1, 4):
        a = 4 + (d - 1) * 6

        @pl.when(z >= d)
        def _(a=a, d=d):
            s = me - 4 * d

            @pl.when(z < 3)
            def _():
                cp(s, up, a).wait_send()

            cp(s, xn, a + 1).wait_send()
            cp(s, sib, a + 2).wait_send()

        @pl.when(z + d <= 3)
        def _(a=a, d=d):
            s = me + 4 * d

            @pl.when(z > 0)
            def _():
                cp(s, dn, a + 3).wait_send()

            cp(s, xn, a + 4).wait_send()
            cp(s, sib, a + 5).wait_send()

    for zz in range(4):
        cp(xo + 4 * (zz - z), sib, 22 + zz).wait_send()
    wt_copy.wait()
    wt_here.wait()
    here.wait()
    for i in range(n_w):
        first[i].wait_send()
        second[i].wait()


def gather_call(tok, gains, wt, weights):
    n_w = len(weights)
    rows, width = tok.shape
    shapes = [
        jax.ShapeDtypeStruct((H, rows, width), BF),
        jax.ShapeDtypeStruct((wt.shape[0], 2 * wt.shape[1]), BF),
        jax.ShapeDtypeStruct((gains.shape[0], 2 * gains.shape[1]), F32),
    ] + [jax.ShapeDtypeStruct(w.shape, BF) for w in weights]
    return pl.pallas_call(
        functools.partial(gather_kernel, n_w),
        out_shape=shapes,
        in_specs=[VMEM, VMEM, ANY] + [ANY] * n_w,
        out_specs=[ANY, ANY, VMEM] + [ANY] * n_w,
        scratch_shapes=[
            pltpu.VMEM((rows, width), BF),
            pltpu.VMEM(gains.shape, BF),
            pltpu.VMEM(gains.shape, BF),
            pltpu.SemaphoreType.DMA((26,)),
            pltpu.SemaphoreType.DMA((H,)),
            pltpu.SemaphoreType.DMA((2 * n_w,)),
            pltpu.SemaphoreType.DMA((2 * n_w,)),
            pltpu.SemaphoreType.DMA((4,)),
            pltpu.SemaphoreType.DMA((2,)),
        ],
        compiler_params=pltpu.CompilerParams(
            collective_id=1, has_side_effects=True, vmem_limit_bytes=32 * 2**20
        ),
        name="gather_hidden",
    )(tok, gains, wt, *weights)


def swap_kernel(n_w, has_y, *refs):
    x_ref = refs[0]
    own = refs[1 : 1 + n_w]
    y_ref = refs[1 + n_w : 1 + n_w + has_y]
    at = 1 + n_w + has_y
    o_ref = refs[at]
    other = refs[at + 1 : at + 1 + n_w]
    y_out = refs[at + 1 + n_w : at + 1 + n_w + has_y]
    ssem, rsem, wssem, wrsem, lsem = refs[at + 1 + n_w + has_y :]
    me, fs, z, x, k = place()
    bar = pltpu.get_barrier_semaphore()
    for i in range(1, H):
        signal((lax.rem(me + i, H), fs))
    if n_w or has_y:
        signal((me, 1 - fs))
    pl.semaphore_wait(bar, H - 1 + (1 if n_w or has_y else 0))
    copies = []
    for i in range(1, H):
        t = lax.rem(me + i, H)
        c = remote(x_ref.at[t], o_ref.at[me], ssem.at[i], rsem.at[i], (t, fs))
        c.start()
        copies.append(c)
    here = pltpu.make_async_copy(x_ref.at[me], o_ref.at[me], lsem)
    here.start()
    if has_y:
        c = remote(y_ref[0], y_out[0], ssem.at[0], rsem.at[0], (me, 1 - fs))
        c.start()
        copies.append(c)
    if n_w:
        first, second = weight_pull(own, other, k, fs, me, wssem, wrsem)
        for c in first:
            c.start()
        for i in range(n_w):
            first[i].wait_recv()
            second[i].start()
        for i in range(n_w):
            first[i].wait_send()
            second[i].wait()
    for c in copies:
        c.wait()
    here.wait()


def swap_call(cid, x, weights=(), y=None):
    n_w, has_y = len(weights), int(y is not None)
    args = [x, *weights] + ([y] if has_y else [])
    out = pl.pallas_call(
        functools.partial(swap_kernel, n_w, has_y),
        out_shape=[jax.ShapeDtypeStruct(a.shape, a.dtype) for a in args],
        in_specs=[ANY] * len(args),
        out_specs=[ANY] * len(args),
        scratch_shapes=[
            pltpu.SemaphoreType.DMA((H,)),
            pltpu.SemaphoreType.DMA((H,)),
            pltpu.SemaphoreType.DMA((max(1, 2 * n_w),)),
            pltpu.SemaphoreType.DMA((max(1, 2 * n_w),)),
            pltpu.SemaphoreType.DMA,
        ],
        compiler_params=pltpu.CompilerParams(collective_id=cid, has_side_effects=True),
        name="swap%d" % cid,
    )(*args)
    return out


def visible(j, i, rows, first_key):
    kpos = j * rows + lax.broadcasted_iota(jnp.int32, (rows, rows), 0)
    qpos = i * rows + lax.broadcasted_iota(jnp.int32, (rows, rows), 1)
    return (kpos <= qpos) & (kpos >= first_key)


def attend_kernel(
    h_ref, wt_ref, scale_ref, first_ref,
    o_ref, o32_ref, lse_ref, qt_ref, q_ref, kt_ref, k_ref, v_ref, raw_ref,
    k_sc, vt_sc,
):
    i = pl.program_id(0)
    last = pl.num_programs(0) - 1
    rows = h_ref.shape[1]
    qkv = dot(wt_ref[...], h_ref[0], NT)
    raw = qkv[:HD]
    raw_ref[0] = raw
    q32 = raw * scale_ref[...]
    qt = q32.astype(BF)
    qt_ref[0] = qt
    q_ref[0] = q32.T.astype(BF)
    kt32 = qkv[HD : 2 * HD]
    vt32 = qkv[2 * HD :]
    kt_ref[0] = kt32.astype(BF)
    key = kt32.T.astype(BF)
    k_ref[0] = key
    v_ref[0] = vt32.T.astype(BF)
    k_sc[i] = key
    vt_sc[i] = vt32.astype(BF)
    first_key = first_ref[0]

    def tile(masked, j, carry):
        run_max, run_sum, acc = carry
        s = dot(k_sc[j], qt)
        if masked:
            s = jnp.where(visible(j, i, rows, first_key), s, neg_big)
        new_max = jnp.maximum(run_max, jnp.max(s, axis=0, keepdims=True))
        p = jnp.exp(s - new_max)
        factor = jnp.exp(run_max - new_max)
        run_sum = run_sum * factor + jnp.sum(p, axis=0, keepdims=True)
        acc = acc * factor + dot(vt_sc[j], p.astype(BF))
        return new_max, run_sum, acc

    carry = (
        jnp.full((1, rows), neg_big, F32),
        jnp.zeros((1, rows), F32),
        jnp.zeros((HD, rows), F32),
    )
    carry = tile(True, i, carry)
    edge = (i == last) | (i == 0)
    carry = lax.fori_loop(1, jnp.where(edge, 1, i), functools.partial(tile, False), carry)
    carry = lax.fori_loop(
        jnp.where(edge, 1, i), i, functools.partial(tile, True), carry
    )
    carry = lax.fori_loop(0, jnp.minimum(i, 1), functools.partial(tile, True), carry)
    run_max, run_sum, acc = carry
    out = acc / run_sum
    o32_ref[0] = out
    o_ref[0] = out.astype(BF)
    lse_ref[0] = run_max + jnp.log(run_sum)


def attend_call(h_all, wt, scale_col, first_key):
    n, rows, width = h_all.shape

    def blk(*shape):
        return pl.BlockSpec((1, *shape), lambda i: (i, 0, 0))

    def whole(a):
        return pl.BlockSpec(a.shape, lambda i: (0,) * a.ndim)

    def out(dtype, *shape):
        return jax.ShapeDtypeStruct((n, *shape), dtype)

    return pl.pallas_call(
        attend_kernel,
        grid=(n,),
        out_shape=[
            out(BF, HD, rows), out(F32, HD, rows), out(F32, 1, rows), out(BF, HD, rows),
            out(BF, rows, HD), out(BF, HD, rows), out(BF, rows, HD), out(BF, rows, HD),
            out(F32, HD, rows),
        ],
        in_specs=[blk(rows, width), whole(wt), whole(scale_col), blk(1, rows)],
        out_specs=[
            blk(HD, rows), blk(HD, rows), blk(1, rows), blk(HD, rows), blk(rows, HD),
            blk(HD, rows), blk(rows, HD), blk(rows, HD), blk(HD, rows),
        ],
        scratch_shapes=[pltpu.VMEM((n, rows, HD), BF), pltpu.VMEM((n, HD, rows), BF)],
        compiler_params=pltpu.CompilerParams(vmem_limit_bytes=48 * 2**20),
        name="attend",
    )(h_all, wt, scale_col, first_key)


def attend_back_kernel(
    h_ref, scale_ref, first_ref, k_ref, v_ref, kt_ref, raw_ref, q_ref, qt_ref, gt_ref, o_ref, lse_ref,
    d_ref, dw_ref, ds_ref,
    g_sc, delta_sc, dq_sc, scale_sc,
):
    j = pl.program_id(0)
    last = pl.num_programs(0) - 1
    rows = h_ref.shape[1]

    @pl.when(j == 0)
    def _():
        def prepare(i, c):
            g = gt_ref[i].astype(F32)
            g_sc[i] = g.T.astype(BF)
            delta_sc[i] = jnp.sum(g * o_ref[i], axis=0, keepdims=True)
            dq_sc[i] = jnp.zeros((HD, rows), F32)
            return c

        lax.fori_loop(0, last + 1, prepare, 0)
        scale_sc[...] = jnp.zeros_like(scale_sc)
        dw_ref[...] = jnp.zeros_like(dw_ref)

    key, value, kt = k_ref[0], v_ref[0], kt_ref[0]

    def tile(masked, i, carry):
        dk, dv = carry
        s = dot(key, qt_ref[i])
        if masked:
            s = jnp.where(visible(j, i, rows, first_ref[i]), s, neg_big)
        p = jnp.exp(s - lse_ref[i])
        dv = dv + dot(p.astype(BF), g_sc[i])
        dp = dot(value, gt_ref[i])
        ds = (p * (dp - delta_sc[i])).astype(BF)
        dk = dk + dot(ds, q_ref[i])
        dq_sc[i] += dot(kt, ds)
        return dk, dv

    carry = (jnp.zeros((rows, HD), F32), jnp.zeros((rows, HD), F32))
    carry = tile(True, j, carry)
    inner_end = jnp.where(j == 0, 1, last)
    carry = lax.fori_loop(j + 1, inner_end, functools.partial(tile, False), carry)
    carry = lax.fori_loop(
        jnp.maximum(j + 1, inner_end), last + 1, functools.partial(tile, True), carry
    )
    dk, dv = carry
    dq = dq_sc[j]
    scale_sc[...] += dq * raw_ref[0]
    grads = jnp.concatenate([dq * scale_ref[...], dk.T, dv.T], axis=0).astype(BF)
    d_ref[0] = grads
    dw_ref[...] += dot(grads, h_ref[0])

    @pl.when(j == last)
    def _():
        ds_ref[...] = jnp.sum(scale_sc[...], axis=1, keepdims=True)


def attend_back_call(h_all, scale_col, first_key, k, v, kt, raw, q, qt, gt, o32, lse):
    n, rows, width = h_all.shape

    def blk(*shape):
        return pl.BlockSpec((1, *shape), lambda i: (i, 0, 0))

    def whole(a):
        return pl.BlockSpec(a.shape, lambda i: (0,) * a.ndim)

    return pl.pallas_call(
        attend_back_kernel,
        grid=(n,),
        out_shape=[
            jax.ShapeDtypeStruct((n, 3 * HD, rows), BF),
            jax.ShapeDtypeStruct((3 * HD, width), F32),
            jax.ShapeDtypeStruct((HD, 1), F32),
        ],
        in_specs=[
            blk(rows, width), whole(scale_col), whole(first_key), blk(rows, HD), blk(rows, HD),
            blk(HD, rows), blk(HD, rows), whole(q), whole(qt), whole(gt), whole(o32), whole(lse),
        ],
        out_specs=[
            blk(3 * HD, rows),
            pl.BlockSpec((3 * HD, width), lambda i: (0, 0)),
            pl.BlockSpec((HD, 1), lambda i: (0, 0)),
        ],
        scratch_shapes=[
            pltpu.VMEM((n, rows, HD), BF),
            pltpu.VMEM((n, 1, rows), F32),
            pltpu.VMEM((n, HD, rows), F32),
            pltpu.VMEM((HD, rows), F32),
        ],
        compiler_params=pltpu.CompilerParams(vmem_limit_bytes=48 * 2**20),
        name="attend_back",
    )(h_all, scale_col, first_key, k, v, kt, raw, q, qt, gt, o32, lse)


def joined(own, other, fs):
    return jnp.where(
        fs == 0, jnp.concatenate([own, other], axis=0), jnp.concatenate([other, own], axis=0)
    )


def fast_local(
    tokens, query_weight, key_weight, value_weight, out_weight, inner_weight, outer_weight,
    attn_gain, mlp_gain, query_scale, doc_starts, cotangent,
):
    me, fs = lax.axis_index("ctx"), lax.axis_index("fs")
    rows, width = tokens.shape[1:]
    tok = tokens[0]
    cot = cotangent[0]

    def head_columns(w):
        return lax.dynamic_slice(w, (0, me * HD), (w.shape[0], HD)).T

    wt = jnp.concatenate([head_columns(w) for w in (query_weight, key_weight, value_weight)], axis=0)
    gains = jnp.stack([attn_gain, mlp_gain])
    positions = jnp.arange(H * rows, dtype=jnp.int32)
    starts = doc_starts[0]
    first_key = jnp.max(
        jnp.where(starts[None, :] <= positions[:, None], starts[None, :], 0), axis=1
    ).reshape(H, 1, rows)
    scale_col = (query_scale / math.sqrt(HD))[:, None]

    h_all, wt_all, gain_full, out_o, inner_o, outer_o = gather_call(
        tok, gains, wt, (out_weight, inner_weight, outer_weight)
    )
    o_t, o32, lse, qt, q, kt, k, v, raw = attend_call(h_all, wt_all, scale_col, first_key)
    attn_t, query_o, key_o, value_o = swap_call(2, o_t, (query_weight, key_weight, value_weight))
    attn_t = attn_t.reshape(width, rows)

    out_full = joined(out_weight, out_o, fs)
    inner_full = joined(inner_weight, inner_o, fs)
    outer_full = joined(outer_weight, outer_o, fs)
    gain_one, gain_two = gain_full[0:1], gain_full[1:2]
    token_rows = tok.astype(F32)
    resid = token_rows + dot(attn_t, out_full, TN)
    scale_two = rms_scale(resid)
    normed_two = resid * scale_two
    hidden_two = (normed_two * gain_two).astype(BF)
    inner_pre = dot(hidden_two, inner_full)
    active = jax.nn.silu(inner_pre).astype(BF)
    result = (resid + dot(active, outer_full)).astype(BF)
    grad_active = dot(cot, outer_full, NT)
    sig = jax.nn.sigmoid(inner_pre)
    grad_inner_pre = (grad_active * sig * (1.0 + inner_pre * (1.0 - sig))).astype(BF)
    grad_hidden_two = dot(grad_inner_pre, inner_full, NT)
    grad_gain_two = jnp.sum(grad_hidden_two * normed_two, axis=0)
    grad_resid = (
        cot.astype(F32) + norm_back(grad_hidden_two * gain_two, normed_two, scale_two)
    ).astype(BF)
    grad_att_t = dot(out_full, grad_resid, NT).astype(BF).reshape(H, HD, rows)
    (g_t,) = swap_call(3, grad_att_t)
    grad_outer = dot(active, cot, TN).astype(BF)
    grad_inner = dot(hidden_two, grad_inner_pre, TN).astype(BF)
    grad_outw = dot(attn_t, grad_resid).astype(BF)

    d_all, dw, dscale = attend_back_call(
        h_all, scale_col, first_key, k, v, kt, raw, q, qt, g_t, o32, lse
    )
    half = width // 2
    dw_mine = lax.dynamic_slice(dw, (0, fs * half), (dw.shape[0], half))
    dw_send = lax.dynamic_slice(dw, (0, (1 - fs) * half), (dw.shape[0], half)).astype(BF)
    d_mine, dw_got = swap_call(4, d_all, (), dw_send)
    dw_sum = (dw_mine + dw_got.astype(F32)).astype(BF)
    d_mine = d_mine.reshape(H, 3, HD, rows)
    query_full = joined(query_weight, query_o, fs)
    key_full = joined(key_weight, key_o, fs)
    value_full = joined(value_weight, value_o, fs)
    grad_hidden_one = sum(
        dot(d_mine[:, i].reshape(width, rows), w, ((0,), (1,)))
        for i, w in enumerate((query_full, key_full, value_full))
    )
    scale_one = rms_scale(token_rows)
    normed_one = token_rows * scale_one
    grad_gain_one = jnp.sum(grad_hidden_one * normed_one, axis=0)
    grad_tokens = (
        grad_resid.astype(F32) + norm_back(grad_hidden_one * gain_one, normed_one, scale_one)
    ).astype(BF)

    dw_all = lax.all_gather(dw_sum, "ctx", axis=0, tiled=False).reshape(H, 3, HD, half)
    dw_qkv = [dw_all[:, i].reshape(width, half).T.astype(F32) for i in range(3)]
    dense = [
        lax.psum(lax.psum_scatter(g, "fs", scatter_dimension=0, tiled=True), "ctx").astype(F32)
        for g in (grad_outw, grad_inner, grad_outer)
    ]
    small = lax.psum(
        jnp.concatenate([grad_gain_one, grad_gain_two, dscale[:, 0]]), ("ctx", "fs")
    )
    gain_one_sum = lax.dynamic_slice(small, (fs * half,), (half,))
    gain_two_sum = lax.dynamic_slice(small, (width + fs * half,), (half,))
    scale_sum = small[2 * width :] / math.sqrt(HD)
    return (
        result[None], grad_tokens[None], *dw_qkv, *dense, gain_one_sum, gain_two_sum, scale_sum,
    )


def solution(mesh):
    placed = (
        P("fs", "ctx", None),
        P("fs", None),
        P("fs", None),
        P("fs", None),
        P("fs", None),
        P("fs", None),
        P("fs", None),
        P("fs"),
        P("fs"),
        P(),
        P("fs", None),
        P("fs", "ctx", None),
    )
    return jax.shard_map(
        fast_local if fast_fits(mesh) else general_local,
        mesh=mesh,
        in_specs=placed,
        out_specs=(
            P("fs", "ctx", None),
            P("fs", "ctx", None),
            P("fs", None),
            P("fs", None),
            P("fs", None),
            P("fs", None),
            P("fs", None),
            P("fs", None),
            P("fs"),
            P("fs"),
            P(),
        ),
        check_vma=False,
    )
```

```python
import functools
import math

import jax
import jax.numpy as jnp
from jax import lax
from jax.experimental import pallas as pl
from jax.experimental.pallas import tpu as pltpu
from jax.sharding import PartitionSpec as P

H = 16
HD = 80


epsilon = 1e-06
neg_big = -1e30


def passed_along(block, axis, distance):
    devices = range(lax.axis_size(axis))
    route = [((i - distance) % len(devices), i) for i in devices]
    return lax.ppermute(block, axis, route)


def shifted(value, axis, steps):
    count = lax.axis_size(axis)
    leading, last = (max(0, -steps), min(count, count - steps))
    return lax.ppermute(value, axis, [(source, source + steps) for source in range(leading, last)])


def rms_scale(values_in):
    return lax.rsqrt(jnp.mean(values_in * values_in, axis=-1, keepdims=True) + epsilon)


def norm_back(grad_normed, normed, scale_rows):
    inner_mean = jnp.mean(grad_normed * normed, axis=-1, keepdims=True)
    return scale_rows * (grad_normed - normed * inner_mean)


def segment_of(positions, starts_row):
    return jnp.sum((starts_row[None, :] <= positions[:, None]).astype(jnp.int32), axis=1) - 1


def block_mask(query_pos, query_seg, key_pos, key_seg):
    return (key_pos[None, :] <= query_pos[:, None]) & (key_seg[None, :] == query_seg[:, None])


def scores_of(query_block, key_block):
    return jnp.einsum("qhd,khd->hqk", query_block, key_block, preferred_element_type=jnp.float32)


def pass_grads(grad_key_acc, grad_value_acc):
    return (
        passed_along(grad_key_acc.astype(jnp.bfloat16), "ctx", 1).astype(grad_key_acc.dtype),
        passed_along(grad_value_acc.astype(jnp.bfloat16), "ctx", 1).astype(grad_value_acc.dtype),
    )


def general_local(
    tokens,
    query_weight,
    key_weight,
    value_weight,
    out_weight,
    inner_weight,
    outer_weight,
    attn_gain,
    mlp_gain,
    query_scale,
    doc_starts,
    cotangent,
):
    row_count = tokens.shape[1]
    model_width = tokens.shape[2]
    ctx_count = lax.axis_size("ctx")
    ctx_place = lax.axis_index("ctx")
    (
        query_full,
        key_full,
        value_full,
        out_full,
        inner_full,
        outer_full,
        attn_gain_full,
        mlp_gain_full,
    ) = (
        lax.all_gather(query_weight, "fs", axis=0, tiled=True),
        lax.all_gather(key_weight, "fs", axis=0, tiled=True),
        lax.all_gather(value_weight, "fs", axis=0, tiled=True),
        lax.all_gather(out_weight, "fs", axis=0, tiled=True),
        lax.all_gather(inner_weight, "fs", axis=0, tiled=True),
        lax.all_gather(outer_weight, "fs", axis=0, tiled=True),
        lax.all_gather(attn_gain, "fs", axis=0, tiled=True),
        lax.all_gather(mlp_gain, "fs", axis=0, tiled=True),
    )
    starts_row = doc_starts[0]
    local_pos = ctx_place * row_count + jnp.arange(row_count, dtype=jnp.int32)
    local_seg = segment_of(local_pos, starts_row)

    def heads_of(flat_block):
        return flat_block.reshape(row_count, H, HD)

    token_rows = tokens[0].astype(jnp.float32)
    scale_one = rms_scale(token_rows)
    normed_one = token_rows * scale_one
    gain_one = attn_gain_full.astype(jnp.float32)
    hidden_one = (normed_one * gain_one).astype(jnp.bfloat16)
    query_raw = jnp.dot(hidden_one, query_full, preferred_element_type=jnp.float32)
    scale_vec = jnp.tile(query_scale, H) / math.sqrt(HD)
    queries = heads_of((query_raw * scale_vec).astype(jnp.bfloat16))
    key_rows = jnp.dot(hidden_one, key_full, preferred_element_type=jnp.float32).astype(
        jnp.bfloat16
    )
    value_rows = jnp.dot(hidden_one, value_full, preferred_element_type=jnp.float32).astype(
        jnp.bfloat16
    )

    def key_info(turn_index):
        source = (ctx_place - turn_index) % ctx_count
        key_pos = source * row_count + jnp.arange(row_count, dtype=jnp.int32)
        return (source, key_pos, segment_of(key_pos, starts_row))

    def keep_state(state_in):
        return state_in

    def attend(softmax_state, key_flat, value_flat, turn_index):
        source, key_pos, key_seg = key_info(turn_index)

        def compute(state_in):
            run_max, run_sum, run_acc = state_in
            key_block = heads_of(key_flat)
            value_block = heads_of(value_flat)
            allowed = block_mask(local_pos, local_seg, key_pos, key_seg)
            scores = jnp.where(allowed[None], scores_of(queries, key_block), neg_big)
            new_max = jnp.maximum(run_max, jnp.max(scores, axis=-1))
            weights = jnp.where(allowed[None], jnp.exp(scores - new_max[..., None]), 0.0)
            factor = jnp.exp(run_max - new_max)
            run_sum = run_sum * factor + jnp.sum(weights, axis=-1)
            run_acc = run_acc * factor[..., None] + jnp.einsum(
                "hqk,khd->hqd",
                weights.astype(jnp.bfloat16),
                value_block,
                preferred_element_type=jnp.float32,
            )
            return (new_max, run_sum, run_acc)

        return lax.cond(source <= ctx_place, compute, keep_state, softmax_state)

    start_state = (
        jnp.full((H, row_count), neg_big, jnp.float32),
        jnp.zeros((H, row_count), jnp.float32),
        jnp.zeros((H, row_count, HD), jnp.float32),
    )
    start_state = attend(start_state, key_rows, value_rows, jnp.int32(0))
    stores = ()

    def forward_turn(turn_index, loop_state):
        key_block, value_block, softmax_state, kept = loop_state
        key_block, value_block = shifted((key_block, value_block), "ctx", 1)
        softmax_state = attend(softmax_state, key_block, value_block, turn_index)
        return (key_block, value_block, softmax_state, kept)

    loop_out = lax.fori_loop(
        1, ctx_count, forward_turn, (key_rows, value_rows, start_state, stores)
    )
    run_max, run_sum, run_acc = loop_out[2]
    stores = loop_out[3]
    log_total = run_max + jnp.log(run_sum)
    attn_heads = run_acc / run_sum[..., None]
    attn_low = (
        jnp.transpose(attn_heads, (1, 0, 2)).reshape(row_count, model_width).astype(jnp.bfloat16)
    )
    resid = token_rows + jnp.dot(attn_low, out_full, preferred_element_type=jnp.float32)
    scale_two = rms_scale(resid)
    normed_two = resid * scale_two
    gain_two = mlp_gain_full.astype(jnp.float32)
    hidden_two = (normed_two * gain_two).astype(jnp.bfloat16)
    inner_pre = jnp.dot(hidden_two, inner_full, preferred_element_type=jnp.float32)
    active = jax.nn.silu(inner_pre).astype(jnp.bfloat16)
    result = resid + jnp.dot(active, outer_full, preferred_element_type=jnp.float32)
    grad_out = cotangent[0]
    grad_active = jnp.dot(grad_out, outer_full.T, preferred_element_type=jnp.float32)
    grad_outer = jnp.dot(active.T, grad_out, preferred_element_type=jnp.float32)
    sigmoid_in = jax.nn.sigmoid(inner_pre)
    grad_inner_pre = (grad_active * sigmoid_in * (1.0 + inner_pre * (1.0 - sigmoid_in))).astype(
        jnp.bfloat16
    )
    grad_inner = jnp.dot(hidden_two.T, grad_inner_pre, preferred_element_type=jnp.float32)
    grad_hidden_two = jnp.dot(grad_inner_pre, inner_full.T, preferred_element_type=jnp.float32)
    grad_gain_two = jnp.sum(grad_hidden_two * normed_two, axis=0)
    grad_resid = grad_out.astype(jnp.float32) + norm_back(
        grad_hidden_two * gain_two, normed_two, scale_two
    )
    grad_resid_low = grad_resid.astype(jnp.bfloat16)
    grad_outw = jnp.dot(attn_low.T, grad_resid_low, preferred_element_type=jnp.float32)
    grad_attended = heads_of(
        jnp.dot(grad_resid_low, out_full.T, preferred_element_type=jnp.float32).astype(jnp.bfloat16)
    )
    row_delta = jnp.einsum("qhd,hqd->hq", grad_attended.astype(jnp.float32), attn_heads)

    def attend_back(grad_parts, key_flat, value_flat, turn_index):
        source, key_pos, key_seg = key_info(turn_index)

        def compute(parts_in):
            grad_query_acc, grad_key_acc, grad_value_acc = parts_in
            key_block = heads_of(key_flat)
            value_block = heads_of(value_flat)
            allowed = block_mask(local_pos, local_seg, key_pos, key_seg)
            scores = scores_of(queries, key_block)
            probabilities = jnp.where(allowed[None], jnp.exp(scores - log_total[..., None]), 0.0)
            grad_value_acc = grad_value_acc + jnp.einsum(
                "hqk,qhd->khd",
                probabilities.astype(jnp.bfloat16),
                grad_attended,
                preferred_element_type=jnp.float32,
            ).reshape(row_count, model_width)
            grad_probs = jnp.einsum(
                "qhd,khd->hqk", grad_attended, value_block, preferred_element_type=jnp.float32
            )
            grad_scores = (probabilities * (grad_probs - row_delta[..., None])).astype(jnp.bfloat16)
            grad_query_acc = grad_query_acc + jnp.einsum(
                "hqk,khd->qhd", grad_scores, key_block, preferred_element_type=jnp.float32
            )
            grad_key_acc = grad_key_acc + jnp.einsum(
                "hqk,qhd->khd", grad_scores, queries, preferred_element_type=jnp.float32
            ).reshape(row_count, model_width)
            return (grad_query_acc, grad_key_acc, grad_value_acc)

        return lax.cond(source <= ctx_place, compute, keep_state, grad_parts)

    def back_compute(turn_index, loop_state):
        key_block, value_block, grad_parts = loop_state
        grad_parts = attend_back(grad_parts, key_block, value_block, turn_index)
        grad_key_acc, grad_value_acc = pass_grads(grad_parts[1], grad_parts[2])
        return (key_block, value_block, (grad_parts[0], grad_key_acc, grad_value_acc))

    def back_turn(turn_index, loop_state):
        key_block, value_block, grad_parts = back_compute(turn_index, loop_state)
        key_block, value_block = shifted((key_block, value_block), "ctx", 1)
        return (key_block, value_block, grad_parts)

    zero_heads = jnp.zeros((row_count, H, HD), jnp.float32)
    zero_flat = jnp.zeros((row_count, model_width), jnp.float32)
    back_state = lax.fori_loop(
        0, ctx_count - 1, back_turn, (key_rows, value_rows, (zero_heads, zero_flat, zero_flat))
    )
    back_state = back_compute(jnp.int32(ctx_count - 1), back_state)
    grad_query_acc, grad_key_acc, grad_value_acc = back_state[2]
    grad_query_flat = grad_query_acc.reshape(row_count, model_width)
    grad_key_low = grad_key_acc.astype(jnp.bfloat16)
    grad_value_low = grad_value_acc.astype(jnp.bfloat16)
    grad_query_raw = (grad_query_flat * scale_vec).astype(jnp.bfloat16)
    grad_scale = jnp.sum(
        (grad_query_flat * query_raw).reshape(row_count, H, HD), axis=(0, 1)
    ) / math.sqrt(HD)
    grad_qw = jnp.dot(hidden_one.T, grad_query_raw, preferred_element_type=jnp.float32)
    grad_kw = jnp.dot(hidden_one.T, grad_key_low, preferred_element_type=jnp.float32)
    grad_vw = jnp.dot(hidden_one.T, grad_value_low, preferred_element_type=jnp.float32)
    grad_hidden_one = (
        jnp.dot(grad_query_raw, query_full.T, preferred_element_type=jnp.float32)
        + jnp.dot(grad_key_low, key_full.T, preferred_element_type=jnp.float32)
        + jnp.dot(grad_value_low, value_full.T, preferred_element_type=jnp.float32)
    )
    grad_gain_one = jnp.sum(grad_hidden_one * normed_one, axis=0)
    grad_tokens = grad_resid_low.astype(jnp.float32) + norm_back(
        grad_hidden_one * gain_one, normed_one, scale_one
    )
    shard_count = lax.axis_size("fs")
    scale_rows = jnp.broadcast_to(grad_scale[None, :], (shard_count, grad_scale.shape[0]))
    shares = (
        lax.psum_scatter(
            grad_qw.astype(jnp.bfloat16), "fs", scatter_dimension=0, tiled=True
        ).astype(jnp.float32),
        lax.psum_scatter(
            grad_kw.astype(jnp.bfloat16), "fs", scatter_dimension=0, tiled=True
        ).astype(jnp.float32),
        lax.psum_scatter(
            grad_vw.astype(jnp.bfloat16), "fs", scatter_dimension=0, tiled=True
        ).astype(jnp.float32),
        lax.psum_scatter(
            grad_outw.astype(jnp.bfloat16), "fs", scatter_dimension=0, tiled=True
        ).astype(jnp.float32),
        lax.psum_scatter(
            grad_inner.astype(jnp.bfloat16), "fs", scatter_dimension=0, tiled=True
        ).astype(jnp.float32),
        lax.psum_scatter(
            grad_outer.astype(jnp.bfloat16), "fs", scatter_dimension=0, tiled=True
        ).astype(jnp.float32),
        lax.psum_scatter(
            grad_gain_one.astype(jnp.bfloat16), "fs", scatter_dimension=0, tiled=True
        ).astype(jnp.float32),
        lax.psum_scatter(
            grad_gain_two.astype(jnp.bfloat16), "fs", scatter_dimension=0, tiled=True
        ).astype(jnp.float32),
        lax.psum_scatter(
            scale_rows.astype(jnp.bfloat16), "fs", scatter_dimension=0, tiled=True
        ).astype(jnp.float32),
    )
    totals = (
        lax.psum(shares[0].astype(jnp.bfloat16), "ctx").astype(jnp.float32),
        lax.psum(shares[1].astype(jnp.bfloat16), "ctx").astype(jnp.float32),
        lax.psum(shares[2].astype(jnp.bfloat16), "ctx").astype(jnp.float32),
        lax.psum(shares[3].astype(jnp.bfloat16), "ctx").astype(jnp.float32),
        lax.psum(shares[4].astype(jnp.bfloat16), "ctx").astype(jnp.float32),
        lax.psum(shares[5].astype(jnp.bfloat16), "ctx").astype(jnp.float32),
        lax.psum(shares[6].astype(jnp.bfloat16), "ctx").astype(jnp.float32),
        lax.psum(shares[7].astype(jnp.bfloat16), "ctx").astype(jnp.float32),
        lax.psum(shares[8].astype(jnp.bfloat16), "ctx").astype(jnp.float32),
    )
    return (
        result[None].astype(jnp.bfloat16),
        grad_tokens[None].astype(jnp.bfloat16),
        totals[0],
        totals[1],
        totals[2],
        totals[3],
        totals[4],
        totals[5],
        totals[6],
        totals[7],
        totals[8][0],
    )


MESH = pl.DeviceIdType.MESH
ANY = pl.BlockSpec(memory_space=pl.ANY)
VMEM = pl.BlockSpec(memory_space=pltpu.VMEM)
BF = jnp.bfloat16
F32 = jnp.float32


def fast_fits(mesh):
    return mesh.shape["ctx"] == H and mesh.shape["fs"] == 2


def remote(src, dst, ssem, rsem, target):
    return pltpu.make_async_remote_copy(
        src_ref=src, dst_ref=dst, send_sem=ssem, recv_sem=rsem, device_id=target, device_id_type=MESH
    )


def signal(target):
    pl.semaphore_signal(
        pltpu.get_barrier_semaphore(), inc=1, device_id=target, device_id_type=MESH
    )


def place():
    me = lax.axis_index("ctx")
    return me, lax.axis_index("fs"), me // 4, lax.rem(me // 2, 2), lax.rem(me, 2)


def dot(a, b, dims=((1,), (0,))):
    return lax.dot_general(a, b, (dims, ((), ())), preferred_element_type=F32)


NT = ((1,), (1,))
TN = ((0,), (0,))


LOG2E = math.log2(math.e)
UNITS = H // 2


def weight_pull(own, other, k, fs, me, ssem, rsem):
    half = own[0].shape[0] // 2
    rows = pl.ds(pl.multiple_of(k * half, 64), half)
    yn = (me, 1 - fs)
    sib = (me + 1 - 2 * k, fs)
    n = len(own)
    first = [remote(own[i].at[rows], other[i].at[rows], ssem.at[i], rsem.at[i], yn) for i in range(n)]
    second = [
        remote(other[i].at[rows], other[i].at[rows], ssem.at[n + i], rsem.at[n + i], sib)
        for i in range(n)
    ]
    return first, second


def visible(j, i, rows, first_key):
    kpos = j * rows + lax.broadcasted_iota(jnp.int32, (rows, rows), 0)
    qpos = i * rows + lax.broadcasted_iota(jnp.int32, (rows, rows), 1)
    return (kpos <= qpos) & (kpos >= first_key)


def forward_kernel(n_w, tok_ref, gain_ref, wt_ref, scale_ref, first_ref, *rest):
    own = rest[:n_w]
    at = n_w
    h_all, gain_full, attn_ref = rest[at : at + 3]
    o32_ref, lse_ref, qt_ref, q_ref, kt_ref, k_ref, v_ref, raw_ref = rest[at + 3 : at + 11]
    other = rest[at + 11 : at + 11 + n_w]
    (
        wt_all, gain_own, gain_other, o_sc, vt_sc, m_sc, l_sc, acc_sc,
        ssem, rsem, osend, orecv, wssem, wrsem, ysem, lsem,
    ) = rest[at + 11 + n_w :]
    me, fs, z, x, k = place()
    sib, xn, yn = (me + 1 - 2 * k, fs), (me + 2 - 4 * x, fs), (me, 1 - fs)
    up, dn = (me + 4, fs), (me - 4, fs)
    rows = tok_ref.shape[0]
    unit_rows = 2 * rows
    bar = pltpu.get_barrier_semaphore()
    for i in range(1, H):
        signal((lax.rem(me + i, H), fs))
    signal(yn)
    gain_own[...] = gain_ref[...]
    tokens = tok_ref[...].astype(F32)
    normed = tokens * lax.rsqrt(jnp.mean(tokens * tokens, axis=-1, keepdims=True) + epsilon)
    pl.semaphore_wait(bar, H)

    gain_copy = remote(gain_own, gain_other, ysem.at[0], ysem.at[1], yn)
    gain_copy.start()
    half = wt_ref.shape[1]
    columns = pl.ds(pl.multiple_of(fs * half, 128), half)
    wt_copy = remote(wt_ref, wt_all.at[:, columns], ysem.at[2], ysem.at[3], yn)
    wt_copy.start()
    wt_here = pltpu.make_async_copy(wt_ref, wt_all.at[:, columns], lsem.at[0])
    wt_here.start()
    first, second = weight_pull(own, other, k, fs, me, wssem, wrsem)
    gain_copy.wait()
    g_here = gain_own[...].astype(F32)
    g_there = gain_other[...].astype(F32)
    gains = jnp.where(
        fs == 0,
        jnp.concatenate([g_here, g_there], axis=1),
        jnp.concatenate([g_there, g_here], axis=1),
    )
    gain_full[...] = gains
    my_rows = pl.ds(pl.multiple_of(k * rows, rows), rows)
    h_all[me // 2, my_rows, :] = (normed * gains[0:1]).astype(BF)

    def slot(s):
        return h_all.at[s // 2, pl.ds(pl.multiple_of(lax.rem(s, 2) * rows, rows), rows)]

    def cp(s, t, si):
        return remote(slot(s), slot(s), ssem.at[si], rsem.at[s], t)

    cp(me, xn, 0).start()

    @pl.when(z < 3)
    def _():
        cp(me, up, 1).start()

    @pl.when(z > 0)
    def _():
        cp(me, dn, 2).start()

    cp(me, sib, 3).start()
    for c in first:
        c.start()
    wt_here.wait()
    wt_copy.wait()

    def project(u):
        qkv = dot(wt_all[...], h_all[u], NT)
        raw = qkv[:HD]
        raw_ref[u] = raw
        q32 = raw * scale_ref[...]
        qt_ref[u] = (q32 * LOG2E).astype(BF)
        q_ref[u] = q32.T.astype(BF)
        kt = qkv[HD : 2 * HD]
        vt = qkv[2 * HD :]
        kt_ref[u] = kt.astype(BF)
        k_ref[u] = kt.T.astype(BF)
        v_ref[u] = vt.T.astype(BF)
        vt_sc[u] = vt.astype(BF)
        m_sc[u] = jnp.full((1, unit_rows), neg_big, F32)
        l_sc[u] = jnp.zeros((1, unit_rows), F32)
        acc_sc[u] = jnp.zeros((HD, unit_rows), F32)

    def pair(j, i):
        s = dot(k_ref[j], qt_ref[i])
        s = jnp.where(visible(j, i, unit_rows, first_ref[i]), s, neg_big)
        run_max = m_sc[i]
        new_max = jnp.maximum(run_max, jnp.max(s, axis=0, keepdims=True))
        p = jnp.exp2(s - new_max)
        factor = jnp.exp2(run_max - new_max)
        l_sc[i] = l_sc[i] * factor + jnp.sum(p, axis=0, keepdims=True)
        acc_sc[i] = acc_sc[i] * factor + dot(vt_sc[j], p.astype(BF))
        m_sc[i] = new_max

    def when_here(uz, ux):
        return 4 * jnp.maximum(uz - z, z - uz) + 2 * jnp.maximum(ux - x, x - ux) + (uz + 4 - z) // 5

    def process(uz, ux):
        u = uz * 2 + ux
        cp(u * 2 + 1 - k, sib, 0).wait_recv()
        project(u)
        pair(u, u)
        mine = when_here(uz, ux)

        def earlier(e, c):
            @pl.when(when_here(e // 2, lax.rem(e, 2)) < mine)
            def _():
                pair(jnp.minimum(e, u), jnp.maximum(e, u))

            return c

        lax.fori_loop(0, UNITS, earlier, 0)

    xo = me + 2 - 4 * x

    def column_arrival(d):
        a = 4 + (d - 1) * 6

        @pl.when(z >= d)
        def _():
            s = me - 4 * d
            cp(s, dn, a).wait_recv()

            @pl.when(z < 3)
            def _():
                cp(s, up, a).start()

            cp(s, xn, a + 1).start()
            cp(s, sib, a + 2).start()

        @pl.when(z + d <= 3)
        def _():
            s = me + 4 * d
            cp(s, up, a + 3).wait_recv()

            @pl.when(z > 0)
            def _():
                cp(s, dn, a + 3).start()

            cp(s, xn, a + 4).start()
            cp(s, sib, a + 5).start()

    def across_arrival(d):
        @pl.when(z >= d)
        def _():
            s = xo - 4 * d
            cp(s, xn, 0).wait_recv()
            cp(s, sib, 22 + z - d).start()

        @pl.when((z + d <= 3) & (d > 0))
        def _():
            s = xo + 4 * d
            cp(s, xn, 0).wait_recv()
            cp(s, sib, 22 + z + d).start()

    def step(d, c):
        @pl.when((d >= 1) & (d <= 3))
        def _():
            column_arrival(d)

        @pl.when(d >= 1)
        def _():
            across_arrival(d - 1)

        for i in range(n_w):
            if i < 4:

                @pl.when(d == i + 1)
                def _(i=i):
                    first[i].wait_recv()
                    second[i].start()

        def compute(n, c2):
            across = 1 - n // 2
            dd = d - across
            uz = z + dd * (2 * lax.rem(n, 2) - 1)
            ux = x + across * (1 - 2 * x)
            ok = (dd >= 0) & (dd <= 3) & (uz >= 0) & (uz <= 3)
            ok = ok & ((dd > 0) | (lax.rem(n, 2) == 0))

            @pl.when(ok)
            def _():
                process(uz, ux)

            return c2

        lax.fori_loop(0, 4, compute, 0)
        return c

    lax.fori_loop(0, 5, step, 0)

    def out_copy(b):
        u = b // 2
        lanes = pl.ds(pl.multiple_of(lax.rem(b, 2) * rows, 128), rows)
        return o_sc.at[u, :, lanes]

    def finish(n, c):
        u = lax.rem(me // 2 + n, UNITS)
        out = acc_sc[u] / l_sc[u]
        o32_ref[u] = out
        o_sc[u] = out.astype(BF)
        lse_ref[u] = m_sc[u] + jnp.log2(l_sc[u])

        def send(e, c2):
            b = u * 2 + e

            @pl.when(b != me)
            def _():
                remote(out_copy(b), attn_ref.at[me], osend.at[b], orecv.at[me], (b, fs)).start()

            @pl.when(b == me)
            def _():
                pltpu.make_async_copy(out_copy(b), attn_ref.at[me], lsem.at[1]).start()

            return c2

        return lax.fori_loop(0, 2, send, c)

    lax.fori_loop(0, UNITS, finish, 0)
    for i in range(4, n_w):
        first[i].wait_recv()
        second[i].start()

    def taken(b, c):
        @pl.when(b != me)
        def _():
            remote(out_copy(b), attn_ref.at[b], osend.at[b], orecv.at[b], (b, fs)).wait()

        return c

    lax.fori_loop(0, H, taken, 0)
    pltpu.make_async_copy(out_copy(me), attn_ref.at[me], lsem.at[1]).wait()
    cp(me, xn, 0).wait_send()

    @pl.when(z < 3)
    def _():
        cp(me, up, 1).wait_send()

    @pl.when(z > 0)
    def _():
        cp(me, dn, 2).wait_send()

    cp(me, sib, 3).wait_send()

    def sent(d, c):
        a = 4 + (d - 1) * 6

        @pl.when(z >= d)
        def _():
            s = me - 4 * d

            @pl.when(z < 3)
            def _():
                cp(s, up, a).wait_send()

            cp(s, xn, a + 1).wait_send()
            cp(s, sib, a + 2).wait_send()

        @pl.when(z + d <= 3)
        def _():
            s = me + 4 * d

            @pl.when(z > 0)
            def _():
                cp(s, dn, a + 3).wait_send()

            cp(s, xn, a + 4).wait_send()
            cp(s, sib, a + 5).wait_send()

        return c

    lax.fori_loop(1, 4, sent, 0)

    def sent_across(zz, c):
        cp(xo + 4 * (zz - z), sib, 22 + zz).wait_send()
        return c

    lax.fori_loop(0, 4, sent_across, 0)
    for i in range(n_w):
        first[i].wait_send()
        second[i].wait()


def forward_call(tok, gains, wt, scale_col, first_key, weights):
    n_w = len(weights)
    rows, width = tok.shape
    ur = 2 * rows

    def out(dtype, *shape):
        return jax.ShapeDtypeStruct((UNITS, *shape), dtype)

    shapes = [
        out(BF, ur, width),
        jax.ShapeDtypeStruct((gains.shape[0], 2 * gains.shape[1]), F32),
        jax.ShapeDtypeStruct((H, HD, rows), BF),
        out(F32, HD, ur), out(F32, 1, ur), out(BF, HD, ur), out(BF, ur, HD), out(BF, HD, ur),
        out(BF, ur, HD), out(BF, ur, HD), out(F32, HD, ur),
    ] + [jax.ShapeDtypeStruct(w.shape, BF) for w in weights]
    return pl.pallas_call(
        functools.partial(forward_kernel, n_w),
        out_shape=shapes,
        in_specs=[VMEM] * 5 + [ANY] * n_w,
        out_specs=[VMEM, VMEM, ANY] + [VMEM] * 8 + [ANY] * n_w,
        scratch_shapes=[
            pltpu.VMEM((wt.shape[0], 2 * wt.shape[1]), BF),
            pltpu.VMEM(gains.shape, BF),
            pltpu.VMEM(gains.shape, BF),
            pltpu.VMEM((UNITS, HD, ur), BF),
            pltpu.VMEM((UNITS, HD, ur), BF),
            pltpu.VMEM((UNITS, 1, ur), F32),
            pltpu.VMEM((UNITS, 1, ur), F32),
            pltpu.VMEM((UNITS, HD, ur), F32),
            pltpu.SemaphoreType.DMA((26,)),
            pltpu.SemaphoreType.DMA((H,)),
            pltpu.SemaphoreType.DMA((H,)),
            pltpu.SemaphoreType.DMA((H,)),
            pltpu.SemaphoreType.DMA((2 * n_w,)),
            pltpu.SemaphoreType.DMA((2 * n_w,)),
            pltpu.SemaphoreType.DMA((4,)),
            pltpu.SemaphoreType.DMA((2,)),
        ],
        compiler_params=pltpu.CompilerParams(
            collective_id=1, has_side_effects=True, vmem_limit_bytes=56 * 2**20
        ),
        name="forward",
    )(tok, gains, wt, scale_col, first_key, *weights)


def swap_kernel(n_w, has_y, *refs):
    x_ref = refs[0]
    own = refs[1 : 1 + n_w]
    y_ref = refs[1 + n_w : 1 + n_w + has_y]
    at = 1 + n_w + has_y
    o_ref = refs[at]
    other = refs[at + 1 : at + 1 + n_w]
    y_out = refs[at + 1 + n_w : at + 1 + n_w + has_y]
    ssem, rsem, wssem, wrsem, lsem = refs[at + 1 + n_w + has_y :]
    me, fs, z, x, k = place()
    bar = pltpu.get_barrier_semaphore()
    for i in range(1, H):
        signal((lax.rem(me + i, H), fs))
    if n_w or has_y:
        signal((me, 1 - fs))
    pl.semaphore_wait(bar, H - 1 + (1 if n_w or has_y else 0))
    copies = []
    for i in range(1, H):
        t = lax.rem(me + i, H)
        c = remote(x_ref.at[t], o_ref.at[me], ssem.at[i], rsem.at[i], (t, fs))
        c.start()
        copies.append(c)
    here = pltpu.make_async_copy(x_ref.at[me], o_ref.at[me], lsem)
    here.start()
    if has_y:
        c = remote(y_ref[0], y_out[0], ssem.at[0], rsem.at[0], (me, 1 - fs))
        c.start()
        copies.append(c)
    if n_w:
        first, second = weight_pull(own, other, k, fs, me, wssem, wrsem)
        for c in first:
            c.start()
        for i in range(n_w):
            first[i].wait_recv()
            second[i].start()
        for i in range(n_w):
            first[i].wait_send()
            second[i].wait()
    for c in copies:
        c.wait()
    here.wait()


def swap_call(cid, x, weights=(), y=None):
    n_w, has_y = len(weights), int(y is not None)
    args = [x, *weights] + ([y] if has_y else [])
    out = pl.pallas_call(
        functools.partial(swap_kernel, n_w, has_y),
        out_shape=[jax.ShapeDtypeStruct(a.shape, a.dtype) for a in args],
        in_specs=[ANY] * len(args),
        out_specs=[ANY] * len(args),
        scratch_shapes=[
            pltpu.SemaphoreType.DMA((H,)),
            pltpu.SemaphoreType.DMA((H,)),
            pltpu.SemaphoreType.DMA((max(1, 2 * n_w),)),
            pltpu.SemaphoreType.DMA((max(1, 2 * n_w),)),
            pltpu.SemaphoreType.DMA,
        ],
        compiler_params=pltpu.CompilerParams(collective_id=cid, has_side_effects=True),
        name="swap%d" % cid,
    )(*args)
    return out


def backward_kernel(
    h_ref, scale_ref, first_ref, k_ref, v_ref, kt_ref, raw_ref, q_ref, qt_ref, gt_ref, o_ref, lse_ref,
    d_ref, dw_ref, ds_ref,
    g_sc, delta_sc, dq_sc, scale_sc, dk_sc, dv_sc,
):
    units, rows = h_ref.shape[:2]

    def prepare(i, c):
        g = jnp.concatenate([gt_ref[2 * i], gt_ref[2 * i + 1]], axis=1).astype(F32)
        g_sc[i] = g.T.astype(BF)
        delta_sc[i] = jnp.sum(g * o_ref[i], axis=0, keepdims=True)
        dq_sc[i] = jnp.zeros((HD, rows), F32)
        return c

    lax.fori_loop(0, units, prepare, 0)
    scale_sc[...] = jnp.zeros_like(scale_sc)
    dw_ref[...] = jnp.zeros_like(dw_ref)

    def pair(masked, j, i):
        s = dot(k_ref[j], qt_ref[i])
        if masked:
            s = jnp.where(visible(j, i, rows, first_ref[i]), s, neg_big)
        p = jnp.exp2(s - lse_ref[i])
        dv_sc[...] += dot(p.astype(BF), g_sc[i])
        g = jnp.concatenate([gt_ref[2 * i], gt_ref[2 * i + 1]], axis=1)
        dp = dot(v_ref[j], g)
        ds = (p * (dp - delta_sc[i])).astype(BF)
        dk_sc[...] += dot(ds, q_ref[i])
        dq_sc[i] += dot(kt_ref[j], ds)

    def column(j, c):
        dk_sc[...] = jnp.zeros_like(dk_sc)
        dv_sc[...] = jnp.zeros_like(dv_sc)
        pair(True, j, j)

        def plain(i, c2):
            pair(False, j, i)
            return c2

        def edge(i, c2):
            pair(True, j, i)
            return c2

        end = jnp.where(j == 0, 1, units - 1)
        lax.fori_loop(j + 1, end, plain, 0)
        lax.fori_loop(jnp.maximum(j + 1, end), units, edge, 0)
        dq = dq_sc[j]
        scale_sc[...] += dq * raw_ref[j]
        grads = jnp.concatenate(
            [dq * scale_ref[...], dk_sc[...].T, dv_sc[...].T], axis=0
        ).astype(BF)
        d_ref[2 * j] = grads[:, : rows // 2]
        d_ref[2 * j + 1] = grads[:, rows // 2 :]
        dw_ref[...] += dot(grads, h_ref[j])
        return c

    lax.fori_loop(0, units, column, 0)
    ds_ref[...] = jnp.sum(scale_sc[...], axis=1, keepdims=True)


def backward_call(h_all, scale_col, first_key, k, v, kt, raw, q, qt, gt, o32, lse):
    n, rows, width = h_all.shape
    args = (h_all, scale_col, first_key, k, v, kt, raw, q, qt, gt, o32, lse)
    return pl.pallas_call(
        backward_kernel,
        out_shape=[
            jax.ShapeDtypeStruct((H, 3 * HD, rows // 2), BF),
            jax.ShapeDtypeStruct((3 * HD, width), F32),
            jax.ShapeDtypeStruct((HD, 1), F32),
        ],
        in_specs=[VMEM] * len(args),
        out_specs=[VMEM] * 3,
        scratch_shapes=[
            pltpu.VMEM((n, rows, HD), BF),
            pltpu.VMEM((n, 1, rows), F32),
            pltpu.VMEM((n, HD, rows), F32),
            pltpu.VMEM((HD, rows), F32),
            pltpu.VMEM((rows, HD), F32),
            pltpu.VMEM((rows, HD), F32),
        ],
        compiler_params=pltpu.CompilerParams(vmem_limit_bytes=56 * 2**20),
        cost_estimate=pl.CostEstimate(flops=40 * 10**9, bytes_accessed=30 * 2**20, transcendentals=10**7),
        name="backward",
    )(*args)


def joined(own, other, fs):
    return jnp.where(
        fs == 0, jnp.concatenate([own, other], axis=0), jnp.concatenate([other, own], axis=0)
    )


def fast_local(
    tokens, query_weight, key_weight, value_weight, out_weight, inner_weight, outer_weight,
    attn_gain, mlp_gain, query_scale, doc_starts, cotangent,
):
    me, fs = lax.axis_index("ctx"), lax.axis_index("fs")
    rows, width = tokens.shape[1:]
    tok = tokens[0]
    cot = cotangent[0]

    def head_columns(w):
        return lax.dynamic_slice(w, (0, me * HD), (w.shape[0], HD)).T

    wt = jnp.concatenate([head_columns(w) for w in (query_weight, key_weight, value_weight)], axis=0)
    gains = jnp.stack([attn_gain, mlp_gain])
    positions = jnp.arange(H * rows, dtype=jnp.int32)
    starts = doc_starts[0]
    first_key = jnp.max(
        jnp.where(starts[None, :] <= positions[:, None], starts[None, :], 0), axis=1
    ).reshape(UNITS, 1, 2 * rows)
    scale_col = (query_scale / math.sqrt(HD))[:, None]

    (
        h_all, gain_full, attn_t, o32, lse, qt, q, kt, k, v, raw,
        out_o, inner_o, outer_o, query_o, key_o,
    ) = forward_call(
        tok, gains, wt, scale_col, first_key,
        (out_weight, inner_weight, outer_weight, query_weight, key_weight),
    )
    attn_t = attn_t.reshape(width, rows)

    out_full = joined(out_weight, out_o, fs)
    inner_full = joined(inner_weight, inner_o, fs)
    outer_full = joined(outer_weight, outer_o, fs)
    gain_one, gain_two = gain_full[0:1], gain_full[1:2]
    token_rows = tok.astype(F32)
    resid = token_rows + dot(attn_t, out_full, TN)
    scale_two = rms_scale(resid)
    normed_two = resid * scale_two
    hidden_two = (normed_two * gain_two).astype(BF)
    inner_pre = dot(hidden_two, inner_full)
    active = jax.nn.silu(inner_pre).astype(BF)
    result = (resid + dot(active, outer_full)).astype(BF)
    grad_active = dot(cot, outer_full, NT)
    sig = jax.nn.sigmoid(inner_pre)
    grad_inner_pre = (grad_active * sig * (1.0 + inner_pre * (1.0 - sig))).astype(BF)
    grad_hidden_two = dot(grad_inner_pre, inner_full, NT)
    grad_gain_two = jnp.sum(grad_hidden_two * normed_two, axis=0)
    grad_resid = (
        cot.astype(F32) + norm_back(grad_hidden_two * gain_two, normed_two, scale_two)
    ).astype(BF)
    grad_att_t = dot(out_full, grad_resid, NT).astype(BF).reshape(H, HD, rows)
    g_t, value_o = swap_call(3, grad_att_t, (value_weight,))
    grad_outer = dot(active, cot, TN).astype(BF)
    grad_inner = dot(hidden_two, grad_inner_pre, TN).astype(BF)
    grad_outw = dot(attn_t, grad_resid).astype(BF)

    d_all, dw, dscale = backward_call(
        h_all, scale_col, first_key, k, v, kt, raw, q, qt, g_t, o32, lse
    )
    half = width // 2
    dw_mine = lax.dynamic_slice(dw, (0, fs * half), (dw.shape[0], half))
    dw_send = lax.dynamic_slice(dw, (0, (1 - fs) * half), (dw.shape[0], half)).astype(BF)
    d_mine, dw_got = swap_call(4, d_all, (), dw_send)
    dw_sum = (dw_mine + dw_got.astype(F32)).astype(BF)
    d_mine = d_mine.reshape(H, 3, HD, rows)
    query_full = joined(query_weight, query_o, fs)
    key_full = joined(key_weight, key_o, fs)
    value_full = joined(value_weight, value_o, fs)
    grad_hidden_one = sum(
        dot(d_mine[:, i].reshape(width, rows), w, ((0,), (1,)))
        for i, w in enumerate((query_full, key_full, value_full))
    )
    scale_one = rms_scale(token_rows)
    normed_one = token_rows * scale_one
    grad_gain_one = jnp.sum(grad_hidden_one * normed_one, axis=0)
    grad_tokens = (
        grad_resid.astype(F32) + norm_back(grad_hidden_one * gain_one, normed_one, scale_one)
    ).astype(BF)

    dw_all = lax.all_gather(dw_sum, "ctx", axis=0, tiled=False).reshape(H, 3, HD, half)
    dw_qkv = [dw_all[:, i].reshape(width, half).T.astype(F32) for i in range(3)]
    dense = [
        lax.psum(lax.psum_scatter(g, "fs", scatter_dimension=0, tiled=True), "ctx").astype(F32)
        for g in (grad_outw, grad_inner, grad_outer)
    ]
    small = lax.psum(
        jnp.concatenate([grad_gain_one, grad_gain_two, dscale[:, 0]]), ("ctx", "fs")
    )
    gain_one_sum = lax.dynamic_slice(small, (fs * half,), (half,))
    gain_two_sum = lax.dynamic_slice(small, (width + fs * half,), (half,))
    scale_sum = small[2 * width :] / math.sqrt(HD)
    return (
        result[None], grad_tokens[None], *dw_qkv, *dense, gain_one_sum, gain_two_sum, scale_sum,
    )


def solution(mesh):
    placed = (
        P("fs", "ctx", None),
        P("fs", None),
        P("fs", None),
        P("fs", None),
        P("fs", None),
        P("fs", None),
        P("fs", None),
        P("fs"),
        P("fs"),
        P(),
        P("fs", None),
        P("fs", "ctx", None),
    )
    return jax.shard_map(
        fast_local if fast_fits(mesh) else general_local,
        mesh=mesh,
        in_specs=placed,
        out_specs=(
            P("fs", "ctx", None),
            P("fs", "ctx", None),
            P("fs", None),
            P("fs", None),
            P("fs", None),
            P("fs", None),
            P("fs", None),
            P("fs", None),
            P("fs"),
            P("fs"),
            P(),
        ),
        check_vma=False,
    )
```

```python
import functools
import math

import jax
import jax.numpy as jnp
from jax import lax
from jax.experimental import pallas as pl
from jax.experimental.pallas import tpu as pltpu
from jax.sharding import PartitionSpec as P

H = 16
HD = 80


epsilon = 1e-06
neg_big = -1e30


def passed_along(block, axis, distance):
    devices = range(lax.axis_size(axis))
    route = [((i - distance) % len(devices), i) for i in devices]
    return lax.ppermute(block, axis, route)


def shifted(value, axis, steps):
    count = lax.axis_size(axis)
    leading, last = (max(0, -steps), min(count, count - steps))
    return lax.ppermute(value, axis, [(source, source + steps) for source in range(leading, last)])


def rms_scale(values_in):
    return lax.rsqrt(jnp.mean(values_in * values_in, axis=-1, keepdims=True) + epsilon)


def norm_back(grad_normed, normed, scale_rows):
    inner_mean = jnp.mean(grad_normed * normed, axis=-1, keepdims=True)
    return scale_rows * (grad_normed - normed * inner_mean)


def segment_of(positions, starts_row):
    return jnp.sum((starts_row[None, :] <= positions[:, None]).astype(jnp.int32), axis=1) - 1


def block_mask(query_pos, query_seg, key_pos, key_seg):
    return (key_pos[None, :] <= query_pos[:, None]) & (key_seg[None, :] == query_seg[:, None])


def scores_of(query_block, key_block):
    return jnp.einsum("qhd,khd->hqk", query_block, key_block, preferred_element_type=jnp.float32)


def pass_grads(grad_key_acc, grad_value_acc):
    return (
        passed_along(grad_key_acc.astype(jnp.bfloat16), "ctx", 1).astype(grad_key_acc.dtype),
        passed_along(grad_value_acc.astype(jnp.bfloat16), "ctx", 1).astype(grad_value_acc.dtype),
    )


def general_local(
    tokens,
    query_weight,
    key_weight,
    value_weight,
    out_weight,
    inner_weight,
    outer_weight,
    attn_gain,
    mlp_gain,
    query_scale,
    doc_starts,
    cotangent,
):
    row_count = tokens.shape[1]
    model_width = tokens.shape[2]
    ctx_count = lax.axis_size("ctx")
    ctx_place = lax.axis_index("ctx")
    (
        query_full,
        key_full,
        value_full,
        out_full,
        inner_full,
        outer_full,
        attn_gain_full,
        mlp_gain_full,
    ) = (
        lax.all_gather(query_weight, "fs", axis=0, tiled=True),
        lax.all_gather(key_weight, "fs", axis=0, tiled=True),
        lax.all_gather(value_weight, "fs", axis=0, tiled=True),
        lax.all_gather(out_weight, "fs", axis=0, tiled=True),
        lax.all_gather(inner_weight, "fs", axis=0, tiled=True),
        lax.all_gather(outer_weight, "fs", axis=0, tiled=True),
        lax.all_gather(attn_gain, "fs", axis=0, tiled=True),
        lax.all_gather(mlp_gain, "fs", axis=0, tiled=True),
    )
    starts_row = doc_starts[0]
    local_pos = ctx_place * row_count + jnp.arange(row_count, dtype=jnp.int32)
    local_seg = segment_of(local_pos, starts_row)

    def heads_of(flat_block):
        return flat_block.reshape(row_count, H, HD)

    token_rows = tokens[0].astype(jnp.float32)
    scale_one = rms_scale(token_rows)
    normed_one = token_rows * scale_one
    gain_one = attn_gain_full.astype(jnp.float32)
    hidden_one = (normed_one * gain_one).astype(jnp.bfloat16)
    query_raw = jnp.dot(hidden_one, query_full, preferred_element_type=jnp.float32)
    scale_vec = jnp.tile(query_scale, H) / math.sqrt(HD)
    queries = heads_of((query_raw * scale_vec).astype(jnp.bfloat16))
    key_rows = jnp.dot(hidden_one, key_full, preferred_element_type=jnp.float32).astype(
        jnp.bfloat16
    )
    value_rows = jnp.dot(hidden_one, value_full, preferred_element_type=jnp.float32).astype(
        jnp.bfloat16
    )

    def key_info(turn_index):
        source = (ctx_place - turn_index) % ctx_count
        key_pos = source * row_count + jnp.arange(row_count, dtype=jnp.int32)
        return (source, key_pos, segment_of(key_pos, starts_row))

    def keep_state(state_in):
        return state_in

    def attend(softmax_state, key_flat, value_flat, turn_index):
        source, key_pos, key_seg = key_info(turn_index)

        def compute(state_in):
            run_max, run_sum, run_acc = state_in
            key_block = heads_of(key_flat)
            value_block = heads_of(value_flat)
            allowed = block_mask(local_pos, local_seg, key_pos, key_seg)
            scores = jnp.where(allowed[None], scores_of(queries, key_block), neg_big)
            new_max = jnp.maximum(run_max, jnp.max(scores, axis=-1))
            weights = jnp.where(allowed[None], jnp.exp(scores - new_max[..., None]), 0.0)
            factor = jnp.exp(run_max - new_max)
            run_sum = run_sum * factor + jnp.sum(weights, axis=-1)
            run_acc = run_acc * factor[..., None] + jnp.einsum(
                "hqk,khd->hqd",
                weights.astype(jnp.bfloat16),
                value_block,
                preferred_element_type=jnp.float32,
            )
            return (new_max, run_sum, run_acc)

        return lax.cond(source <= ctx_place, compute, keep_state, softmax_state)

    start_state = (
        jnp.full((H, row_count), neg_big, jnp.float32),
        jnp.zeros((H, row_count), jnp.float32),
        jnp.zeros((H, row_count, HD), jnp.float32),
    )
    start_state = attend(start_state, key_rows, value_rows, jnp.int32(0))
    stores = ()

    def forward_turn(turn_index, loop_state):
        key_block, value_block, softmax_state, kept = loop_state
        key_block, value_block = shifted((key_block, value_block), "ctx", 1)
        softmax_state = attend(softmax_state, key_block, value_block, turn_index)
        return (key_block, value_block, softmax_state, kept)

    loop_out = lax.fori_loop(
        1, ctx_count, forward_turn, (key_rows, value_rows, start_state, stores)
    )
    run_max, run_sum, run_acc = loop_out[2]
    stores = loop_out[3]
    log_total = run_max + jnp.log(run_sum)
    attn_heads = run_acc / run_sum[..., None]
    attn_low = (
        jnp.transpose(attn_heads, (1, 0, 2)).reshape(row_count, model_width).astype(jnp.bfloat16)
    )
    resid = token_rows + jnp.dot(attn_low, out_full, preferred_element_type=jnp.float32)
    scale_two = rms_scale(resid)
    normed_two = resid * scale_two
    gain_two = mlp_gain_full.astype(jnp.float32)
    hidden_two = (normed_two * gain_two).astype(jnp.bfloat16)
    inner_pre = jnp.dot(hidden_two, inner_full, preferred_element_type=jnp.float32)
    active = jax.nn.silu(inner_pre).astype(jnp.bfloat16)
    result = resid + jnp.dot(active, outer_full, preferred_element_type=jnp.float32)
    grad_out = cotangent[0]
    grad_active = jnp.dot(grad_out, outer_full.T, preferred_element_type=jnp.float32)
    grad_outer = jnp.dot(active.T, grad_out, preferred_element_type=jnp.float32)
    sigmoid_in = jax.nn.sigmoid(inner_pre)
    grad_inner_pre = (grad_active * sigmoid_in * (1.0 + inner_pre * (1.0 - sigmoid_in))).astype(
        jnp.bfloat16
    )
    grad_inner = jnp.dot(hidden_two.T, grad_inner_pre, preferred_element_type=jnp.float32)
    grad_hidden_two = jnp.dot(grad_inner_pre, inner_full.T, preferred_element_type=jnp.float32)
    grad_gain_two = jnp.sum(grad_hidden_two * normed_two, axis=0)
    grad_resid = grad_out.astype(jnp.float32) + norm_back(
        grad_hidden_two * gain_two, normed_two, scale_two
    )
    grad_resid_low = grad_resid.astype(jnp.bfloat16)
    grad_outw = jnp.dot(attn_low.T, grad_resid_low, preferred_element_type=jnp.float32)
    grad_attended = heads_of(
        jnp.dot(grad_resid_low, out_full.T, preferred_element_type=jnp.float32).astype(jnp.bfloat16)
    )
    row_delta = jnp.einsum("qhd,hqd->hq", grad_attended.astype(jnp.float32), attn_heads)

    def attend_back(grad_parts, key_flat, value_flat, turn_index):
        source, key_pos, key_seg = key_info(turn_index)

        def compute(parts_in):
            grad_query_acc, grad_key_acc, grad_value_acc = parts_in
            key_block = heads_of(key_flat)
            value_block = heads_of(value_flat)
            allowed = block_mask(local_pos, local_seg, key_pos, key_seg)
            scores = scores_of(queries, key_block)
            probabilities = jnp.where(allowed[None], jnp.exp(scores - log_total[..., None]), 0.0)
            grad_value_acc = grad_value_acc + jnp.einsum(
                "hqk,qhd->khd",
                probabilities.astype(jnp.bfloat16),
                grad_attended,
                preferred_element_type=jnp.float32,
            ).reshape(row_count, model_width)
            grad_probs = jnp.einsum(
                "qhd,khd->hqk", grad_attended, value_block, preferred_element_type=jnp.float32
            )
            grad_scores = (probabilities * (grad_probs - row_delta[..., None])).astype(jnp.bfloat16)
            grad_query_acc = grad_query_acc + jnp.einsum(
                "hqk,khd->qhd", grad_scores, key_block, preferred_element_type=jnp.float32
            )
            grad_key_acc = grad_key_acc + jnp.einsum(
                "hqk,qhd->khd", grad_scores, queries, preferred_element_type=jnp.float32
            ).reshape(row_count, model_width)
            return (grad_query_acc, grad_key_acc, grad_value_acc)

        return lax.cond(source <= ctx_place, compute, keep_state, grad_parts)

    def back_compute(turn_index, loop_state):
        key_block, value_block, grad_parts = loop_state
        grad_parts = attend_back(grad_parts, key_block, value_block, turn_index)
        grad_key_acc, grad_value_acc = pass_grads(grad_parts[1], grad_parts[2])
        return (key_block, value_block, (grad_parts[0], grad_key_acc, grad_value_acc))

    def back_turn(turn_index, loop_state):
        key_block, value_block, grad_parts = back_compute(turn_index, loop_state)
        key_block, value_block = shifted((key_block, value_block), "ctx", 1)
        return (key_block, value_block, grad_parts)

    zero_heads = jnp.zeros((row_count, H, HD), jnp.float32)
    zero_flat = jnp.zeros((row_count, model_width), jnp.float32)
    back_state = lax.fori_loop(
        0, ctx_count - 1, back_turn, (key_rows, value_rows, (zero_heads, zero_flat, zero_flat))
    )
    back_state = back_compute(jnp.int32(ctx_count - 1), back_state)
    grad_query_acc, grad_key_acc, grad_value_acc = back_state[2]
    grad_query_flat = grad_query_acc.reshape(row_count, model_width)
    grad_key_low = grad_key_acc.astype(jnp.bfloat16)
    grad_value_low = grad_value_acc.astype(jnp.bfloat16)
    grad_query_raw = (grad_query_flat * scale_vec).astype(jnp.bfloat16)
    grad_scale = jnp.sum(
        (grad_query_flat * query_raw).reshape(row_count, H, HD), axis=(0, 1)
    ) / math.sqrt(HD)
    grad_qw = jnp.dot(hidden_one.T, grad_query_raw, preferred_element_type=jnp.float32)
    grad_kw = jnp.dot(hidden_one.T, grad_key_low, preferred_element_type=jnp.float32)
    grad_vw = jnp.dot(hidden_one.T, grad_value_low, preferred_element_type=jnp.float32)
    grad_hidden_one = (
        jnp.dot(grad_query_raw, query_full.T, preferred_element_type=jnp.float32)
        + jnp.dot(grad_key_low, key_full.T, preferred_element_type=jnp.float32)
        + jnp.dot(grad_value_low, value_full.T, preferred_element_type=jnp.float32)
    )
    grad_gain_one = jnp.sum(grad_hidden_one * normed_one, axis=0)
    grad_tokens = grad_resid_low.astype(jnp.float32) + norm_back(
        grad_hidden_one * gain_one, normed_one, scale_one
    )
    shard_count = lax.axis_size("fs")
    scale_rows = jnp.broadcast_to(grad_scale[None, :], (shard_count, grad_scale.shape[0]))
    shares = (
        lax.psum_scatter(
            grad_qw.astype(jnp.bfloat16), "fs", scatter_dimension=0, tiled=True
        ).astype(jnp.float32),
        lax.psum_scatter(
            grad_kw.astype(jnp.bfloat16), "fs", scatter_dimension=0, tiled=True
        ).astype(jnp.float32),
        lax.psum_scatter(
            grad_vw.astype(jnp.bfloat16), "fs", scatter_dimension=0, tiled=True
        ).astype(jnp.float32),
        lax.psum_scatter(
            grad_outw.astype(jnp.bfloat16), "fs", scatter_dimension=0, tiled=True
        ).astype(jnp.float32),
        lax.psum_scatter(
            grad_inner.astype(jnp.bfloat16), "fs", scatter_dimension=0, tiled=True
        ).astype(jnp.float32),
        lax.psum_scatter(
            grad_outer.astype(jnp.bfloat16), "fs", scatter_dimension=0, tiled=True
        ).astype(jnp.float32),
        lax.psum_scatter(
            grad_gain_one.astype(jnp.bfloat16), "fs", scatter_dimension=0, tiled=True
        ).astype(jnp.float32),
        lax.psum_scatter(
            grad_gain_two.astype(jnp.bfloat16), "fs", scatter_dimension=0, tiled=True
        ).astype(jnp.float32),
        lax.psum_scatter(
            scale_rows.astype(jnp.bfloat16), "fs", scatter_dimension=0, tiled=True
        ).astype(jnp.float32),
    )
    totals = (
        lax.psum(shares[0].astype(jnp.bfloat16), "ctx").astype(jnp.float32),
        lax.psum(shares[1].astype(jnp.bfloat16), "ctx").astype(jnp.float32),
        lax.psum(shares[2].astype(jnp.bfloat16), "ctx").astype(jnp.float32),
        lax.psum(shares[3].astype(jnp.bfloat16), "ctx").astype(jnp.float32),
        lax.psum(shares[4].astype(jnp.bfloat16), "ctx").astype(jnp.float32),
        lax.psum(shares[5].astype(jnp.bfloat16), "ctx").astype(jnp.float32),
        lax.psum(shares[6].astype(jnp.bfloat16), "ctx").astype(jnp.float32),
        lax.psum(shares[7].astype(jnp.bfloat16), "ctx").astype(jnp.float32),
        lax.psum(shares[8].astype(jnp.bfloat16), "ctx").astype(jnp.float32),
    )
    return (
        result[None].astype(jnp.bfloat16),
        grad_tokens[None].astype(jnp.bfloat16),
        totals[0],
        totals[1],
        totals[2],
        totals[3],
        totals[4],
        totals[5],
        totals[6],
        totals[7],
        totals[8][0],
    )


MESH = pl.DeviceIdType.MESH
ANY = pl.BlockSpec(memory_space=pl.ANY)
VMEM = pl.BlockSpec(memory_space=pltpu.VMEM)
BF = jnp.bfloat16
F32 = jnp.float32


def fast_fits(mesh):
    return mesh.shape["ctx"] == H and mesh.shape["fs"] == 2


def remote(src, dst, ssem, rsem, target):
    return pltpu.make_async_remote_copy(
        src_ref=src, dst_ref=dst, send_sem=ssem, recv_sem=rsem, device_id=target, device_id_type=MESH
    )


def signal(target):
    pl.semaphore_signal(
        pltpu.get_barrier_semaphore(), inc=1, device_id=target, device_id_type=MESH
    )


def place():
    me = lax.axis_index("ctx")
    return me, lax.axis_index("fs"), me // 4, lax.rem(me // 2, 2), lax.rem(me, 2)


def dot(a, b, dims=((1,), (0,))):
    return lax.dot_general(a, b, (dims, ((), ())), preferred_element_type=F32)


NT = ((1,), (1,))
TN = ((0,), (0,))


LOG2E = math.log2(math.e)
UNITS = H // 2


def weight_pull(own, other, k, fs, me, ssem, rsem):
    half = own[0].shape[0] // 2
    rows = pl.ds(pl.multiple_of(k * half, 64), half)
    yn = (me, 1 - fs)
    sib = (me + 1 - 2 * k, fs)
    n = len(own)
    first = [remote(own[i].at[rows], other[i].at[rows], ssem.at[i], rsem.at[i], yn) for i in range(n)]
    second = [
        remote(other[i].at[rows], other[i].at[rows], ssem.at[n + i], rsem.at[n + i], sib)
        for i in range(n)
    ]
    return first, second


def visible(j, i, rows, first_key):
    kpos = j * rows + lax.broadcasted_iota(jnp.int32, (rows, rows), 0)
    qpos = i * rows + lax.broadcasted_iota(jnp.int32, (rows, rows), 1)
    return (kpos <= qpos) & (kpos >= first_key)


def forward_kernel(n_w, tok_ref, gain_ref, wt_ref, scale_ref, first_ref, *rest):
    own = rest[:n_w]
    at = n_w
    h_all, gain_full, attn_ref = rest[at : at + 3]
    o32_ref, lse_ref, qt_ref, q_ref, kt_ref, k_ref, v_ref, raw_ref = rest[at + 3 : at + 11]
    other = rest[at + 11 : at + 11 + n_w]
    (
        wt_all, gain_own, gain_other, o_sc, vt_sc, m_sc, l_sc, acc_sc,
        ssem, rsem, osend, orecv, wssem, wrsem, ysem, lsem,
    ) = rest[at + 11 + n_w :]
    me, fs, z, x, k = place()
    sib, xn, yn = (me + 1 - 2 * k, fs), (me + 2 - 4 * x, fs), (me, 1 - fs)
    up, dn = (me + 4, fs), (me - 4, fs)
    rows = tok_ref.shape[0]
    unit_rows = 2 * rows
    bar = pltpu.get_barrier_semaphore()
    for i in range(1, H):
        signal((lax.rem(me + i, H), fs))
    signal(yn)
    gain_own[...] = gain_ref[...]
    tokens = tok_ref[...].astype(F32)
    normed = tokens * lax.rsqrt(jnp.mean(tokens * tokens, axis=-1, keepdims=True) + epsilon)
    pl.semaphore_wait(bar, H)

    gain_copy = remote(gain_own, gain_other, ysem.at[0], ysem.at[1], yn)
    gain_copy.start()
    half = wt_ref.shape[1]
    columns = pl.ds(pl.multiple_of(fs * half, 128), half)
    wt_copy = remote(wt_ref, wt_all.at[:, columns], ysem.at[2], ysem.at[3], yn)
    wt_copy.start()
    wt_here = pltpu.make_async_copy(wt_ref, wt_all.at[:, columns], lsem.at[0])
    wt_here.start()
    first, second = weight_pull(own, other, k, fs, me, wssem, wrsem)
    gain_copy.wait()
    g_here = gain_own[...].astype(F32)
    g_there = gain_other[...].astype(F32)
    gains = jnp.where(
        fs == 0,
        jnp.concatenate([g_here, g_there], axis=1),
        jnp.concatenate([g_there, g_here], axis=1),
    )
    gain_full[...] = gains
    my_rows = pl.ds(pl.multiple_of(k * rows, rows), rows)
    h_all[me // 2, my_rows, :] = (normed * gains[0:1]).astype(BF)

    def slot(s):
        return h_all.at[s // 2, pl.ds(pl.multiple_of(lax.rem(s, 2) * rows, rows), rows)]

    def cp(s, t, si):
        return remote(slot(s), slot(s), ssem.at[si], rsem.at[s], t)

    cp(me, xn, 0).start()

    @pl.when(z < 3)
    def _():
        cp(me, up, 1).start()

    @pl.when(z > 0)
    def _():
        cp(me, dn, 2).start()

    cp(me, sib, 3).start()
    for c in first:
        c.start()
    wt_here.wait()
    wt_copy.wait()

    def project(u):
        qkv = dot(wt_all[...], h_all[u], NT)
        raw = qkv[:HD]
        raw_ref[u] = raw
        q32 = raw * scale_ref[...]
        qt_ref[u] = (q32 * LOG2E).astype(BF)
        q_ref[u] = q32.T.astype(BF)
        kt = qkv[HD : 2 * HD]
        vt = qkv[2 * HD :]
        kt_ref[u] = kt.astype(BF)
        k_ref[u] = kt.T.astype(BF)
        v_ref[u] = vt.T.astype(BF)
        vt_sc[u] = vt.astype(BF)
        m_sc[u] = jnp.full((1, unit_rows), neg_big, F32)
        l_sc[u] = jnp.zeros((1, unit_rows), F32)
        acc_sc[u] = jnp.zeros((HD, unit_rows), F32)

    def pair(j, i):
        s = dot(k_ref[j], qt_ref[i])
        s = jnp.where(visible(j, i, unit_rows, first_ref[i]), s, neg_big)
        run_max = m_sc[i]
        new_max = jnp.maximum(run_max, jnp.max(s, axis=0, keepdims=True))
        p = jnp.exp2(s - new_max)
        factor = jnp.exp2(run_max - new_max)
        l_sc[i] = l_sc[i] * factor + jnp.sum(p, axis=0, keepdims=True)
        acc_sc[i] = acc_sc[i] * factor + dot(vt_sc[j], p.astype(BF))
        m_sc[i] = new_max

    def when_here(uz, ux):
        return 4 * jnp.maximum(uz - z, z - uz) + 2 * jnp.maximum(ux - x, x - ux) + (uz + 4 - z) // 5

    def process(uz, ux):
        u = uz * 2 + ux
        cp(u * 2 + 1 - k, sib, 0).wait_recv()
        project(u)
        pair(u, u)
        mine = when_here(uz, ux)

        def earlier(e, c):
            @pl.when(when_here(e // 2, lax.rem(e, 2)) < mine)
            def _():
                pair(jnp.minimum(e, u), jnp.maximum(e, u))

            return c

        lax.fori_loop(0, UNITS, earlier, 0)

    xo = me + 2 - 4 * x

    def column_arrival(d):
        a = 4 + (d - 1) * 6

        @pl.when(z >= d)
        def _():
            s = me - 4 * d
            cp(s, dn, a).wait_recv()

            @pl.when(z < 3)
            def _():
                cp(s, up, a).start()

            cp(s, xn, a + 1).start()
            cp(s, sib, a + 2).start()

        @pl.when(z + d <= 3)
        def _():
            s = me + 4 * d
            cp(s, up, a + 3).wait_recv()

            @pl.when(z > 0)
            def _():
                cp(s, dn, a + 3).start()

            cp(s, xn, a + 4).start()
            cp(s, sib, a + 5).start()

    def across_arrival(d):
        @pl.when(z >= d)
        def _():
            s = xo - 4 * d
            cp(s, xn, 0).wait_recv()
            cp(s, sib, 22 + z - d).start()

        @pl.when((z + d <= 3) & (d > 0))
        def _():
            s = xo + 4 * d
            cp(s, xn, 0).wait_recv()
            cp(s, sib, 22 + z + d).start()

    def step(d, c):
        @pl.when((d >= 1) & (d <= 3))
        def _():
            column_arrival(d)

        @pl.when(d >= 1)
        def _():
            across_arrival(d - 1)

        for i in range(n_w):
            if i < 4:

                @pl.when(d == i + 1)
                def _(i=i):
                    first[i].wait_recv()
                    second[i].start()

        def compute(n, c2):
            across = 1 - n // 2
            dd = d - across
            uz = z + dd * (2 * lax.rem(n, 2) - 1)
            ux = x + across * (1 - 2 * x)
            ok = (dd >= 0) & (dd <= 3) & (uz >= 0) & (uz <= 3)
            ok = ok & ((dd > 0) | (lax.rem(n, 2) == 0))

            @pl.when(ok)
            def _():
                process(uz, ux)

            return c2

        lax.fori_loop(0, 4, compute, 0)
        return c

    lax.fori_loop(0, 5, step, 0)

    def out_copy(b):
        u = b // 2
        lanes = pl.ds(pl.multiple_of(lax.rem(b, 2) * rows, 128), rows)
        return o_sc.at[u, :, lanes]

    def finish(n, c):
        u = lax.rem(me // 2 + n, UNITS)
        out = acc_sc[u] / l_sc[u]
        o32_ref[u] = out
        o_sc[u] = out.astype(BF)
        lse_ref[u] = m_sc[u] + jnp.log2(l_sc[u])

        def send(e, c2):
            b = u * 2 + e

            @pl.when(b != me)
            def _():
                remote(out_copy(b), attn_ref.at[me], osend.at[b], orecv.at[me], (b, fs)).start()

            @pl.when(b == me)
            def _():
                pltpu.make_async_copy(out_copy(b), attn_ref.at[me], lsem.at[1]).start()

            return c2

        return lax.fori_loop(0, 2, send, c)

    lax.fori_loop(0, UNITS, finish, 0)
    for i in range(4, n_w):
        first[i].wait_recv()
        second[i].start()

    def taken(b, c):
        @pl.when(b != me)
        def _():
            remote(out_copy(b), attn_ref.at[b], osend.at[b], orecv.at[b], (b, fs)).wait()

        return c

    lax.fori_loop(0, H, taken, 0)
    pltpu.make_async_copy(out_copy(me), attn_ref.at[me], lsem.at[1]).wait()
    cp(me, xn, 0).wait_send()

    @pl.when(z < 3)
    def _():
        cp(me, up, 1).wait_send()

    @pl.when(z > 0)
    def _():
        cp(me, dn, 2).wait_send()

    cp(me, sib, 3).wait_send()

    def sent(d, c):
        a = 4 + (d - 1) * 6

        @pl.when(z >= d)
        def _():
            s = me - 4 * d

            @pl.when(z < 3)
            def _():
                cp(s, up, a).wait_send()

            cp(s, xn, a + 1).wait_send()
            cp(s, sib, a + 2).wait_send()

        @pl.when(z + d <= 3)
        def _():
            s = me + 4 * d

            @pl.when(z > 0)
            def _():
                cp(s, dn, a + 3).wait_send()

            cp(s, xn, a + 4).wait_send()
            cp(s, sib, a + 5).wait_send()

        return c

    lax.fori_loop(1, 4, sent, 0)

    def sent_across(zz, c):
        cp(xo + 4 * (zz - z), sib, 22 + zz).wait_send()
        return c

    lax.fori_loop(0, 4, sent_across, 0)
    for i in range(n_w):
        first[i].wait_send()
        second[i].wait()


def forward_call(tok, gains, wt, scale_col, first_key, weights):
    n_w = len(weights)
    rows, width = tok.shape
    ur = 2 * rows

    def out(dtype, *shape):
        return jax.ShapeDtypeStruct((UNITS, *shape), dtype)

    shapes = [
        out(BF, ur, width),
        jax.ShapeDtypeStruct((gains.shape[0], 2 * gains.shape[1]), F32),
        jax.ShapeDtypeStruct((H, HD, rows), BF),
        out(F32, HD, ur), out(F32, 1, ur), out(BF, HD, ur), out(BF, ur, HD), out(BF, HD, ur),
        out(BF, ur, HD), out(BF, ur, HD), out(F32, HD, ur),
    ] + [jax.ShapeDtypeStruct(w.shape, BF) for w in weights]
    return pl.pallas_call(
        functools.partial(forward_kernel, n_w),
        out_shape=shapes,
        in_specs=[VMEM] * 5 + [ANY] * n_w,
        out_specs=[VMEM, VMEM, ANY] + [VMEM] * 8 + [ANY] * n_w,
        scratch_shapes=[
            pltpu.VMEM((wt.shape[0], 2 * wt.shape[1]), BF),
            pltpu.VMEM(gains.shape, BF),
            pltpu.VMEM(gains.shape, BF),
            pltpu.VMEM((UNITS, HD, ur), BF),
            pltpu.VMEM((UNITS, HD, ur), BF),
            pltpu.VMEM((UNITS, 1, ur), F32),
            pltpu.VMEM((UNITS, 1, ur), F32),
            pltpu.VMEM((UNITS, HD, ur), F32),
            pltpu.SemaphoreType.DMA((26,)),
            pltpu.SemaphoreType.DMA((H,)),
            pltpu.SemaphoreType.DMA((H,)),
            pltpu.SemaphoreType.DMA((H,)),
            pltpu.SemaphoreType.DMA((2 * n_w,)),
            pltpu.SemaphoreType.DMA((2 * n_w,)),
            pltpu.SemaphoreType.DMA((4,)),
            pltpu.SemaphoreType.DMA((2,)),
        ],
        compiler_params=pltpu.CompilerParams(
            collective_id=1, has_side_effects=True, vmem_limit_bytes=56 * 2**20
        ),
        name="forward",
    )(tok, gains, wt, scale_col, first_key, *weights)


def half_rows(start, size, align):
    return pl.ds(pl.multiple_of(start, align), size)


def backward_kernel(
    n_w, gt_ref, *rest,
):
    dense = rest[:3]
    own = rest[3 : 3 + n_w]
    at = 3 + n_w
    h_ref, scale_ref, first_ref, k_ref, v_ref, kt_ref, raw_ref, q_ref, qt_ref, o_ref, lse_ref = rest[
        at : at + 11
    ]
    at += 11
    got_ref, piece_ref, ds_ref = rest[at : at + 3]
    other = rest[at + 3 : at + 3 + n_w]
    (
        g_in, g_sc, delta_sc, dq_sc, scale_sc, dk_sc, dv_sc, d_sc, dw_sc, dw_out, dw_got,
        s1, r0, ra, rb, r2, rz,
        gsend, grecv, qsend, qrecv, ksend, krecv, wssem, wrsem, dsend, drecv, psend, precv, lsem,
    ) = rest[at + 3 + n_w :]
    me, fs, z, x, k = place()
    sib, xn, yn = (me + 1 - 2 * k, fs), (me + 2 - 4 * x, fs), (me, 1 - fs)
    units, rows = h_ref.shape[:2]
    block = rows // 2
    n_g = 3
    part = s1.shape[2]
    width = s1.shape[3]
    cols = width // 2
    bar = pltpu.get_barrier_semaphore()
    for i in range(1, H):
        signal((lax.rem(me + i, H), fs))
    signal(yn)

    def mine(g, f):
        return pltpu.make_async_copy(
            dense[g].at[half_rows(f * 2 * part + k * part, part, 64)], s1.at[g, f], lsem.at[g * 2 + f]
        )

    def theirs(g, f):
        return remote(
            dense[g].at[half_rows(f * 2 * part + (1 - k) * part, part, 64)],
            r0.at[g, f], dsend.at[g * 2 + f], drecv.at[g * 2 + f], sib,
        )

    for g in range(n_g):
        for f in range(2):
            mine(g, f).start()
    pl.semaphore_wait(bar, H)

    def lanes(b):
        return half_rows(lax.rem(b, 2) * block, block, 128)

    def g_copy(b, t):
        return remote(
            gt_ref.at[b], g_in.at[t // 2, :, lanes(t)], gsend.at[b], grecv.at[t], (b, fs)
        )

    def g_start(n, c):
        g_copy(lax.rem(me + n, H), me).start()
        return c

    lax.fori_loop(1, H, g_start, 0)
    g_here = pltpu.make_async_copy(gt_ref.at[me], g_in.at[me // 2, :, lanes(me)], lsem.at[6])
    g_here.start()
    for g in range(n_g):
        for f in range(2):
            theirs(g, f).start()
    first, second = weight_pull(own, other, k, fs, me, wssem, wrsem)
    for c in first:
        c.start()

    top, bottom = slice(0, part // 2), slice(part // 2, part)
    x_here = half_rows(x * cols, cols, 128)
    x_there = half_rows((1 - x) * cols, cols, 128)
    up_a = remote(s1.at[:, 1 - fs, top, :], ra, psend.at[0], precv.at[0], yn)
    up_b = remote(s1.at[:, :, bottom, x_there], rb, psend.at[1], precv.at[1], xn)
    two_a = remote(s1.at[:, fs, top, x_there], r2.at[:, top], psend.at[2], precv.at[2], xn)
    two_b = remote(s1.at[:, 1 - fs, bottom, x_here], r2.at[:, bottom], psend.at[3], precv.at[3], yn)
    slab = part // 4

    def z_copy(t, slot, sem):
        return remote(
            s1.at[:, fs, half_rows(t * slab, slab, 16), x_here],
            rz.at[slot], psend.at[4 + sem], precv.at[4 + slot], (me + 4 * (t - z), fs),
        )

    for g in range(n_g):
        for f in range(2):
            mine(g, f).wait()
            theirs(g, f).wait()

            def add(i, c, g=g, f=f):
                r = half_rows(i * 32, 32, 32)
                s1[g, f, r, :] += r0[g, f, r, :]
                return c

            lax.fori_loop(0, part // 32, add, 0)
    up_a.start()
    up_b.start()

    def after_one():
        up_a.wait()
        up_b.wait()
        for g in range(n_g):

            def add(i, c, g=g):
                r = half_rows(i * 32, 32, 32)
                s1[g, fs, r, :] += ra[g, r, :]
                low = half_rows(part // 2 + i * 32, 32, 32)
                for f in range(2):
                    s1[g, f, low, x_here] += rb[g, f, r, :]
                return c

            lax.fori_loop(0, part // 64, add, 0)
        two_a.start()
        two_b.start()

    def after_two():
        two_a.wait()
        two_b.wait()
        for g in range(n_g):

            def add(i, c, g=g):
                r = half_rows(i * 32, 32, 32)
                s1[g, fs, r, x_here] += r2[g, r, :]
                return c

            lax.fori_loop(0, part // 32, add, 0)
        for d in range(1, 4):
            t = lax.rem(z + d, 4)
            z_copy(t, z, d).start()

    def after_three():
        for d in range(1, 4):
            t = lax.rem(z + d, 4)
            z_copy(t, t, d).wait()
        here = half_rows(z * slab, slab, 16)
        for g in range(n_g):
            total = s1[g, fs, here, x_here].astype(F32)
            for d in range(1, 4):
                total = total + rz[lax.rem(z + d, 4), g].astype(F32)
            piece_ref[g] = total.astype(BF)

    scale_sc[...] = jnp.zeros_like(scale_sc)
    dw_sc[...] = jnp.zeros_like(dw_sc)

    def g_taken(n, c):
        b = lax.rem(me + n, H)
        g_copy(b, b).wait()
        return c

    g_here.wait()
    lax.fori_loop(1, H, g_taken, 0)

    def prepare(i, c):
        g = g_in[i].astype(F32)
        g_sc[i] = g.T.astype(BF)
        delta_sc[i] = jnp.sum(g * o_ref[i], axis=0, keepdims=True)
        dq_sc[i] = jnp.zeros((HD, rows), F32)
        return c

    lax.fori_loop(0, units, prepare, 0)

    def pair(masked, j, i):
        s = dot(k_ref[j], qt_ref[i])
        if masked:
            s = jnp.where(visible(j, i, rows, first_ref[i]), s, neg_big)
        p = jnp.exp2(s - lse_ref[i])
        dv_sc[...] += dot(p.astype(BF), g_sc[i])
        dp = dot(v_ref[j], g_in[i])
        ds = (p * (dp - delta_sc[i])).astype(BF)
        dk_sc[...] += dot(ds, q_ref[i])
        dq_sc[i] += dot(kt_ref[j], ds)

    def out(b, lo, n):
        return d_sc.at[b // 2, pl.ds(lo, n), :, lanes(b)]

    def to(t, lo, n):
        return got_ref.at[pl.ds(lo, n), half_rows(t * HD, HD, 16)]

    def kv_copy(b, t):
        return remote(out(b, 1, 2), to(t, 1, 2), ksend.at[b], krecv.at[t], (b, fs))

    def q_copy(b, t):
        return remote(out(b, 0, 1), to(t, 0, 1), qsend.at[b], qrecv.at[t], (b, fs))

    kv_here = pltpu.make_async_copy(out(me, 1, 2), to(me, 1, 2), lsem.at[7])
    q_here = pltpu.make_async_copy(out(me, 0, 1), to(me, 0, 1), lsem.at[8])

    def column(n, c):
        j = lax.rem(me // 2 + n, units)
        dk_sc[...] = jnp.zeros_like(dk_sc)
        dv_sc[...] = jnp.zeros_like(dv_sc)
        pair(True, j, j)

        def plain(i, c2):
            pair(False, j, i)
            return c2

        def edge(i, c2):
            pair(True, j, i)
            return c2

        end = jnp.where(j == 0, 1, units - 1)
        lax.fori_loop(j + 1, end, plain, 0)
        lax.fori_loop(jnp.maximum(j + 1, end), units, edge, 0)
        d_sc[j, 1] = dk_sc[...].T.astype(BF)
        d_sc[j, 2] = dv_sc[...].T.astype(BF)

        def send(e, c2):
            b = 2 * j + e

            @pl.when(b != me)
            def _():
                kv_copy(b, me).start()

            @pl.when(b == me)
            def _():
                kv_here.start()

            return c2

        lax.fori_loop(0, 2, send, 0)
        for e in range(2):
            dw_sc[1 + e] += dot(d_sc[j, 1 + e], h_ref[j])

        @pl.when(n == 3)
        def _():
            after_one()

        @pl.when(n == 6)
        def _():
            after_two()

        return c

    lax.fori_loop(0, units, column, 0)

    def queries(n, c):
        i = lax.rem(me // 2 + n, units)
        dq = dq_sc[i]
        scale_sc[...] += dq * raw_ref[i]
        d_sc[i, 0] = (dq * scale_ref[...]).astype(BF)

        def send(e, c2):
            b = 2 * i + e

            @pl.when(b != me)
            def _():
                q_copy(b, me).start()

            @pl.when(b == me)
            def _():
                q_here.start()

            return c2

        lax.fori_loop(0, 2, send, 0)
        return c

    lax.fori_loop(0, units, queries, 0)
    for i in range(n_w):
        first[i].wait_recv()
        second[i].start()

    def query_weight(i, c):
        dw_sc[0] += dot(d_sc[i, 0], h_ref[i])
        return c

    lax.fori_loop(0, units, query_weight, 0)
    half = dw_out.shape[2]
    dw_out[...] = dw_sc[:, :, half_rows((1 - fs) * half, half, 128)].astype(BF)
    dw_copy = remote(dw_out, dw_got, psend.at[8], precv.at[8], yn)
    dw_copy.start()
    ds_ref[...] = jnp.sum(scale_sc[...], axis=1, keepdims=True)
    after_three()
    dw_copy.wait()
    piece_ref[n_g:] = (dw_sc[:, :, half_rows(fs * half, half, 128)] + dw_got[...].astype(F32)).astype(BF)

    def taken(n, c):
        b = lax.rem(me + n, H)
        kv_copy(b, b).wait()
        q_copy(b, b).wait()
        return c

    lax.fori_loop(1, H, taken, 0)
    kv_here.wait()
    q_here.wait()
    for i in range(n_w):
        first[i].wait_send()
        second[i].wait()


def backward_call(gt, dense, weights, h_all, scale_col, first_key, k, v, kt, raw, q, qt, o32, lse):
    n_w = len(weights)
    n, rows, width = h_all.shape
    vm = (h_all, scale_col, first_key, k, v, kt, raw, q, qt, o32, lse)
    half = width // 2
    part = dense[0].shape[0] // 4
    sem = pltpu.SemaphoreType.DMA
    return pl.pallas_call(
        functools.partial(backward_kernel, n_w),
        out_shape=[
            jax.ShapeDtypeStruct((3, H * HD, rows // 2), BF),
            jax.ShapeDtypeStruct((6, part // 4, half), BF),
            jax.ShapeDtypeStruct((HD, 1), F32),
        ]
        + [jax.ShapeDtypeStruct(w.shape, BF) for w in weights],
        in_specs=[ANY] * (4 + n_w) + [VMEM] * len(vm),
        out_specs=[ANY, VMEM, VMEM] + [ANY] * n_w,
        scratch_shapes=[
            pltpu.VMEM((n, HD, rows), BF),
            pltpu.VMEM((n, rows, HD), BF),
            pltpu.VMEM((n, 1, rows), F32),
            pltpu.VMEM((n, HD, rows), F32),
            pltpu.VMEM((HD, rows), F32),
            pltpu.VMEM((rows, HD), F32),
            pltpu.VMEM((rows, HD), F32),
            pltpu.VMEM((n, 3, HD, rows), BF),
            pltpu.VMEM((3, HD, width), F32),
            pltpu.VMEM((3, HD, half), BF),
            pltpu.VMEM((3, HD, half), BF),
            pltpu.VMEM((3, 2, part, width), BF),
            pltpu.VMEM((3, 2, part, width), BF),
            pltpu.VMEM((3, part // 2, width), BF),
            pltpu.VMEM((3, 2, part // 2, half), BF),
            pltpu.VMEM((3, part, half), BF),
            pltpu.VMEM((4, 3, part // 4, half), BF),
            sem((H,)), sem((H,)), sem((H,)), sem((H,)), sem((H,)), sem((H,)),
            sem((max(1, 2 * n_w),)), sem((max(1, 2 * n_w),)), sem((6,)), sem((6,)), sem((9,)), sem((9,)),
            sem((9,)),
        ],
        compiler_params=pltpu.CompilerParams(
            collective_id=2, has_side_effects=True, vmem_limit_bytes=60 * 2**20
        ),
        name="backward",
    )(gt, *dense, *weights, *vm)


def final_kernel(
    piece_ref, tok_ref, gr_ref, gain_ref, small_ref, d_ref,
    qo_ref, ko_ref, vo_ref, qn_ref, kn_ref, vn_ref,
    all_ref, tg_ref, sums_ref,
    e_sc, small_out, small_in, small_y, small_got, ssem, rsem, vsend, vrecv, ysem, lsem,
):
    me, fs, z, x, k = place()
    sib, xn, yn = (me + 1 - 2 * k, fs), (me + 2 - 4 * x, fs), (me, 1 - fs)
    up, dn = (me + 4, fs), (me - 4, fs)
    bar = pltpu.get_barrier_semaphore()
    for i in range(1, H):
        signal((lax.rem(me + i, H), fs))
    signal(yn)
    here = pltpu.make_async_copy(piece_ref, all_ref.at[me], lsem.at[0])
    here.start()
    pl.semaphore_wait(bar, H)

    def cp(s, t, si, mine=False):
        return remote(
            piece_ref if mine else all_ref.at[s], all_ref.at[s], ssem.at[si], rsem.at[s], t
        )

    cp(me, xn, 0, True).start()

    @pl.when(z < 3)
    def _():
        cp(me, up, 1, True).start()

    @pl.when(z > 0)
    def _():
        cp(me, dn, 2, True).start()

    cp(me, sib, 3, True).start()

    half = qo_ref.shape[0]
    for w, (a, b) in enumerate(((qo_ref, qn_ref), (ko_ref, kn_ref), (vo_ref, vn_ref))):
        for r, m in ((fs, a), (1 - fs, b)):
            rows = half_rows(r * half, half, 128)
            term = dot(m[...], d_ref[w])
            if w == 0:
                e_sc[rows, :] = term
            else:
                e_sc[rows, :] += term
    grad_hidden = e_sc[...].T
    tokens = tok_ref[...].astype(F32)
    scale = lax.rsqrt(jnp.mean(tokens * tokens, axis=-1, keepdims=True) + epsilon)
    normed = tokens * scale
    small_out[...] = small_ref[...]
    small_out[0:1, :] = jnp.sum(grad_hidden * normed, axis=0, keepdims=True)

    def v_copy(b, t):
        return remote(small_out, small_in.at[t], vsend.at[b], vrecv.at[t], (b, fs))

    def v_start(n, c):
        v_copy(lax.rem(me + n, H), me).start()
        return c

    lax.fori_loop(1, H, v_start, 0)
    e = grad_hidden * gain_ref[0:1, :]
    tg_ref[...] = (
        gr_ref[...].astype(F32) + scale * (e - normed * jnp.mean(e * normed, axis=-1, keepdims=True))
    ).astype(BF)

    xo = me + 2 - 4 * x

    def column_arrival(d):
        a = 4 + (d - 1) * 6

        @pl.when(z >= d)
        def _():
            s = me - 4 * d
            cp(s, dn, a).wait_recv()

            @pl.when(z < 3)
            def _():
                cp(s, up, a).start()

            cp(s, xn, a + 1).start()
            cp(s, sib, a + 2).start()

        @pl.when(z + d <= 3)
        def _():
            s = me + 4 * d
            cp(s, up, a + 3).wait_recv()

            @pl.when(z > 0)
            def _():
                cp(s, dn, a + 3).start()

            cp(s, xn, a + 4).start()
            cp(s, sib, a + 5).start()

    def across_arrival(d):
        @pl.when(z >= d)
        def _():
            s = xo - 4 * d
            cp(s, xn, 0).wait_recv()
            cp(s, sib, 22 + z - d).start()

        @pl.when((z + d <= 3) & (d > 0))
        def _():
            s = xo + 4 * d
            cp(s, xn, 0).wait_recv()
            cp(s, sib, 22 + z + d).start()

    column_arrival(1)

    def v_taken(n, c):
        b = lax.rem(me + n, H)
        v_copy(b, b).wait()
        return c

    lax.fori_loop(1, H, v_taken, 0)

    def v_add(n, total):
        return total + small_in[lax.rem(me + n, H)]

    small_y[...] = lax.fori_loop(1, H, v_add, small_out[...])
    y_copy = remote(small_y, small_got, ysem.at[0], ysem.at[1], yn)
    y_copy.start()
    across_arrival(0)
    column_arrival(2)
    across_arrival(1)
    y_copy.wait()
    sums_ref[...] = small_y[...] + small_got[...]
    column_arrival(3)
    across_arrival(2)
    across_arrival(3)

    def from_sib(n, c):
        cp(n * 2 + 1 - k, sib, 0).wait_recv()
        return c

    lax.fori_loop(0, UNITS, from_sib, 0)
    here.wait()
    cp(me, xn, 0, True).wait_send()

    @pl.when(z < 3)
    def _():
        cp(me, up, 1, True).wait_send()

    @pl.when(z > 0)
    def _():
        cp(me, dn, 2, True).wait_send()

    cp(me, sib, 3, True).wait_send()

    def sent(d, c):
        a = 4 + (d - 1) * 6

        @pl.when(z >= d)
        def _():
            s = me - 4 * d

            @pl.when(z < 3)
            def _():
                cp(s, up, a).wait_send()

            cp(s, xn, a + 1).wait_send()
            cp(s, sib, a + 2).wait_send()

        @pl.when(z + d <= 3)
        def _():
            s = me + 4 * d

            @pl.when(z > 0)
            def _():
                cp(s, dn, a + 3).wait_send()

            cp(s, xn, a + 4).wait_send()
            cp(s, sib, a + 5).wait_send()

        return c

    lax.fori_loop(1, 4, sent, 0)

    def sent_across(zz, c):
        cp(xo + 4 * (zz - z), sib, 22 + zz).wait_send()
        return c

    lax.fori_loop(0, 4, sent_across, 0)


def final_call(piece, tok, grad_resid, gain_full, small, d_all, own, other):
    rows, width = tok.shape
    sem = pltpu.SemaphoreType.DMA
    return pl.pallas_call(
        final_kernel,
        out_shape=[
            jax.ShapeDtypeStruct((H, *piece.shape), BF),
            jax.ShapeDtypeStruct((rows, width), BF),
            jax.ShapeDtypeStruct(small.shape, F32),
        ],
        in_specs=[VMEM] * 12,
        out_specs=[ANY, VMEM, VMEM],
        scratch_shapes=[
            pltpu.VMEM((width, rows), F32),
            pltpu.VMEM(small.shape, F32),
            pltpu.VMEM((H, *small.shape), F32),
            pltpu.VMEM(small.shape, F32),
            pltpu.VMEM(small.shape, F32),
            sem((26,)), sem((H,)), sem((H,)), sem((H,)), sem((2,)), sem((1,)),
        ],
        compiler_params=pltpu.CompilerParams(
            collective_id=3, has_side_effects=True, vmem_limit_bytes=56 * 2**20
        ),
        name="final",
    )(piece, tok, grad_resid, gain_full, small, d_all, *own, *other)


def spread_kernel(dense_ref, heads_ref, dense_out, heads_out):
    for zz in range(4):
        for xx in range(2):
            slab, cols = dense_ref.shape[-2:]
            dense_out[0, zz * slab : (zz + 1) * slab, xx * cols : (xx + 1) * cols] = dense_ref[
                zz, xx, 0, 0
            ].astype(F32)
    n, _, hd, cols = heads_ref.shape
    heads_out[0] = heads_ref[...].reshape(n * hd, cols).astype(F32).T


def spread_call(pieces):
    n, parts, slab, cols = pieces.shape
    split = pieces.reshape(4, 2, 2, parts, slab, cols)
    return pl.pallas_call(
        spread_kernel,
        grid=(3, 2),
        out_shape=[
            jax.ShapeDtypeStruct((3, 8 * slab, 2 * cols), F32),
            jax.ShapeDtypeStruct((3, cols, n * slab), F32),
        ],
        in_specs=[
            pl.BlockSpec((4, 2, 1, 1, slab, cols), lambda w, h: (0, 0, h, w, 0, 0)),
            pl.BlockSpec((n // 2, 1, slab, cols), lambda w, h: (h, 3 + w, 0, 0)),
        ],
        out_specs=[
            pl.BlockSpec((1, 4 * slab, 2 * cols), lambda w, h: (w, h, 0)),
            pl.BlockSpec((1, cols, n * slab // 2), lambda w, h: (w, 0, h)),
        ],
        compiler_params=pltpu.CompilerParams(vmem_limit_bytes=48 * 2**20),
        name="spread",
    )(split, pieces)


def joined(own, other, fs):
    return jnp.where(
        fs == 0, jnp.concatenate([own, other], axis=0), jnp.concatenate([other, own], axis=0)
    )


def fast_local(
    tokens, query_weight, key_weight, value_weight, out_weight, inner_weight, outer_weight,
    attn_gain, mlp_gain, query_scale, doc_starts, cotangent,
):
    me, fs = lax.axis_index("ctx"), lax.axis_index("fs")
    rows, width = tokens.shape[1:]
    tok = tokens[0]
    cot = cotangent[0]

    def head_columns(w):
        return lax.dynamic_slice(w, (0, me * HD), (w.shape[0], HD)).T

    wt = jnp.concatenate([head_columns(w) for w in (query_weight, key_weight, value_weight)], axis=0)
    gains = jnp.stack([attn_gain, mlp_gain])
    positions = jnp.arange(H * rows, dtype=jnp.int32)
    starts = doc_starts[0]
    first_key = jnp.max(
        jnp.where(starts[None, :] <= positions[:, None], starts[None, :], 0), axis=1
    ).reshape(UNITS, 1, 2 * rows)
    scale_col = (query_scale / math.sqrt(HD))[:, None]

    (
        h_all, gain_full, attn_t, o32, lse, qt, q, kt, k, v, raw,
        out_o, inner_o, outer_o, query_o, key_o,
    ) = forward_call(
        tok, gains, wt, scale_col, first_key,
        (out_weight, inner_weight, outer_weight, query_weight, key_weight),
    )
    attn_t = attn_t.reshape(width, rows)

    out_full = joined(out_weight, out_o, fs)
    inner_full = joined(inner_weight, inner_o, fs)
    outer_full = joined(outer_weight, outer_o, fs)
    gain_one, gain_two = gain_full[0:1], gain_full[1:2]
    token_rows = tok.astype(F32)
    resid = token_rows + dot(attn_t, out_full, TN)
    scale_two = rms_scale(resid)
    normed_two = resid * scale_two
    hidden_two = (normed_two * gain_two).astype(BF)
    inner_pre = dot(hidden_two, inner_full)
    active = jax.nn.silu(inner_pre).astype(BF)
    result = (resid + dot(active, outer_full)).astype(BF)
    grad_active = dot(cot, outer_full, NT)
    sig = jax.nn.sigmoid(inner_pre)
    grad_inner_pre = (grad_active * sig * (1.0 + inner_pre * (1.0 - sig))).astype(BF)
    grad_hidden_two = dot(grad_inner_pre, inner_full, NT)
    grad_gain_two = jnp.sum(grad_hidden_two * normed_two, axis=0)
    grad_resid = (
        cot.astype(F32) + norm_back(grad_hidden_two * gain_two, normed_two, scale_two)
    ).astype(BF)
    grad_att_t = dot(out_full, grad_resid, NT).astype(BF).reshape(H, HD, rows)
    grad_outer = dot(active, cot, TN).astype(BF)
    grad_inner = dot(hidden_two, grad_inner_pre, TN).astype(BF)
    grad_outw = dot(attn_t, grad_resid).astype(BF)
    d_all, piece, dscale, value_o = backward_call(
        grad_att_t, (grad_outw, grad_inner, grad_outer), (value_weight,),
        h_all, scale_col, first_key, k, v, kt, raw, q, qt, o32, lse,
    )
    half = width // 2
    small = jnp.zeros((8, width), F32).at[1].set(grad_gain_two).at[2, :HD].set(dscale[:, 0])
    pieces, grad_tokens, sums = final_call(
        piece, tok, grad_resid, gain_full, small, d_all,
        (query_weight, key_weight, value_weight), (query_o, key_o, value_o),
    )
    dense, heads = spread_call(pieces)
    gain_sums = lax.dynamic_slice(sums, (0, fs * half), (2, half))
    return (
        result[None], grad_tokens[None], heads[0], heads[1], heads[2], dense[0], dense[1], dense[2],
        gain_sums[0], gain_sums[1], sums[2, :HD] / math.sqrt(HD),
    )


def solution(mesh):
    placed = (
        P("fs", "ctx", None),
        P("fs", None),
        P("fs", None),
        P("fs", None),
        P("fs", None),
        P("fs", None),
        P("fs", None),
        P("fs"),
        P("fs"),
        P(),
        P("fs", None),
        P("fs", "ctx", None),
    )
    return jax.shard_map(
        fast_local if fast_fits(mesh) else general_local,
        mesh=mesh,
        in_specs=placed,
        out_specs=(
            P("fs", "ctx", None),
            P("fs", "ctx", None),
            P("fs", None),
            P("fs", None),
            P("fs", None),
            P("fs", None),
            P("fs", None),
            P("fs", None),
            P("fs"),
            P("fs"),
            P(),
        ),
        check_vma=False,
    )
```

```python
import functools
import math

import jax
import jax.numpy as jnp
from jax import lax
from jax.experimental import pallas as pl
from jax.experimental.pallas import tpu as pltpu
from jax.sharding import PartitionSpec as P

H = 16
HD = 80


epsilon = 1e-06
neg_big = -1e30


def passed_along(block, axis, distance):
    devices = range(lax.axis_size(axis))
    route = [((i - distance) % len(devices), i) for i in devices]
    return lax.ppermute(block, axis, route)


def shifted(value, axis, steps):
    count = lax.axis_size(axis)
    leading, last = (max(0, -steps), min(count, count - steps))
    return lax.ppermute(value, axis, [(source, source + steps) for source in range(leading, last)])


def rms_scale(values_in):
    return lax.rsqrt(jnp.mean(values_in * values_in, axis=-1, keepdims=True) + epsilon)


def norm_back(grad_normed, normed, scale_rows):
    inner_mean = jnp.mean(grad_normed * normed, axis=-1, keepdims=True)
    return scale_rows * (grad_normed - normed * inner_mean)


def segment_of(positions, starts_row):
    return jnp.sum((starts_row[None, :] <= positions[:, None]).astype(jnp.int32), axis=1) - 1


def block_mask(query_pos, query_seg, key_pos, key_seg):
    return (key_pos[None, :] <= query_pos[:, None]) & (key_seg[None, :] == query_seg[:, None])


def scores_of(query_block, key_block):
    return jnp.einsum("qhd,khd->hqk", query_block, key_block, preferred_element_type=jnp.float32)


def pass_grads(grad_key_acc, grad_value_acc):
    return (
        passed_along(grad_key_acc.astype(jnp.bfloat16), "ctx", 1).astype(grad_key_acc.dtype),
        passed_along(grad_value_acc.astype(jnp.bfloat16), "ctx", 1).astype(grad_value_acc.dtype),
    )


def general_local(
    tokens,
    query_weight,
    key_weight,
    value_weight,
    out_weight,
    inner_weight,
    outer_weight,
    attn_gain,
    mlp_gain,
    query_scale,
    doc_starts,
    cotangent,
):
    row_count = tokens.shape[1]
    model_width = tokens.shape[2]
    ctx_count = lax.axis_size("ctx")
    ctx_place = lax.axis_index("ctx")
    (
        query_full,
        key_full,
        value_full,
        out_full,
        inner_full,
        outer_full,
        attn_gain_full,
        mlp_gain_full,
    ) = (
        lax.all_gather(query_weight, "fs", axis=0, tiled=True),
        lax.all_gather(key_weight, "fs", axis=0, tiled=True),
        lax.all_gather(value_weight, "fs", axis=0, tiled=True),
        lax.all_gather(out_weight, "fs", axis=0, tiled=True),
        lax.all_gather(inner_weight, "fs", axis=0, tiled=True),
        lax.all_gather(outer_weight, "fs", axis=0, tiled=True),
        lax.all_gather(attn_gain, "fs", axis=0, tiled=True),
        lax.all_gather(mlp_gain, "fs", axis=0, tiled=True),
    )
    starts_row = doc_starts[0]
    local_pos = ctx_place * row_count + jnp.arange(row_count, dtype=jnp.int32)
    local_seg = segment_of(local_pos, starts_row)

    def heads_of(flat_block):
        return flat_block.reshape(row_count, H, HD)

    token_rows = tokens[0].astype(jnp.float32)
    scale_one = rms_scale(token_rows)
    normed_one = token_rows * scale_one
    gain_one = attn_gain_full.astype(jnp.float32)
    hidden_one = (normed_one * gain_one).astype(jnp.bfloat16)
    query_raw = jnp.dot(hidden_one, query_full, preferred_element_type=jnp.float32)
    scale_vec = jnp.tile(query_scale, H) / math.sqrt(HD)
    queries = heads_of((query_raw * scale_vec).astype(jnp.bfloat16))
    key_rows = jnp.dot(hidden_one, key_full, preferred_element_type=jnp.float32).astype(
        jnp.bfloat16
    )
    value_rows = jnp.dot(hidden_one, value_full, preferred_element_type=jnp.float32).astype(
        jnp.bfloat16
    )

    def key_info(turn_index):
        source = (ctx_place - turn_index) % ctx_count
        key_pos = source * row_count + jnp.arange(row_count, dtype=jnp.int32)
        return (source, key_pos, segment_of(key_pos, starts_row))

    def keep_state(state_in):
        return state_in

    def attend(softmax_state, key_flat, value_flat, turn_index):
        source, key_pos, key_seg = key_info(turn_index)

        def compute(state_in):
            run_max, run_sum, run_acc = state_in
            key_block = heads_of(key_flat)
            value_block = heads_of(value_flat)
            allowed = block_mask(local_pos, local_seg, key_pos, key_seg)
            scores = jnp.where(allowed[None], scores_of(queries, key_block), neg_big)
            new_max = jnp.maximum(run_max, jnp.max(scores, axis=-1))
            weights = jnp.where(allowed[None], jnp.exp(scores - new_max[..., None]), 0.0)
            factor = jnp.exp(run_max - new_max)
            run_sum = run_sum * factor + jnp.sum(weights, axis=-1)
            run_acc = run_acc * factor[..., None] + jnp.einsum(
                "hqk,khd->hqd",
                weights.astype(jnp.bfloat16),
                value_block,
                preferred_element_type=jnp.float32,
            )
            return (new_max, run_sum, run_acc)

        return lax.cond(source <= ctx_place, compute, keep_state, softmax_state)

    start_state = (
        jnp.full((H, row_count), neg_big, jnp.float32),
        jnp.zeros((H, row_count), jnp.float32),
        jnp.zeros((H, row_count, HD), jnp.float32),
    )
    start_state = attend(start_state, key_rows, value_rows, jnp.int32(0))
    stores = ()

    def forward_turn(turn_index, loop_state):
        key_block, value_block, softmax_state, kept = loop_state
        key_block, value_block = shifted((key_block, value_block), "ctx", 1)
        softmax_state = attend(softmax_state, key_block, value_block, turn_index)
        return (key_block, value_block, softmax_state, kept)

    loop_out = lax.fori_loop(
        1, ctx_count, forward_turn, (key_rows, value_rows, start_state, stores)
    )
    run_max, run_sum, run_acc = loop_out[2]
    stores = loop_out[3]
    log_total = run_max + jnp.log(run_sum)
    attn_heads = run_acc / run_sum[..., None]
    attn_low = (
        jnp.transpose(attn_heads, (1, 0, 2)).reshape(row_count, model_width).astype(jnp.bfloat16)
    )
    resid = token_rows + jnp.dot(attn_low, out_full, preferred_element_type=jnp.float32)
    scale_two = rms_scale(resid)
    normed_two = resid * scale_two
    gain_two = mlp_gain_full.astype(jnp.float32)
    hidden_two = (normed_two * gain_two).astype(jnp.bfloat16)
    inner_pre = jnp.dot(hidden_two, inner_full, preferred_element_type=jnp.float32)
    active = jax.nn.silu(inner_pre).astype(jnp.bfloat16)
    result = resid + jnp.dot(active, outer_full, preferred_element_type=jnp.float32)
    grad_out = cotangent[0]
    grad_active = jnp.dot(grad_out, outer_full.T, preferred_element_type=jnp.float32)
    grad_outer = jnp.dot(active.T, grad_out, preferred_element_type=jnp.float32)
    sigmoid_in = jax.nn.sigmoid(inner_pre)
    grad_inner_pre = (grad_active * sigmoid_in * (1.0 + inner_pre * (1.0 - sigmoid_in))).astype(
        jnp.bfloat16
    )
    grad_inner = jnp.dot(hidden_two.T, grad_inner_pre, preferred_element_type=jnp.float32)
    grad_hidden_two = jnp.dot(grad_inner_pre, inner_full.T, preferred_element_type=jnp.float32)
    grad_gain_two = jnp.sum(grad_hidden_two * normed_two, axis=0)
    grad_resid = grad_out.astype(jnp.float32) + norm_back(
        grad_hidden_two * gain_two, normed_two, scale_two
    )
    grad_resid_low = grad_resid.astype(jnp.bfloat16)
    grad_outw = jnp.dot(attn_low.T, grad_resid_low, preferred_element_type=jnp.float32)
    grad_attended = heads_of(
        jnp.dot(grad_resid_low, out_full.T, preferred_element_type=jnp.float32).astype(jnp.bfloat16)
    )
    row_delta = jnp.einsum("qhd,hqd->hq", grad_attended.astype(jnp.float32), attn_heads)

    def attend_back(grad_parts, key_flat, value_flat, turn_index):
        source, key_pos, key_seg = key_info(turn_index)

        def compute(parts_in):
            grad_query_acc, grad_key_acc, grad_value_acc = parts_in
            key_block = heads_of(key_flat)
            value_block = heads_of(value_flat)
            allowed = block_mask(local_pos, local_seg, key_pos, key_seg)
            scores = scores_of(queries, key_block)
            probabilities = jnp.where(allowed[None], jnp.exp(scores - log_total[..., None]), 0.0)
            grad_value_acc = grad_value_acc + jnp.einsum(
                "hqk,qhd->khd",
                probabilities.astype(jnp.bfloat16),
                grad_attended,
                preferred_element_type=jnp.float32,
            ).reshape(row_count, model_width)
            grad_probs = jnp.einsum(
                "qhd,khd->hqk", grad_attended, value_block, preferred_element_type=jnp.float32
            )
            grad_scores = (probabilities * (grad_probs - row_delta[..., None])).astype(jnp.bfloat16)
            grad_query_acc = grad_query_acc + jnp.einsum(
                "hqk,khd->qhd", grad_scores, key_block, preferred_element_type=jnp.float32
            )
            grad_key_acc = grad_key_acc + jnp.einsum(
                "hqk,qhd->khd", grad_scores, queries, preferred_element_type=jnp.float32
            ).reshape(row_count, model_width)
            return (grad_query_acc, grad_key_acc, grad_value_acc)

        return lax.cond(source <= ctx_place, compute, keep_state, grad_parts)

    def back_compute(turn_index, loop_state):
        key_block, value_block, grad_parts = loop_state
        grad_parts = attend_back(grad_parts, key_block, value_block, turn_index)
        grad_key_acc, grad_value_acc = pass_grads(grad_parts[1], grad_parts[2])
        return (key_block, value_block, (grad_parts[0], grad_key_acc, grad_value_acc))

    def back_turn(turn_index, loop_state):
        key_block, value_block, grad_parts = back_compute(turn_index, loop_state)
        key_block, value_block = shifted((key_block, value_block), "ctx", 1)
        return (key_block, value_block, grad_parts)

    zero_heads = jnp.zeros((row_count, H, HD), jnp.float32)
    zero_flat = jnp.zeros((row_count, model_width), jnp.float32)
    back_state = lax.fori_loop(
        0, ctx_count - 1, back_turn, (key_rows, value_rows, (zero_heads, zero_flat, zero_flat))
    )
    back_state = back_compute(jnp.int32(ctx_count - 1), back_state)
    grad_query_acc, grad_key_acc, grad_value_acc = back_state[2]
    grad_query_flat = grad_query_acc.reshape(row_count, model_width)
    grad_key_low = grad_key_acc.astype(jnp.bfloat16)
    grad_value_low = grad_value_acc.astype(jnp.bfloat16)
    grad_query_raw = (grad_query_flat * scale_vec).astype(jnp.bfloat16)
    grad_scale = jnp.sum(
        (grad_query_flat * query_raw).reshape(row_count, H, HD), axis=(0, 1)
    ) / math.sqrt(HD)
    grad_qw = jnp.dot(hidden_one.T, grad_query_raw, preferred_element_type=jnp.float32)
    grad_kw = jnp.dot(hidden_one.T, grad_key_low, preferred_element_type=jnp.float32)
    grad_vw = jnp.dot(hidden_one.T, grad_value_low, preferred_element_type=jnp.float32)
    grad_hidden_one = (
        jnp.dot(grad_query_raw, query_full.T, preferred_element_type=jnp.float32)
        + jnp.dot(grad_key_low, key_full.T, preferred_element_type=jnp.float32)
        + jnp.dot(grad_value_low, value_full.T, preferred_element_type=jnp.float32)
    )
    grad_gain_one = jnp.sum(grad_hidden_one * normed_one, axis=0)
    grad_tokens = grad_resid_low.astype(jnp.float32) + norm_back(
        grad_hidden_one * gain_one, normed_one, scale_one
    )
    shard_count = lax.axis_size("fs")
    scale_rows = jnp.broadcast_to(grad_scale[None, :], (shard_count, grad_scale.shape[0]))
    shares = (
        lax.psum_scatter(
            grad_qw.astype(jnp.bfloat16), "fs", scatter_dimension=0, tiled=True
        ).astype(jnp.float32),
        lax.psum_scatter(
            grad_kw.astype(jnp.bfloat16), "fs", scatter_dimension=0, tiled=True
        ).astype(jnp.float32),
        lax.psum_scatter(
            grad_vw.astype(jnp.bfloat16), "fs", scatter_dimension=0, tiled=True
        ).astype(jnp.float32),
        lax.psum_scatter(
            grad_outw.astype(jnp.bfloat16), "fs", scatter_dimension=0, tiled=True
        ).astype(jnp.float32),
        lax.psum_scatter(
            grad_inner.astype(jnp.bfloat16), "fs", scatter_dimension=0, tiled=True
        ).astype(jnp.float32),
        lax.psum_scatter(
            grad_outer.astype(jnp.bfloat16), "fs", scatter_dimension=0, tiled=True
        ).astype(jnp.float32),
        lax.psum_scatter(
            grad_gain_one.astype(jnp.bfloat16), "fs", scatter_dimension=0, tiled=True
        ).astype(jnp.float32),
        lax.psum_scatter(
            grad_gain_two.astype(jnp.bfloat16), "fs", scatter_dimension=0, tiled=True
        ).astype(jnp.float32),
        lax.psum_scatter(
            scale_rows.astype(jnp.bfloat16), "fs", scatter_dimension=0, tiled=True
        ).astype(jnp.float32),
    )
    totals = (
        lax.psum(shares[0].astype(jnp.bfloat16), "ctx").astype(jnp.float32),
        lax.psum(shares[1].astype(jnp.bfloat16), "ctx").astype(jnp.float32),
        lax.psum(shares[2].astype(jnp.bfloat16), "ctx").astype(jnp.float32),
        lax.psum(shares[3].astype(jnp.bfloat16), "ctx").astype(jnp.float32),
        lax.psum(shares[4].astype(jnp.bfloat16), "ctx").astype(jnp.float32),
        lax.psum(shares[5].astype(jnp.bfloat16), "ctx").astype(jnp.float32),
        lax.psum(shares[6].astype(jnp.bfloat16), "ctx").astype(jnp.float32),
        lax.psum(shares[7].astype(jnp.bfloat16), "ctx").astype(jnp.float32),
        lax.psum(shares[8].astype(jnp.bfloat16), "ctx").astype(jnp.float32),
    )
    return (
        result[None].astype(jnp.bfloat16),
        grad_tokens[None].astype(jnp.bfloat16),
        totals[0],
        totals[1],
        totals[2],
        totals[3],
        totals[4],
        totals[5],
        totals[6],
        totals[7],
        totals[8][0],
    )


MESH = pl.DeviceIdType.MESH
ANY = pl.BlockSpec(memory_space=pl.ANY)
VMEM = pl.BlockSpec(memory_space=pltpu.VMEM)
BF = jnp.bfloat16
F32 = jnp.float32


def fast_fits(mesh):
    return mesh.shape["ctx"] == H and mesh.shape["fs"] == 2


def remote(src, dst, ssem, rsem, target):
    return pltpu.make_async_remote_copy(
        src_ref=src, dst_ref=dst, send_sem=ssem, recv_sem=rsem, device_id=target, device_id_type=MESH
    )


def signal(target):
    pl.semaphore_signal(
        pltpu.get_barrier_semaphore(), inc=1, device_id=target, device_id_type=MESH
    )


def place():
    me = lax.axis_index("ctx")
    return me, lax.axis_index("fs"), me // 4, lax.rem(me // 2, 2), lax.rem(me, 2)


def dot(a, b, dims=((1,), (0,))):
    return lax.dot_general(a, b, (dims, ((), ())), preferred_element_type=F32)


NT = ((1,), (1,))
TN = ((0,), (0,))


LOG2E = math.log2(math.e)
UNITS = H // 2


def weight_pull(own, other, k, fs, me, ssem, rsem):
    half = own[0].shape[0] // 2
    rows = pl.ds(pl.multiple_of(k * half, 64), half)
    yn = (me, 1 - fs)
    sib = (me + 1 - 2 * k, fs)
    n = len(own)
    first = [remote(own[i].at[rows], other[i].at[rows], ssem.at[i], rsem.at[i], yn) for i in range(n)]
    second = [
        remote(other[i].at[rows], other[i].at[rows], ssem.at[n + i], rsem.at[n + i], sib)
        for i in range(n)
    ]
    return first, second


def visible(j, i, rows, first_key):
    kpos = j * rows + lax.broadcasted_iota(jnp.int32, (rows, rows), 0)
    qpos = i * rows + lax.broadcasted_iota(jnp.int32, (rows, rows), 1)
    return (kpos <= qpos) & (kpos >= first_key)


def forward_kernel(n_w, tok_ref, gain_ref, wt_ref, scale_ref, first_ref, *rest):
    own = rest[:n_w]
    at = n_w
    h_all, gain_full, attn_ref = rest[at : at + 3]
    o32_ref, lse_ref, qt_ref, q_ref, kt_ref, k_ref, v_ref, raw_ref = rest[at + 3 : at + 11]
    other = rest[at + 11 : at + 11 + n_w]
    (
        wt_all, gain_own, gain_other, o_sc, vt_sc, m_sc, l_sc, acc_sc,
        ssem, rsem, osend, orecv, wssem, wrsem, ysem, lsem,
    ) = rest[at + 11 + n_w :]
    me, fs, z, x, k = place()
    sib, xn, yn = (me + 1 - 2 * k, fs), (me + 2 - 4 * x, fs), (me, 1 - fs)
    up, dn = (me + 4, fs), (me - 4, fs)
    rows = tok_ref.shape[0]
    unit_rows = 2 * rows
    bar = pltpu.get_barrier_semaphore()
    for i in range(1, H):
        signal((lax.rem(me + i, H), fs))
    signal(yn)
    gain_own[...] = gain_ref[...]
    tokens = tok_ref[...].astype(F32)
    normed = tokens * lax.rsqrt(jnp.mean(tokens * tokens, axis=-1, keepdims=True) + epsilon)
    pl.semaphore_wait(bar, H)

    gain_copy = remote(gain_own, gain_other, ysem.at[0], ysem.at[1], yn)
    gain_copy.start()
    half = wt_ref.shape[1]
    columns = pl.ds(pl.multiple_of(fs * half, 128), half)
    wt_copy = remote(wt_ref, wt_all.at[:, columns], ysem.at[2], ysem.at[3], yn)
    wt_copy.start()
    wt_here = pltpu.make_async_copy(wt_ref, wt_all.at[:, columns], lsem.at[0])
    wt_here.start()
    first, second = weight_pull(own, other, k, fs, me, wssem, wrsem)
    gain_copy.wait()
    g_here = gain_own[...].astype(F32)
    g_there = gain_other[...].astype(F32)
    gains = jnp.where(
        fs == 0,
        jnp.concatenate([g_here, g_there], axis=1),
        jnp.concatenate([g_there, g_here], axis=1),
    )
    gain_full[...] = gains
    my_rows = pl.ds(pl.multiple_of(k * rows, rows), rows)
    h_all[me // 2, my_rows, :] = (normed * gains[0:1]).astype(BF)

    def slot(s):
        return h_all.at[s // 2, pl.ds(pl.multiple_of(lax.rem(s, 2) * rows, rows), rows)]

    def cp(s, t, si):
        return remote(slot(s), slot(s), ssem.at[si], rsem.at[s], t)

    cp(me, xn, 0).start()

    @pl.when(z < 3)
    def _():
        cp(me, up, 1).start()

    @pl.when(z > 0)
    def _():
        cp(me, dn, 2).start()

    cp(me, sib, 3).start()
    for c in first:
        c.start()
    wt_here.wait()
    wt_copy.wait()

    def project(u):
        qkv = dot(wt_all[...], h_all[u], NT)
        raw = qkv[:HD]
        raw_ref[u] = raw
        q32 = raw * scale_ref[...]
        qt_ref[u] = (q32 * LOG2E).astype(BF)
        q_ref[u] = q32.T.astype(BF)
        kt = qkv[HD : 2 * HD]
        vt = qkv[2 * HD :]
        kt_ref[u] = kt.astype(BF)
        k_ref[u] = kt.T.astype(BF)
        v_ref[u] = vt.T.astype(BF)
        vt_sc[u] = vt.astype(BF)
        m_sc[u] = jnp.full((1, unit_rows), neg_big, F32)
        l_sc[u] = jnp.zeros((1, unit_rows), F32)
        acc_sc[u] = jnp.zeros((HD, unit_rows), F32)

    def pair(j, i):
        s = dot(k_ref[j], qt_ref[i])
        s = jnp.where(visible(j, i, unit_rows, first_ref[i]), s, neg_big)
        run_max = m_sc[i]
        new_max = jnp.maximum(run_max, jnp.max(s, axis=0, keepdims=True))
        p = jnp.exp2(s - new_max)
        factor = jnp.exp2(run_max - new_max)
        l_sc[i] = l_sc[i] * factor + jnp.sum(p, axis=0, keepdims=True)
        acc_sc[i] = acc_sc[i] * factor + dot(vt_sc[j], p.astype(BF))
        m_sc[i] = new_max

    def when_here(uz, ux):
        return 4 * jnp.maximum(uz - z, z - uz) + 2 * jnp.maximum(ux - x, x - ux) + (uz + 4 - z) // 5

    def process(uz, ux):
        u = uz * 2 + ux
        cp(u * 2 + 1 - k, sib, 0).wait_recv()
        project(u)
        pair(u, u)
        mine = when_here(uz, ux)

        def earlier(e, c):
            @pl.when(when_here(e // 2, lax.rem(e, 2)) < mine)
            def _():
                pair(jnp.minimum(e, u), jnp.maximum(e, u))

            return c

        lax.fori_loop(0, UNITS, earlier, 0)

    xo = me + 2 - 4 * x

    def column_arrival(d):
        a = 4 + (d - 1) * 6

        @pl.when(z >= d)
        def _():
            s = me - 4 * d
            cp(s, dn, a).wait_recv()

            @pl.when(z < 3)
            def _():
                cp(s, up, a).start()

            cp(s, xn, a + 1).start()
            cp(s, sib, a + 2).start()

        @pl.when(z + d <= 3)
        def _():
            s = me + 4 * d
            cp(s, up, a + 3).wait_recv()

            @pl.when(z > 0)
            def _():
                cp(s, dn, a + 3).start()

            cp(s, xn, a + 4).start()
            cp(s, sib, a + 5).start()

    def across_arrival(d):
        @pl.when(z >= d)
        def _():
            s = xo - 4 * d
            cp(s, xn, 0).wait_recv()
            cp(s, sib, 22 + z - d).start()

        @pl.when((z + d <= 3) & (d > 0))
        def _():
            s = xo + 4 * d
            cp(s, xn, 0).wait_recv()
            cp(s, sib, 22 + z + d).start()

    def step(d, c):
        @pl.when((d >= 1) & (d <= 3))
        def _():
            column_arrival(d)

        @pl.when(d >= 1)
        def _():
            across_arrival(d - 1)

        for i in range(n_w):
            if i < 4:

                @pl.when(d == i + 1)
                def _(i=i):
                    first[i].wait_recv()
                    second[i].start()

        def compute(n, c2):
            across = 1 - n // 2
            dd = d - across
            uz = z + dd * (2 * lax.rem(n, 2) - 1)
            ux = x + across * (1 - 2 * x)
            ok = (dd >= 0) & (dd <= 3) & (uz >= 0) & (uz <= 3)
            ok = ok & ((dd > 0) | (lax.rem(n, 2) == 0))

            @pl.when(ok)
            def _():
                process(uz, ux)

            return c2

        lax.fori_loop(0, 4, compute, 0)
        return c

    lax.fori_loop(0, 5, step, 0)

    def out_copy(b):
        u = b // 2
        lanes = pl.ds(pl.multiple_of(lax.rem(b, 2) * rows, 128), rows)
        return o_sc.at[u, :, lanes]

    def finish(n, c):
        u = lax.rem(me // 2 + n, UNITS)
        out = acc_sc[u] / l_sc[u]
        o32_ref[u] = out
        o_sc[u] = out.astype(BF)
        lse_ref[u] = m_sc[u] + jnp.log2(l_sc[u])

        def send(e, c2):
            b = u * 2 + e

            @pl.when(b != me)
            def _():
                remote(out_copy(b), attn_ref.at[me], osend.at[b], orecv.at[me], (b, fs)).start()

            @pl.when(b == me)
            def _():
                pltpu.make_async_copy(out_copy(b), attn_ref.at[me], lsem.at[1]).start()

            return c2

        return lax.fori_loop(0, 2, send, c)

    lax.fori_loop(0, UNITS, finish, 0)
    for i in range(4, n_w):
        first[i].wait_recv()
        second[i].start()

    def taken(b, c):
        @pl.when(b != me)
        def _():
            remote(out_copy(b), attn_ref.at[b], osend.at[b], orecv.at[b], (b, fs)).wait()

        return c

    lax.fori_loop(0, H, taken, 0)
    pltpu.make_async_copy(out_copy(me), attn_ref.at[me], lsem.at[1]).wait()
    cp(me, xn, 0).wait_send()

    @pl.when(z < 3)
    def _():
        cp(me, up, 1).wait_send()

    @pl.when(z > 0)
    def _():
        cp(me, dn, 2).wait_send()

    cp(me, sib, 3).wait_send()

    def sent(d, c):
        a = 4 + (d - 1) * 6

        @pl.when(z >= d)
        def _():
            s = me - 4 * d

            @pl.when(z < 3)
            def _():
                cp(s, up, a).wait_send()

            cp(s, xn, a + 1).wait_send()
            cp(s, sib, a + 2).wait_send()

        @pl.when(z + d <= 3)
        def _():
            s = me + 4 * d

            @pl.when(z > 0)
            def _():
                cp(s, dn, a + 3).wait_send()

            cp(s, xn, a + 4).wait_send()
            cp(s, sib, a + 5).wait_send()

        return c

    lax.fori_loop(1, 4, sent, 0)

    def sent_across(zz, c):
        cp(xo + 4 * (zz - z), sib, 22 + zz).wait_send()
        return c

    lax.fori_loop(0, 4, sent_across, 0)
    for i in range(n_w):
        first[i].wait_send()
        second[i].wait()


def forward_call(tok, gains, wt, scale_col, first_key, weights):
    n_w = len(weights)
    rows, width = tok.shape
    ur = 2 * rows

    def out(dtype, *shape):
        return jax.ShapeDtypeStruct((UNITS, *shape), dtype)

    shapes = [
        out(BF, ur, width),
        jax.ShapeDtypeStruct((gains.shape[0], 2 * gains.shape[1]), F32),
        jax.ShapeDtypeStruct((H, HD, rows), BF),
        out(F32, HD, ur), out(F32, 1, ur), out(BF, HD, ur), out(BF, ur, HD), out(BF, HD, ur),
        out(BF, ur, HD), out(BF, ur, HD), out(F32, HD, ur),
    ] + [jax.ShapeDtypeStruct(w.shape, BF) for w in weights]
    return pl.pallas_call(
        functools.partial(forward_kernel, n_w),
        out_shape=shapes,
        in_specs=[VMEM] * 5 + [ANY] * n_w,
        out_specs=[VMEM, VMEM, ANY] + [VMEM] * 8 + [ANY] * n_w,
        scratch_shapes=[
            pltpu.VMEM((wt.shape[0], 2 * wt.shape[1]), BF),
            pltpu.VMEM(gains.shape, BF),
            pltpu.VMEM(gains.shape, BF),
            pltpu.VMEM((UNITS, HD, ur), BF),
            pltpu.VMEM((UNITS, HD, ur), BF),
            pltpu.VMEM((UNITS, 1, ur), F32),
            pltpu.VMEM((UNITS, 1, ur), F32),
            pltpu.VMEM((UNITS, HD, ur), F32),
            pltpu.SemaphoreType.DMA((26,)),
            pltpu.SemaphoreType.DMA((H,)),
            pltpu.SemaphoreType.DMA((H,)),
            pltpu.SemaphoreType.DMA((H,)),
            pltpu.SemaphoreType.DMA((2 * n_w,)),
            pltpu.SemaphoreType.DMA((2 * n_w,)),
            pltpu.SemaphoreType.DMA((4,)),
            pltpu.SemaphoreType.DMA((2,)),
        ],
        compiler_params=pltpu.CompilerParams(
            collective_id=1, has_side_effects=True, vmem_limit_bytes=56 * 2**20
        ),
        name="forward",
    )(tok, gains, wt, scale_col, first_key, *weights)


def half_rows(start, size, align):
    return pl.ds(pl.multiple_of(start, align), size)


def tail_kernel(n_w, gt_ref, *rest):
    own = rest[:3]
    held = rest[3 : 6 - n_w]
    at = 6 - n_w
    (
        attn_ref, gr_ref, hid_ref, gip_ref, act_ref, cot_ref, tok_ref, gain_ref, g2_ref,
        h_ref, scale_ref, first_ref, k_ref, v_ref, kt_ref, raw_ref, q_ref, qt_ref, o_ref, lse_ref,
    ) = rest[at : at + 20]
    at += 20
    all_ref, tg_ref, sums_ref = rest[at : at + 3]
    pulled = rest[at + 3 : at + 3 + n_w]
    (
        g_in, g_sc, delta_sc, dq_sc, scale_sc, dk_sc, dv_sc, d_sc, got, dw_sc, dw_out, dw_got, piece,
        s1, r0, so, ra, rb, r2, rz, e_sc, small_out, small_in, small_y, small_got,
        gsend, grecv, qsend, qrecv, ksend, krecv, wssem, wrsem, dsend, drecv, psend, precv,
        asend, arecv, vsend, vrecv, lsem, wsem,
    ) = rest[at + 3 + n_w :]
    me, fs, z, x, k = place()
    sib, xn, yn = (me + 1 - 2 * k, fs), (me + 2 - 4 * x, fs), (me, 1 - fs)
    up, dn = (me + 4, fs), (me - 4, fs)
    units, rows = h_ref.shape[:2]
    block = rows // 2
    n_g = 3
    part = s1.shape[2]
    width = s1.shape[3]
    cols = width // 2
    bar = pltpu.get_barrier_semaphore()
    for i in range(1, H):
        signal((lax.rem(me + i, H), fs))
    signal(yn)
    pl.semaphore_wait(bar, H)

    def lanes(b):
        return half_rows(lax.rem(b, 2) * block, block, 128)

    def g_copy(b, t):
        return remote(
            gt_ref.at[b], g_in.at[t // 2, :, lanes(t)], gsend.at[b], grecv.at[t], (b, fs)
        )

    def g_start(n, c):
        g_copy(lax.rem(me + n, H), me).start()
        return c

    lax.fori_loop(1, H, g_start, 0)
    g_here = pltpu.make_async_copy(gt_ref.at[me], g_in.at[me // 2, :, lanes(me)], lsem.at[0])
    g_here.start()

    def theirs(g):
        return remote(so.at[g], r0.at[g], dsend.at[g], drecv.at[g], sib)

    def dense_rows(g, start):
        r = half_rows(start, part, 64)
        if g == 0:
            return dot(attn_ref[r, :], gr_ref[...])
        a, b = ((hid_ref, gip_ref), (act_ref, cot_ref))[g - 1]
        return dot(a[r, :], b[...])

    for g in range(n_g):
        for f in range(2):
            so[g, f] = dense_rows(g, f * 2 * part + (1 - k) * part).astype(BF)
        theirs(g).start()
    for g in range(n_g):
        for f in range(2):
            s1[g, f] = dense_rows(g, f * 2 * part + k * part).astype(BF)

    top, bottom = slice(0, part // 2), slice(part // 2, part)
    x_here = half_rows(x * cols, cols, 128)
    x_there = half_rows((1 - x) * cols, cols, 128)

    def stage(g, i):
        ends = (
            (s1.at[g, 1 - fs, top, :], ra.at[g], yn),
            (s1.at[g, :, bottom, x_there], rb.at[g], xn),
            (s1.at[g, fs, top, x_there], r2.at[g, top], xn),
            (s1.at[g, 1 - fs, bottom, x_here], r2.at[g, bottom], yn),
        )[i]
        return remote(ends[0], ends[1], psend.at[i, g], precv.at[i, g], ends[2])

    slab = part // 4

    def z_copy(t, slot, sem):
        return remote(
            s1.at[:, fs, half_rows(t * slab, slab, 16), x_here],
            rz.at[slot], psend.at[4, sem], precv.at[4, slot], (me + 4 * (t - z), fs),
        )

    for g in range(n_g):
        theirs(g).wait()

        def add(i, c, g=g):
            r = half_rows(i * 32, 32, 32)
            for f in range(2):
                s1[g, f, r, :] += r0[g, f, r, :]
            return c

        lax.fori_loop(0, part // 32, add, 0)
        stage(g, 0).start()
        stage(g, 1).start()

    loads = []
    for w in range(3):
        for f in range(2):
            loads.append(
                pltpu.make_async_copy(own[w].at[pl.ds(f * part, part)], r0.at[w, f], wsem.at[w * 2 + f])
            )
            loads[-1].start()
    for w in range(3 - n_w):
        for f in range(2):
            loads.append(
                pltpu.make_async_copy(held[w].at[pl.ds(f * part, part)], so.at[w, f], wsem.at[6 + w * 2 + f])
            )
            loads[-1].start()
    first, second = weight_pull(own[3 - n_w :], pulled, k, fs, me, wssem, wrsem)

    def after_one():
        for g in range(n_g):
            stage(g, 0).wait()
            stage(g, 1).wait()

            def add(i, c, g=g):
                r = half_rows(i * 32, 32, 32)
                s1[g, fs, r, :] += ra[g, r, :]
                low = half_rows(part // 2 + i * 32, 32, 32)
                for f in range(2):
                    s1[g, f, low, x_here] += rb[g, f, r, :]
                return c

            lax.fori_loop(0, part // 64, add, 0)
            stage(g, 2).start()
            stage(g, 3).start()
        for c in first:
            c.start()

    def after_two():
        for g in range(n_g):
            stage(g, 2).wait()
            stage(g, 3).wait()

            def add(i, c, g=g):
                r = half_rows(i * 32, 32, 32)
                s1[g, fs, r, x_here] += r2[g, r, :]
                return c

            lax.fori_loop(0, part // 32, add, 0)
        for d in range(1, 4):
            t = lax.rem(z + d, 4)
            z_copy(t, z, d).start()

    def after_three():
        for d in range(1, 4):
            t = lax.rem(z + d, 4)
            z_copy(t, t, d).wait()
        here = half_rows(z * slab, slab, 16)
        for g in range(n_g):
            total = s1[g, fs, here, x_here].astype(F32)
            for d in range(1, 4):
                total = total + rz[lax.rem(z + d, 4), g].astype(F32)
            piece[0, g] = total.astype(BF)

    scale_sc[...] = jnp.zeros_like(scale_sc)
    dw_sc[...] = jnp.zeros_like(dw_sc)

    def g_taken(n, c):
        b = lax.rem(me + n, H)
        g_copy(b, b).wait()
        return c

    g_here.wait()
    lax.fori_loop(1, H, g_taken, 0)

    def prepare(i, c):
        g = g_in[i].astype(F32)
        g_sc[i] = g.T.astype(BF)
        delta_sc[i] = jnp.sum(g * o_ref[i], axis=0, keepdims=True)
        dq_sc[i] = jnp.zeros((HD, rows), F32)
        return c

    lax.fori_loop(0, units, prepare, 0)

    def pair(masked, j, i):
        s = dot(k_ref[j], qt_ref[i])
        if masked:
            s = jnp.where(visible(j, i, rows, first_ref[i]), s, neg_big)
        p = jnp.exp2(s - lse_ref[i])
        dv_sc[...] += dot(p.astype(BF), g_sc[i])
        dp = dot(v_ref[j], g_in[i])
        ds = (p * (dp - delta_sc[i])).astype(BF)
        dk_sc[...] += dot(ds, q_ref[i])
        dq_sc[i] += dot(kt_ref[j], ds)

    def out(b, lo, n):
        return d_sc.at[b // 2, pl.ds(lo, n), :, lanes(b)]

    def to(t, lo, n):
        return got.at[pl.ds(lo, n), half_rows(t * HD, HD, 16)]

    def kv_copy(b, t):
        return remote(out(b, 1, 2), to(t, 1, 2), ksend.at[b], krecv.at[t], (b, fs))

    def q_copy(b, t):
        return remote(out(b, 0, 1), to(t, 0, 1), qsend.at[b], qrecv.at[t], (b, fs))

    kv_here = pltpu.make_async_copy(out(me, 1, 2), to(me, 1, 2), lsem.at[1])
    q_here = pltpu.make_async_copy(out(me, 0, 1), to(me, 0, 1), lsem.at[2])

    def column(n, c):
        j = lax.rem(me // 2 + n, units)
        dk_sc[...] = jnp.zeros_like(dk_sc)
        dv_sc[...] = jnp.zeros_like(dv_sc)
        pair(True, j, j)

        def plain(i, c2):
            pair(False, j, i)
            return c2

        def edge(i, c2):
            pair(True, j, i)
            return c2

        end = jnp.where(j == 0, 1, units - 1)
        lax.fori_loop(j + 1, end, plain, 0)
        lax.fori_loop(jnp.maximum(j + 1, end), units, edge, 0)
        d_sc[j, 1] = dk_sc[...].T.astype(BF)
        d_sc[j, 2] = dv_sc[...].T.astype(BF)

        def send(e, c2):
            b = 2 * j + e

            @pl.when(b != me)
            def _():
                kv_copy(b, me).start()

            @pl.when(b == me)
            def _():
                kv_here.start()

            return c2

        lax.fori_loop(0, 2, send, 0)
        for e in range(2):
            dw_sc[1 + e] += dot(d_sc[j, 1 + e], h_ref[j])

        @pl.when(n == ONE_AT)
        def _():
            after_one()

        @pl.when(n == TWO_AT)
        def _():
            after_two()

        return c

    lax.fori_loop(0, units, column, 0)

    def queries(n, c):
        i = lax.rem(me // 2 + n, units)
        dq = dq_sc[i]
        scale_sc[...] += dq * raw_ref[i]
        d_sc[i, 0] = (dq * scale_ref[...]).astype(BF)

        def send(e, c2):
            b = 2 * i + e

            @pl.when(b != me)
            def _():
                q_copy(b, me).start()

            @pl.when(b == me)
            def _():
                q_here.start()

            return c2

        lax.fori_loop(0, 2, send, 0)
        return c

    lax.fori_loop(0, units, queries, 0)
    for i in range(n_w):
        first[i].wait_recv()
        second[i].start()

    def query_weight(i, c):
        dw_sc[0] += dot(d_sc[i, 0], h_ref[i])
        return c

    lax.fori_loop(0, units, query_weight, 0)
    half = dw_out.shape[2]
    dw_out[...] = dw_sc[:, :, half_rows((1 - fs) * half, half, 128)].astype(BF)
    dw_copy = remote(dw_out, dw_got, vsend.at[H], vrecv.at[H], yn)
    dw_copy.start()
    small_out[...] = jnp.zeros_like(small_out)
    small_out[1:2, :] = g2_ref[...]
    small_out[2:3, :HD] = jnp.sum(scale_sc[...].T, axis=0, keepdims=True)

    def cp(p, s, t, si, mine=False):
        here = all_ref.at[s, p]
        return remote(piece.at[p] if mine else here, here, asend.at[p, si], arecv.at[p, s], t)

    def keep(p):
        return pltpu.make_async_copy(piece.at[p], all_ref.at[me, p], lsem.at[3 + p])

    def begin(p):
        keep(p).start()
        cp(p, me, xn, 0, True).start()

        @pl.when(z < 3)
        def _():
            cp(p, me, up, 1, True).start()

        @pl.when(z > 0)
        def _():
            cp(p, me, dn, 2, True).start()

        cp(p, me, sib, 3, True).start()

    def column_arrival(p, d):
        a = 4 + (d - 1) * 6

        @pl.when(z >= d)
        def _():
            s = me - 4 * d
            cp(p, s, dn, a).wait_recv()

            @pl.when(z < 3)
            def _():
                cp(p, s, up, a).start()

            cp(p, s, xn, a + 1).start()
            cp(p, s, sib, a + 2).start()

        @pl.when(z + d <= 3)
        def _():
            s = me + 4 * d
            cp(p, s, up, a + 3).wait_recv()

            @pl.when(z > 0)
            def _():
                cp(p, s, dn, a + 3).start()

            cp(p, s, xn, a + 4).start()
            cp(p, s, sib, a + 5).start()

    xo = me + 2 - 4 * x

    def across_arrival(p, d):
        @pl.when(z >= d)
        def _():
            s = xo - 4 * d
            cp(p, s, xn, 0).wait_recv()
            cp(p, s, sib, 22 + z - d).start()

        if d > 0:

            @pl.when(z + d <= 3)
            def _():
                s = xo + 4 * d
                cp(p, s, xn, 0).wait_recv()
                cp(p, s, sib, 22 + z + d).start()

    dw_copy.wait()
    piece[1] = (dw_sc[:, :, half_rows(fs * half, half, 128)] + dw_got[...].astype(F32)).astype(BF)
    begin(1)
    after_three()
    begin(0)
    column_arrival(1, 1)

    for w in range(3 - n_w, 3):
        i = w - (3 - n_w)
        second[i].wait()
        first[i].wait_send()
        for f in range(2):
            loads.append(
                pltpu.make_async_copy(pulled[i].at[pl.ds(f * part, part)], so.at[w, f], wsem.at[6 + w * 2 + f])
            )
            loads[-1].start()

    def taken(n, c):
        b = lax.rem(me + n, H)
        kv_copy(b, b).wait()
        q_copy(b, b).wait()
        return c

    lax.fori_loop(1, H, taken, 0)
    kv_here.wait()
    q_here.wait()
    for c in loads:
        c.wait()

    def input_grad(w):
        for r, m in ((fs, r0), (1 - fs, so)):
            for f in range(2):
                at_rows = half_rows((r * 2 + f) * part, part, 64)
                term = dot(m[w, f], got[w])
                if w == 0:
                    e_sc[at_rows, :] = term
                else:
                    e_sc[at_rows, :] += term

    input_grad(0)
    column_arrival(0, 1)
    column_arrival(1, 2)
    input_grad(1)
    across_arrival(1, 0)
    across_arrival(0, 0)
    column_arrival(0, 2)
    column_arrival(1, 3)
    input_grad(2)
    grad_hidden = e_sc[...].T
    tokens = tok_ref[...].astype(F32)
    scale = lax.rsqrt(jnp.mean(tokens * tokens, axis=-1, keepdims=True) + epsilon)
    normed = tokens * scale
    small_out[0:1, :] = jnp.sum(grad_hidden * normed, axis=0, keepdims=True)

    def v_copy(b, t):
        return remote(small_out, small_in.at[t], vsend.at[b], vrecv.at[t], (b, fs))

    def v_start(n, c):
        v_copy(lax.rem(me + n, H), me).start()
        return c

    lax.fori_loop(1, H, v_start, 0)
    across_arrival(1, 1)
    across_arrival(0, 1)
    column_arrival(0, 3)
    e = grad_hidden * gain_ref[0:1, :]
    tg_ref[...] = (
        gr_ref[...].astype(F32) + scale * (e - normed * jnp.mean(e * normed, axis=-1, keepdims=True))
    ).astype(BF)

    def v_taken(n, c):
        b = lax.rem(me + n, H)
        v_copy(b, b).wait()
        return c

    lax.fori_loop(1, H, v_taken, 0)

    def v_add(n, total):
        return total + small_in[lax.rem(me + n, H)]

    small_y[...] = lax.fori_loop(1, H, v_add, small_out[...])
    y_copy = remote(small_y, small_got, vsend.at[H + 1], vrecv.at[H + 1], yn)
    y_copy.start()
    for d in range(2, 4):
        across_arrival(1, d)
        across_arrival(0, d)
    y_copy.wait()
    sums_ref[...] = small_y[...] + small_got[...]

    for p in range(2):

        def from_sib(n, c, p=p):
            cp(p, n * 2 + 1 - k, sib, 0).wait_recv()
            return c

        lax.fori_loop(0, UNITS, from_sib, 0)
        keep(p).wait()
        cp(p, me, xn, 0, True).wait_send()

        @pl.when(z < 3)
        def _(p=p):
            cp(p, me, up, 1, True).wait_send()

        @pl.when(z > 0)
        def _(p=p):
            cp(p, me, dn, 2, True).wait_send()

        cp(p, me, sib, 3, True).wait_send()

        def sent(d, c, p=p):
            a = 4 + (d - 1) * 6

            @pl.when(z >= d)
            def _():
                s = me - 4 * d

                @pl.when(z < 3)
                def _():
                    cp(p, s, up, a).wait_send()

                cp(p, s, xn, a + 1).wait_send()
                cp(p, s, sib, a + 2).wait_send()

            @pl.when(z + d <= 3)
            def _():
                s = me + 4 * d

                @pl.when(z > 0)
                def _():
                    cp(p, s, dn, a + 3).wait_send()

                cp(p, s, xn, a + 4).wait_send()
                cp(p, s, sib, a + 5).wait_send()

            return c

        lax.fori_loop(1, 4, sent, 0)

        def sent_across(zz, c, p=p):
            cp(p, xo + 4 * (zz - z), sib, 22 + zz).wait_send()
            return c

        lax.fori_loop(0, 4, sent_across, 0)


ONE_AT = 2
TWO_AT = 5


def tail_call(gt, own, held, vm):
    n_w = 3 - len(held)
    rows, width = vm[1].shape
    n, ur = vm[9].shape[:2]
    half = width // 2
    part = width // 4
    sem = pltpu.SemaphoreType.DMA
    return pl.pallas_call(
        functools.partial(tail_kernel, n_w),
        out_shape=[
            jax.ShapeDtypeStruct((H, 2, 3, part // 4, half), BF),
            jax.ShapeDtypeStruct((rows, width), BF),
            jax.ShapeDtypeStruct((8, width), F32),
        ]
        + [jax.ShapeDtypeStruct(own[0].shape, BF)] * n_w,
        in_specs=[ANY] * (4 + len(held)) + [VMEM] * len(vm),
        out_specs=[ANY, VMEM, VMEM] + [ANY] * n_w,
        scratch_shapes=[
            pltpu.VMEM((n, HD, ur), BF),
            pltpu.VMEM((n, ur, HD), BF),
            pltpu.VMEM((n, 1, ur), F32),
            pltpu.VMEM((n, HD, ur), F32),
            pltpu.VMEM((HD, ur), F32),
            pltpu.VMEM((ur, HD), F32),
            pltpu.VMEM((ur, HD), F32),
            pltpu.VMEM((n, 3, HD, ur), BF),
            pltpu.VMEM((3, H * HD, rows), BF),
            pltpu.VMEM((3, HD, width), F32),
            pltpu.VMEM((3, HD, half), BF),
            pltpu.VMEM((3, HD, half), BF),
            pltpu.VMEM((2, 3, part // 4, half), BF),
            pltpu.VMEM((3, 2, part, width), BF),
            pltpu.VMEM((3, 2, part, width), BF),
            pltpu.VMEM((3, 2, part, width), BF),
            pltpu.VMEM((3, part // 2, width), BF),
            pltpu.VMEM((3, 2, part // 2, half), BF),
            pltpu.VMEM((3, part, half), BF),
            pltpu.VMEM((4, 3, part // 4, half), BF),
            pltpu.VMEM((width, rows), F32),
            pltpu.VMEM((8, width), F32),
            pltpu.VMEM((H, 8, width), F32),
            pltpu.VMEM((8, width), F32),
            pltpu.VMEM((8, width), F32),
            sem((H,)), sem((H,)), sem((H,)), sem((H,)), sem((H,)), sem((H,)),
            sem((max(1, 2 * n_w),)), sem((max(1, 2 * n_w),)), sem((3,)), sem((3,)), sem((5, 4)), sem((5, 4)),
            sem((2, 26)), sem((2, H)), sem((H + 2,)), sem((H + 2,)), sem((5,)), sem((12,)),
        ],
        compiler_params=pltpu.CompilerParams(
            collective_id=2, has_side_effects=True, vmem_limit_bytes=62 * 2**20
        ),
        name="tail",
    )(gt, *own, *held, *vm)


def spread_kernel(dense_ref, heads_ref, *outs):
    slab, cols = dense_ref.shape[-2:]
    n, _, _, hd, _ = heads_ref.shape
    for zz in range(4):
        for xx in range(2):
            outs[0][zz * slab : (zz + 1) * slab, xx * cols : (xx + 1) * cols] = dense_ref[
                zz, xx, 0, 0, 0
            ].astype(F32)
    outs[1][...] = heads_ref[...].reshape(n * hd, cols).astype(F32).T


def spread_call(pieces, w):
    n, _, _, slab, cols = pieces.shape
    split = pieces.reshape(4, 2, 2, 2, 3, slab, cols)
    return pl.pallas_call(
        spread_kernel,
        grid=(2,),
        out_shape=[
            jax.ShapeDtypeStruct((8 * slab, 2 * cols), F32),
            jax.ShapeDtypeStruct((cols, n * slab), F32),
        ],
        in_specs=[
            pl.BlockSpec((4, 2, 1, 1, 1, slab, cols), lambda h: (0, 0, h, 0, w, 0, 0)),
            pl.BlockSpec((n // 2, 1, 1, slab, cols), lambda h: (h, 1, w, 0, 0)),
        ],
        out_specs=[
            pl.BlockSpec((4 * slab, 2 * cols), lambda h: (h, 0)),
            pl.BlockSpec((cols, n * slab // 2), lambda h: (0, h)),
        ],
        compiler_params=pltpu.CompilerParams(vmem_limit_bytes=48 * 2**20),
        name="spread",
    )(split, pieces)


def joined(own, other, fs):
    return jnp.where(
        fs == 0, jnp.concatenate([own, other], axis=0), jnp.concatenate([other, own], axis=0)
    )


def fast_local(
    tokens, query_weight, key_weight, value_weight, out_weight, inner_weight, outer_weight,
    attn_gain, mlp_gain, query_scale, doc_starts, cotangent,
):
    me, fs = lax.axis_index("ctx"), lax.axis_index("fs")
    rows, width = tokens.shape[1:]
    tok = tokens[0]
    cot = cotangent[0]

    def head_columns(w):
        return lax.dynamic_slice(w, (0, me * HD), (w.shape[0], HD)).T

    wt = jnp.concatenate([head_columns(w) for w in (query_weight, key_weight, value_weight)], axis=0)
    gains = jnp.stack([attn_gain, mlp_gain])
    positions = jnp.arange(H * rows, dtype=jnp.int32)
    starts = doc_starts[0]
    first_key = jnp.max(
        jnp.where(starts[None, :] <= positions[:, None], starts[None, :], 0), axis=1
    ).reshape(UNITS, 1, 2 * rows)
    scale_col = (query_scale / math.sqrt(HD))[:, None]

    (
        h_all, gain_full, attn_t, o32, lse, qt, q, kt, k, v, raw,
        out_o, inner_o, outer_o, query_o,
    ) = forward_call(
        tok, gains, wt, scale_col, first_key,
        (out_weight, inner_weight, outer_weight, query_weight),
    )
    attn_t = attn_t.reshape(width, rows)

    out_full = joined(out_weight, out_o, fs)
    inner_full = joined(inner_weight, inner_o, fs)
    outer_full = joined(outer_weight, outer_o, fs)
    gain_one, gain_two = gain_full[0:1], gain_full[1:2]
    token_rows = tok.astype(F32)
    resid = token_rows + dot(attn_t, out_full, TN)
    scale_two = rms_scale(resid)
    normed_two = resid * scale_two
    hidden_two = (normed_two * gain_two).astype(BF)
    inner_pre = dot(hidden_two, inner_full)
    active = jax.nn.silu(inner_pre).astype(BF)
    result = (resid + dot(active, outer_full)).astype(BF)
    grad_active = dot(cot, outer_full, NT)
    sig = jax.nn.sigmoid(inner_pre)
    grad_inner_pre = (grad_active * sig * (1.0 + inner_pre * (1.0 - sig))).astype(BF)
    grad_hidden_two = dot(grad_inner_pre, inner_full, NT)
    grad_gain_two = jnp.sum(grad_hidden_two * normed_two, axis=0)
    grad_resid = (
        cot.astype(F32) + norm_back(grad_hidden_two * gain_two, normed_two, scale_two)
    ).astype(BF)
    grad_att_t = dot(out_full, grad_resid, NT).astype(BF).reshape(H, HD, rows)
    half = width // 2
    pieces, grad_tokens, sums, *_ = tail_call(
        grad_att_t, (query_weight, key_weight, value_weight), (query_o,),
        (
            attn_t, grad_resid, hidden_two.T, grad_inner_pre, active.T, cot, tok, gain_full,
            grad_gain_two[None], h_all, scale_col, first_key, k, v, kt, raw, q, qt, o32, lse,
        ),
    )
    (out_g, query_g), (inner_g, key_g), (outer_g, value_g) = [spread_call(pieces, w) for w in range(3)]
    gain_sums = lax.dynamic_slice(sums, (0, fs * half), (2, half))
    return (
        result[None], grad_tokens[None], query_g, key_g, value_g, out_g, inner_g, outer_g,
        gain_sums[0], gain_sums[1], sums[2, :HD] / math.sqrt(HD),
    )


def solution(mesh):
    placed = (
        P("fs", "ctx", None),
        P("fs", None),
        P("fs", None),
        P("fs", None),
        P("fs", None),
        P("fs", None),
        P("fs", None),
        P("fs"),
        P("fs"),
        P(),
        P("fs", None),
        P("fs", "ctx", None),
    )
    return jax.shard_map(
        fast_local if fast_fits(mesh) else general_local,
        mesh=mesh,
        in_specs=placed,
        out_specs=(
            P("fs", "ctx", None),
            P("fs", "ctx", None),
            P("fs", None),
            P("fs", None),
            P("fs", None),
            P("fs", None),
            P("fs", None),
            P("fs", None),
            P("fs"),
            P("fs"),
            P(),
        ),
        check_vma=False,
    )
```

```python
import functools
import math

import jax
import jax.numpy as jnp
from jax import lax
from jax.experimental import pallas as pl
from jax.experimental.pallas import tpu as pltpu
from jax.sharding import PartitionSpec as P

H = 16
HD = 80


epsilon = 1e-06
neg_big = -1e30


def passed_along(block, axis, distance):
    devices = range(lax.axis_size(axis))
    route = [((i - distance) % len(devices), i) for i in devices]
    return lax.ppermute(block, axis, route)


def shifted(value, axis, steps):
    count = lax.axis_size(axis)
    leading, last = (max(0, -steps), min(count, count - steps))
    return lax.ppermute(value, axis, [(source, source + steps) for source in range(leading, last)])


def rms_scale(values_in):
    return lax.rsqrt(jnp.mean(values_in * values_in, axis=-1, keepdims=True) + epsilon)


def norm_back(grad_normed, normed, scale_rows):
    inner_mean = jnp.mean(grad_normed * normed, axis=-1, keepdims=True)
    return scale_rows * (grad_normed - normed * inner_mean)


def segment_of(positions, starts_row):
    return jnp.sum((starts_row[None, :] <= positions[:, None]).astype(jnp.int32), axis=1) - 1


def block_mask(query_pos, query_seg, key_pos, key_seg):
    return (key_pos[None, :] <= query_pos[:, None]) & (key_seg[None, :] == query_seg[:, None])


def scores_of(query_block, key_block):
    return jnp.einsum("qhd,khd->hqk", query_block, key_block, preferred_element_type=jnp.float32)


def pass_grads(grad_key_acc, grad_value_acc):
    return (
        passed_along(grad_key_acc.astype(jnp.bfloat16), "ctx", 1).astype(grad_key_acc.dtype),
        passed_along(grad_value_acc.astype(jnp.bfloat16), "ctx", 1).astype(grad_value_acc.dtype),
    )


def general_local(
    tokens,
    query_weight,
    key_weight,
    value_weight,
    out_weight,
    inner_weight,
    outer_weight,
    attn_gain,
    mlp_gain,
    query_scale,
    doc_starts,
    cotangent,
):
    row_count = tokens.shape[1]
    model_width = tokens.shape[2]
    ctx_count = lax.axis_size("ctx")
    ctx_place = lax.axis_index("ctx")
    (
        query_full,
        key_full,
        value_full,
        out_full,
        inner_full,
        outer_full,
        attn_gain_full,
        mlp_gain_full,
    ) = (
        lax.all_gather(query_weight, "fs", axis=0, tiled=True),
        lax.all_gather(key_weight, "fs", axis=0, tiled=True),
        lax.all_gather(value_weight, "fs", axis=0, tiled=True),
        lax.all_gather(out_weight, "fs", axis=0, tiled=True),
        lax.all_gather(inner_weight, "fs", axis=0, tiled=True),
        lax.all_gather(outer_weight, "fs", axis=0, tiled=True),
        lax.all_gather(attn_gain, "fs", axis=0, tiled=True),
        lax.all_gather(mlp_gain, "fs", axis=0, tiled=True),
    )
    starts_row = doc_starts[0]
    local_pos = ctx_place * row_count + jnp.arange(row_count, dtype=jnp.int32)
    local_seg = segment_of(local_pos, starts_row)

    def heads_of(flat_block):
        return flat_block.reshape(row_count, H, HD)

    token_rows = tokens[0].astype(jnp.float32)
    scale_one = rms_scale(token_rows)
    normed_one = token_rows * scale_one
    gain_one = attn_gain_full.astype(jnp.float32)
    hidden_one = (normed_one * gain_one).astype(jnp.bfloat16)
    query_raw = jnp.dot(hidden_one, query_full, preferred_element_type=jnp.float32)
    scale_vec = jnp.tile(query_scale, H) / math.sqrt(HD)
    queries = heads_of((query_raw * scale_vec).astype(jnp.bfloat16))
    key_rows = jnp.dot(hidden_one, key_full, preferred_element_type=jnp.float32).astype(
        jnp.bfloat16
    )
    value_rows = jnp.dot(hidden_one, value_full, preferred_element_type=jnp.float32).astype(
        jnp.bfloat16
    )

    def key_info(turn_index):
        source = (ctx_place - turn_index) % ctx_count
        key_pos = source * row_count + jnp.arange(row_count, dtype=jnp.int32)
        return (source, key_pos, segment_of(key_pos, starts_row))

    def keep_state(state_in):
        return state_in

    def attend(softmax_state, key_flat, value_flat, turn_index):
        source, key_pos, key_seg = key_info(turn_index)

        def compute(state_in):
            run_max, run_sum, run_acc = state_in
            key_block = heads_of(key_flat)
            value_block = heads_of(value_flat)
            allowed = block_mask(local_pos, local_seg, key_pos, key_seg)
            scores = jnp.where(allowed[None], scores_of(queries, key_block), neg_big)
            new_max = jnp.maximum(run_max, jnp.max(scores, axis=-1))
            weights = jnp.where(allowed[None], jnp.exp(scores - new_max[..., None]), 0.0)
            factor = jnp.exp(run_max - new_max)
            run_sum = run_sum * factor + jnp.sum(weights, axis=-1)
            run_acc = run_acc * factor[..., None] + jnp.einsum(
                "hqk,khd->hqd",
                weights.astype(jnp.bfloat16),
                value_block,
                preferred_element_type=jnp.float32,
            )
            return (new_max, run_sum, run_acc)

        return lax.cond(source <= ctx_place, compute, keep_state, softmax_state)

    start_state = (
        jnp.full((H, row_count), neg_big, jnp.float32),
        jnp.zeros((H, row_count), jnp.float32),
        jnp.zeros((H, row_count, HD), jnp.float32),
    )
    start_state = attend(start_state, key_rows, value_rows, jnp.int32(0))
    stores = ()

    def forward_turn(turn_index, loop_state):
        key_block, value_block, softmax_state, kept = loop_state
        key_block, value_block = shifted((key_block, value_block), "ctx", 1)
        softmax_state = attend(softmax_state, key_block, value_block, turn_index)
        return (key_block, value_block, softmax_state, kept)

    loop_out = lax.fori_loop(
        1, ctx_count, forward_turn, (key_rows, value_rows, start_state, stores)
    )
    run_max, run_sum, run_acc = loop_out[2]
    stores = loop_out[3]
    log_total = run_max + jnp.log(run_sum)
    attn_heads = run_acc / run_sum[..., None]
    attn_low = (
        jnp.transpose(attn_heads, (1, 0, 2)).reshape(row_count, model_width).astype(jnp.bfloat16)
    )
    resid = token_rows + jnp.dot(attn_low, out_full, preferred_element_type=jnp.float32)
    scale_two = rms_scale(resid)
    normed_two = resid * scale_two
    gain_two = mlp_gain_full.astype(jnp.float32)
    hidden_two = (normed_two * gain_two).astype(jnp.bfloat16)
    inner_pre = jnp.dot(hidden_two, inner_full, preferred_element_type=jnp.float32)
    active = jax.nn.silu(inner_pre).astype(jnp.bfloat16)
    result = resid + jnp.dot(active, outer_full, preferred_element_type=jnp.float32)
    grad_out = cotangent[0]
    grad_active = jnp.dot(grad_out, outer_full.T, preferred_element_type=jnp.float32)
    grad_outer = jnp.dot(active.T, grad_out, preferred_element_type=jnp.float32)
    sigmoid_in = jax.nn.sigmoid(inner_pre)
    grad_inner_pre = (grad_active * sigmoid_in * (1.0 + inner_pre * (1.0 - sigmoid_in))).astype(
        jnp.bfloat16
    )
    grad_inner = jnp.dot(hidden_two.T, grad_inner_pre, preferred_element_type=jnp.float32)
    grad_hidden_two = jnp.dot(grad_inner_pre, inner_full.T, preferred_element_type=jnp.float32)
    grad_gain_two = jnp.sum(grad_hidden_two * normed_two, axis=0)
    grad_resid = grad_out.astype(jnp.float32) + norm_back(
        grad_hidden_two * gain_two, normed_two, scale_two
    )
    grad_resid_low = grad_resid.astype(jnp.bfloat16)
    grad_outw = jnp.dot(attn_low.T, grad_resid_low, preferred_element_type=jnp.float32)
    grad_attended = heads_of(
        jnp.dot(grad_resid_low, out_full.T, preferred_element_type=jnp.float32).astype(jnp.bfloat16)
    )
    row_delta = jnp.einsum("qhd,hqd->hq", grad_attended.astype(jnp.float32), attn_heads)

    def attend_back(grad_parts, key_flat, value_flat, turn_index):
        source, key_pos, key_seg = key_info(turn_index)

        def compute(parts_in):
            grad_query_acc, grad_key_acc, grad_value_acc = parts_in
            key_block = heads_of(key_flat)
            value_block = heads_of(value_flat)
            allowed = block_mask(local_pos, local_seg, key_pos, key_seg)
            scores = scores_of(queries, key_block)
            probabilities = jnp.where(allowed[None], jnp.exp(scores - log_total[..., None]), 0.0)
            grad_value_acc = grad_value_acc + jnp.einsum(
                "hqk,qhd->khd",
                probabilities.astype(jnp.bfloat16),
                grad_attended,
                preferred_element_type=jnp.float32,
            ).reshape(row_count, model_width)
            grad_probs = jnp.einsum(
                "qhd,khd->hqk", grad_attended, value_block, preferred_element_type=jnp.float32
            )
            grad_scores = (probabilities * (grad_probs - row_delta[..., None])).astype(jnp.bfloat16)
            grad_query_acc = grad_query_acc + jnp.einsum(
                "hqk,khd->qhd", grad_scores, key_block, preferred_element_type=jnp.float32
            )
            grad_key_acc = grad_key_acc + jnp.einsum(
                "hqk,qhd->khd", grad_scores, queries, preferred_element_type=jnp.float32
            ).reshape(row_count, model_width)
            return (grad_query_acc, grad_key_acc, grad_value_acc)

        return lax.cond(source <= ctx_place, compute, keep_state, grad_parts)

    def back_compute(turn_index, loop_state):
        key_block, value_block, grad_parts = loop_state
        grad_parts = attend_back(grad_parts, key_block, value_block, turn_index)
        grad_key_acc, grad_value_acc = pass_grads(grad_parts[1], grad_parts[2])
        return (key_block, value_block, (grad_parts[0], grad_key_acc, grad_value_acc))

    def back_turn(turn_index, loop_state):
        key_block, value_block, grad_parts = back_compute(turn_index, loop_state)
        key_block, value_block = shifted((key_block, value_block), "ctx", 1)
        return (key_block, value_block, grad_parts)

    zero_heads = jnp.zeros((row_count, H, HD), jnp.float32)
    zero_flat = jnp.zeros((row_count, model_width), jnp.float32)
    back_state = lax.fori_loop(
        0, ctx_count - 1, back_turn, (key_rows, value_rows, (zero_heads, zero_flat, zero_flat))
    )
    back_state = back_compute(jnp.int32(ctx_count - 1), back_state)
    grad_query_acc, grad_key_acc, grad_value_acc = back_state[2]
    grad_query_flat = grad_query_acc.reshape(row_count, model_width)
    grad_key_low = grad_key_acc.astype(jnp.bfloat16)
    grad_value_low = grad_value_acc.astype(jnp.bfloat16)
    grad_query_raw = (grad_query_flat * scale_vec).astype(jnp.bfloat16)
    grad_scale = jnp.sum(
        (grad_query_flat * query_raw).reshape(row_count, H, HD), axis=(0, 1)
    ) / math.sqrt(HD)
    grad_qw = jnp.dot(hidden_one.T, grad_query_raw, preferred_element_type=jnp.float32)
    grad_kw = jnp.dot(hidden_one.T, grad_key_low, preferred_element_type=jnp.float32)
    grad_vw = jnp.dot(hidden_one.T, grad_value_low, preferred_element_type=jnp.float32)
    grad_hidden_one = (
        jnp.dot(grad_query_raw, query_full.T, preferred_element_type=jnp.float32)
        + jnp.dot(grad_key_low, key_full.T, preferred_element_type=jnp.float32)
        + jnp.dot(grad_value_low, value_full.T, preferred_element_type=jnp.float32)
    )
    grad_gain_one = jnp.sum(grad_hidden_one * normed_one, axis=0)
    grad_tokens = grad_resid_low.astype(jnp.float32) + norm_back(
        grad_hidden_one * gain_one, normed_one, scale_one
    )
    shard_count = lax.axis_size("fs")
    scale_rows = jnp.broadcast_to(grad_scale[None, :], (shard_count, grad_scale.shape[0]))
    shares = (
        lax.psum_scatter(
            grad_qw.astype(jnp.bfloat16), "fs", scatter_dimension=0, tiled=True
        ).astype(jnp.float32),
        lax.psum_scatter(
            grad_kw.astype(jnp.bfloat16), "fs", scatter_dimension=0, tiled=True
        ).astype(jnp.float32),
        lax.psum_scatter(
            grad_vw.astype(jnp.bfloat16), "fs", scatter_dimension=0, tiled=True
        ).astype(jnp.float32),
        lax.psum_scatter(
            grad_outw.astype(jnp.bfloat16), "fs", scatter_dimension=0, tiled=True
        ).astype(jnp.float32),
        lax.psum_scatter(
            grad_inner.astype(jnp.bfloat16), "fs", scatter_dimension=0, tiled=True
        ).astype(jnp.float32),
        lax.psum_scatter(
            grad_outer.astype(jnp.bfloat16), "fs", scatter_dimension=0, tiled=True
        ).astype(jnp.float32),
        lax.psum_scatter(
            grad_gain_one.astype(jnp.bfloat16), "fs", scatter_dimension=0, tiled=True
        ).astype(jnp.float32),
        lax.psum_scatter(
            grad_gain_two.astype(jnp.bfloat16), "fs", scatter_dimension=0, tiled=True
        ).astype(jnp.float32),
        lax.psum_scatter(
            scale_rows.astype(jnp.bfloat16), "fs", scatter_dimension=0, tiled=True
        ).astype(jnp.float32),
    )
    totals = (
        lax.psum(shares[0].astype(jnp.bfloat16), "ctx").astype(jnp.float32),
        lax.psum(shares[1].astype(jnp.bfloat16), "ctx").astype(jnp.float32),
        lax.psum(shares[2].astype(jnp.bfloat16), "ctx").astype(jnp.float32),
        lax.psum(shares[3].astype(jnp.bfloat16), "ctx").astype(jnp.float32),
        lax.psum(shares[4].astype(jnp.bfloat16), "ctx").astype(jnp.float32),
        lax.psum(shares[5].astype(jnp.bfloat16), "ctx").astype(jnp.float32),
        lax.psum(shares[6].astype(jnp.bfloat16), "ctx").astype(jnp.float32),
        lax.psum(shares[7].astype(jnp.bfloat16), "ctx").astype(jnp.float32),
        lax.psum(shares[8].astype(jnp.bfloat16), "ctx").astype(jnp.float32),
    )
    return (
        result[None].astype(jnp.bfloat16),
        grad_tokens[None].astype(jnp.bfloat16),
        totals[0],
        totals[1],
        totals[2],
        totals[3],
        totals[4],
        totals[5],
        totals[6],
        totals[7],
        totals[8][0],
    )


MESH = pl.DeviceIdType.MESH
ANY = pl.BlockSpec(memory_space=pl.ANY)
VMEM = pl.BlockSpec(memory_space=pltpu.VMEM)
BF = jnp.bfloat16
F32 = jnp.float32


def fast_fits(mesh):
    return mesh.shape["ctx"] == H and mesh.shape["fs"] == 2


def remote(src, dst, ssem, rsem, target):
    return pltpu.make_async_remote_copy(
        src_ref=src, dst_ref=dst, send_sem=ssem, recv_sem=rsem, device_id=target, device_id_type=MESH
    )


def signal(target):
    pl.semaphore_signal(
        pltpu.get_barrier_semaphore(), inc=1, device_id=target, device_id_type=MESH
    )


def place():
    me = lax.axis_index("ctx")
    return me, lax.axis_index("fs"), me // 4, lax.rem(me // 2, 2), lax.rem(me, 2)


def dot(a, b, dims=((1,), (0,))):
    return lax.dot_general(a, b, (dims, ((), ())), preferred_element_type=F32)


NT = ((1,), (1,))
TN = ((0,), (0,))


LOG2E = math.log2(math.e)
N_SHARED = 0
PULL = (1, 0)
UNITS = H // 2


def weight_pull(own, other, k, fs, me, ssem, rsem):
    half = own[0].shape[0] // 2
    rows = pl.ds(pl.multiple_of(k * half, 64), half)
    yn = (me, 1 - fs)
    sib = (me + 1 - 2 * k, fs)
    n = len(own)

    def first(i):
        return remote(own[i].at[rows], other[i].at[rows], ssem.at[i], rsem.at[i], yn)

    def second(i):
        return remote(other[i].at[rows], other[i].at[rows], ssem.at[n + i], rsem.at[n + i], sib)

    return first, second


def weight_share(own, other, k, x, fs, me, ssem, rsem):
    quarter = own[0].shape[0] // 4 if own else 32
    yn, sib, xn = (me, 1 - fs), (me + 1 - 2 * k, fs), (me + 2 - 4 * x, fs)

    def rows(c, a):
        return pl.ds(pl.multiple_of((c * 2 + a) * quarter, 32), quarter)

    def over_y(i):
        r = rows(k, x)
        return remote(own[i].at[r], other[i].at[r], ssem.at[i, 0], rsem.at[i, 0], yn)

    def over_x(i, a):
        r = rows(k, a)
        return remote(other[i].at[r], other[i].at[r], ssem.at[i, 1], rsem.at[i, 1], xn)

    def over_core(i, c, a, n):
        r = rows(c, a)
        return remote(other[i].at[r], other[i].at[r], ssem.at[i, 2 + n], rsem.at[i, 2 + n], sib)

    return over_y, over_x, over_core


def visible(j, i, rows, first_key):
    kpos = j * rows + lax.broadcasted_iota(jnp.int32, (rows, rows), 0)
    qpos = i * rows + lax.broadcasted_iota(jnp.int32, (rows, rows), 1)
    return (kpos <= qpos) & (kpos >= first_key)


def forward_kernel(n_w, n_x, tok_ref, gain_ref, wt_ref, scale_ref, first_ref, *rest):
    own = rest[:n_w]
    at = n_w
    gain_full, attn_ref = rest[at : at + 2]
    kept = rest[at + 2 : at + 11]
    other = rest[at + 11 : at + 11 + n_w]
    (
        wt_all, gain_own, gain_other, o_sc, vt_sc, m_sc, l_sc, acc_sc,
        h_all, o32_ref, lse_ref, qt_ref, q_ref, kt_ref, k_ref, v_ref, raw_ref,
        ssem, rsem, osend, orecv, wssem, wrsem, xssem, xrsem, ysem, lsem, ksem,
    ) = rest[at + 11 + n_w :]
    me, fs, z, x, k = place()
    sib, xn, yn = (me + 1 - 2 * k, fs), (me + 2 - 4 * x, fs), (me, 1 - fs)
    up, dn = (me + 4, fs), (me - 4, fs)
    rows = tok_ref.shape[0]
    here = (h_all, o32_ref, lse_ref, qt_ref, q_ref, kt_ref, k_ref, v_ref, raw_ref)

    def keep(i, u):
        return pltpu.make_async_copy(here[i].at[u], kept[i].at[u], ksem.at[i, u])

    unit_rows = 2 * rows
    bar = pltpu.get_barrier_semaphore()
    for i in range(1, H):
        signal((lax.rem(me + i, H), fs))
    signal(yn)
    gain_own[...] = gain_ref[...]
    tokens = tok_ref[...].astype(F32)
    normed = tokens * lax.rsqrt(jnp.mean(tokens * tokens, axis=-1, keepdims=True) + epsilon)
    pl.semaphore_wait(bar, H)

    gain_copy = remote(gain_own, gain_other, ysem.at[0], ysem.at[1], yn)
    gain_copy.start()
    half = wt_ref.shape[1]
    columns = pl.ds(pl.multiple_of(fs * half, 128), half)
    wt_copy = remote(wt_ref, wt_all.at[:, columns], ysem.at[2], ysem.at[3], yn)
    wt_copy.start()
    wt_here = pltpu.make_async_copy(wt_ref, wt_all.at[:, columns], lsem.at[0])
    wt_here.start()
    n_y = n_w - n_x
    first, second = weight_pull(own[:n_y], other[:n_y], k, fs, me, wssem, wrsem)
    over_y, over_x, over_core = weight_share(own[n_y:], other[n_y:], k, x, fs, me, xssem, xrsem)
    gain_copy.wait()
    g_here = gain_own[...].astype(F32)
    g_there = gain_other[...].astype(F32)
    gains = jnp.where(
        fs == 0,
        jnp.concatenate([g_here, g_there], axis=1),
        jnp.concatenate([g_there, g_here], axis=1),
    )
    gain_full[...] = gains
    my_rows = pl.ds(pl.multiple_of(k * rows, rows), rows)
    h_all[me // 2, my_rows, :] = (normed * gains[0:1]).astype(BF)

    def slot(s):
        return h_all.at[s // 2, pl.ds(pl.multiple_of(lax.rem(s, 2) * rows, rows), rows)]

    def cp(s, t, si):
        return remote(slot(s), slot(s), ssem.at[si], rsem.at[s], t)

    cp(me, xn, 0).start()

    @pl.when(z < 3)
    def _():
        cp(me, up, 1).start()

    @pl.when(z > 0)
    def _():
        cp(me, dn, 2).start()

    cp(me, sib, 3).start()
    for i in range(n_y):
        first(i).start()
    for i in range(n_x):
        over_y(i).start()
    wt_here.wait()
    wt_copy.wait()

    def project(u):
        qkv = dot(wt_all[...], h_all[u], NT)
        raw = qkv[:HD]
        raw_ref[u] = raw
        q32 = raw * scale_ref[...]
        qt_ref[u] = (q32 * LOG2E).astype(BF)
        q_ref[u] = q32.T.astype(BF)
        kt = qkv[HD : 2 * HD]
        vt = qkv[2 * HD :]
        kt_ref[u] = kt.astype(BF)
        k_ref[u] = kt.T.astype(BF)
        v_ref[u] = vt.T.astype(BF)
        vt_sc[u] = vt.astype(BF)
        m_sc[u] = jnp.full((1, unit_rows), neg_big, F32)
        l_sc[u] = jnp.zeros((1, unit_rows), F32)
        acc_sc[u] = jnp.zeros((HD, unit_rows), F32)

    def pair(j, i):
        s = dot(k_ref[j], qt_ref[i])
        s = jnp.where(visible(j, i, unit_rows, first_ref[i]), s, neg_big)
        run_max = m_sc[i]
        new_max = jnp.maximum(run_max, jnp.max(s, axis=0, keepdims=True))
        p = jnp.exp2(s - new_max)
        factor = jnp.exp2(run_max - new_max)
        l_sc[i] = l_sc[i] * factor + jnp.sum(p, axis=0, keepdims=True)
        acc_sc[i] = acc_sc[i] * factor + dot(vt_sc[j], p.astype(BF))
        m_sc[i] = new_max

    def when_here(uz, ux):
        return 4 * jnp.maximum(uz - z, z - uz) + 2 * jnp.maximum(ux - x, x - ux) + (uz + 4 - z) // 5

    def process(uz, ux):
        u = uz * 2 + ux
        cp(u * 2 + 1 - k, sib, 0).wait_recv()
        project(u)
        for i in (0, 3, 4, 5, 6, 7, 8):
            keep(i, u).start()
        pair(u, u)
        mine = when_here(uz, ux)

        def earlier(e, c):
            @pl.when(when_here(e // 2, lax.rem(e, 2)) < mine)
            def _():
                pair(jnp.minimum(e, u), jnp.maximum(e, u))

            return c

        lax.fori_loop(0, UNITS, earlier, 0)

    xo = me + 2 - 4 * x

    def column_arrival(d):
        a = 4 + (d - 1) * 6

        @pl.when(z >= d)
        def _():
            s = me - 4 * d
            cp(s, dn, a).wait_recv()

            @pl.when(z < 3)
            def _():
                cp(s, up, a).start()

            cp(s, xn, a + 1).start()
            cp(s, sib, a + 2).start()

        @pl.when(z + d <= 3)
        def _():
            s = me + 4 * d
            cp(s, up, a + 3).wait_recv()

            @pl.when(z > 0)
            def _():
                cp(s, dn, a + 3).start()

            cp(s, xn, a + 4).start()
            cp(s, sib, a + 5).start()

    def across_arrival(d):
        @pl.when(z >= d)
        def _():
            s = xo - 4 * d
            cp(s, xn, 0).wait_recv()
            cp(s, sib, 22 + z - d).start()

        @pl.when((z + d <= 3) & (d > 0))
        def _():
            s = xo + 4 * d
            cp(s, xn, 0).wait_recv()
            cp(s, sib, 22 + z + d).start()

    def step(d, c):
        @pl.when((d >= 1) & (d <= 3))
        def _():
            column_arrival(d)

        @pl.when(d >= 1)
        def _():
            across_arrival(d - 1)

        for i in range(min(n_y, 4)):

            @pl.when(d == i + 1)
            def _(i=i):
                first(i).wait_recv()
                second(i).start()

        def compute(n, c2):
            across = 1 - n // 2
            dd = d - across
            uz = z + dd * (2 * lax.rem(n, 2) - 1)
            ux = x + across * (1 - 2 * x)
            ok = (dd >= 0) & (dd <= 3) & (uz >= 0) & (uz <= 3)
            ok = ok & ((dd > 0) | (lax.rem(n, 2) == 0))

            @pl.when(ok)
            def _():
                process(uz, ux)

            return c2

        lax.fori_loop(0, 4, compute, 0)
        return c

    lax.fori_loop(0, 5, step, 0)

    def out_copy(b):
        u = b // 2
        lanes = pl.ds(pl.multiple_of(lax.rem(b, 2) * rows, 128), rows)
        return o_sc.at[u, :, lanes]

    def finish(n, c):
        u = lax.rem(me // 2 + n, UNITS)
        out = acc_sc[u] / l_sc[u]
        o32_ref[u] = out
        o_sc[u] = out.astype(BF)
        lse_ref[u] = m_sc[u] + jnp.log2(l_sc[u])
        keep(1, u).start()
        keep(2, u).start()

        def send(e, c2):
            b = u * 2 + e

            @pl.when(b != me)
            def _():
                remote(out_copy(b), attn_ref.at[me], osend.at[b], orecv.at[me], (b, fs)).start()

            @pl.when(b == me)
            def _():
                pltpu.make_async_copy(out_copy(b), attn_ref.at[me], lsem.at[1]).start()

            return c2

        return lax.fori_loop(0, 2, send, c)

    lax.fori_loop(0, UNITS, finish, 0)
    for i in range(4, n_y):
        first(i).wait_recv()
        second(i).start()
    for i in range(n_x):
        over_y(i).wait_recv()
        over_x(i, x).start()
        over_core(i, k, x, 0).start()

    def taken(b, c):
        @pl.when(b != me)
        def _():
            remote(out_copy(b), attn_ref.at[b], osend.at[b], orecv.at[b], (b, fs)).wait()

        return c

    lax.fori_loop(0, H, taken, 0)
    pltpu.make_async_copy(out_copy(me), attn_ref.at[me], lsem.at[1]).wait()

    def all_kept(u, c):
        for i in range(9):
            keep(i, u).wait()
        return c

    lax.fori_loop(0, UNITS, all_kept, 0)
    cp(me, xn, 0).wait_send()

    @pl.when(z < 3)
    def _():
        cp(me, up, 1).wait_send()

    @pl.when(z > 0)
    def _():
        cp(me, dn, 2).wait_send()

    cp(me, sib, 3).wait_send()

    def sent(d, c):
        a = 4 + (d - 1) * 6

        @pl.when(z >= d)
        def _():
            s = me - 4 * d

            @pl.when(z < 3)
            def _():
                cp(s, up, a).wait_send()

            cp(s, xn, a + 1).wait_send()
            cp(s, sib, a + 2).wait_send()

        @pl.when(z + d <= 3)
        def _():
            s = me + 4 * d

            @pl.when(z > 0)
            def _():
                cp(s, dn, a + 3).wait_send()

            cp(s, xn, a + 4).wait_send()
            cp(s, sib, a + 5).wait_send()

        return c

    lax.fori_loop(1, 4, sent, 0)

    def sent_across(zz, c):
        cp(xo + 4 * (zz - z), sib, 22 + zz).wait_send()
        return c

    lax.fori_loop(0, 4, sent_across, 0)
    for i in range(n_x):
        over_x(i, 1 - x).wait_recv()
        over_core(i, k, 1 - x, 1).start()
    for i in range(n_y):
        first(i).wait_send()
        second(i).wait()
    for i in range(n_x):
        over_y(i).wait_send()
        over_x(i, x).wait_send()
        over_core(i, k, x, 0).wait_send()
        over_core(i, k, 1 - x, 1).wait_send()
        over_core(i, 1 - k, x, 0).wait_recv()
        over_core(i, 1 - k, 1 - x, 1).wait_recv()


def forward_call(tok, gains, wt, scale_col, first_key, weights, n_x):
    n_w = len(weights)
    rows, width = tok.shape
    ur = 2 * rows

    def out(dtype, *shape):
        return jax.ShapeDtypeStruct((UNITS, *shape), dtype)

    kept = [
        out(BF, ur, width), out(F32, HD, ur), out(F32, 1, ur), out(BF, HD, ur), out(BF, ur, HD),
        out(BF, HD, ur), out(BF, ur, HD), out(BF, ur, HD), out(F32, HD, ur),
    ]
    shapes = [
        jax.ShapeDtypeStruct((gains.shape[0], 2 * gains.shape[1]), F32),
        jax.ShapeDtypeStruct((H, HD, rows), BF),
        *kept,
    ] + [jax.ShapeDtypeStruct(w.shape, BF) for w in weights]
    return pl.pallas_call(
        functools.partial(forward_kernel, n_w, n_x),
        out_shape=shapes,
        in_specs=[VMEM] * 5 + [ANY] * n_w,
        out_specs=[VMEM] + [ANY] * (10 + n_w),
        scratch_shapes=[
            pltpu.VMEM((wt.shape[0], 2 * wt.shape[1]), BF),
            pltpu.VMEM(gains.shape, BF),
            pltpu.VMEM(gains.shape, BF),
            pltpu.VMEM((UNITS, HD, ur), BF),
            pltpu.VMEM((UNITS, HD, ur), BF),
            pltpu.VMEM((UNITS, 1, ur), F32),
            pltpu.VMEM((UNITS, 1, ur), F32),
            pltpu.VMEM((UNITS, HD, ur), F32),
            *[pltpu.VMEM(a.shape, a.dtype) for a in kept],
            pltpu.SemaphoreType.DMA((26,)),
            pltpu.SemaphoreType.DMA((H,)),
            pltpu.SemaphoreType.DMA((H,)),
            pltpu.SemaphoreType.DMA((H,)),
            pltpu.SemaphoreType.DMA((2 * n_w,)),
            pltpu.SemaphoreType.DMA((2 * n_w,)),
            pltpu.SemaphoreType.DMA((max(1, n_x), 4)),
            pltpu.SemaphoreType.DMA((max(1, n_x), 4)),
            pltpu.SemaphoreType.DMA((4,)),
            pltpu.SemaphoreType.DMA((2,)),
            pltpu.SemaphoreType.DMA((9, UNITS)),
        ],
        compiler_params=pltpu.CompilerParams(
            collective_id=1, has_side_effects=True, vmem_limit_bytes=56 * 2**20
        ),
        name="forward",
    )(tok, gains, wt, scale_col, first_key, *weights)


def half_rows(start, size, align):
    return pl.ds(pl.multiple_of(start, align), size)


def tail_kernel(gt_ref, *rest):
    own = rest[:3]
    n_w = len(PULL)
    held = rest[3 : 6 - n_w]
    at = 6 - n_w
    (
        attn_ref, gr_ref, hid_ref, gip_ref, act_ref, cot_ref, tok_ref, gain_ref, g2_ref,
        scale_ref, first_ref,
    ) = rest[at : at + 11]
    kept = rest[at + 11 : at + 20]
    at += 20
    all_ref, tg_ref, sums_ref = rest[at : at + 3]
    pulled = rest[at + 3 : at + 3 + n_w]
    (
        h_ref, o_ref, lse_ref, qt_ref, q_ref, kt_ref, k_ref, v_ref, raw_ref,
        g_in, g_sc, delta_sc, dq_sc, scale_sc, dk_sc, dv_sc, d_sc, got, dw_sc, dw_out, dw_got, piece,
        s1, r0, so, ra, rb, r2, rz, e_sc, small_out, small_in, small_z,
        gsend, grecv, qsend, qrecv, ksend, krecv, dsend, drecv, psend, precv,
        asend, arecv, vsend, vrecv, lsem, wsem, ksem, wssem, wrsem,
    ) = rest[at + 3 + n_w :]
    me, fs, z, x, k = place()
    sib, xn, yn = (me + 1 - 2 * k, fs), (me + 2 - 4 * x, fs), (me, 1 - fs)
    up, dn = (me + 4, fs), (me - 4, fs)
    units, rows = h_ref.shape[:2]
    block = rows // 2
    n_g = 3
    part = s1.shape[2]
    width = s1.shape[3]
    cols = width // 2
    bar = pltpu.get_barrier_semaphore()
    for i in range(1, H):
        signal((lax.rem(me + i, H), fs))
    signal(yn)
    here = (h_ref, o_ref, lse_ref, qt_ref, q_ref, kt_ref, k_ref, v_ref, raw_ref)
    back = [pltpu.make_async_copy(kept[i], here[i], ksem.at[i]) for i in range(9)]
    for c in back[1:]:
        c.start()
    back[0].start()
    pl.semaphore_wait(bar, H)

    def lanes(b):
        return half_rows(lax.rem(b, 2) * block, block, 128)

    def g_copy(b, t):
        return remote(
            gt_ref.at[b], g_in.at[t // 2, :, lanes(t)], gsend.at[b], grecv.at[t], (b, fs)
        )

    def g_start(n, c):
        g_copy(lax.rem(me + n, H), me).start()
        return c

    lax.fori_loop(1, H, g_start, 0)
    g_here = pltpu.make_async_copy(gt_ref.at[me], g_in.at[me // 2, :, lanes(me)], lsem.at[0])
    g_here.start()
    first, second = weight_pull([own[w] for w in PULL], pulled, k, fs, me, wssem, wrsem)

    def theirs(g):
        return remote(so.at[g], r0.at[g], dsend.at[g], drecv.at[g], sib)

    def dense_rows(g, start):
        r = half_rows(start, part, 64)
        if g == 0:
            return dot(attn_ref[r, :], gr_ref[...])
        a, b = ((hid_ref, gip_ref), (act_ref, cot_ref))[g - 1]
        return dot(a[r, :], b[...])

    for g in range(n_g):
        for f in range(2):
            so[g, f] = dense_rows(g, f * 2 * part + (1 - k) * part).astype(BF)
        theirs(g).start()
    for g in range(n_g):
        for f in range(2):
            s1[g, f] = dense_rows(g, f * 2 * part + k * part).astype(BF)

    top, bottom = slice(0, part // 2), slice(part // 2, part)
    x_here = half_rows(x * cols, cols, 128)
    x_there = half_rows((1 - x) * cols, cols, 128)

    def stage(g, i):
        ends = (
            (s1.at[g, 1 - fs, top, :], ra.at[g], yn),
            (s1.at[g, :, bottom, x_there], rb.at[g], xn),
            (s1.at[g, fs, top, x_there], r2.at[g, top], xn),
            (s1.at[g, 1 - fs, bottom, x_here], r2.at[g, bottom], yn),
        )[i]
        return remote(ends[0], ends[1], psend.at[i, g], precv.at[i, g], ends[2])

    slab = part // 4

    zb = lax.rem(z, 2)
    near, far = (me + 4 - 8 * zb, fs), (me + 8 - 16 * (z // 2), fs)

    def z_rows(t):
        return s1.at[:, fs, half_rows(t * slab, slab, 16), x_here]

    def z_near(i):
        return remote(z_rows(1 - zb + 2 * i), rz.at[i], psend.at[4, i], precv.at[4, i], near)

    def z_far():
        return remote(
            z_rows(zb + 2 * (1 - z // 2)), rz.at[2], psend.at[4, 2], precv.at[4, 2], far
        )

    for g in range(n_g):
        theirs(g).wait()

        def add(i, c, g=g):
            r = half_rows(i * 32, 32, 32)
            for f in range(2):
                s1[g, f, r, :] += r0[g, f, r, :]
            return c

        lax.fori_loop(0, part // 32, add, 0)
        stage(g, 0).start()
        stage(g, 1).start()

    loads = []
    for w in range(3):
        for f in range(2):
            loads.append(
                pltpu.make_async_copy(own[w].at[pl.ds(f * part, part)], r0.at[w, f], wsem.at[w * 2 + f])
            )
            loads[-1].start()


    def load_other(src, w, f):
        return pltpu.make_async_copy(
            src.at[pl.ds(f * part, part)], so.at[w, f], wsem.at[6 + w * 2 + f]
        )

    for i, w in enumerate(w for w in range(3) if w not in PULL):
        for f in range(2):
            loads.append(load_other(held[i], w, f))
            loads[-1].start()

    def after_one():
        for g in range(n_g):
            stage(g, 0).wait()
            stage(g, 1).wait()

            def add(i, c, g=g):
                r = half_rows(i * 32, 32, 32)
                s1[g, fs, r, :] += ra[g, r, :]
                low = half_rows(part // 2 + i * 32, 32, 32)
                for f in range(2):
                    s1[g, f, low, x_here] += rb[g, f, r, :]
                return c

            lax.fori_loop(0, part // 64, add, 0)
            stage(g, 2).start()
            stage(g, 3).start()
        for i in range(n_w):
            first(i).start()

    def after_two():
        for g in range(n_g):
            stage(g, 2).wait()
            stage(g, 3).wait()

            def add(i, c, g=g):
                r = half_rows(i * 32, 32, 32)
                s1[g, fs, r, x_here] += r2[g, r, :]
                return c

            lax.fori_loop(0, part // 32, add, 0)
        for i in range(2):
            z_near(i).start()

    def after_near():
        for i in range(2):
            z_near(i).wait()
            r = half_rows((zb + 2 * i) * slab, slab, 16)
            for g in range(n_g):
                s1[g, fs, r, x_here] += rz[i, g]
        z_far().start()

    def after_far():
        z_far().wait()
        r = half_rows(z * slab, slab, 16)
        for g in range(n_g):
            piece[g] = s1[g, fs, r, x_here] + rz[2, g]

    scale_sc[...] = jnp.zeros_like(scale_sc)
    dw_sc[...] = jnp.zeros_like(dw_sc)

    def g_taken(n, c):
        b = lax.rem(me + n, H)
        g_copy(b, b).wait()
        return c

    for c in back[1:]:
        c.wait()
    g_here.wait()
    lax.fori_loop(1, H, g_taken, 0)

    def prepare(i, c):
        g = g_in[i].astype(F32)
        g_sc[i] = g.T.astype(BF)
        delta_sc[i] = jnp.sum(g * o_ref[i], axis=0, keepdims=True)
        dq_sc[i] = jnp.zeros((HD, rows), F32)
        return c

    lax.fori_loop(0, units, prepare, 0)

    back[0].wait()

    def pair(masked, j, i):
        s = dot(k_ref[j], qt_ref[i])
        if masked:
            s = jnp.where(visible(j, i, rows, first_ref[i]), s, neg_big)
        p = jnp.exp2(s - lse_ref[i])
        dv_sc[...] += dot(p.astype(BF), g_sc[i])
        dp = dot(v_ref[j], g_in[i])
        ds = (p * (dp - delta_sc[i])).astype(BF)
        dk_sc[...] += dot(ds, q_ref[i])
        dq_sc[i] += dot(kt_ref[j], ds)

    def out(b, lo, n):
        return d_sc.at[b // 2, pl.ds(lo, n), :, lanes(b)]

    def to(t, lo, n):
        return got.at[pl.ds(lo, n), half_rows(t * HD, HD, 16)]

    def kv_copy(b, t):
        return remote(out(b, 1, 2), to(t, 1, 2), ksend.at[b], krecv.at[t], (b, fs))

    def q_copy(b, t):
        return remote(out(b, 0, 1), to(t, 0, 1), qsend.at[b], qrecv.at[t], (b, fs))

    kv_here = pltpu.make_async_copy(out(me, 1, 2), to(me, 1, 2), lsem.at[1])
    q_here = pltpu.make_async_copy(out(me, 0, 1), to(me, 0, 1), lsem.at[2])

    def column(n, c):
        j = lax.rem(me // 2 + n, units)
        dk_sc[...] = jnp.zeros_like(dk_sc)
        dv_sc[...] = jnp.zeros_like(dv_sc)
        pair(True, j, j)

        def plain(i, c2):
            pair(False, j, i)
            return c2

        def edge(i, c2):
            pair(True, j, i)
            return c2

        end = jnp.where(j == 0, 1, units - 1)
        lax.fori_loop(j + 1, end, plain, 0)
        lax.fori_loop(jnp.maximum(j + 1, end), units, edge, 0)
        d_sc[j, 1] = dk_sc[...].T.astype(BF)
        d_sc[j, 2] = dv_sc[...].T.astype(BF)

        def send(e, c2):
            b = 2 * j + e

            @pl.when(b != me)
            def _():
                kv_copy(b, me).start()

            @pl.when(b == me)
            def _():
                kv_here.start()

            return c2

        lax.fori_loop(0, 2, send, 0)
        for e in range(2):
            dw_sc[1 + e] += dot(d_sc[j, 1 + e], h_ref[j])

        @pl.when(n == ONE_AT)
        def _():
            after_one()

        @pl.when(n == TWO_AT)
        def _():
            after_two()

        return c

    lax.fori_loop(0, units, column, 0)
    half = dw_out.shape[2]

    def dw_copy(n, lo, size):
        return remote(
            dw_out.at[pl.ds(lo, size)], dw_got.at[pl.ds(lo, size)], vsend.at[6 + n], vrecv.at[6 + n], yn
        )

    def dw_send(n, lo, size):
        away = half_rows((1 - fs) * half, half, 128)
        dw_out[lo : lo + size] = dw_sc[lo : lo + size, :, away].astype(BF)
        dw_copy(n, lo, size).start()

    def dw_take(n, lo, size):
        dw_copy(n, lo, size).wait()
        keep = half_rows(fs * half, half, 128)
        total = dw_sc[lo : lo + size, :, keep] + dw_got[lo : lo + size].astype(F32)
        piece[3 + lo : 3 + lo + size] = total.astype(BF)

    dw_send(0, 1, 2)

    def queries(n, c):
        i = lax.rem(me // 2 + n, units)
        dq = dq_sc[i]
        scale_sc[...] += dq * raw_ref[i]
        d_sc[i, 0] = (dq * scale_ref[...]).astype(BF)

        def send(e, c2):
            b = 2 * i + e

            @pl.when(b != me)
            def _():
                q_copy(b, me).start()

            @pl.when(b == me)
            def _():
                q_here.start()

            return c2

        lax.fori_loop(0, 2, send, 0)
        return c

    lax.fori_loop(0, units, queries, 0)
    def query_weight(i, c):
        dw_sc[0] += dot(d_sc[i, 0], h_ref[i])
        return c

    lax.fori_loop(0, units, query_weight, 0)
    dw_send(1, 0, 1)
    small_out[...] = jnp.zeros_like(small_out)
    small_out[1:2, :] = g2_ref[...]
    small_out[2:3, :HD] = jnp.sum(scale_sc[...].T, axis=0, keepdims=True)

    spans = (pl.ds(0, 3), pl.ds(4, 2), pl.ds(3, 1))

    def cp(p, s, t, si, mine=False):
        here = all_ref.at[s, spans[p]]
        return remote(piece.at[spans[p]] if mine else here, here, asend.at[p, si], arecv.at[p, s], t)

    def keep(p):
        return pltpu.make_async_copy(
            piece.at[spans[p]], all_ref.at[me, spans[p]], lsem.at[3 + p]
        )

    def begin(p):
        keep(p).start()
        cp(p, me, xn, 0, True).start()

        @pl.when(z < 3)
        def _():
            cp(p, me, up, 1, True).start()

        @pl.when(z > 0)
        def _():
            cp(p, me, dn, 2, True).start()

        cp(p, me, sib, 3, True).start()

    def column_arrival(p, d):
        a = 4 + (d - 1) * 6

        @pl.when(z >= d)
        def _():
            s = me - 4 * d
            cp(p, s, dn, a).wait_recv()

            @pl.when(z < 3)
            def _():
                cp(p, s, up, a).start()

            cp(p, s, xn, a + 1).start()
            cp(p, s, sib, a + 2).start()

        @pl.when(z + d <= 3)
        def _():
            s = me + 4 * d
            cp(p, s, up, a + 3).wait_recv()

            @pl.when(z > 0)
            def _():
                cp(p, s, dn, a + 3).start()

            cp(p, s, xn, a + 4).start()
            cp(p, s, sib, a + 5).start()

    xo = me + 2 - 4 * x

    def across_arrival(p, d):
        @pl.when(z >= d)
        def _():
            s = xo - 4 * d
            cp(p, s, xn, 0).wait_recv()
            cp(p, s, sib, 22 + z - d).start()

        if d > 0:

            @pl.when(z + d <= 3)
            def _():
                s = xo + 4 * d
                cp(p, s, xn, 0).wait_recv()
                cp(p, s, sib, 22 + z + d).start()


    def kv_taken(n, c):
        b = lax.rem(me + n, H)
        kv_copy(b, b).wait()
        return c

    def q_taken(n, c):
        b = lax.rem(me + n, H)
        q_copy(b, b).wait()
        return c

    def input_grad(w, start):
        for r, m in ((fs, r0), (1 - fs, so)):
            for f in range(2):
                at_rows = half_rows((r * 2 + f) * part, part, 64)
                term = dot(m[w, f], got[w])
                if start:
                    e_sc[at_rows, :] = term
                else:
                    e_sc[at_rows, :] += term

    def pass_on(i):
        first(i).wait_recv()
        second(i).start()

    def load_pulled(i):
        second(i).wait()
        first(i).wait_send()
        late = [load_other(pulled[i], PULL[i], f) for f in range(2)]
        for c in late:
            c.start()
        for c in late:
            c.wait()

    def v_copy(i, t):
        n = (0, 1, 8)[i]
        return remote(small_out, small_in.at[i], vsend.at[n], vrecv.at[n], t)

    def v_column(d):
        t = lax.rem(z + d, 4)
        return t, remote(
            small_z.at[z], small_z.at[z], vsend.at[2 + d], vrecv.at[2 + z], (me + 4 * (t - z), fs)
        )

    dw_take(0, 1, 2)
    begin(1)
    after_near()
    dw_take(1, 0, 1)
    begin(2)
    pass_on(0)
    lax.fori_loop(1, H, kv_taken, 0)
    kv_here.wait()
    for c in loads:
        c.wait()
    input_grad(2, True)
    column_arrival(1, 1)
    column_arrival(2, 1)
    load_pulled(0)
    input_grad(1, False)
    across_arrival(1, 0)
    across_arrival(2, 0)
    after_far()
    begin(0)
    column_arrival(1, 2)
    column_arrival(2, 2)
    pass_on(1)
    across_arrival(1, 1)
    across_arrival(2, 1)
    lax.fori_loop(1, H, q_taken, 0)
    q_here.wait()
    load_pulled(1)
    input_grad(0, False)
    column_arrival(0, 1)
    column_arrival(1, 3)
    column_arrival(2, 3)
    across_arrival(0, 0)
    grad_hidden = e_sc[...].T
    tokens = tok_ref[...].astype(F32)
    scale = lax.rsqrt(jnp.mean(tokens * tokens, axis=-1, keepdims=True) + epsilon)
    normed = tokens * scale
    small_out[0:1, :] = jnp.sum(grad_hidden * normed, axis=0, keepdims=True)
    v_copy(0, sib).start()
    across_arrival(1, 2)
    across_arrival(2, 2)
    column_arrival(0, 2)
    e = grad_hidden * gain_ref[0:1, :]
    tg_ref[...] = (
        gr_ref[...].astype(F32) + scale * (e - normed * jnp.mean(e * normed, axis=-1, keepdims=True))
    ).astype(BF)
    v_copy(0, sib).wait()
    small_out[...] += small_in[0]
    v_copy(1, xn).start()
    across_arrival(0, 1)
    v_copy(1, xn).wait()
    small_z[z] = small_out[...] + small_in[1]
    for d in range(1, 4):
        v_column(d)[1].start()
    across_arrival(1, 3)
    across_arrival(2, 3)
    for d in range(1, 4):
        t, c = v_column(d)
        c.wait_send()
        remote(small_z.at[t], small_z.at[t], vsend.at[2 + d], vrecv.at[2 + t], xn).wait_recv()
    small_out[...] = (small_z[0] + small_z[1]) + (small_z[2] + small_z[3])
    v_copy(2, yn).start()
    column_arrival(0, 3)
    across_arrival(0, 2)
    v_copy(2, yn).wait()
    sums_ref[...] = small_out[...] + small_in[2]
    across_arrival(0, 3)

    for p in (1, 2, 0):

        def from_sib(n, c, p=p):
            cp(p, n * 2 + 1 - k, sib, 0).wait_recv()
            return c

        lax.fori_loop(0, UNITS, from_sib, 0)
        keep(p).wait()
        cp(p, me, xn, 0, True).wait_send()

        @pl.when(z < 3)
        def _(p=p):
            cp(p, me, up, 1, True).wait_send()

        @pl.when(z > 0)
        def _(p=p):
            cp(p, me, dn, 2, True).wait_send()

        cp(p, me, sib, 3, True).wait_send()

        def sent(d, c, p=p):
            a = 4 + (d - 1) * 6

            @pl.when(z >= d)
            def _():
                s = me - 4 * d

                @pl.when(z < 3)
                def _():
                    cp(p, s, up, a).wait_send()

                cp(p, s, xn, a + 1).wait_send()
                cp(p, s, sib, a + 2).wait_send()

            @pl.when(z + d <= 3)
            def _():
                s = me + 4 * d

                @pl.when(z > 0)
                def _():
                    cp(p, s, dn, a + 3).wait_send()

                cp(p, s, xn, a + 4).wait_send()
                cp(p, s, sib, a + 5).wait_send()

            return c

        lax.fori_loop(1, 4, sent, 0)

        def sent_across(zz, c, p=p):
            cp(p, xo + 4 * (zz - z), sib, 22 + zz).wait_send()
            return c

        lax.fori_loop(0, 4, sent_across, 0)


ONE_AT = 3
TWO_AT = 6


def tail_call(gt, own, held, vm, kept):
    n_w = len(PULL)
    rows, width = vm[1].shape
    n, ur = kept[0].shape[:2]
    half = width // 2
    part = width // 4
    sem = pltpu.SemaphoreType.DMA
    return pl.pallas_call(
        tail_kernel,
        out_shape=[
            jax.ShapeDtypeStruct((H, 6, part // 4, half), BF),
            jax.ShapeDtypeStruct((rows, width), BF),
            jax.ShapeDtypeStruct((8, width), F32),
        ]
        + [jax.ShapeDtypeStruct(own[0].shape, BF)] * n_w,
        in_specs=[ANY] * (4 + len(held)) + [VMEM] * len(vm) + [ANY] * len(kept),
        out_specs=[ANY, VMEM, VMEM] + [ANY] * n_w,
        scratch_shapes=[
            *[pltpu.VMEM(a.shape, a.dtype) for a in kept],
            pltpu.VMEM((n, HD, ur), BF),
            pltpu.VMEM((n, ur, HD), BF),
            pltpu.VMEM((n, 1, ur), F32),
            pltpu.VMEM((n, HD, ur), F32),
            pltpu.VMEM((HD, ur), F32),
            pltpu.VMEM((ur, HD), F32),
            pltpu.VMEM((ur, HD), F32),
            pltpu.VMEM((n, 3, HD, ur), BF),
            pltpu.VMEM((3, H * HD, rows), BF),
            pltpu.VMEM((3, HD, width), F32),
            pltpu.VMEM((3, HD, half), BF),
            pltpu.VMEM((3, HD, half), BF),
            pltpu.VMEM((6, part // 4, half), BF),
            pltpu.VMEM((3, 2, part, width), BF),
            pltpu.VMEM((3, 2, part, width), BF),
            pltpu.VMEM((3, 2, part, width), BF),
            pltpu.VMEM((3, part // 2, width), BF),
            pltpu.VMEM((3, 2, part // 2, half), BF),
            pltpu.VMEM((3, part, half), BF),
            pltpu.VMEM((3, 3, part // 4, half), BF),
            pltpu.VMEM((width, rows), F32),
            pltpu.VMEM((8, width), F32),
            pltpu.VMEM((3, 8, width), F32),
            pltpu.VMEM((4, 8, width), F32),
            sem((H,)), sem((H,)), sem((H,)), sem((H,)), sem((H,)), sem((H,)),
            sem((3,)), sem((3,)), sem((5, 4)), sem((5, 4)),
            sem((3, 26)), sem((3, H)), sem((9,)), sem((9,)), sem((6,)), sem((12,)),
            sem((9,)), sem((max(1, 2 * n_w),)), sem((max(1, 2 * n_w),)),
        ],
        compiler_params=pltpu.CompilerParams(
            collective_id=2, has_side_effects=True, vmem_limit_bytes=62 * 2**20
        ),
        name="tail",
    )(gt, *own, *held, *vm, *kept)


def spread_kernel(dense_ref, heads_ref, *outs):
    slab, cols = dense_ref.shape[-2:]
    n, _, hd, _ = heads_ref.shape
    for zz in range(4):
        for xx in range(2):
            outs[0][zz * slab : (zz + 1) * slab, xx * cols : (xx + 1) * cols] = dense_ref[
                zz, xx, 0, 0
            ].astype(F32)
    outs[1][...] = heads_ref[...].reshape(n * hd, cols).astype(F32).T


def spread_call(pieces, w):
    n, parts, slab, cols = pieces.shape
    split = pieces.reshape(4, 2, 2, parts, slab, cols)
    return pl.pallas_call(
        spread_kernel,
        grid=(2,),
        out_shape=[
            jax.ShapeDtypeStruct((8 * slab, 2 * cols), F32),
            jax.ShapeDtypeStruct((cols, n * slab), F32),
        ],
        in_specs=[
            pl.BlockSpec((4, 2, 1, 1, slab, cols), lambda h: (0, 0, h, w, 0, 0)),
            pl.BlockSpec((n // 2, 1, slab, cols), lambda h: (h, 3 + w, 0, 0)),
        ],
        out_specs=[
            pl.BlockSpec((4 * slab, 2 * cols), lambda h: (h, 0)),
            pl.BlockSpec((cols, n * slab // 2), lambda h: (0, h)),
        ],
        compiler_params=pltpu.CompilerParams(vmem_limit_bytes=48 * 2**20),
        name="spread",
    )(split, pieces)


def joined(own, other, fs):
    return jnp.where(
        fs == 0, jnp.concatenate([own, other], axis=0), jnp.concatenate([other, own], axis=0)
    )


def fast_local(
    tokens, query_weight, key_weight, value_weight, out_weight, inner_weight, outer_weight,
    attn_gain, mlp_gain, query_scale, doc_starts, cotangent,
):
    me, fs = lax.axis_index("ctx"), lax.axis_index("fs")
    rows, width = tokens.shape[1:]
    tok = tokens[0]
    cot = cotangent[0]

    def head_columns(w):
        return lax.dynamic_slice(w, (0, me * HD), (w.shape[0], HD)).T

    wt = jnp.concatenate([head_columns(w) for w in (query_weight, key_weight, value_weight)], axis=0)
    gains = jnp.stack([attn_gain, mlp_gain])
    positions = jnp.arange(H * rows, dtype=jnp.int32)
    starts = doc_starts[0]
    first_key = jnp.max(
        jnp.where(starts[None, :] <= positions[:, None], starts[None, :], 0), axis=1
    ).reshape(UNITS, 1, 2 * rows)
    scale_col = (query_scale / math.sqrt(HD))[:, None]

    (
        gain_full, attn_t, h_all, o32, lse, qt, q, kt, k, v, raw,
        out_o, inner_o, outer_o, value_o,
    ) = forward_call(
        tok, gains, wt, scale_col, first_key,
        (out_weight, inner_weight, outer_weight, value_weight), N_SHARED,
    )
    attn_t = attn_t.reshape(width, rows)

    out_full = joined(out_weight, out_o, fs)
    inner_full = joined(inner_weight, inner_o, fs)
    outer_full = joined(outer_weight, outer_o, fs)
    gain_one, gain_two = gain_full[0:1], gain_full[1:2]
    token_rows = tok.astype(F32)
    resid = token_rows + dot(attn_t, out_full, TN)
    scale_two = rms_scale(resid)
    normed_two = resid * scale_two
    hidden_two = (normed_two * gain_two).astype(BF)
    inner_pre = dot(hidden_two, inner_full)
    active = jax.nn.silu(inner_pre).astype(BF)
    result = (resid + dot(active, outer_full)).astype(BF)
    grad_active = dot(cot, outer_full, NT)
    sig = jax.nn.sigmoid(inner_pre)
    grad_inner_pre = (grad_active * sig * (1.0 + inner_pre * (1.0 - sig))).astype(BF)
    grad_hidden_two = dot(grad_inner_pre, inner_full, NT)
    grad_gain_two = jnp.sum(grad_hidden_two * normed_two, axis=0)
    grad_resid = (
        cot.astype(F32) + norm_back(grad_hidden_two * gain_two, normed_two, scale_two)
    ).astype(BF)
    grad_att_t = dot(out_full, grad_resid, NT).astype(BF).reshape(H, HD, rows)
    half = width // 2
    pieces, grad_tokens, sums, *_ = tail_call(
        grad_att_t, (query_weight, key_weight, value_weight), (value_o,),
        (
            attn_t, grad_resid, hidden_two.T, grad_inner_pre, active.T, cot, tok, gain_full,
            grad_gain_two[None], scale_col, first_key,
        ),
        (h_all, o32, lse, qt, q, kt, k, v, raw),
    )
    (out_g, query_g), (inner_g, key_g), (outer_g, value_g) = [spread_call(pieces, w) for w in range(3)]
    gain_sums = lax.dynamic_slice(sums, (0, fs * half), (2, half))
    return (
        result[None], grad_tokens[None], query_g, key_g, value_g, out_g, inner_g, outer_g,
        gain_sums[0], gain_sums[1], sums[2, :HD] / math.sqrt(HD),
    )


def solution(mesh):
    placed = (
        P("fs", "ctx", None),
        P("fs", None),
        P("fs", None),
        P("fs", None),
        P("fs", None),
        P("fs", None),
        P("fs", None),
        P("fs"),
        P("fs"),
        P(),
        P("fs", None),
        P("fs", "ctx", None),
    )
    return jax.shard_map(
        fast_local if fast_fits(mesh) else general_local,
        mesh=mesh,
        in_specs=placed,
        out_specs=(
            P("fs", "ctx", None),
            P("fs", "ctx", None),
            P("fs", None),
            P("fs", None),
            P("fs", None),
            P("fs", None),
            P("fs", None),
            P("fs", None),
            P("fs"),
            P("fs"),
            P(),
        ),
        check_vma=False,
    )
```

```python
import functools
import math

import jax
import jax.numpy as jnp
from jax import lax
from jax.experimental import pallas as pl
from jax.experimental.pallas import tpu as pltpu
from jax.sharding import PartitionSpec as P

H = 16
HD = 80


epsilon = 1e-06
neg_big = -1e30


def passed_along(block, axis, distance):
    devices = range(lax.axis_size(axis))
    route = [((i - distance) % len(devices), i) for i in devices]
    return lax.ppermute(block, axis, route)


def shifted(value, axis, steps):
    count = lax.axis_size(axis)
    leading, last = (max(0, -steps), min(count, count - steps))
    return lax.ppermute(value, axis, [(source, source + steps) for source in range(leading, last)])


def rms_scale(values_in):
    return lax.rsqrt(jnp.mean(values_in * values_in, axis=-1, keepdims=True) + epsilon)


def norm_back(grad_normed, normed, scale_rows):
    inner_mean = jnp.mean(grad_normed * normed, axis=-1, keepdims=True)
    return scale_rows * (grad_normed - normed * inner_mean)


def segment_of(positions, starts_row):
    return jnp.sum((starts_row[None, :] <= positions[:, None]).astype(jnp.int32), axis=1) - 1


def block_mask(query_pos, query_seg, key_pos, key_seg):
    return (key_pos[None, :] <= query_pos[:, None]) & (key_seg[None, :] == query_seg[:, None])


def scores_of(query_block, key_block):
    return jnp.einsum("qhd,khd->hqk", query_block, key_block, preferred_element_type=jnp.float32)


def pass_grads(grad_key_acc, grad_value_acc):
    return (
        passed_along(grad_key_acc.astype(jnp.bfloat16), "ctx", 1).astype(grad_key_acc.dtype),
        passed_along(grad_value_acc.astype(jnp.bfloat16), "ctx", 1).astype(grad_value_acc.dtype),
    )


def general_local(
    tokens,
    query_weight,
    key_weight,
    value_weight,
    out_weight,
    inner_weight,
    outer_weight,
    attn_gain,
    mlp_gain,
    query_scale,
    doc_starts,
    cotangent,
):
    row_count = tokens.shape[1]
    model_width = tokens.shape[2]
    ctx_count = lax.axis_size("ctx")
    ctx_place = lax.axis_index("ctx")
    (
        query_full,
        key_full,
        value_full,
        out_full,
        inner_full,
        outer_full,
        attn_gain_full,
        mlp_gain_full,
    ) = (
        lax.all_gather(query_weight, "fs", axis=0, tiled=True),
        lax.all_gather(key_weight, "fs", axis=0, tiled=True),
        lax.all_gather(value_weight, "fs", axis=0, tiled=True),
        lax.all_gather(out_weight, "fs", axis=0, tiled=True),
        lax.all_gather(inner_weight, "fs", axis=0, tiled=True),
        lax.all_gather(outer_weight, "fs", axis=0, tiled=True),
        lax.all_gather(attn_gain, "fs", axis=0, tiled=True),
        lax.all_gather(mlp_gain, "fs", axis=0, tiled=True),
    )
    starts_row = doc_starts[0]
    local_pos = ctx_place * row_count + jnp.arange(row_count, dtype=jnp.int32)
    local_seg = segment_of(local_pos, starts_row)

    def heads_of(flat_block):
        return flat_block.reshape(row_count, H, HD)

    token_rows = tokens[0].astype(jnp.float32)
    scale_one = rms_scale(token_rows)
    normed_one = token_rows * scale_one
    gain_one = attn_gain_full.astype(jnp.float32)
    hidden_one = (normed_one * gain_one).astype(jnp.bfloat16)
    query_raw = jnp.dot(hidden_one, query_full, preferred_element_type=jnp.float32)
    scale_vec = jnp.tile(query_scale, H) / math.sqrt(HD)
    queries = heads_of((query_raw * scale_vec).astype(jnp.bfloat16))
    key_rows = jnp.dot(hidden_one, key_full, preferred_element_type=jnp.float32).astype(
        jnp.bfloat16
    )
    value_rows = jnp.dot(hidden_one, value_full, preferred_element_type=jnp.float32).astype(
        jnp.bfloat16
    )

    def key_info(turn_index):
        source = (ctx_place - turn_index) % ctx_count
        key_pos = source * row_count + jnp.arange(row_count, dtype=jnp.int32)
        return (source, key_pos, segment_of(key_pos, starts_row))

    def keep_state(state_in):
        return state_in

    def attend(softmax_state, key_flat, value_flat, turn_index):
        source, key_pos, key_seg = key_info(turn_index)

        def compute(state_in):
            run_max, run_sum, run_acc = state_in
            key_block = heads_of(key_flat)
            value_block = heads_of(value_flat)
            allowed = block_mask(local_pos, local_seg, key_pos, key_seg)
            scores = jnp.where(allowed[None], scores_of(queries, key_block), neg_big)
            new_max = jnp.maximum(run_max, jnp.max(scores, axis=-1))
            weights = jnp.where(allowed[None], jnp.exp(scores - new_max[..., None]), 0.0)
            factor = jnp.exp(run_max - new_max)
            run_sum = run_sum * factor + jnp.sum(weights, axis=-1)
            run_acc = run_acc * factor[..., None] + jnp.einsum(
                "hqk,khd->hqd",
                weights.astype(jnp.bfloat16),
                value_block,
                preferred_element_type=jnp.float32,
            )
            return (new_max, run_sum, run_acc)

        return lax.cond(source <= ctx_place, compute, keep_state, softmax_state)

    start_state = (
        jnp.full((H, row_count), neg_big, jnp.float32),
        jnp.zeros((H, row_count), jnp.float32),
        jnp.zeros((H, row_count, HD), jnp.float32),
    )
    start_state = attend(start_state, key_rows, value_rows, jnp.int32(0))
    stores = ()

    def forward_turn(turn_index, loop_state):
        key_block, value_block, softmax_state, kept = loop_state
        key_block, value_block = shifted((key_block, value_block), "ctx", 1)
        softmax_state = attend(softmax_state, key_block, value_block, turn_index)
        return (key_block, value_block, softmax_state, kept)

    loop_out = lax.fori_loop(
        1, ctx_count, forward_turn, (key_rows, value_rows, start_state, stores)
    )
    run_max, run_sum, run_acc = loop_out[2]
    stores = loop_out[3]
    log_total = run_max + jnp.log(run_sum)
    attn_heads = run_acc / run_sum[..., None]
    attn_low = (
        jnp.transpose(attn_heads, (1, 0, 2)).reshape(row_count, model_width).astype(jnp.bfloat16)
    )
    resid = token_rows + jnp.dot(attn_low, out_full, preferred_element_type=jnp.float32)
    scale_two = rms_scale(resid)
    normed_two = resid * scale_two
    gain_two = mlp_gain_full.astype(jnp.float32)
    hidden_two = (normed_two * gain_two).astype(jnp.bfloat16)
    inner_pre = jnp.dot(hidden_two, inner_full, preferred_element_type=jnp.float32)
    active = jax.nn.silu(inner_pre).astype(jnp.bfloat16)
    result = resid + jnp.dot(active, outer_full, preferred_element_type=jnp.float32)
    grad_out = cotangent[0]
    grad_active = jnp.dot(grad_out, outer_full.T, preferred_element_type=jnp.float32)
    grad_outer = jnp.dot(active.T, grad_out, preferred_element_type=jnp.float32)
    sigmoid_in = jax.nn.sigmoid(inner_pre)
    grad_inner_pre = (grad_active * sigmoid_in * (1.0 + inner_pre * (1.0 - sigmoid_in))).astype(
        jnp.bfloat16
    )
    grad_inner = jnp.dot(hidden_two.T, grad_inner_pre, preferred_element_type=jnp.float32)
    grad_hidden_two = jnp.dot(grad_inner_pre, inner_full.T, preferred_element_type=jnp.float32)
    grad_gain_two = jnp.sum(grad_hidden_two * normed_two, axis=0)
    grad_resid = grad_out.astype(jnp.float32) + norm_back(
        grad_hidden_two * gain_two, normed_two, scale_two
    )
    grad_resid_low = grad_resid.astype(jnp.bfloat16)
    grad_outw = jnp.dot(attn_low.T, grad_resid_low, preferred_element_type=jnp.float32)
    grad_attended = heads_of(
        jnp.dot(grad_resid_low, out_full.T, preferred_element_type=jnp.float32).astype(jnp.bfloat16)
    )
    row_delta = jnp.einsum("qhd,hqd->hq", grad_attended.astype(jnp.float32), attn_heads)

    def attend_back(grad_parts, key_flat, value_flat, turn_index):
        source, key_pos, key_seg = key_info(turn_index)

        def compute(parts_in):
            grad_query_acc, grad_key_acc, grad_value_acc = parts_in
            key_block = heads_of(key_flat)
            value_block = heads_of(value_flat)
            allowed = block_mask(local_pos, local_seg, key_pos, key_seg)
            scores = scores_of(queries, key_block)
            probabilities = jnp.where(allowed[None], jnp.exp(scores - log_total[..., None]), 0.0)
            grad_value_acc = grad_value_acc + jnp.einsum(
                "hqk,qhd->khd",
                probabilities.astype(jnp.bfloat16),
                grad_attended,
                preferred_element_type=jnp.float32,
            ).reshape(row_count, model_width)
            grad_probs = jnp.einsum(
                "qhd,khd->hqk", grad_attended, value_block, preferred_element_type=jnp.float32
            )
            grad_scores = (probabilities * (grad_probs - row_delta[..., None])).astype(jnp.bfloat16)
            grad_query_acc = grad_query_acc + jnp.einsum(
                "hqk,khd->qhd", grad_scores, key_block, preferred_element_type=jnp.float32
            )
            grad_key_acc = grad_key_acc + jnp.einsum(
                "hqk,qhd->khd", grad_scores, queries, preferred_element_type=jnp.float32
            ).reshape(row_count, model_width)
            return (grad_query_acc, grad_key_acc, grad_value_acc)

        return lax.cond(source <= ctx_place, compute, keep_state, grad_parts)

    def back_compute(turn_index, loop_state):
        key_block, value_block, grad_parts = loop_state
        grad_parts = attend_back(grad_parts, key_block, value_block, turn_index)
        grad_key_acc, grad_value_acc = pass_grads(grad_parts[1], grad_parts[2])
        return (key_block, value_block, (grad_parts[0], grad_key_acc, grad_value_acc))

    def back_turn(turn_index, loop_state):
        key_block, value_block, grad_parts = back_compute(turn_index, loop_state)
        key_block, value_block = shifted((key_block, value_block), "ctx", 1)
        return (key_block, value_block, grad_parts)

    zero_heads = jnp.zeros((row_count, H, HD), jnp.float32)
    zero_flat = jnp.zeros((row_count, model_width), jnp.float32)
    back_state = lax.fori_loop(
        0, ctx_count - 1, back_turn, (key_rows, value_rows, (zero_heads, zero_flat, zero_flat))
    )
    back_state = back_compute(jnp.int32(ctx_count - 1), back_state)
    grad_query_acc, grad_key_acc, grad_value_acc = back_state[2]
    grad_query_flat = grad_query_acc.reshape(row_count, model_width)
    grad_key_low = grad_key_acc.astype(jnp.bfloat16)
    grad_value_low = grad_value_acc.astype(jnp.bfloat16)
    grad_query_raw = (grad_query_flat * scale_vec).astype(jnp.bfloat16)
    grad_scale = jnp.sum(
        (grad_query_flat * query_raw).reshape(row_count, H, HD), axis=(0, 1)
    ) / math.sqrt(HD)
    grad_qw = jnp.dot(hidden_one.T, grad_query_raw, preferred_element_type=jnp.float32)
    grad_kw = jnp.dot(hidden_one.T, grad_key_low, preferred_element_type=jnp.float32)
    grad_vw = jnp.dot(hidden_one.T, grad_value_low, preferred_element_type=jnp.float32)
    grad_hidden_one = (
        jnp.dot(grad_query_raw, query_full.T, preferred_element_type=jnp.float32)
        + jnp.dot(grad_key_low, key_full.T, preferred_element_type=jnp.float32)
        + jnp.dot(grad_value_low, value_full.T, preferred_element_type=jnp.float32)
    )
    grad_gain_one = jnp.sum(grad_hidden_one * normed_one, axis=0)
    grad_tokens = grad_resid_low.astype(jnp.float32) + norm_back(
        grad_hidden_one * gain_one, normed_one, scale_one
    )
    shard_count = lax.axis_size("fs")
    scale_rows = jnp.broadcast_to(grad_scale[None, :], (shard_count, grad_scale.shape[0]))
    shares = (
        lax.psum_scatter(
            grad_qw.astype(jnp.bfloat16), "fs", scatter_dimension=0, tiled=True
        ).astype(jnp.float32),
        lax.psum_scatter(
            grad_kw.astype(jnp.bfloat16), "fs", scatter_dimension=0, tiled=True
        ).astype(jnp.float32),
        lax.psum_scatter(
            grad_vw.astype(jnp.bfloat16), "fs", scatter_dimension=0, tiled=True
        ).astype(jnp.float32),
        lax.psum_scatter(
            grad_outw.astype(jnp.bfloat16), "fs", scatter_dimension=0, tiled=True
        ).astype(jnp.float32),
        lax.psum_scatter(
            grad_inner.astype(jnp.bfloat16), "fs", scatter_dimension=0, tiled=True
        ).astype(jnp.float32),
        lax.psum_scatter(
            grad_outer.astype(jnp.bfloat16), "fs", scatter_dimension=0, tiled=True
        ).astype(jnp.float32),
        lax.psum_scatter(
            grad_gain_one.astype(jnp.bfloat16), "fs", scatter_dimension=0, tiled=True
        ).astype(jnp.float32),
        lax.psum_scatter(
            grad_gain_two.astype(jnp.bfloat16), "fs", scatter_dimension=0, tiled=True
        ).astype(jnp.float32),
        lax.psum_scatter(
            scale_rows.astype(jnp.bfloat16), "fs", scatter_dimension=0, tiled=True
        ).astype(jnp.float32),
    )
    totals = (
        lax.psum(shares[0].astype(jnp.bfloat16), "ctx").astype(jnp.float32),
        lax.psum(shares[1].astype(jnp.bfloat16), "ctx").astype(jnp.float32),
        lax.psum(shares[2].astype(jnp.bfloat16), "ctx").astype(jnp.float32),
        lax.psum(shares[3].astype(jnp.bfloat16), "ctx").astype(jnp.float32),
        lax.psum(shares[4].astype(jnp.bfloat16), "ctx").astype(jnp.float32),
        lax.psum(shares[5].astype(jnp.bfloat16), "ctx").astype(jnp.float32),
        lax.psum(shares[6].astype(jnp.bfloat16), "ctx").astype(jnp.float32),
        lax.psum(shares[7].astype(jnp.bfloat16), "ctx").astype(jnp.float32),
        lax.psum(shares[8].astype(jnp.bfloat16), "ctx").astype(jnp.float32),
    )
    return (
        result[None].astype(jnp.bfloat16),
        grad_tokens[None].astype(jnp.bfloat16),
        totals[0],
        totals[1],
        totals[2],
        totals[3],
        totals[4],
        totals[5],
        totals[6],
        totals[7],
        totals[8][0],
    )


MESH = pl.DeviceIdType.MESH
ANY = pl.BlockSpec(memory_space=pl.ANY)
VMEM = pl.BlockSpec(memory_space=pltpu.VMEM)
BF = jnp.bfloat16
F32 = jnp.float32


def fast_fits(mesh):
    return mesh.shape["ctx"] == H and mesh.shape["fs"] == 2


def remote(src, dst, ssem, rsem, target):
    return pltpu.make_async_remote_copy(
        src_ref=src, dst_ref=dst, send_sem=ssem, recv_sem=rsem, device_id=target, device_id_type=MESH
    )


def signal(target):
    pl.semaphore_signal(
        pltpu.get_barrier_semaphore(), inc=1, device_id=target, device_id_type=MESH
    )


def place():
    me = lax.axis_index("ctx")
    return me, lax.axis_index("fs"), me // 4, lax.rem(me // 2, 2), lax.rem(me, 2)


def dot(a, b, dims=((1,), (0,))):
    return lax.dot_general(a, b, (dims, ((), ())), preferred_element_type=F32)


NT = ((1,), (1,))
TN = ((0,), (0,))


LOG2E = math.log2(math.e)
N_SHARED = 0
PULL = (1, 0)
UNITS = H // 2


def weight_pull(own, other, k, fs, me, ssem, rsem):
    half = own[0].shape[0] // 2
    rows = pl.ds(pl.multiple_of(k * half, 64), half)
    yn = (me, 1 - fs)
    sib = (me + 1 - 2 * k, fs)
    n = len(own)

    def first(i):
        return remote(own[i].at[rows], other[i].at[rows], ssem.at[i], rsem.at[i], yn)

    def second(i):
        return remote(other[i].at[rows], other[i].at[rows], ssem.at[n + i], rsem.at[n + i], sib)

    return first, second


def weight_share(own, other, k, x, fs, me, ssem, rsem):
    quarter = own[0].shape[0] // 4 if own else 32
    yn, sib, xn = (me, 1 - fs), (me + 1 - 2 * k, fs), (me + 2 - 4 * x, fs)

    def rows(c, a):
        return pl.ds(pl.multiple_of((c * 2 + a) * quarter, 32), quarter)

    def over_y(i):
        r = rows(k, x)
        return remote(own[i].at[r], other[i].at[r], ssem.at[i, 0], rsem.at[i, 0], yn)

    def over_x(i, a):
        r = rows(k, a)
        return remote(other[i].at[r], other[i].at[r], ssem.at[i, 1], rsem.at[i, 1], xn)

    def over_core(i, c, a, n):
        r = rows(c, a)
        return remote(other[i].at[r], other[i].at[r], ssem.at[i, 2 + n], rsem.at[i, 2 + n], sib)

    return over_y, over_x, over_core


def visible(j, i, rows, first_key):
    kpos = j * rows + lax.broadcasted_iota(jnp.int32, (rows, rows), 0)
    qpos = i * rows + lax.broadcasted_iota(jnp.int32, (rows, rows), 1)
    return (kpos <= qpos) & (kpos >= first_key)


def forward_kernel(n_w, n_x, tok_ref, gain_ref, wt_ref, scale_ref, first_ref, *rest):
    own = rest[:n_w]
    at = n_w
    gain_full, attn_ref = rest[at : at + 2]
    kept = rest[at + 2 : at + 11]
    other = rest[at + 11 : at + 11 + n_w]
    (
        wt_all, gain_own, gain_other, o_sc, vt_sc, m_sc, l_sc, acc_sc,
        h_all, o32_ref, lse_ref, qt_ref, q_ref, kt_ref, k_ref, v_ref, raw_ref,
        ssem, rsem, osend, orecv, wssem, wrsem, xssem, xrsem, ysem, lsem, ksem,
    ) = rest[at + 11 + n_w :]
    me, fs, z, x, k = place()
    sib, xn, yn = (me + 1 - 2 * k, fs), (me + 2 - 4 * x, fs), (me, 1 - fs)
    up, dn = (me + 4, fs), (me - 4, fs)
    rows = tok_ref.shape[0]
    here = (h_all, o32_ref, lse_ref, qt_ref, q_ref, kt_ref, k_ref, v_ref, raw_ref)

    def keep(i, u):
        return pltpu.make_async_copy(here[i].at[u], kept[i].at[u], ksem.at[i, u])

    unit_rows = 2 * rows
    bar = pltpu.get_barrier_semaphore()
    for i in range(1, H):
        signal((lax.rem(me + i, H), fs))
    signal(yn)
    gain_own[...] = gain_ref[...]
    tokens = tok_ref[...].astype(F32)
    normed = tokens * lax.rsqrt(jnp.mean(tokens * tokens, axis=-1, keepdims=True) + epsilon)
    pl.semaphore_wait(bar, H)

    gain_copy = remote(gain_own, gain_other, ysem.at[0], ysem.at[1], yn)
    gain_copy.start()
    half = wt_ref.shape[1]
    columns = pl.ds(pl.multiple_of(fs * half, 128), half)
    wt_copy = remote(wt_ref, wt_all.at[:, columns], ysem.at[2], ysem.at[3], yn)
    wt_copy.start()
    wt_here = pltpu.make_async_copy(wt_ref, wt_all.at[:, columns], lsem.at[0])
    wt_here.start()
    n_y = n_w - n_x
    first, second = weight_pull(own[:n_y], other[:n_y], k, fs, me, wssem, wrsem)
    over_y, over_x, over_core = weight_share(own[n_y:], other[n_y:], k, x, fs, me, xssem, xrsem)
    gain_copy.wait()
    g_here = gain_own[...].astype(F32)
    g_there = gain_other[...].astype(F32)
    gains = jnp.where(
        fs == 0,
        jnp.concatenate([g_here, g_there], axis=1),
        jnp.concatenate([g_there, g_here], axis=1),
    )
    gain_full[...] = gains
    my_rows = pl.ds(pl.multiple_of(k * rows, rows), rows)
    h_all[me // 2, my_rows, :] = (normed * gains[0:1]).astype(BF)

    def slot(s):
        return h_all.at[s // 2, pl.ds(pl.multiple_of(lax.rem(s, 2) * rows, rows), rows)]

    def cp(s, t, si):
        return remote(slot(s), slot(s), ssem.at[si], rsem.at[s], t)

    cp(me, xn, 0).start()

    @pl.when(z < 3)
    def _():
        cp(me, up, 1).start()

    @pl.when(z > 0)
    def _():
        cp(me, dn, 2).start()

    cp(me, sib, 3).start()
    for i in range(n_y):
        first(i).start()
    for i in range(n_x):
        over_y(i).start()
    wt_here.wait()
    wt_copy.wait()

    def project(u):
        qkv = dot(wt_all[...], h_all[u], NT)
        raw = qkv[:HD]
        raw_ref[u] = raw
        q32 = raw * scale_ref[...]
        qt_ref[u] = (q32 * LOG2E).astype(BF)
        q_ref[u] = q32.T.astype(BF)
        kt = qkv[HD : 2 * HD]
        vt = qkv[2 * HD :]
        kt_ref[u] = kt.astype(BF)
        k_ref[u] = kt.T.astype(BF)
        v_ref[u] = vt.T.astype(BF)
        vt_sc[u] = vt.astype(BF)
        m_sc[u] = jnp.full((1, unit_rows), neg_big, F32)
        l_sc[u] = jnp.zeros((1, unit_rows), F32)
        acc_sc[u] = jnp.zeros((HD, unit_rows), F32)

    def pair(j, i):
        s = dot(k_ref[j], qt_ref[i])
        s = jnp.where(visible(j, i, unit_rows, first_ref[i]), s, neg_big)
        run_max = m_sc[i]
        new_max = jnp.maximum(run_max, jnp.max(s, axis=0, keepdims=True))
        p = jnp.exp2(s - new_max)
        factor = jnp.exp2(run_max - new_max)
        l_sc[i] = l_sc[i] * factor + jnp.sum(p, axis=0, keepdims=True)
        acc_sc[i] = acc_sc[i] * factor + dot(vt_sc[j], p.astype(BF))
        m_sc[i] = new_max

    def when_here(uz, ux):
        return 4 * jnp.maximum(uz - z, z - uz) + 2 * jnp.maximum(ux - x, x - ux) + (uz + 4 - z) // 5

    def process(uz, ux):
        u = uz * 2 + ux
        cp(u * 2 + 1 - k, sib, 0).wait_recv()
        project(u)
        for i in (0, 3, 4, 5, 6, 7, 8):
            keep(i, u).start()
        pair(u, u)
        mine = when_here(uz, ux)

        def earlier(e, c):
            @pl.when(when_here(e // 2, lax.rem(e, 2)) < mine)
            def _():
                pair(jnp.minimum(e, u), jnp.maximum(e, u))

            return c

        lax.fori_loop(0, UNITS, earlier, 0)

    xo = me + 2 - 4 * x

    def column_arrival(d):
        a = 4 + (d - 1) * 6

        @pl.when(z >= d)
        def _():
            s = me - 4 * d
            cp(s, dn, a).wait_recv()

            @pl.when(z < 3)
            def _():
                cp(s, up, a).start()

            cp(s, xn, a + 1).start()
            cp(s, sib, a + 2).start()

        @pl.when(z + d <= 3)
        def _():
            s = me + 4 * d
            cp(s, up, a + 3).wait_recv()

            @pl.when(z > 0)
            def _():
                cp(s, dn, a + 3).start()

            cp(s, xn, a + 4).start()
            cp(s, sib, a + 5).start()

    def across_arrival(d):
        @pl.when(z >= d)
        def _():
            s = xo - 4 * d
            cp(s, xn, 0).wait_recv()
            cp(s, sib, 22 + z - d).start()

        @pl.when((z + d <= 3) & (d > 0))
        def _():
            s = xo + 4 * d
            cp(s, xn, 0).wait_recv()
            cp(s, sib, 22 + z + d).start()

    def step(d, c):
        @pl.when((d >= 1) & (d <= 3))
        def _():
            column_arrival(d)

        @pl.when(d >= 1)
        def _():
            across_arrival(d - 1)

        for i in range(1):

            @pl.when(d == i + 2)
            def _(i=i):
                first(i).wait_recv()
                second(i).start()

        def compute(n, c2):
            across = 1 - n // 2
            dd = d - across
            uz = z + dd * (2 * lax.rem(n, 2) - 1)
            ux = x + across * (1 - 2 * x)
            ok = (dd >= 0) & (dd <= 3) & (uz >= 0) & (uz <= 3)
            ok = ok & ((dd > 0) | (lax.rem(n, 2) == 0))

            @pl.when(ok)
            def _():
                process(uz, ux)

            return c2

        lax.fori_loop(0, 4, compute, 0)
        return c

    lax.fori_loop(0, 5, step, 0)

    def out_copy(b):
        u = b // 2
        lanes = pl.ds(pl.multiple_of(lax.rem(b, 2) * rows, 128), rows)
        return o_sc.at[u, :, lanes]

    def finish(n, c):
        u = lax.rem(me // 2 + n, UNITS)
        out = acc_sc[u] / l_sc[u]
        o32_ref[u] = out
        o_sc[u] = out.astype(BF)
        lse_ref[u] = m_sc[u] + jnp.log2(l_sc[u])
        keep(1, u).start()
        keep(2, u).start()

        def send(e, c2):
            b = u * 2 + e

            @pl.when(b != me)
            def _():
                remote(out_copy(b), attn_ref.at[me], osend.at[b], orecv.at[me], (b, fs)).start()

            @pl.when(b == me)
            def _():
                pltpu.make_async_copy(out_copy(b), attn_ref.at[me], lsem.at[1]).start()

            return c2

        return lax.fori_loop(0, 2, send, c)

    lax.fori_loop(0, UNITS, finish, 0)
    for i in range(1, n_y):
        first(i).wait_recv()
        second(i).start()
    for i in range(n_x):
        over_y(i).wait_recv()
        over_x(i, x).start()
        over_core(i, k, x, 0).start()

    def taken(b, c):
        @pl.when(b != me)
        def _():
            remote(out_copy(b), attn_ref.at[b], osend.at[b], orecv.at[b], (b, fs)).wait()

        return c

    lax.fori_loop(0, H, taken, 0)
    pltpu.make_async_copy(out_copy(me), attn_ref.at[me], lsem.at[1]).wait()

    def all_kept(u, c):
        for i in range(9):
            keep(i, u).wait()
        return c

    lax.fori_loop(0, UNITS, all_kept, 0)
    cp(me, xn, 0).wait_send()

    @pl.when(z < 3)
    def _():
        cp(me, up, 1).wait_send()

    @pl.when(z > 0)
    def _():
        cp(me, dn, 2).wait_send()

    cp(me, sib, 3).wait_send()

    def sent(d, c):
        a = 4 + (d - 1) * 6

        @pl.when(z >= d)
        def _():
            s = me - 4 * d

            @pl.when(z < 3)
            def _():
                cp(s, up, a).wait_send()

            cp(s, xn, a + 1).wait_send()
            cp(s, sib, a + 2).wait_send()

        @pl.when(z + d <= 3)
        def _():
            s = me + 4 * d

            @pl.when(z > 0)
            def _():
                cp(s, dn, a + 3).wait_send()

            cp(s, xn, a + 4).wait_send()
            cp(s, sib, a + 5).wait_send()

        return c

    lax.fori_loop(1, 4, sent, 0)

    def sent_across(zz, c):
        cp(xo + 4 * (zz - z), sib, 22 + zz).wait_send()
        return c

    lax.fori_loop(0, 4, sent_across, 0)
    for i in range(n_x):
        over_x(i, 1 - x).wait_recv()
        over_core(i, k, 1 - x, 1).start()
    for i in range(n_y):
        first(i).wait_send()
        second(i).wait()
    for i in range(n_x):
        over_y(i).wait_send()
        over_x(i, x).wait_send()
        over_core(i, k, x, 0).wait_send()
        over_core(i, k, 1 - x, 1).wait_send()
        over_core(i, 1 - k, x, 0).wait_recv()
        over_core(i, 1 - k, 1 - x, 1).wait_recv()


def forward_call(tok, gains, wt, scale_col, first_key, weights, n_x):
    n_w = len(weights)
    rows, width = tok.shape
    ur = 2 * rows

    def out(dtype, *shape):
        return jax.ShapeDtypeStruct((UNITS, *shape), dtype)

    kept = [
        out(BF, ur, width), out(F32, HD, ur), out(F32, 1, ur), out(BF, HD, ur), out(BF, ur, HD),
        out(BF, HD, ur), out(BF, ur, HD), out(BF, ur, HD), out(F32, HD, ur),
    ]
    shapes = [
        jax.ShapeDtypeStruct((gains.shape[0], 2 * gains.shape[1]), F32),
        jax.ShapeDtypeStruct((H, HD, rows), BF),
        *kept,
    ] + [jax.ShapeDtypeStruct(w.shape, BF) for w in weights]
    return pl.pallas_call(
        functools.partial(forward_kernel, n_w, n_x),
        out_shape=shapes,
        in_specs=[VMEM] * 5 + [ANY] * n_w,
        out_specs=[VMEM] + [ANY] * (10 + n_w),
        scratch_shapes=[
            pltpu.VMEM((wt.shape[0], 2 * wt.shape[1]), BF),
            pltpu.VMEM(gains.shape, BF),
            pltpu.VMEM(gains.shape, BF),
            pltpu.VMEM((UNITS, HD, ur), BF),
            pltpu.VMEM((UNITS, HD, ur), BF),
            pltpu.VMEM((UNITS, 1, ur), F32),
            pltpu.VMEM((UNITS, 1, ur), F32),
            pltpu.VMEM((UNITS, HD, ur), F32),
            *[pltpu.VMEM(a.shape, a.dtype) for a in kept],
            pltpu.SemaphoreType.DMA((26,)),
            pltpu.SemaphoreType.DMA((H,)),
            pltpu.SemaphoreType.DMA((H,)),
            pltpu.SemaphoreType.DMA((H,)),
            pltpu.SemaphoreType.DMA((2 * n_w,)),
            pltpu.SemaphoreType.DMA((2 * n_w,)),
            pltpu.SemaphoreType.DMA((max(1, n_x), 4)),
            pltpu.SemaphoreType.DMA((max(1, n_x), 4)),
            pltpu.SemaphoreType.DMA((4,)),
            pltpu.SemaphoreType.DMA((2,)),
            pltpu.SemaphoreType.DMA((9, UNITS)),
        ],
        compiler_params=pltpu.CompilerParams(
            collective_id=1, has_side_effects=True, vmem_limit_bytes=56 * 2**20
        ),
        name="forward",
    )(tok, gains, wt, scale_col, first_key, *weights)


def half_rows(start, size, align):
    return pl.ds(pl.multiple_of(start, align), size)


def tail_kernel(gt_ref, *rest):
    own = rest[:3]
    n_w = len(PULL)
    held = rest[3 : 6 - n_w]
    at = 6 - n_w
    (
        attn_ref, gr_ref, hid_ref, gip_ref, act_ref, cot_ref, tok_ref, gain_ref, g2_ref,
        scale_ref, first_ref,
    ) = rest[at : at + 11]
    kept = rest[at + 11 : at + 20]
    at += 20
    all_ref, tg_ref, sums_ref = rest[at : at + 3]
    pulled = rest[at + 3 : at + 3 + n_w]
    (
        h_ref, o_ref, lse_ref, qt_ref, q_ref, kt_ref, k_ref, v_ref, raw_ref,
        g_in, g_sc, delta_sc, dq_sc, scale_sc, dk_sc, dv_sc, d_sc, got, dw_sc, dw_out, dw_got, piece,
        s1, r0, so, ra, rb, r2, rz, e_sc, small_out, small_in, small_z,
        gsend, grecv, qsend, qrecv, ksend, krecv, dsend, drecv, psend, precv,
        asend, arecv, vsend, vrecv, lsem, wsem, ksem, wssem, wrsem,
    ) = rest[at + 3 + n_w :]
    me, fs, z, x, k = place()
    sib, xn, yn = (me + 1 - 2 * k, fs), (me + 2 - 4 * x, fs), (me, 1 - fs)
    up, dn = (me + 4, fs), (me - 4, fs)
    units, rows = h_ref.shape[:2]
    block = rows // 2
    n_g = 3
    part = s1.shape[2]
    width = s1.shape[3]
    cols = width // 2
    bar = pltpu.get_barrier_semaphore()
    for i in range(1, H):
        signal((lax.rem(me + i, H), fs))
    signal(yn)
    here = (h_ref, o_ref, lse_ref, qt_ref, q_ref, kt_ref, k_ref, v_ref, raw_ref)
    back = [pltpu.make_async_copy(kept[i], here[i], ksem.at[i]) for i in range(9)]
    for c in back[1:]:
        c.start()
    back[0].start()
    pl.semaphore_wait(bar, H)

    def lanes(b):
        return half_rows(lax.rem(b, 2) * block, block, 128)

    def g_copy(b, t):
        return remote(
            gt_ref.at[b], g_in.at[t // 2, :, lanes(t)], gsend.at[b], grecv.at[t], (b, fs)
        )

    def g_start(n, c):
        g_copy(lax.rem(me + n, H), me).start()
        return c

    lax.fori_loop(1, H, g_start, 0)
    g_here = pltpu.make_async_copy(gt_ref.at[me], g_in.at[me // 2, :, lanes(me)], lsem.at[0])
    g_here.start()
    first, second = weight_pull([own[w] for w in PULL], pulled, k, fs, me, wssem, wrsem)

    def theirs(g):
        return remote(so.at[g], r0.at[g], dsend.at[g], drecv.at[g], sib)

    def dense_rows(g, start):
        r = half_rows(start, part, 64)
        if g == 0:
            return dot(attn_ref[r, :], gr_ref[...])
        a, b = ((hid_ref, gip_ref), (act_ref, cot_ref))[g - 1]
        return dot(a[r, :], b[...])

    for g in range(n_g):
        for f in range(2):
            so[g, f] = dense_rows(g, f * 2 * part + (1 - k) * part).astype(BF)
        theirs(g).start()
    for g in range(n_g):
        for f in range(2):
            s1[g, f] = dense_rows(g, f * 2 * part + k * part).astype(BF)

    top, bottom = slice(0, part // 2), slice(part // 2, part)
    x_here = half_rows(x * cols, cols, 128)
    x_there = half_rows((1 - x) * cols, cols, 128)

    def stage(g, i):
        ends = (
            (s1.at[g, 1 - fs, top, :], ra.at[g], yn),
            (s1.at[g, :, bottom, x_there], rb.at[g], xn),
            (s1.at[g, fs, top, x_there], r2.at[g, top], xn),
            (s1.at[g, 1 - fs, bottom, x_here], r2.at[g, bottom], yn),
        )[i]
        return remote(ends[0], ends[1], psend.at[i, g], precv.at[i, g], ends[2])

    slab = part // 4

    zb = lax.rem(z, 2)
    near, far = (me + 4 - 8 * zb, fs), (me + 8 - 16 * (z // 2), fs)

    def z_rows(t):
        return s1.at[:, fs, half_rows(t * slab, slab, 16), x_here]

    def z_near(i):
        return remote(z_rows(1 - zb + 2 * i), rz.at[i], psend.at[4, i], precv.at[4, i], near)

    def z_far():
        return remote(
            z_rows(zb + 2 * (1 - z // 2)), rz.at[2], psend.at[4, 2], precv.at[4, 2], far
        )

    for g in range(n_g):
        theirs(g).wait()

        def add(i, c, g=g):
            r = half_rows(i * 32, 32, 32)
            for f in range(2):
                s1[g, f, r, :] += r0[g, f, r, :]
            return c

        lax.fori_loop(0, part // 32, add, 0)
        stage(g, 0).start()
        stage(g, 1).start()

    loads = []
    for w in range(3):
        for f in range(2):
            loads.append(
                pltpu.make_async_copy(own[w].at[pl.ds(f * part, part)], r0.at[w, f], wsem.at[w * 2 + f])
            )
            loads[-1].start()


    def load_other(src, w, f):
        return pltpu.make_async_copy(
            src.at[pl.ds(f * part, part)], so.at[w, f], wsem.at[6 + w * 2 + f]
        )

    for i, w in enumerate(w for w in range(3) if w not in PULL):
        for f in range(2):
            loads.append(load_other(held[i], w, f))
            loads[-1].start()

    def after_one():
        for g in range(n_g):
            stage(g, 0).wait()
            stage(g, 1).wait()

            def add(i, c, g=g):
                r = half_rows(i * 32, 32, 32)
                s1[g, fs, r, :] += ra[g, r, :]
                low = half_rows(part // 2 + i * 32, 32, 32)
                for f in range(2):
                    s1[g, f, low, x_here] += rb[g, f, r, :]
                return c

            lax.fori_loop(0, part // 64, add, 0)
            stage(g, 2).start()
            stage(g, 3).start()
        for i in range(n_w):
            first(i).start()

    def after_two():
        for g in range(n_g):
            stage(g, 2).wait()
            stage(g, 3).wait()

            def add(i, c, g=g):
                r = half_rows(i * 32, 32, 32)
                s1[g, fs, r, x_here] += r2[g, r, :]
                return c

            lax.fori_loop(0, part // 32, add, 0)
        for i in range(2):
            z_near(i).start()

    def after_near():
        for i in range(2):
            z_near(i).wait()
            r = half_rows((zb + 2 * i) * slab, slab, 16)
            for g in range(n_g):
                s1[g, fs, r, x_here] += rz[i, g]
        z_far().start()

    def after_far():
        z_far().wait()
        r = half_rows(z * slab, slab, 16)
        for g in range(n_g):
            piece[g] = s1[g, fs, r, x_here] + rz[2, g]

    scale_sc[...] = jnp.zeros_like(scale_sc)
    dw_sc[...] = jnp.zeros_like(dw_sc)

    def g_taken(n, c):
        b = lax.rem(me + n, H)
        g_copy(b, b).wait()
        return c

    for c in back[1:]:
        c.wait()
    g_here.wait()
    lax.fori_loop(1, H, g_taken, 0)

    def prepare(i, c):
        g = g_in[i].astype(F32)
        g_sc[i] = g.T.astype(BF)
        delta_sc[i] = jnp.sum(g * o_ref[i], axis=0, keepdims=True)
        dq_sc[i] = jnp.zeros((HD, rows), F32)
        return c

    lax.fori_loop(0, units, prepare, 0)

    back[0].wait()

    def pair(masked, j, i):
        s = dot(k_ref[j], qt_ref[i])
        if masked:
            s = jnp.where(visible(j, i, rows, first_ref[i]), s, neg_big)
        p = jnp.exp2(s - lse_ref[i])
        dv_sc[...] += dot(p.astype(BF), g_sc[i])
        dp = dot(v_ref[j], g_in[i])
        ds = (p * (dp - delta_sc[i])).astype(BF)
        dk_sc[...] += dot(ds, q_ref[i])
        dq_sc[i] += dot(kt_ref[j], ds)

    def out(b, lo, n):
        return d_sc.at[b // 2, pl.ds(lo, n), :, lanes(b)]

    def to(t, lo, n):
        return got.at[pl.ds(lo, n), half_rows(t * HD, HD, 16)]

    def kv_copy(b, t):
        return remote(out(b, 1, 2), to(t, 1, 2), ksend.at[b], krecv.at[t], (b, fs))

    def q_copy(b, t):
        return remote(out(b, 0, 1), to(t, 0, 1), qsend.at[b], qrecv.at[t], (b, fs))

    kv_here = pltpu.make_async_copy(out(me, 1, 2), to(me, 1, 2), lsem.at[1])
    q_here = pltpu.make_async_copy(out(me, 0, 1), to(me, 0, 1), lsem.at[2])

    def column(n, c):
        j = lax.rem(me // 2 + n, units)
        dk_sc[...] = jnp.zeros_like(dk_sc)
        dv_sc[...] = jnp.zeros_like(dv_sc)
        pair(True, j, j)

        def plain(i, c2):
            pair(False, j, i)
            return c2

        def edge(i, c2):
            pair(True, j, i)
            return c2

        end = jnp.where(j == 0, 1, units - 1)
        lax.fori_loop(j + 1, end, plain, 0)
        lax.fori_loop(jnp.maximum(j + 1, end), units, edge, 0)
        d_sc[j, 1] = dk_sc[...].T.astype(BF)
        d_sc[j, 2] = dv_sc[...].T.astype(BF)

        def send(e, c2):
            b = 2 * j + e

            @pl.when(b != me)
            def _():
                kv_copy(b, me).start()

            @pl.when(b == me)
            def _():
                kv_here.start()

            return c2

        lax.fori_loop(0, 2, send, 0)
        for e in range(2):
            dw_sc[1 + e] += dot(d_sc[j, 1 + e], h_ref[j])

        @pl.when(n == ONE_AT)
        def _():
            after_one()

        @pl.when(n == TWO_AT)
        def _():
            after_two()

        return c

    lax.fori_loop(0, units, column, 0)
    half = dw_out.shape[2]

    def dw_copy(n, lo, size):
        return remote(
            dw_out.at[pl.ds(lo, size)], dw_got.at[pl.ds(lo, size)], vsend.at[6 + n], vrecv.at[6 + n], yn
        )

    def dw_send(n, lo, size):
        away = half_rows((1 - fs) * half, half, 128)
        dw_out[lo : lo + size] = dw_sc[lo : lo + size, :, away].astype(BF)
        dw_copy(n, lo, size).start()

    def dw_take(n, lo, size):
        dw_copy(n, lo, size).wait()
        keep = half_rows(fs * half, half, 128)
        total = dw_sc[lo : lo + size, :, keep] + dw_got[lo : lo + size].astype(F32)
        piece[3 + lo : 3 + lo + size] = total.astype(BF)

    dw_send(0, 1, 2)

    def queries(n, c):
        i = lax.rem(me // 2 + n, units)
        dq = dq_sc[i]
        scale_sc[...] += dq * raw_ref[i]
        d_sc[i, 0] = (dq * scale_ref[...]).astype(BF)

        def send(e, c2):
            b = 2 * i + e

            @pl.when(b != me)
            def _():
                q_copy(b, me).start()

            @pl.when(b == me)
            def _():
                q_here.start()

            return c2

        lax.fori_loop(0, 2, send, 0)
        return c

    lax.fori_loop(0, units, queries, 0)
    def query_weight(i, c):
        dw_sc[0] += dot(d_sc[i, 0], h_ref[i])
        return c

    lax.fori_loop(0, units, query_weight, 0)
    dw_send(1, 0, 1)
    small_out[...] = jnp.zeros_like(small_out)
    small_out[1:2, :] = g2_ref[...]
    small_out[2:3, :HD] = jnp.sum(scale_sc[...].T, axis=0, keepdims=True)

    spans = (pl.ds(0, 3), pl.ds(4, 2), pl.ds(3, 1))

    def cp(p, s, t, si, mine=False):
        here = all_ref.at[s, spans[p]]
        return remote(piece.at[spans[p]] if mine else here, here, asend.at[p, si], arecv.at[p, s], t)

    def keep(p):
        return pltpu.make_async_copy(
            piece.at[spans[p]], all_ref.at[me, spans[p]], lsem.at[3 + p]
        )

    def begin(p):
        keep(p).start()
        cp(p, me, xn, 0, True).start()

        @pl.when(z < 3)
        def _():
            cp(p, me, up, 1, True).start()

        @pl.when(z > 0)
        def _():
            cp(p, me, dn, 2, True).start()

        cp(p, me, sib, 3, True).start()

    def column_arrival(p, d):
        a = 4 + (d - 1) * 6

        @pl.when(z >= d)
        def _():
            s = me - 4 * d
            cp(p, s, dn, a).wait_recv()

            @pl.when(z < 3)
            def _():
                cp(p, s, up, a).start()

            cp(p, s, xn, a + 1).start()
            cp(p, s, sib, a + 2).start()

        @pl.when(z + d <= 3)
        def _():
            s = me + 4 * d
            cp(p, s, up, a + 3).wait_recv()

            @pl.when(z > 0)
            def _():
                cp(p, s, dn, a + 3).start()

            cp(p, s, xn, a + 4).start()
            cp(p, s, sib, a + 5).start()

    xo = me + 2 - 4 * x

    def across_arrival(p, d):
        @pl.when(z >= d)
        def _():
            s = xo - 4 * d
            cp(p, s, xn, 0).wait_recv()
            cp(p, s, sib, 22 + z - d).start()

        if d > 0:

            @pl.when(z + d <= 3)
            def _():
                s = xo + 4 * d
                cp(p, s, xn, 0).wait_recv()
                cp(p, s, sib, 22 + z + d).start()


    def kv_taken(n, c):
        b = lax.rem(me + n, H)
        kv_copy(b, b).wait()
        return c

    def q_taken(n, c):
        b = lax.rem(me + n, H)
        q_copy(b, b).wait()
        return c

    def input_grad(w, start):
        for r, m in ((fs, r0), (1 - fs, so)):
            for f in range(2):
                at_rows = half_rows((r * 2 + f) * part, part, 64)
                term = dot(m[w, f], got[w])
                if start:
                    e_sc[at_rows, :] = term
                else:
                    e_sc[at_rows, :] += term

    def pass_on(i):
        first(i).wait_recv()
        second(i).start()

    def load_pulled(i):
        second(i).wait()
        first(i).wait_send()
        late = [load_other(pulled[i], PULL[i], f) for f in range(2)]
        for c in late:
            c.start()
        for c in late:
            c.wait()

    def v_copy(i, t):
        n = (0, 1, 8)[i]
        return remote(small_out, small_in.at[i], vsend.at[n], vrecv.at[n], t)

    def v_column(d):
        t = lax.rem(z + d, 4)
        return t, remote(
            small_z.at[z], small_z.at[z], vsend.at[2 + d], vrecv.at[2 + z], (me + 4 * (t - z), fs)
        )

    dw_take(0, 1, 2)
    begin(1)
    after_near()
    dw_take(1, 0, 1)
    begin(2)
    pass_on(0)
    column_arrival(1, 1)
    column_arrival(2, 1)
    lax.fori_loop(1, H, kv_taken, 0)
    kv_here.wait()
    for c in loads:
        c.wait()
    input_grad(2, True)
    load_pulled(0)
    input_grad(1, False)
    across_arrival(1, 0)
    across_arrival(2, 0)
    after_far()
    begin(0)
    column_arrival(1, 2)
    column_arrival(2, 2)
    column_arrival(0, 1)
    across_arrival(0, 0)
    across_arrival(1, 1)
    across_arrival(2, 1)
    pass_on(1)
    lax.fori_loop(1, H, q_taken, 0)
    q_here.wait()
    load_pulled(1)
    input_grad(0, False)
    column_arrival(1, 3)
    column_arrival(2, 3)
    grad_hidden = e_sc[...].T
    tokens = tok_ref[...].astype(F32)
    scale = lax.rsqrt(jnp.mean(tokens * tokens, axis=-1, keepdims=True) + epsilon)
    normed = tokens * scale
    small_out[0:1, :] = jnp.sum(grad_hidden * normed, axis=0, keepdims=True)
    v_copy(0, sib).start()
    column_arrival(0, 2)
    across_arrival(1, 2)
    across_arrival(2, 2)
    e = grad_hidden * gain_ref[0:1, :]
    tg_ref[...] = (
        gr_ref[...].astype(F32) + scale * (e - normed * jnp.mean(e * normed, axis=-1, keepdims=True))
    ).astype(BF)
    v_copy(0, sib).wait()
    small_out[...] += small_in[0]
    v_copy(1, xn).start()
    across_arrival(0, 1)
    v_copy(1, xn).wait()
    small_z[z] = small_out[...] + small_in[1]
    for d in range(1, 4):
        v_column(d)[1].start()
    column_arrival(0, 3)
    across_arrival(1, 3)
    across_arrival(2, 3)
    for d in range(1, 4):
        t, c = v_column(d)
        c.wait_send()
        remote(small_z.at[t], small_z.at[t], vsend.at[2 + d], vrecv.at[2 + t], xn).wait_recv()
    small_out[...] = (small_z[0] + small_z[1]) + (small_z[2] + small_z[3])
    v_copy(2, yn).start()
    across_arrival(0, 2)
    v_copy(2, yn).wait()
    sums_ref[...] = small_out[...] + small_in[2]
    across_arrival(0, 3)

    for p in (1, 2, 0):

        def from_sib(n, c, p=p):
            cp(p, n * 2 + 1 - k, sib, 0).wait_recv()
            return c

        lax.fori_loop(0, UNITS, from_sib, 0)
        keep(p).wait()
        cp(p, me, xn, 0, True).wait_send()

        @pl.when(z < 3)
        def _(p=p):
            cp(p, me, up, 1, True).wait_send()

        @pl.when(z > 0)
        def _(p=p):
            cp(p, me, dn, 2, True).wait_send()

        cp(p, me, sib, 3, True).wait_send()

        def sent(d, c, p=p):
            a = 4 + (d - 1) * 6

            @pl.when(z >= d)
            def _():
                s = me - 4 * d

                @pl.when(z < 3)
                def _():
                    cp(p, s, up, a).wait_send()

                cp(p, s, xn, a + 1).wait_send()
                cp(p, s, sib, a + 2).wait_send()

            @pl.when(z + d <= 3)
            def _():
                s = me + 4 * d

                @pl.when(z > 0)
                def _():
                    cp(p, s, dn, a + 3).wait_send()

                cp(p, s, xn, a + 4).wait_send()
                cp(p, s, sib, a + 5).wait_send()

            return c

        lax.fori_loop(1, 4, sent, 0)

        def sent_across(zz, c, p=p):
            cp(p, xo + 4 * (zz - z), sib, 22 + zz).wait_send()
            return c

        lax.fori_loop(0, 4, sent_across, 0)


ONE_AT = 3
TWO_AT = 6


def tail_call(gt, own, held, vm, kept):
    n_w = len(PULL)
    rows, width = vm[1].shape
    n, ur = kept[0].shape[:2]
    half = width // 2
    part = width // 4
    sem = pltpu.SemaphoreType.DMA
    return pl.pallas_call(
        tail_kernel,
        out_shape=[
            jax.ShapeDtypeStruct((H, 6, part // 4, half), BF),
            jax.ShapeDtypeStruct((rows, width), BF),
            jax.ShapeDtypeStruct((8, width), F32),
        ]
        + [jax.ShapeDtypeStruct(own[0].shape, BF)] * n_w,
        in_specs=[ANY] * (4 + len(held)) + [VMEM] * len(vm) + [ANY] * len(kept),
        out_specs=[ANY, VMEM, VMEM] + [ANY] * n_w,
        scratch_shapes=[
            *[pltpu.VMEM(a.shape, a.dtype) for a in kept],
            pltpu.VMEM((n, HD, ur), BF),
            pltpu.VMEM((n, ur, HD), BF),
            pltpu.VMEM((n, 1, ur), F32),
            pltpu.VMEM((n, HD, ur), F32),
            pltpu.VMEM((HD, ur), F32),
            pltpu.VMEM((ur, HD), F32),
            pltpu.VMEM((ur, HD), F32),
            pltpu.VMEM((n, 3, HD, ur), BF),
            pltpu.VMEM((3, H * HD, rows), BF),
            pltpu.VMEM((3, HD, width), F32),
            pltpu.VMEM((3, HD, half), BF),
            pltpu.VMEM((3, HD, half), BF),
            pltpu.VMEM((6, part // 4, half), BF),
            pltpu.VMEM((3, 2, part, width), BF),
            pltpu.VMEM((3, 2, part, width), BF),
            pltpu.VMEM((3, 2, part, width), BF),
            pltpu.VMEM((3, part // 2, width), BF),
            pltpu.VMEM((3, 2, part // 2, half), BF),
            pltpu.VMEM((3, part, half), BF),
            pltpu.VMEM((3, 3, part // 4, half), BF),
            pltpu.VMEM((width, rows), F32),
            pltpu.VMEM((8, width), F32),
            pltpu.VMEM((3, 8, width), F32),
            pltpu.VMEM((4, 8, width), F32),
            sem((H,)), sem((H,)), sem((H,)), sem((H,)), sem((H,)), sem((H,)),
            sem((3,)), sem((3,)), sem((5, 4)), sem((5, 4)),
            sem((3, 26)), sem((3, H)), sem((9,)), sem((9,)), sem((6,)), sem((12,)),
            sem((9,)), sem((max(1, 2 * n_w),)), sem((max(1, 2 * n_w),)),
        ],
        compiler_params=pltpu.CompilerParams(
            collective_id=2, has_side_effects=True, vmem_limit_bytes=62 * 2**20
        ),
        name="tail",
    )(gt, *own, *held, *vm, *kept)


def spread_kernel(dense_ref, heads_ref, *outs):
    slab, cols = dense_ref.shape[-2:]
    n, _, hd, _ = heads_ref.shape
    for w in range(3):

        @pl.when(pl.program_id(0) // 2 == w)
        def _(w=w):
            for zz in range(4):
                for xx in range(2):
                    outs[w][zz * slab : (zz + 1) * slab, xx * cols : (xx + 1) * cols] = dense_ref[
                        zz, xx, 0, 0
                    ].astype(F32)
            outs[3 + w][...] = heads_ref[...].reshape(n * hd, cols).astype(F32).T


def spread_call(pieces):
    n, parts, slab, cols = pieces.shape
    split = pieces.reshape(4, 2, 2, parts, slab, cols)

    def half(w):
        return lambda i: jnp.clip(i - 2 * w, 0, 1)

    def dense_spec(w):
        return pl.BlockSpec((4 * slab, 2 * cols), lambda i: (half(w)(i), 0))

    def heads_spec(w):
        return pl.BlockSpec((cols, n * slab // 2), lambda i: (0, half(w)(i)))

    return pl.pallas_call(
        spread_kernel,
        grid=(6,),
        out_shape=[jax.ShapeDtypeStruct((8 * slab, 2 * cols), F32)] * 3
        + [jax.ShapeDtypeStruct((cols, n * slab), F32)] * 3,
        in_specs=[
            pl.BlockSpec((4, 2, 1, 1, slab, cols), lambda i: (0, 0, lax.rem(i, 2), i // 2, 0, 0)),
            pl.BlockSpec((n // 2, 1, slab, cols), lambda i: (lax.rem(i, 2), 3 + i // 2, 0, 0)),
        ],
        out_specs=[dense_spec(w) for w in range(3)] + [heads_spec(w) for w in range(3)],
        compiler_params=pltpu.CompilerParams(vmem_limit_bytes=48 * 2**20),
        name="spread",
    )(split, pieces)


def dense_kernel(attn_ref, tok_ref, cot_ref, gain_ref, *rest):
    weights = rest[:6]
    out_ref, gr_ref, hid_ref, gip_ref, act_ref, ga_ref, g2_ref, w_sc, sem = rest[6:]
    fs = lax.axis_index("fs")
    half = weights[0].shape[0]
    loads = []
    for n, w in enumerate((0, 1, 2)):
        for o in range(2):
            r = pl.ds(pl.multiple_of((fs if o == 0 else 1 - fs) * half, 128), half)
            loads.append(pltpu.make_async_copy(weights[2 * w + o], w_sc.at[w, r], sem.at[n, o]))
            loads[-1].start()
    gain = gain_ref[1:2, :]
    tokens = tok_ref[...].astype(F32)
    cot = cot_ref[...]
    for c in loads[:2]:
        c.wait()
    resid = tokens + dot(attn_ref[...], w_sc[0], TN)
    scale = lax.rsqrt(jnp.mean(resid * resid, axis=-1, keepdims=True) + epsilon)
    normed = resid * scale
    hidden32 = normed * gain
    hidden = hidden32.astype(BF)
    hid_ref[...] = hidden32.T.astype(BF)
    for c in loads[2:4]:
        c.wait()
    pre = dot(hidden, w_sc[1])
    sig = 1.0 / (1.0 + jnp.exp(-pre))
    active32 = pre * sig
    active = active32.astype(BF)
    act_ref[...] = active32.T.astype(BF)
    for c in loads[4:]:
        c.wait()
    grad_active = dot(cot, w_sc[2], NT)
    gip = (grad_active * sig * (1.0 + pre * (1.0 - sig))).astype(BF)
    gip_ref[...] = gip
    grad_hidden = dot(gip, w_sc[1], NT)
    g2_ref[...] = jnp.sum(grad_hidden * normed, axis=0, keepdims=True)
    g = grad_hidden * gain
    gr = (
        cot.astype(F32) + scale * (g - normed * jnp.mean(g * normed, axis=-1, keepdims=True))
    ).astype(BF)
    gr_ref[...] = gr
    ga_ref[...] = dot(w_sc[0], gr, NT).astype(BF)
    out_ref[...] = (resid + dot(active, w_sc[2])).astype(BF)


def dense_call(attn_t, tok, cot, gain_full, weights):
    rows, width = tok.shape
    tall = jax.ShapeDtypeStruct((width, rows), BF)
    wide = jax.ShapeDtypeStruct((rows, width), BF)
    return pl.pallas_call(
        dense_kernel,
        out_shape=[wide, wide, tall, wide, tall, tall, jax.ShapeDtypeStruct((1, width), F32)],
        in_specs=[VMEM] * 4 + [ANY] * 6,
        out_specs=[VMEM] * 7,
        scratch_shapes=[
            pltpu.VMEM((3, 2 * weights[0].shape[0], width), BF),
            pltpu.SemaphoreType.DMA((3, 2)),
        ],
        compiler_params=pltpu.CompilerParams(vmem_limit_bytes=56 * 2**20),
        name="dense",
    )(attn_t, tok, cot, gain_full, *weights)


def fast_local(
    tokens, query_weight, key_weight, value_weight, out_weight, inner_weight, outer_weight,
    attn_gain, mlp_gain, query_scale, doc_starts, cotangent,
):
    me, fs = lax.axis_index("ctx"), lax.axis_index("fs")
    rows, width = tokens.shape[1:]
    tok = tokens[0]
    cot = cotangent[0]

    def head_columns(w):
        return lax.dynamic_slice(w, (0, me * HD), (w.shape[0], HD)).T

    wt = jnp.concatenate([head_columns(w) for w in (query_weight, key_weight, value_weight)], axis=0)
    gains = jnp.stack([attn_gain, mlp_gain])
    positions = jnp.arange(H * rows, dtype=jnp.int32)
    starts = doc_starts[0]
    first_key = jnp.max(
        jnp.where(starts[None, :] <= positions[:, None], starts[None, :], 0), axis=1
    ).reshape(UNITS, 1, 2 * rows)
    scale_col = (query_scale / math.sqrt(HD))[:, None]

    (
        gain_full, attn_t, h_all, o32, lse, qt, q, kt, k, v, raw,
        out_o, inner_o, outer_o, value_o,
    ) = forward_call(
        tok, gains, wt, scale_col, first_key,
        (out_weight, inner_weight, outer_weight, value_weight), N_SHARED,
    )
    attn_t = attn_t.reshape(width, rows)

    result, grad_resid, hidden_t, grad_inner_pre, active_t, grad_att_t, grad_gain_two = dense_call(
        attn_t, tok, cot, gain_full,
        (out_weight, out_o, inner_weight, inner_o, outer_weight, outer_o),
    )
    grad_att_t = grad_att_t.reshape(H, HD, rows)
    half = width // 2
    pieces, grad_tokens, sums, *_ = tail_call(
        grad_att_t, (query_weight, key_weight, value_weight), (value_o,),
        (
            attn_t, grad_resid, hidden_t, grad_inner_pre, active_t, cot, tok, gain_full,
            grad_gain_two, scale_col, first_key,
        ),
        (h_all, o32, lse, qt, q, kt, k, v, raw),
    )
    out_g, inner_g, outer_g, query_g, key_g, value_g = spread_call(pieces)
    gain_sums = lax.dynamic_slice(sums, (0, fs * half), (2, half))
    return (
        result[None], grad_tokens[None], query_g, key_g, value_g, out_g, inner_g, outer_g,
        gain_sums[0], gain_sums[1], sums[2, :HD] / math.sqrt(HD),
    )


def solution(mesh):
    placed = (
        P("fs", "ctx", None),
        P("fs", None),
        P("fs", None),
        P("fs", None),
        P("fs", None),
        P("fs", None),
        P("fs", None),
        P("fs"),
        P("fs"),
        P(),
        P("fs", None),
        P("fs", "ctx", None),
    )
    return jax.shard_map(
        fast_local if fast_fits(mesh) else general_local,
        mesh=mesh,
        in_specs=placed,
        out_specs=(
            P("fs", "ctx", None),
            P("fs", "ctx", None),
            P("fs", None),
            P("fs", None),
            P("fs", None),
            P("fs", None),
            P("fs", None),
            P("fs", None),
            P("fs"),
            P("fs"),
            P(),
        ),
        check_vma=False,
    )
```

```python
import functools
import math

import jax
import jax.numpy as jnp
from jax import lax
from jax.experimental import pallas as pl
from jax.experimental.pallas import tpu as pltpu
from jax.sharding import PartitionSpec as P

H = 16
HD = 80


epsilon = 1e-06
neg_big = -1e30


def passed_along(block, axis, distance):
    devices = range(lax.axis_size(axis))
    route = [((i - distance) % len(devices), i) for i in devices]
    return lax.ppermute(block, axis, route)


def shifted(value, axis, steps):
    count = lax.axis_size(axis)
    leading, last = (max(0, -steps), min(count, count - steps))
    return lax.ppermute(value, axis, [(source, source + steps) for source in range(leading, last)])


def rms_scale(values_in):
    return lax.rsqrt(jnp.mean(values_in * values_in, axis=-1, keepdims=True) + epsilon)


def norm_back(grad_normed, normed, scale_rows):
    inner_mean = jnp.mean(grad_normed * normed, axis=-1, keepdims=True)
    return scale_rows * (grad_normed - normed * inner_mean)


def segment_of(positions, starts_row):
    return jnp.sum((starts_row[None, :] <= positions[:, None]).astype(jnp.int32), axis=1) - 1


def block_mask(query_pos, query_seg, key_pos, key_seg):
    return (key_pos[None, :] <= query_pos[:, None]) & (key_seg[None, :] == query_seg[:, None])


def scores_of(query_block, key_block):
    return jnp.einsum("qhd,khd->hqk", query_block, key_block, preferred_element_type=jnp.float32)


def pass_grads(grad_key_acc, grad_value_acc):
    return (
        passed_along(grad_key_acc.astype(jnp.bfloat16), "ctx", 1).astype(grad_key_acc.dtype),
        passed_along(grad_value_acc.astype(jnp.bfloat16), "ctx", 1).astype(grad_value_acc.dtype),
    )


def general_local(
    tokens,
    query_weight,
    key_weight,
    value_weight,
    out_weight,
    inner_weight,
    outer_weight,
    attn_gain,
    mlp_gain,
    query_scale,
    doc_starts,
    cotangent,
):
    row_count = tokens.shape[1]
    model_width = tokens.shape[2]
    ctx_count = lax.axis_size("ctx")
    ctx_place = lax.axis_index("ctx")
    (
        query_full,
        key_full,
        value_full,
        out_full,
        inner_full,
        outer_full,
        attn_gain_full,
        mlp_gain_full,
    ) = (
        lax.all_gather(query_weight, "fs", axis=0, tiled=True),
        lax.all_gather(key_weight, "fs", axis=0, tiled=True),
        lax.all_gather(value_weight, "fs", axis=0, tiled=True),
        lax.all_gather(out_weight, "fs", axis=0, tiled=True),
        lax.all_gather(inner_weight, "fs", axis=0, tiled=True),
        lax.all_gather(outer_weight, "fs", axis=0, tiled=True),
        lax.all_gather(attn_gain, "fs", axis=0, tiled=True),
        lax.all_gather(mlp_gain, "fs", axis=0, tiled=True),
    )
    starts_row = doc_starts[0]
    local_pos = ctx_place * row_count + jnp.arange(row_count, dtype=jnp.int32)
    local_seg = segment_of(local_pos, starts_row)

    def heads_of(flat_block):
        return flat_block.reshape(row_count, H, HD)

    token_rows = tokens[0].astype(jnp.float32)
    scale_one = rms_scale(token_rows)
    normed_one = token_rows * scale_one
    gain_one = attn_gain_full.astype(jnp.float32)
    hidden_one = (normed_one * gain_one).astype(jnp.bfloat16)
    query_raw = jnp.dot(hidden_one, query_full, preferred_element_type=jnp.float32)
    scale_vec = jnp.tile(query_scale, H) / math.sqrt(HD)
    queries = heads_of((query_raw * scale_vec).astype(jnp.bfloat16))
    key_rows = jnp.dot(hidden_one, key_full, preferred_element_type=jnp.float32).astype(
        jnp.bfloat16
    )
    value_rows = jnp.dot(hidden_one, value_full, preferred_element_type=jnp.float32).astype(
        jnp.bfloat16
    )

    def key_info(turn_index):
        source = (ctx_place - turn_index) % ctx_count
        key_pos = source * row_count + jnp.arange(row_count, dtype=jnp.int32)
        return (source, key_pos, segment_of(key_pos, starts_row))

    def keep_state(state_in):
        return state_in

    def attend(softmax_state, key_flat, value_flat, turn_index):
        source, key_pos, key_seg = key_info(turn_index)

        def compute(state_in):
            run_max, run_sum, run_acc = state_in
            key_block = heads_of(key_flat)
            value_block = heads_of(value_flat)
            allowed = block_mask(local_pos, local_seg, key_pos, key_seg)
            scores = jnp.where(allowed[None], scores_of(queries, key_block), neg_big)
            new_max = jnp.maximum(run_max, jnp.max(scores, axis=-1))
            weights = jnp.where(allowed[None], jnp.exp(scores - new_max[..., None]), 0.0)
            factor = jnp.exp(run_max - new_max)
            run_sum = run_sum * factor + jnp.sum(weights, axis=-1)
            run_acc = run_acc * factor[..., None] + jnp.einsum(
                "hqk,khd->hqd",
                weights.astype(jnp.bfloat16),
                value_block,
                preferred_element_type=jnp.float32,
            )
            return (new_max, run_sum, run_acc)

        return lax.cond(source <= ctx_place, compute, keep_state, softmax_state)

    start_state = (
        jnp.full((H, row_count), neg_big, jnp.float32),
        jnp.zeros((H, row_count), jnp.float32),
        jnp.zeros((H, row_count, HD), jnp.float32),
    )
    start_state = attend(start_state, key_rows, value_rows, jnp.int32(0))
    stores = ()

    def forward_turn(turn_index, loop_state):
        key_block, value_block, softmax_state, kept = loop_state
        key_block, value_block = shifted((key_block, value_block), "ctx", 1)
        softmax_state = attend(softmax_state, key_block, value_block, turn_index)
        return (key_block, value_block, softmax_state, kept)

    loop_out = lax.fori_loop(
        1, ctx_count, forward_turn, (key_rows, value_rows, start_state, stores)
    )
    run_max, run_sum, run_acc = loop_out[2]
    stores = loop_out[3]
    log_total = run_max + jnp.log(run_sum)
    attn_heads = run_acc / run_sum[..., None]
    attn_low = (
        jnp.transpose(attn_heads, (1, 0, 2)).reshape(row_count, model_width).astype(jnp.bfloat16)
    )
    resid = token_rows + jnp.dot(attn_low, out_full, preferred_element_type=jnp.float32)
    scale_two = rms_scale(resid)
    normed_two = resid * scale_two
    gain_two = mlp_gain_full.astype(jnp.float32)
    hidden_two = (normed_two * gain_two).astype(jnp.bfloat16)
    inner_pre = jnp.dot(hidden_two, inner_full, preferred_element_type=jnp.float32)
    active = jax.nn.silu(inner_pre).astype(jnp.bfloat16)
    result = resid + jnp.dot(active, outer_full, preferred_element_type=jnp.float32)
    grad_out = cotangent[0]
    grad_active = jnp.dot(grad_out, outer_full.T, preferred_element_type=jnp.float32)
    grad_outer = jnp.dot(active.T, grad_out, preferred_element_type=jnp.float32)
    sigmoid_in = jax.nn.sigmoid(inner_pre)
    grad_inner_pre = (grad_active * sigmoid_in * (1.0 + inner_pre * (1.0 - sigmoid_in))).astype(
        jnp.bfloat16
    )
    grad_inner = jnp.dot(hidden_two.T, grad_inner_pre, preferred_element_type=jnp.float32)
    grad_hidden_two = jnp.dot(grad_inner_pre, inner_full.T, preferred_element_type=jnp.float32)
    grad_gain_two = jnp.sum(grad_hidden_two * normed_two, axis=0)
    grad_resid = grad_out.astype(jnp.float32) + norm_back(
        grad_hidden_two * gain_two, normed_two, scale_two
    )
    grad_resid_low = grad_resid.astype(jnp.bfloat16)
    grad_outw = jnp.dot(attn_low.T, grad_resid_low, preferred_element_type=jnp.float32)
    grad_attended = heads_of(
        jnp.dot(grad_resid_low, out_full.T, preferred_element_type=jnp.float32).astype(jnp.bfloat16)
    )
    row_delta = jnp.einsum("qhd,hqd->hq", grad_attended.astype(jnp.float32), attn_heads)

    def attend_back(grad_parts, key_flat, value_flat, turn_index):
        source, key_pos, key_seg = key_info(turn_index)

        def compute(parts_in):
            grad_query_acc, grad_key_acc, grad_value_acc = parts_in
            key_block = heads_of(key_flat)
            value_block = heads_of(value_flat)
            allowed = block_mask(local_pos, local_seg, key_pos, key_seg)
            scores = scores_of(queries, key_block)
            probabilities = jnp.where(allowed[None], jnp.exp(scores - log_total[..., None]), 0.0)
            grad_value_acc = grad_value_acc + jnp.einsum(
                "hqk,qhd->khd",
                probabilities.astype(jnp.bfloat16),
                grad_attended,
                preferred_element_type=jnp.float32,
            ).reshape(row_count, model_width)
            grad_probs = jnp.einsum(
                "qhd,khd->hqk", grad_attended, value_block, preferred_element_type=jnp.float32
            )
            grad_scores = (probabilities * (grad_probs - row_delta[..., None])).astype(jnp.bfloat16)
            grad_query_acc = grad_query_acc + jnp.einsum(
                "hqk,khd->qhd", grad_scores, key_block, preferred_element_type=jnp.float32
            )
            grad_key_acc = grad_key_acc + jnp.einsum(
                "hqk,qhd->khd", grad_scores, queries, preferred_element_type=jnp.float32
            ).reshape(row_count, model_width)
            return (grad_query_acc, grad_key_acc, grad_value_acc)

        return lax.cond(source <= ctx_place, compute, keep_state, grad_parts)

    def back_compute(turn_index, loop_state):
        key_block, value_block, grad_parts = loop_state
        grad_parts = attend_back(grad_parts, key_block, value_block, turn_index)
        grad_key_acc, grad_value_acc = pass_grads(grad_parts[1], grad_parts[2])
        return (key_block, value_block, (grad_parts[0], grad_key_acc, grad_value_acc))

    def back_turn(turn_index, loop_state):
        key_block, value_block, grad_parts = back_compute(turn_index, loop_state)
        key_block, value_block = shifted((key_block, value_block), "ctx", 1)
        return (key_block, value_block, grad_parts)

    zero_heads = jnp.zeros((row_count, H, HD), jnp.float32)
    zero_flat = jnp.zeros((row_count, model_width), jnp.float32)
    back_state = lax.fori_loop(
        0, ctx_count - 1, back_turn, (key_rows, value_rows, (zero_heads, zero_flat, zero_flat))
    )
    back_state = back_compute(jnp.int32(ctx_count - 1), back_state)
    grad_query_acc, grad_key_acc, grad_value_acc = back_state[2]
    grad_query_flat = grad_query_acc.reshape(row_count, model_width)
    grad_key_low = grad_key_acc.astype(jnp.bfloat16)
    grad_value_low = grad_value_acc.astype(jnp.bfloat16)
    grad_query_raw = (grad_query_flat * scale_vec).astype(jnp.bfloat16)
    grad_scale = jnp.sum(
        (grad_query_flat * query_raw).reshape(row_count, H, HD), axis=(0, 1)
    ) / math.sqrt(HD)
    grad_qw = jnp.dot(hidden_one.T, grad_query_raw, preferred_element_type=jnp.float32)
    grad_kw = jnp.dot(hidden_one.T, grad_key_low, preferred_element_type=jnp.float32)
    grad_vw = jnp.dot(hidden_one.T, grad_value_low, preferred_element_type=jnp.float32)
    grad_hidden_one = (
        jnp.dot(grad_query_raw, query_full.T, preferred_element_type=jnp.float32)
        + jnp.dot(grad_key_low, key_full.T, preferred_element_type=jnp.float32)
        + jnp.dot(grad_value_low, value_full.T, preferred_element_type=jnp.float32)
    )
    grad_gain_one = jnp.sum(grad_hidden_one * normed_one, axis=0)
    grad_tokens = grad_resid_low.astype(jnp.float32) + norm_back(
        grad_hidden_one * gain_one, normed_one, scale_one
    )
    shard_count = lax.axis_size("fs")
    scale_rows = jnp.broadcast_to(grad_scale[None, :], (shard_count, grad_scale.shape[0]))
    shares = (
        lax.psum_scatter(
            grad_qw.astype(jnp.bfloat16), "fs", scatter_dimension=0, tiled=True
        ).astype(jnp.float32),
        lax.psum_scatter(
            grad_kw.astype(jnp.bfloat16), "fs", scatter_dimension=0, tiled=True
        ).astype(jnp.float32),
        lax.psum_scatter(
            grad_vw.astype(jnp.bfloat16), "fs", scatter_dimension=0, tiled=True
        ).astype(jnp.float32),
        lax.psum_scatter(
            grad_outw.astype(jnp.bfloat16), "fs", scatter_dimension=0, tiled=True
        ).astype(jnp.float32),
        lax.psum_scatter(
            grad_inner.astype(jnp.bfloat16), "fs", scatter_dimension=0, tiled=True
        ).astype(jnp.float32),
        lax.psum_scatter(
            grad_outer.astype(jnp.bfloat16), "fs", scatter_dimension=0, tiled=True
        ).astype(jnp.float32),
        lax.psum_scatter(
            grad_gain_one.astype(jnp.bfloat16), "fs", scatter_dimension=0, tiled=True
        ).astype(jnp.float32),
        lax.psum_scatter(
            grad_gain_two.astype(jnp.bfloat16), "fs", scatter_dimension=0, tiled=True
        ).astype(jnp.float32),
        lax.psum_scatter(
            scale_rows.astype(jnp.bfloat16), "fs", scatter_dimension=0, tiled=True
        ).astype(jnp.float32),
    )
    totals = (
        lax.psum(shares[0].astype(jnp.bfloat16), "ctx").astype(jnp.float32),
        lax.psum(shares[1].astype(jnp.bfloat16), "ctx").astype(jnp.float32),
        lax.psum(shares[2].astype(jnp.bfloat16), "ctx").astype(jnp.float32),
        lax.psum(shares[3].astype(jnp.bfloat16), "ctx").astype(jnp.float32),
        lax.psum(shares[4].astype(jnp.bfloat16), "ctx").astype(jnp.float32),
        lax.psum(shares[5].astype(jnp.bfloat16), "ctx").astype(jnp.float32),
        lax.psum(shares[6].astype(jnp.bfloat16), "ctx").astype(jnp.float32),
        lax.psum(shares[7].astype(jnp.bfloat16), "ctx").astype(jnp.float32),
        lax.psum(shares[8].astype(jnp.bfloat16), "ctx").astype(jnp.float32),
    )
    return (
        result[None].astype(jnp.bfloat16),
        grad_tokens[None].astype(jnp.bfloat16),
        totals[0],
        totals[1],
        totals[2],
        totals[3],
        totals[4],
        totals[5],
        totals[6],
        totals[7],
        totals[8][0],
    )


MESH = pl.DeviceIdType.MESH
ANY = pl.BlockSpec(memory_space=pl.ANY)
VMEM = pl.BlockSpec(memory_space=pltpu.VMEM)
BF = jnp.bfloat16
F32 = jnp.float32


def fast_fits(mesh):
    return mesh.shape["ctx"] == H and mesh.shape["fs"] == 2


def remote(src, dst, ssem, rsem, target):
    return pltpu.make_async_remote_copy(
        src_ref=src, dst_ref=dst, send_sem=ssem, recv_sem=rsem, device_id=target, device_id_type=MESH
    )


def signal(target):
    pl.semaphore_signal(
        pltpu.get_barrier_semaphore(), inc=1, device_id=target, device_id_type=MESH
    )


def place():
    me = lax.axis_index("ctx")
    return me, lax.axis_index("fs"), me // 4, lax.rem(me // 2, 2), lax.rem(me, 2)


def dot(a, b, dims=((1,), (0,))):
    return lax.dot_general(a, b, (dims, ((), ())), preferred_element_type=F32)


NT = ((1,), (1,))
TN = ((0,), (0,))


LOG2E = math.log2(math.e)
N_SHARED = 0
PULL = (1, 0)
UNITS = H // 2


def weight_pull(own, other, k, fs, me, ssem, rsem):
    half = own[0].shape[0] // 2
    rows = pl.ds(pl.multiple_of(k * half, 64), half)
    yn = (me, 1 - fs)
    sib = (me + 1 - 2 * k, fs)
    n = len(own)

    def first(i):
        return remote(own[i].at[rows], other[i].at[rows], ssem.at[i], rsem.at[i], yn)

    def second(i):
        return remote(other[i].at[rows], other[i].at[rows], ssem.at[n + i], rsem.at[n + i], sib)

    return first, second


def weight_share(own, other, k, x, fs, me, ssem, rsem):
    quarter = own[0].shape[0] // 4 if own else 32
    yn, sib, xn = (me, 1 - fs), (me + 1 - 2 * k, fs), (me + 2 - 4 * x, fs)

    def rows(c, a):
        return pl.ds(pl.multiple_of((c * 2 + a) * quarter, 32), quarter)

    def over_y(i):
        r = rows(k, x)
        return remote(own[i].at[r], other[i].at[r], ssem.at[i, 0], rsem.at[i, 0], yn)

    def over_x(i, a):
        r = rows(k, a)
        return remote(other[i].at[r], other[i].at[r], ssem.at[i, 1], rsem.at[i, 1], xn)

    def over_core(i, c, a, n):
        r = rows(c, a)
        return remote(other[i].at[r], other[i].at[r], ssem.at[i, 2 + n], rsem.at[i, 2 + n], sib)

    return over_y, over_x, over_core


def visible(j, i, rows, first_key):
    kpos = j * rows + lax.broadcasted_iota(jnp.int32, (rows, rows), 0)
    qpos = i * rows + lax.broadcasted_iota(jnp.int32, (rows, rows), 1)
    return (kpos <= qpos) & (kpos >= first_key)


def forward_kernel(n_w, n_x, tok_ref, gain_ref, wt_ref, scale_ref, first_ref, *rest):
    own = rest[:n_w]
    at = n_w
    gain_full, attn_ref = rest[at : at + 2]
    kept = rest[at + 2 : at + 11]
    other = rest[at + 11 : at + 11 + n_w]
    (
        wt_all, gain_own, gain_other, o_sc, vt_sc, m_sc, l_sc, acc_sc,
        h_all, o32_ref, lse_ref, qt_ref, q_ref, kt_ref, k_ref, v_ref, raw_ref,
        ssem, rsem, osend, orecv, wssem, wrsem, xssem, xrsem, ysem, lsem, ksem,
    ) = rest[at + 11 + n_w :]
    me, fs, z, x, k = place()
    sib, xn, yn = (me + 1 - 2 * k, fs), (me + 2 - 4 * x, fs), (me, 1 - fs)
    up, dn = (me + 4, fs), (me - 4, fs)
    rows = tok_ref.shape[0]
    here = (h_all, o32_ref, lse_ref, qt_ref, q_ref, kt_ref, k_ref, v_ref, raw_ref)

    def keep(i, u):
        return pltpu.make_async_copy(here[i].at[u], kept[i].at[u], ksem.at[i, u])

    unit_rows = 2 * rows
    bar = pltpu.get_barrier_semaphore()
    for i in range(1, H):
        signal((lax.rem(me + i, H), fs))
    signal(yn)
    gain_own[...] = gain_ref[...]
    tokens = tok_ref[...].astype(F32)
    normed = tokens * lax.rsqrt(jnp.mean(tokens * tokens, axis=-1, keepdims=True) + epsilon)
    pl.semaphore_wait(bar, H)

    gain_copy = remote(gain_own, gain_other, ysem.at[0], ysem.at[1], yn)
    gain_copy.start()
    half = wt_ref.shape[1]
    columns = pl.ds(pl.multiple_of(fs * half, 128), half)
    wt_copy = remote(wt_ref, wt_all.at[:, columns], ysem.at[2], ysem.at[3], yn)
    wt_copy.start()
    wt_here = pltpu.make_async_copy(wt_ref, wt_all.at[:, columns], lsem.at[0])
    wt_here.start()
    n_y = n_w - n_x
    first, second = weight_pull(own[:n_y], other[:n_y], k, fs, me, wssem, wrsem)
    over_y, over_x, over_core = weight_share(own[n_y:], other[n_y:], k, x, fs, me, xssem, xrsem)
    gain_copy.wait()
    g_here = gain_own[...].astype(F32)
    g_there = gain_other[...].astype(F32)
    gains = jnp.where(
        fs == 0,
        jnp.concatenate([g_here, g_there], axis=1),
        jnp.concatenate([g_there, g_here], axis=1),
    )
    gain_full[...] = gains
    my_rows = pl.ds(pl.multiple_of(k * rows, rows), rows)
    h_all[me // 2, my_rows, :] = (normed * gains[0:1]).astype(BF)

    def slot(s):
        return h_all.at[s // 2, pl.ds(pl.multiple_of(lax.rem(s, 2) * rows, rows), rows)]

    def cp(s, t, si):
        return remote(slot(s), slot(s), ssem.at[si], rsem.at[s], t)

    cp(me, xn, 0).start()

    @pl.when(z < 3)
    def _():
        cp(me, up, 1).start()

    @pl.when(z > 0)
    def _():
        cp(me, dn, 2).start()

    cp(me, sib, 3).start()
    for i in range(n_y):
        first(i).start()
    for i in range(n_x):
        over_y(i).start()
    wt_here.wait()
    wt_copy.wait()

    def project(u):
        qkv = dot(wt_all[...], h_all[u], NT)
        raw = qkv[:HD]
        raw_ref[u] = raw
        q32 = raw * scale_ref[...]
        qt_ref[u] = (q32 * LOG2E).astype(BF)
        q_ref[u] = q32.T.astype(BF)
        kt = qkv[HD : 2 * HD]
        vt = qkv[2 * HD :]
        kt_ref[u] = kt.astype(BF)
        k_ref[u] = kt.T.astype(BF)
        v_ref[u] = vt.T.astype(BF)
        vt_sc[u] = vt.astype(BF)
        m_sc[u] = jnp.full((1, unit_rows), neg_big, F32)
        l_sc[u] = jnp.zeros((1, unit_rows), F32)
        acc_sc[u] = jnp.zeros((HD, unit_rows), F32)

    def pair(j, i):
        s = dot(k_ref[j], qt_ref[i])
        s = jnp.where(visible(j, i, unit_rows, first_ref[i]), s, neg_big)
        run_max = m_sc[i]
        new_max = jnp.maximum(run_max, jnp.max(s, axis=0, keepdims=True))
        p = jnp.exp2(s - new_max)
        factor = jnp.exp2(run_max - new_max)
        l_sc[i] = l_sc[i] * factor + jnp.sum(p, axis=0, keepdims=True)
        acc_sc[i] = acc_sc[i] * factor + dot(vt_sc[j], p.astype(BF))
        m_sc[i] = new_max

    def when_here(uz, ux):
        return 4 * jnp.maximum(uz - z, z - uz) + 2 * jnp.maximum(ux - x, x - ux) + (uz + 4 - z) // 5

    def process(uz, ux):
        u = uz * 2 + ux
        cp(u * 2 + 1 - k, sib, 0).wait_recv()
        project(u)
        for i in (0, 3, 4, 5, 6, 7, 8):
            keep(i, u).start()
        pair(u, u)
        mine = when_here(uz, ux)

        def earlier(e, c):
            @pl.when(when_here(e // 2, lax.rem(e, 2)) < mine)
            def _():
                pair(jnp.minimum(e, u), jnp.maximum(e, u))

            return c

        lax.fori_loop(0, UNITS, earlier, 0)

    xo = me + 2 - 4 * x

    def column_arrival(d):
        a = 4 + (d - 1) * 6

        @pl.when(z >= d)
        def _():
            s = me - 4 * d
            cp(s, dn, a).wait_recv()

            @pl.when(z < 3)
            def _():
                cp(s, up, a).start()

            cp(s, xn, a + 1).start()
            cp(s, sib, a + 2).start()

        @pl.when(z + d <= 3)
        def _():
            s = me + 4 * d
            cp(s, up, a + 3).wait_recv()

            @pl.when(z > 0)
            def _():
                cp(s, dn, a + 3).start()

            cp(s, xn, a + 4).start()
            cp(s, sib, a + 5).start()

    def across_arrival(d):
        @pl.when(z >= d)
        def _():
            s = xo - 4 * d
            cp(s, xn, 0).wait_recv()
            cp(s, sib, 22 + z - d).start()

        @pl.when((z + d <= 3) & (d > 0))
        def _():
            s = xo + 4 * d
            cp(s, xn, 0).wait_recv()
            cp(s, sib, 22 + z + d).start()

    def step(d, c):
        @pl.when((d >= 1) & (d <= 3))
        def _():
            column_arrival(d)

        @pl.when(d >= 1)
        def _():
            across_arrival(d - 1)

        for i in range(1):

            @pl.when(d == i + 2)
            def _(i=i):
                first(i).wait_recv()
                second(i).start()

        def compute(n, c2):
            across = 1 - n // 2
            dd = d - across
            uz = z + dd * (2 * lax.rem(n, 2) - 1)
            ux = x + across * (1 - 2 * x)
            ok = (dd >= 0) & (dd <= 3) & (uz >= 0) & (uz <= 3)
            ok = ok & ((dd > 0) | (lax.rem(n, 2) == 0))

            @pl.when(ok)
            def _():
                process(uz, ux)

            return c2

        lax.fori_loop(0, 4, compute, 0)
        return c

    lax.fori_loop(0, 5, step, 0)

    def out_copy(b):
        u = b // 2
        lanes = pl.ds(pl.multiple_of(lax.rem(b, 2) * rows, 128), rows)
        return o_sc.at[u, :, lanes]

    def finish(n, c):
        u = lax.rem(me // 2 + n, UNITS)
        out = acc_sc[u] / l_sc[u]
        o32_ref[u] = out
        o_sc[u] = out.astype(BF)
        lse_ref[u] = m_sc[u] + jnp.log2(l_sc[u])
        keep(1, u).start()
        keep(2, u).start()

        def send(e, c2):
            b = u * 2 + e

            @pl.when(b != me)
            def _():
                remote(out_copy(b), attn_ref.at[me], osend.at[b], orecv.at[me], (b, fs)).start()

            @pl.when(b == me)
            def _():
                pltpu.make_async_copy(out_copy(b), attn_ref.at[me], lsem.at[1]).start()

            return c2

        return lax.fori_loop(0, 2, send, c)

    lax.fori_loop(0, UNITS, finish, 0)
    for i in range(1, n_y):
        first(i).wait_recv()
        second(i).start()
    for i in range(n_x):
        over_y(i).wait_recv()
        over_x(i, x).start()
        over_core(i, k, x, 0).start()

    def taken(b, c):
        @pl.when(b != me)
        def _():
            remote(out_copy(b), attn_ref.at[b], osend.at[b], orecv.at[b], (b, fs)).wait()

        return c

    lax.fori_loop(0, H, taken, 0)
    pltpu.make_async_copy(out_copy(me), attn_ref.at[me], lsem.at[1]).wait()

    def all_kept(u, c):
        for i in range(9):
            keep(i, u).wait()
        return c

    lax.fori_loop(0, UNITS, all_kept, 0)
    cp(me, xn, 0).wait_send()

    @pl.when(z < 3)
    def _():
        cp(me, up, 1).wait_send()

    @pl.when(z > 0)
    def _():
        cp(me, dn, 2).wait_send()

    cp(me, sib, 3).wait_send()

    def sent(d, c):
        a = 4 + (d - 1) * 6

        @pl.when(z >= d)
        def _():
            s = me - 4 * d

            @pl.when(z < 3)
            def _():
                cp(s, up, a).wait_send()

            cp(s, xn, a + 1).wait_send()
            cp(s, sib, a + 2).wait_send()

        @pl.when(z + d <= 3)
        def _():
            s = me + 4 * d

            @pl.when(z > 0)
            def _():
                cp(s, dn, a + 3).wait_send()

            cp(s, xn, a + 4).wait_send()
            cp(s, sib, a + 5).wait_send()

        return c

    lax.fori_loop(1, 4, sent, 0)

    def sent_across(zz, c):
        cp(xo + 4 * (zz - z), sib, 22 + zz).wait_send()
        return c

    lax.fori_loop(0, 4, sent_across, 0)
    for i in range(n_x):
        over_x(i, 1 - x).wait_recv()
        over_core(i, k, 1 - x, 1).start()
    for i in range(n_y):
        first(i).wait_send()
        second(i).wait()
    for i in range(n_x):
        over_y(i).wait_send()
        over_x(i, x).wait_send()
        over_core(i, k, x, 0).wait_send()
        over_core(i, k, 1 - x, 1).wait_send()
        over_core(i, 1 - k, x, 0).wait_recv()
        over_core(i, 1 - k, 1 - x, 1).wait_recv()


def forward_call(tok, gains, wt, scale_col, first_key, weights, n_x):
    n_w = len(weights)
    rows, width = tok.shape
    ur = 2 * rows

    def out(dtype, *shape):
        return jax.ShapeDtypeStruct((UNITS, *shape), dtype)

    kept = [
        out(BF, ur, width), out(F32, HD, ur), out(F32, 1, ur), out(BF, HD, ur), out(BF, ur, HD),
        out(BF, HD, ur), out(BF, ur, HD), out(BF, ur, HD), out(F32, HD, ur),
    ]
    shapes = [
        jax.ShapeDtypeStruct((gains.shape[0], 2 * gains.shape[1]), F32),
        jax.ShapeDtypeStruct((H, HD, rows), BF),
        *kept,
    ] + [jax.ShapeDtypeStruct(w.shape, BF) for w in weights]
    return pl.pallas_call(
        functools.partial(forward_kernel, n_w, n_x),
        out_shape=shapes,
        in_specs=[VMEM] * 5 + [ANY] * n_w,
        out_specs=[VMEM] + [ANY] * (10 + n_w),
        scratch_shapes=[
            pltpu.VMEM((wt.shape[0], 2 * wt.shape[1]), BF),
            pltpu.VMEM(gains.shape, BF),
            pltpu.VMEM(gains.shape, BF),
            pltpu.VMEM((UNITS, HD, ur), BF),
            pltpu.VMEM((UNITS, HD, ur), BF),
            pltpu.VMEM((UNITS, 1, ur), F32),
            pltpu.VMEM((UNITS, 1, ur), F32),
            pltpu.VMEM((UNITS, HD, ur), F32),
            *[pltpu.VMEM(a.shape, a.dtype) for a in kept],
            pltpu.SemaphoreType.DMA((26,)),
            pltpu.SemaphoreType.DMA((H,)),
            pltpu.SemaphoreType.DMA((H,)),
            pltpu.SemaphoreType.DMA((H,)),
            pltpu.SemaphoreType.DMA((2 * n_w,)),
            pltpu.SemaphoreType.DMA((2 * n_w,)),
            pltpu.SemaphoreType.DMA((max(1, n_x), 4)),
            pltpu.SemaphoreType.DMA((max(1, n_x), 4)),
            pltpu.SemaphoreType.DMA((4,)),
            pltpu.SemaphoreType.DMA((2,)),
            pltpu.SemaphoreType.DMA((9, UNITS)),
        ],
        compiler_params=pltpu.CompilerParams(
            collective_id=1, has_side_effects=True, vmem_limit_bytes=56 * 2**20
        ),
        name="forward",
    )(tok, gains, wt, scale_col, first_key, *weights)


def half_rows(start, size, align):
    return pl.ds(pl.multiple_of(start, align), size)


def tail_kernel(*rest):
    own = rest[:3]
    n_w = len(PULL)
    held = rest[3 : 6 - n_w]
    at = 6 - n_w
    mats = rest[at : at + 6]
    attn_ref, cot_ref, tok_ref, gain_ref, scale_ref, first_ref = rest[at + 6 : at + 12]
    kept = rest[at + 12 : at + 21]
    at += 21
    all_ref, tg_ref, sums_ref, out_ref = rest[at : at + 4]
    pulled = rest[at + 4 : at + 4 + n_w]
    (
        h_ref, o_ref, lse_ref, qt_ref, q_ref, kt_ref, k_ref, v_ref, raw_ref,
        g_in, g_sc, delta_sc, scale_sc, dk_sc, dv_sc, d_sc, got, dw_sc, dw_out, dw_got, piece,
        ws, r0, ra, rb, r2, rz, small_out, small_in, small_z,
        gsend, grecv, qsend, qrecv, ksend, krecv, dsend, drecv, psend, precv,
        asend, arecv, vsend, vrecv, lsem, wsem, ksem, wssem, wrsem,
        gt_ref, gr_ref, hid_ref, gip_ref, act_ref, g2_ref, msem,
    ) = rest[at + 4 + n_w :]
    me, fs, z, x, k = place()
    sib, xn, yn = (me + 1 - 2 * k, fs), (me + 2 - 4 * x, fs), (me, 1 - fs)
    up, dn = (me + 4, fs), (me - 4, fs)
    units, rows = h_ref.shape[:2]
    block = rows // 2
    n_g = 3
    part, width = ws.shape[2:]
    so, s1 = ws.at[:, pl.ds(0, 2)], ws.at[:, pl.ds(2, 2)]
    cols = width // 2
    bar = pltpu.get_barrier_semaphore()
    for i in range(1, H):
        signal((lax.rem(me + i, H), fs))
    signal(yn)
    dq_sc = o_ref
    here = (h_ref, o_ref, lse_ref, qt_ref, q_ref, kt_ref, k_ref, v_ref, raw_ref)
    back = [pltpu.make_async_copy(kept[i], here[i], ksem.at[i]) for i in range(9)]
    for c in back[1:]:
        c.start()
    back[0].start()
    loads = []
    for n in range(3):
        for o in range(2):
            for f in range(2):
                to = ws.at[n, 2 * (fs if o == 0 else 1 - fs) + f]
                src = mats[2 * n + o].at[pl.ds(f * part, part)]
                loads.append(pltpu.make_async_copy(src, to, msem.at[n, 2 * o + f]))
                loads[-1].start()

    def mat(n):
        return ws[n].reshape(4 * part, width)

    pl.semaphore_wait(bar, H)
    first, second = weight_pull([own[w] for w in PULL], pulled, k, fs, me, wssem, wrsem)
    for i in range(EARLY):
        first(i).start()
    gain = gain_ref[1:2, :]
    for c in loads[:4]:
        c.wait()
    resid = tok_ref[...].astype(F32) + dot(attn_ref[...], mat(0), TN)
    scale_two = lax.rsqrt(jnp.mean(resid * resid, axis=-1, keepdims=True) + epsilon)
    normed_two = resid * scale_two
    hidden32 = normed_two * gain
    for c in loads[4:8]:
        c.wait()
    pre = dot(hidden32.astype(BF), mat(1))
    sig = 1.0 / (1.0 + jnp.exp(-pre))
    active32 = pre * sig
    for c in loads[8:]:
        c.wait()
    grad_active = dot(cot_ref[...], mat(2), NT)
    gip_ref[...] = (grad_active * sig * (1.0 + pre * (1.0 - sig))).astype(BF)
    grad_two = dot(gip_ref[...], mat(1), NT)
    g2_ref[...] = jnp.sum(grad_two * normed_two, axis=0, keepdims=True)
    g = grad_two * gain
    gr_ref[...] = (
        cot_ref[...].astype(F32)
        + scale_two * (g - normed_two * jnp.mean(g * normed_two, axis=-1, keepdims=True))
    ).astype(BF)
    gt_ref[...] = dot(mat(0), gr_ref[...], NT).astype(BF)

    def lanes(b):
        return half_rows(lax.rem(b, 2) * block, block, 128)

    def g_copy(b, t):
        return remote(
            gt_ref.at[half_rows(b * HD, HD, 16)], g_in.at[t // 2, :, lanes(t)],
            gsend.at[b], grecv.at[t], (b, fs),
        )

    def g_start(n, c):
        g_copy(lax.rem(me + n, H), me).start()
        return c

    lax.fori_loop(1, H, g_start, 0)
    g_here = pltpu.make_async_copy(
        gt_ref.at[half_rows(me * HD, HD, 16)], g_in.at[me // 2, :, lanes(me)], lsem.at[0]
    )
    g_here.start()
    hid_ref[...] = hidden32.T.astype(BF)
    act_ref[...] = active32.T.astype(BF)
    out_ref[...] = (resid + dot(active32.astype(BF), mat(2))).astype(BF)

    def theirs(g):
        return remote(so.at[g], r0.at[g], dsend.at[g], drecv.at[g], sib)

    def dense_rows(g, start):
        r = half_rows(start, part, 64)
        if g == 0:
            return dot(attn_ref[r, :], gr_ref[...])
        a, b = ((hid_ref, gip_ref), (act_ref, cot_ref))[g - 1]
        return dot(a[r, :], b[...])

    for g in range(n_g):
        for f in range(2):
            so[g, f] = dense_rows(g, f * 2 * part + (1 - k) * part).astype(BF)
        theirs(g).start()
    for g in range(n_g):
        for f in range(2):
            s1[g, f] = dense_rows(g, f * 2 * part + k * part).astype(BF)

    top, bottom = slice(0, part // 2), slice(part // 2, part)
    x_here = half_rows(x * cols, cols, 128)
    x_there = half_rows((1 - x) * cols, cols, 128)

    def stage(g, i):
        ends = (
            (s1.at[g, 1 - fs, top, :], ra.at[g], yn),
            (s1.at[g, :, bottom, x_there], rb.at[g], xn),
            (s1.at[g, fs, top, x_there], r2.at[g, top], xn),
            (s1.at[g, 1 - fs, bottom, x_here], r2.at[g, bottom], yn),
        )[i]
        return remote(ends[0], ends[1], psend.at[i, g], precv.at[i, g], ends[2])

    slab = part // 4

    zb = lax.rem(z, 2)
    near, far = (me + 4 - 8 * zb, fs), (me + 8 - 16 * (z // 2), fs)

    def z_rows(t):
        return s1.at[:, fs, half_rows(t * slab, slab, 16), x_here]

    def z_near(i):
        return remote(z_rows(1 - zb + 2 * i), rz.at[i], psend.at[4, i], precv.at[4, i], near)

    def z_far():
        return remote(
            z_rows(zb + 2 * (1 - z // 2)), rz.at[2], psend.at[4, 2], precv.at[4, 2], far
        )

    for g in range(n_g):
        theirs(g).wait()

        def add(i, c, g=g):
            r = half_rows(i * 32, 32, 32)
            for f in range(2):
                s1[g, f, r, :] += r0[g, f, r, :]
            return c

        lax.fori_loop(0, part // 32, add, 0)
        stage(g, 0).start()
        stage(g, 1).start()

    loads = []
    for w in range(3):
        for f in range(2):
            loads.append(
                pltpu.make_async_copy(own[w].at[pl.ds(f * part, part)], r0.at[w, f], wsem.at[w * 2 + f])
            )
            loads[-1].start()


    def load_other(src, w, f):
        return pltpu.make_async_copy(
            src.at[pl.ds(f * part, part)], so.at[w, f], wsem.at[6 + w * 2 + f]
        )

    for i, w in enumerate(w for w in range(3) if w not in PULL):
        for f in range(2):
            loads.append(load_other(held[i], w, f))
            loads[-1].start()

    def after_one():
        for g in range(n_g):
            stage(g, 0).wait()
            stage(g, 1).wait()

            def add(i, c, g=g):
                r = half_rows(i * 32, 32, 32)
                s1[g, fs, r, :] += ra[g, r, :]
                low = half_rows(part // 2 + i * 32, 32, 32)
                for f in range(2):
                    s1[g, f, low, x_here] += rb[g, f, r, :]
                return c

            lax.fori_loop(0, part // 64, add, 0)
            stage(g, 2).start()
            stage(g, 3).start()
        for i in range(EARLY, n_w):
            first(i).start()

    def after_two():
        for g in range(n_g):
            stage(g, 2).wait()
            stage(g, 3).wait()

            def add(i, c, g=g):
                r = half_rows(i * 32, 32, 32)
                s1[g, fs, r, x_here] += r2[g, r, :]
                return c

            lax.fori_loop(0, part // 32, add, 0)
        for i in range(2):
            z_near(i).start()

    def after_near():
        for i in range(2):
            z_near(i).wait()
            r = half_rows((zb + 2 * i) * slab, slab, 16)
            for g in range(n_g):
                s1[g, fs, r, x_here] += rz[i, g]
        z_far().start()

    def after_far():
        z_far().wait()
        r = half_rows(z * slab, slab, 16)
        for g in range(n_g):
            piece[g] = s1[g, fs, r, x_here] + rz[2, g]

    scale_sc[...] = jnp.zeros_like(scale_sc)
    dw_sc[...] = jnp.zeros_like(dw_sc)

    def g_taken(n, c):
        b = lax.rem(me + n, H)
        g_copy(b, b).wait()
        return c

    for c in back[1:]:
        c.wait()
    g_here.wait()
    lax.fori_loop(1, H, g_taken, 0)

    def prepare(i, c):
        g = g_in[i].astype(F32)
        g_sc[i] = g.T.astype(BF)
        delta_sc[i] = jnp.sum(g * o_ref[i], axis=0, keepdims=True)
        dq_sc[i] = jnp.zeros((HD, rows), F32)
        return c

    lax.fori_loop(0, units, prepare, 0)

    back[0].wait()

    def pair(masked, j, i):
        s = dot(k_ref[j], qt_ref[i])
        if masked:
            s = jnp.where(visible(j, i, rows, first_ref[i]), s, neg_big)
        p = jnp.exp2(s - lse_ref[i])
        dv_sc[...] += dot(p.astype(BF), g_sc[i])
        dp = dot(v_ref[j], g_in[i])
        ds = (p * (dp - delta_sc[i])).astype(BF)
        dk_sc[...] += dot(ds, q_ref[i])
        dq_sc[i] += dot(kt_ref[j], ds)

    def out(b, lo, n):
        return d_sc.at[b // 2, pl.ds(lo, n), :, lanes(b)]

    def to(t, lo, n):
        return got.at[pl.ds(lo, n), half_rows(t * HD, HD, 16)]

    def kv_copy(b, t):
        return remote(out(b, 1, 2), to(t, 1, 2), ksend.at[b], krecv.at[t], (b, fs))

    def q_copy(b, t):
        return remote(out(b, 0, 1), to(t, 0, 1), qsend.at[b], qrecv.at[t], (b, fs))

    kv_here = pltpu.make_async_copy(out(me, 1, 2), to(me, 1, 2), lsem.at[1])
    q_here = pltpu.make_async_copy(out(me, 0, 1), to(me, 0, 1), lsem.at[2])

    def column(n, c):
        j = lax.rem(me // 2 + n, units)
        dk_sc[...] = jnp.zeros_like(dk_sc)
        dv_sc[...] = jnp.zeros_like(dv_sc)
        pair(True, j, j)

        def plain(i, c2):
            pair(False, j, i)
            return c2

        def edge(i, c2):
            pair(True, j, i)
            return c2

        end = jnp.where(j == 0, 1, units - 1)
        lax.fori_loop(j + 1, end, plain, 0)
        lax.fori_loop(jnp.maximum(j + 1, end), units, edge, 0)
        d_sc[j, 1] = dk_sc[...].T.astype(BF)
        d_sc[j, 2] = dv_sc[...].T.astype(BF)

        def send(e, c2):
            b = 2 * j + e

            @pl.when(b != me)
            def _():
                kv_copy(b, me).start()

            @pl.when(b == me)
            def _():
                kv_here.start()

            return c2

        lax.fori_loop(0, 2, send, 0)
        for e in range(2):
            dw_sc[1 + e] += dot(d_sc[j, 1 + e], h_ref[j])

        @pl.when(n == ONE_AT)
        def _():
            after_one()

        @pl.when(n == TWO_AT)
        def _():
            after_two()

        return c

    lax.fori_loop(0, units, column, 0)
    half = dw_out.shape[2]

    def dw_copy(n, lo, size):
        return remote(
            dw_out.at[pl.ds(lo, size)], dw_got.at[pl.ds(lo, size)], vsend.at[6 + n], vrecv.at[6 + n], yn
        )

    def dw_send(n, lo, size):
        away = half_rows((1 - fs) * half, half, 128)
        dw_out[lo : lo + size] = dw_sc[lo : lo + size, :, away].astype(BF)
        dw_copy(n, lo, size).start()

    def dw_take(n, lo, size):
        dw_copy(n, lo, size).wait()
        keep = half_rows(fs * half, half, 128)
        total = dw_sc[lo : lo + size, :, keep] + dw_got[lo : lo + size].astype(F32)
        piece[3 + lo : 3 + lo + size] = total.astype(BF)

    dw_send(0, 1, 2)

    def queries(n, c):
        i = lax.rem(me // 2 + n, units)
        dq = dq_sc[i]
        scale_sc[...] += dq * raw_ref[i]
        d_sc[i, 0] = (dq * scale_ref[...]).astype(BF)

        def send(e, c2):
            b = 2 * i + e

            @pl.when(b != me)
            def _():
                q_copy(b, me).start()

            @pl.when(b == me)
            def _():
                q_here.start()

            return c2

        lax.fori_loop(0, 2, send, 0)
        return c

    lax.fori_loop(0, units, queries, 0)
    def query_weight(i, c):
        dw_sc[0] += dot(d_sc[i, 0], h_ref[i])
        return c

    lax.fori_loop(0, units, query_weight, 0)
    dw_send(1, 0, 1)
    small_out[...] = jnp.zeros_like(small_out)
    small_out[1:2, :] = g2_ref[...]
    small_out[2:3, :HD] = jnp.sum(scale_sc[...].T, axis=0, keepdims=True)

    spans = (pl.ds(0, 3), pl.ds(4, 2), pl.ds(3, 1))

    def cp(p, s, t, si, mine=False):
        here = all_ref.at[s, spans[p]]
        return remote(piece.at[spans[p]] if mine else here, here, asend.at[p, si], arecv.at[p, s], t)

    def keep(p):
        return pltpu.make_async_copy(
            piece.at[spans[p]], all_ref.at[me, spans[p]], lsem.at[3 + p]
        )

    def begin(p):
        keep(p).start()
        cp(p, me, xn, 0, True).start()

        @pl.when(z < 3)
        def _():
            cp(p, me, up, 1, True).start()

        @pl.when(z > 0)
        def _():
            cp(p, me, dn, 2, True).start()

        cp(p, me, sib, 3, True).start()

    def column_arrival(p, d):
        a = 4 + (d - 1) * 6

        @pl.when(z >= d)
        def _():
            s = me - 4 * d
            cp(p, s, dn, a).wait_recv()

            @pl.when(z < 3)
            def _():
                cp(p, s, up, a).start()

            cp(p, s, xn, a + 1).start()
            cp(p, s, sib, a + 2).start()

        @pl.when(z + d <= 3)
        def _():
            s = me + 4 * d
            cp(p, s, up, a + 3).wait_recv()

            @pl.when(z > 0)
            def _():
                cp(p, s, dn, a + 3).start()

            cp(p, s, xn, a + 4).start()
            cp(p, s, sib, a + 5).start()

    xo = me + 2 - 4 * x

    def across_arrival(p, d):
        @pl.when(z >= d)
        def _():
            s = xo - 4 * d
            cp(p, s, xn, 0).wait_recv()
            cp(p, s, sib, 22 + z - d).start()

        if d > 0:

            @pl.when(z + d <= 3)
            def _():
                s = xo + 4 * d
                cp(p, s, xn, 0).wait_recv()
                cp(p, s, sib, 22 + z + d).start()


    def kv_taken(n, c):
        b = lax.rem(me + n, H)
        kv_copy(b, b).wait()
        return c

    def q_taken(n, c):
        b = lax.rem(me + n, H)
        q_copy(b, b).wait()
        return c

    def input_grad(w, start):
        for r, m in ((fs, r0), (1 - fs, so)):
            for f in range(2):
                side = half_rows(r * block, block, 128)
                term = dot(m[w, f], got[w]).reshape(units // 2, HD, block)
                span = pl.ds(f * (units // 2), units // 2)
                if start:
                    raw_ref[span, :, side] = term
                else:
                    raw_ref[span, :, side] += term

    def pass_on(i):
        first(i).wait_recv()
        second(i).start()

    def load_pulled(i):
        second(i).wait()
        first(i).wait_send()
        late = [load_other(pulled[i], PULL[i], f) for f in range(2)]
        for c in late:
            c.start()
        for c in late:
            c.wait()

    def v_copy(i, t):
        n = (0, 1, 8)[i]
        return remote(small_out, small_in.at[i], vsend.at[n], vrecv.at[n], t)

    def v_column(d):
        t = lax.rem(z + d, 4)
        return t, remote(
            small_z.at[z], small_z.at[z], vsend.at[2 + d], vrecv.at[2 + z], (me + 4 * (t - z), fs)
        )

    dw_take(0, 1, 2)
    begin(1)
    after_near()
    dw_take(1, 0, 1)
    begin(2)
    pass_on(0)
    column_arrival(1, 1)
    column_arrival(2, 1)
    lax.fori_loop(1, H, kv_taken, 0)
    kv_here.wait()
    for c in loads:
        c.wait()
    input_grad(2, True)
    load_pulled(0)
    input_grad(1, False)
    across_arrival(1, 0)
    across_arrival(2, 0)
    after_far()
    begin(0)
    column_arrival(1, 2)
    column_arrival(2, 2)
    column_arrival(0, 1)
    across_arrival(0, 0)
    across_arrival(1, 1)
    across_arrival(2, 1)
    pass_on(1)
    lax.fori_loop(1, H, q_taken, 0)
    q_here.wait()
    load_pulled(1)
    input_grad(0, False)
    column_arrival(1, 3)
    column_arrival(2, 3)
    grad_hidden = jnp.concatenate(
        [raw_ref[:, :, r * block : (r + 1) * block].reshape(width // 2, block).T for r in range(2)],
        axis=1,
    )
    tokens = tok_ref[...].astype(F32)
    scale = lax.rsqrt(jnp.mean(tokens * tokens, axis=-1, keepdims=True) + epsilon)
    normed = tokens * scale
    small_out[0:1, :] = jnp.sum(grad_hidden * normed, axis=0, keepdims=True)
    v_copy(0, sib).start()
    column_arrival(0, 2)
    across_arrival(1, 2)
    across_arrival(2, 2)
    e = grad_hidden * gain_ref[0:1, :]
    tg_ref[...] = (
        gr_ref[...].astype(F32) + scale * (e - normed * jnp.mean(e * normed, axis=-1, keepdims=True))
    ).astype(BF)
    v_copy(0, sib).wait()
    small_out[...] += small_in[0]
    v_copy(1, xn).start()
    across_arrival(0, 1)
    v_copy(1, xn).wait()
    small_z[z] = small_out[...] + small_in[1]
    for d in range(1, 4):
        v_column(d)[1].start()
    column_arrival(0, 3)
    across_arrival(1, 3)
    across_arrival(2, 3)
    for d in range(1, 4):
        t, c = v_column(d)
        c.wait_send()
        remote(small_z.at[t], small_z.at[t], vsend.at[2 + d], vrecv.at[2 + t], xn).wait_recv()
    small_out[...] = (small_z[0] + small_z[1]) + (small_z[2] + small_z[3])
    v_copy(2, yn).start()
    across_arrival(0, 2)
    v_copy(2, yn).wait()
    sums_ref[...] = small_out[...] + small_in[2]
    across_arrival(0, 3)

    for p in (1, 2, 0):

        def from_sib(n, c, p=p):
            cp(p, n * 2 + 1 - k, sib, 0).wait_recv()
            return c

        lax.fori_loop(0, UNITS, from_sib, 0)
        keep(p).wait()
        cp(p, me, xn, 0, True).wait_send()

        @pl.when(z < 3)
        def _(p=p):
            cp(p, me, up, 1, True).wait_send()

        @pl.when(z > 0)
        def _(p=p):
            cp(p, me, dn, 2, True).wait_send()

        cp(p, me, sib, 3, True).wait_send()

        def sent(d, c, p=p):
            a = 4 + (d - 1) * 6

            @pl.when(z >= d)
            def _():
                s = me - 4 * d

                @pl.when(z < 3)
                def _():
                    cp(p, s, up, a).wait_send()

                cp(p, s, xn, a + 1).wait_send()
                cp(p, s, sib, a + 2).wait_send()

            @pl.when(z + d <= 3)
            def _():
                s = me + 4 * d

                @pl.when(z > 0)
                def _():
                    cp(p, s, dn, a + 3).wait_send()

                cp(p, s, xn, a + 4).wait_send()
                cp(p, s, sib, a + 5).wait_send()

            return c

        lax.fori_loop(1, 4, sent, 0)

        def sent_across(zz, c, p=p):
            cp(p, xo + 4 * (zz - z), sib, 22 + zz).wait_send()
            return c

        lax.fori_loop(0, 4, sent_across, 0)


EARLY = 1
ONE_AT = 4
TWO_AT = 7


def tail_call(own, held, mats, vm, kept):
    n_w = len(PULL)
    rows, width = vm[2].shape
    n, ur = kept[0].shape[:2]
    half = width // 2
    part = width // 4
    sem = pltpu.SemaphoreType.DMA
    return pl.pallas_call(
        tail_kernel,
        out_shape=[
            jax.ShapeDtypeStruct((H, 6, part // 4, half), BF),
            jax.ShapeDtypeStruct((rows, width), BF),
            jax.ShapeDtypeStruct((8, width), F32),
            jax.ShapeDtypeStruct((rows, width), BF),
        ]
        + [jax.ShapeDtypeStruct(own[0].shape, BF)] * n_w,
        in_specs=[ANY] * (9 + len(held)) + [VMEM] * len(vm) + [ANY] * len(kept),
        out_specs=[ANY, VMEM, VMEM, VMEM] + [ANY] * n_w,
        scratch_shapes=[
            *[pltpu.VMEM(a.shape, a.dtype) for a in kept],
            pltpu.VMEM((n, HD, ur), BF),
            pltpu.VMEM((n, ur, HD), BF),
            pltpu.VMEM((n, 1, ur), F32),
            pltpu.VMEM((HD, ur), F32),
            pltpu.VMEM((ur, HD), F32),
            pltpu.VMEM((ur, HD), F32),
            pltpu.VMEM((n, 3, HD, ur), BF),
            pltpu.VMEM((3, H * HD, rows), BF),
            pltpu.VMEM((3, HD, width), F32),
            pltpu.VMEM((3, HD, half), BF),
            pltpu.VMEM((3, HD, half), BF),
            pltpu.VMEM((6, part // 4, half), BF),
            pltpu.VMEM((3, 4, part, width), BF),
            pltpu.VMEM((3, 2, part, width), BF),
            pltpu.VMEM((3, part // 2, width), BF),
            pltpu.VMEM((3, 2, part // 2, half), BF),
            pltpu.VMEM((3, part, half), BF),
            pltpu.VMEM((3, 3, part // 4, half), BF),
            pltpu.VMEM((8, width), F32),
            pltpu.VMEM((3, 8, width), F32),
            pltpu.VMEM((4, 8, width), F32),
            sem((H,)), sem((H,)), sem((H,)), sem((H,)), sem((H,)), sem((H,)),
            sem((3,)), sem((3,)), sem((5, 4)), sem((5, 4)),
            sem((3, 26)), sem((3, H)), sem((9,)), sem((9,)), sem((6,)), sem((12,)),
            sem((9,)), sem((max(1, 2 * n_w),)), sem((max(1, 2 * n_w),)),
            pltpu.VMEM((H * HD, rows), BF), pltpu.VMEM((rows, width), BF), pltpu.VMEM((width, rows), BF),
            pltpu.VMEM((rows, width), BF), pltpu.VMEM((width, rows), BF), pltpu.VMEM((1, width), F32),
            sem((3, 4)),
        ],
        compiler_params=pltpu.CompilerParams(
            collective_id=2, has_side_effects=True, vmem_limit_bytes=63 * 2**20
        ),
        name="tail",
    )(*own, *held, *mats, *vm, *kept)


def spread_kernel(dense_ref, heads_ref, *outs):
    slab, cols = dense_ref.shape[-2:]
    n, _, hd, _ = heads_ref.shape
    for w in range(3):

        @pl.when(pl.program_id(0) // 2 == w)
        def _(w=w):
            for zz in range(4):
                for xx in range(2):
                    outs[w][zz * slab : (zz + 1) * slab, xx * cols : (xx + 1) * cols] = dense_ref[
                        zz, xx, 0, 0
                    ].astype(F32)
            outs[3 + w][...] = heads_ref[...].reshape(n * hd, cols).astype(F32).T


def spread_call(pieces):
    n, parts, slab, cols = pieces.shape
    split = pieces.reshape(4, 2, 2, parts, slab, cols)

    def half(w):
        return lambda i: jnp.clip(i - 2 * w, 0, 1)

    def dense_spec(w):
        return pl.BlockSpec((4 * slab, 2 * cols), lambda i: (half(w)(i), 0))

    def heads_spec(w):
        return pl.BlockSpec((cols, n * slab // 2), lambda i: (0, half(w)(i)))

    return pl.pallas_call(
        spread_kernel,
        grid=(6,),
        out_shape=[jax.ShapeDtypeStruct((8 * slab, 2 * cols), F32)] * 3
        + [jax.ShapeDtypeStruct((cols, n * slab), F32)] * 3,
        in_specs=[
            pl.BlockSpec((4, 2, 1, 1, slab, cols), lambda i: (0, 0, lax.rem(i, 2), i // 2, 0, 0)),
            pl.BlockSpec((n // 2, 1, slab, cols), lambda i: (lax.rem(i, 2), 3 + i // 2, 0, 0)),
        ],
        out_specs=[dense_spec(w) for w in range(3)] + [heads_spec(w) for w in range(3)],
        compiler_params=pltpu.CompilerParams(vmem_limit_bytes=48 * 2**20),
        name="spread",
    )(split, pieces)


def fast_local(
    tokens, query_weight, key_weight, value_weight, out_weight, inner_weight, outer_weight,
    attn_gain, mlp_gain, query_scale, doc_starts, cotangent,
):
    me, fs = lax.axis_index("ctx"), lax.axis_index("fs")
    rows, width = tokens.shape[1:]
    tok = tokens[0]
    cot = cotangent[0]

    def head_columns(w):
        return lax.dynamic_slice(w, (0, me * HD), (w.shape[0], HD)).T

    wt = jnp.concatenate([head_columns(w) for w in (query_weight, key_weight, value_weight)], axis=0)
    gains = jnp.stack([attn_gain, mlp_gain])
    positions = jnp.arange(H * rows, dtype=jnp.int32)
    starts = doc_starts[0]
    first_key = jnp.max(
        jnp.where(starts[None, :] <= positions[:, None], starts[None, :], 0), axis=1
    ).reshape(UNITS, 1, 2 * rows)
    scale_col = (query_scale / math.sqrt(HD))[:, None]

    (
        gain_full, attn_t, h_all, o32, lse, qt, q, kt, k, v, raw,
        out_o, inner_o, outer_o, value_o,
    ) = forward_call(
        tok, gains, wt, scale_col, first_key,
        (out_weight, inner_weight, outer_weight, value_weight), N_SHARED,
    )
    attn_t = attn_t.reshape(width, rows)

    half = width // 2
    pieces, grad_tokens, sums, result, *_ = tail_call(
        (query_weight, key_weight, value_weight), (value_o,),
        (out_weight, out_o, inner_weight, inner_o, outer_weight, outer_o),
        (attn_t, cot, tok, gain_full, scale_col, first_key),
        (h_all, o32, lse, qt, q, kt, k, v, raw),
    )
    out_g, inner_g, outer_g, query_g, key_g, value_g = spread_call(pieces)
    gain_sums = lax.dynamic_slice(sums, (0, fs * half), (2, half))
    return (
        result[None], grad_tokens[None], query_g, key_g, value_g, out_g, inner_g, outer_g,
        gain_sums[0], gain_sums[1], sums[2, :HD] / math.sqrt(HD),
    )


def solution(mesh):
    placed = (
        P("fs", "ctx", None),
        P("fs", None),
        P("fs", None),
        P("fs", None),
        P("fs", None),
        P("fs", None),
        P("fs", None),
        P("fs"),
        P("fs"),
        P(),
        P("fs", None),
        P("fs", "ctx", None),
    )
    return jax.shard_map(
        fast_local if fast_fits(mesh) else general_local,
        mesh=mesh,
        in_specs=placed,
        out_specs=(
            P("fs", "ctx", None),
            P("fs", "ctx", None),
            P("fs", None),
            P("fs", None),
            P("fs", None),
            P("fs", None),
            P("fs", None),
            P("fs", None),
            P("fs"),
            P("fs"),
            P(),
        ),
        check_vma=False,
    )
```

```python
import functools
import math

import jax
import jax.numpy as jnp
from jax import lax
from jax.experimental import pallas as pl
from jax.experimental.pallas import tpu as pltpu
from jax.sharding import PartitionSpec as P

H = 16
HD = 80


epsilon = 1e-06
neg_big = -1e30


def passed_along(block, axis, distance):
    devices = range(lax.axis_size(axis))
    route = [((i - distance) % len(devices), i) for i in devices]
    return lax.ppermute(block, axis, route)


def shifted(value, axis, steps):
    count = lax.axis_size(axis)
    leading, last = (max(0, -steps), min(count, count - steps))
    return lax.ppermute(value, axis, [(source, source + steps) for source in range(leading, last)])


def rms_scale(values_in):
    return lax.rsqrt(jnp.mean(values_in * values_in, axis=-1, keepdims=True) + epsilon)


def norm_back(grad_normed, normed, scale_rows):
    inner_mean = jnp.mean(grad_normed * normed, axis=-1, keepdims=True)
    return scale_rows * (grad_normed - normed * inner_mean)


def segment_of(positions, starts_row):
    return jnp.sum((starts_row[None, :] <= positions[:, None]).astype(jnp.int32), axis=1) - 1


def block_mask(query_pos, query_seg, key_pos, key_seg):
    return (key_pos[None, :] <= query_pos[:, None]) & (key_seg[None, :] == query_seg[:, None])


def scores_of(query_block, key_block):
    return jnp.einsum("qhd,khd->hqk", query_block, key_block, preferred_element_type=jnp.float32)


def pass_grads(grad_key_acc, grad_value_acc):
    return (
        passed_along(grad_key_acc.astype(jnp.bfloat16), "ctx", 1).astype(grad_key_acc.dtype),
        passed_along(grad_value_acc.astype(jnp.bfloat16), "ctx", 1).astype(grad_value_acc.dtype),
    )


def general_local(
    tokens,
    query_weight,
    key_weight,
    value_weight,
    out_weight,
    inner_weight,
    outer_weight,
    attn_gain,
    mlp_gain,
    query_scale,
    doc_starts,
    cotangent,
):
    row_count = tokens.shape[1]
    model_width = tokens.shape[2]
    ctx_count = lax.axis_size("ctx")
    ctx_place = lax.axis_index("ctx")
    (
        query_full,
        key_full,
        value_full,
        out_full,
        inner_full,
        outer_full,
        attn_gain_full,
        mlp_gain_full,
    ) = (
        lax.all_gather(query_weight, "fs", axis=0, tiled=True),
        lax.all_gather(key_weight, "fs", axis=0, tiled=True),
        lax.all_gather(value_weight, "fs", axis=0, tiled=True),
        lax.all_gather(out_weight, "fs", axis=0, tiled=True),
        lax.all_gather(inner_weight, "fs", axis=0, tiled=True),
        lax.all_gather(outer_weight, "fs", axis=0, tiled=True),
        lax.all_gather(attn_gain, "fs", axis=0, tiled=True),
        lax.all_gather(mlp_gain, "fs", axis=0, tiled=True),
    )
    starts_row = doc_starts[0]
    local_pos = ctx_place * row_count + jnp.arange(row_count, dtype=jnp.int32)
    local_seg = segment_of(local_pos, starts_row)

    def heads_of(flat_block):
        return flat_block.reshape(row_count, H, HD)

    token_rows = tokens[0].astype(jnp.float32)
    scale_one = rms_scale(token_rows)
    normed_one = token_rows * scale_one
    gain_one = attn_gain_full.astype(jnp.float32)
    hidden_one = (normed_one * gain_one).astype(jnp.bfloat16)
    query_raw = jnp.dot(hidden_one, query_full, preferred_element_type=jnp.float32)
    scale_vec = jnp.tile(query_scale, H) / math.sqrt(HD)
    queries = heads_of((query_raw * scale_vec).astype(jnp.bfloat16))
    key_rows = jnp.dot(hidden_one, key_full, preferred_element_type=jnp.float32).astype(
        jnp.bfloat16
    )
    value_rows = jnp.dot(hidden_one, value_full, preferred_element_type=jnp.float32).astype(
        jnp.bfloat16
    )

    def key_info(turn_index):
        source = (ctx_place - turn_index) % ctx_count
        key_pos = source * row_count + jnp.arange(row_count, dtype=jnp.int32)
        return (source, key_pos, segment_of(key_pos, starts_row))

    def keep_state(state_in):
        return state_in

    def attend(softmax_state, key_flat, value_flat, turn_index):
        source, key_pos, key_seg = key_info(turn_index)

        def compute(state_in):
            run_max, run_sum, run_acc = state_in
            key_block = heads_of(key_flat)
            value_block = heads_of(value_flat)
            allowed = block_mask(local_pos, local_seg, key_pos, key_seg)
            scores = jnp.where(allowed[None], scores_of(queries, key_block), neg_big)
            new_max = jnp.maximum(run_max, jnp.max(scores, axis=-1))
            weights = jnp.where(allowed[None], jnp.exp(scores - new_max[..., None]), 0.0)
            factor = jnp.exp(run_max - new_max)
            run_sum = run_sum * factor + jnp.sum(weights, axis=-1)
            run_acc = run_acc * factor[..., None] + jnp.einsum(
                "hqk,khd->hqd",
                weights.astype(jnp.bfloat16),
                value_block,
                preferred_element_type=jnp.float32,
            )
            return (new_max, run_sum, run_acc)

        return lax.cond(source <= ctx_place, compute, keep_state, softmax_state)

    start_state = (
        jnp.full((H, row_count), neg_big, jnp.float32),
        jnp.zeros((H, row_count), jnp.float32),
        jnp.zeros((H, row_count, HD), jnp.float32),
    )
    start_state = attend(start_state, key_rows, value_rows, jnp.int32(0))
    stores = ()

    def forward_turn(turn_index, loop_state):
        key_block, value_block, softmax_state, kept = loop_state
        key_block, value_block = shifted((key_block, value_block), "ctx", 1)
        softmax_state = attend(softmax_state, key_block, value_block, turn_index)
        return (key_block, value_block, softmax_state, kept)

    loop_out = lax.fori_loop(
        1, ctx_count, forward_turn, (key_rows, value_rows, start_state, stores)
    )
    run_max, run_sum, run_acc = loop_out[2]
    stores = loop_out[3]
    log_total = run_max + jnp.log(run_sum)
    attn_heads = run_acc / run_sum[..., None]
    attn_low = (
        jnp.transpose(attn_heads, (1, 0, 2)).reshape(row_count, model_width).astype(jnp.bfloat16)
    )
    resid = token_rows + jnp.dot(attn_low, out_full, preferred_element_type=jnp.float32)
    scale_two = rms_scale(resid)
    normed_two = resid * scale_two
    gain_two = mlp_gain_full.astype(jnp.float32)
    hidden_two = (normed_two * gain_two).astype(jnp.bfloat16)
    inner_pre = jnp.dot(hidden_two, inner_full, preferred_element_type=jnp.float32)
    active = jax.nn.silu(inner_pre).astype(jnp.bfloat16)
    result = resid + jnp.dot(active, outer_full, preferred_element_type=jnp.float32)
    grad_out = cotangent[0]
    grad_active = jnp.dot(grad_out, outer_full.T, preferred_element_type=jnp.float32)
    grad_outer = jnp.dot(active.T, grad_out, preferred_element_type=jnp.float32)
    sigmoid_in = jax.nn.sigmoid(inner_pre)
    grad_inner_pre = (grad_active * sigmoid_in * (1.0 + inner_pre * (1.0 - sigmoid_in))).astype(
        jnp.bfloat16
    )
    grad_inner = jnp.dot(hidden_two.T, grad_inner_pre, preferred_element_type=jnp.float32)
    grad_hidden_two = jnp.dot(grad_inner_pre, inner_full.T, preferred_element_type=jnp.float32)
    grad_gain_two = jnp.sum(grad_hidden_two * normed_two, axis=0)
    grad_resid = grad_out.astype(jnp.float32) + norm_back(
        grad_hidden_two * gain_two, normed_two, scale_two
    )
    grad_resid_low = grad_resid.astype(jnp.bfloat16)
    grad_outw = jnp.dot(attn_low.T, grad_resid_low, preferred_element_type=jnp.float32)
    grad_attended = heads_of(
        jnp.dot(grad_resid_low, out_full.T, preferred_element_type=jnp.float32).astype(jnp.bfloat16)
    )
    row_delta = jnp.einsum("qhd,hqd->hq", grad_attended.astype(jnp.float32), attn_heads)

    def attend_back(grad_parts, key_flat, value_flat, turn_index):
        source, key_pos, key_seg = key_info(turn_index)

        def compute(parts_in):
            grad_query_acc, grad_key_acc, grad_value_acc = parts_in
            key_block = heads_of(key_flat)
            value_block = heads_of(value_flat)
            allowed = block_mask(local_pos, local_seg, key_pos, key_seg)
            scores = scores_of(queries, key_block)
            probabilities = jnp.where(allowed[None], jnp.exp(scores - log_total[..., None]), 0.0)
            grad_value_acc = grad_value_acc + jnp.einsum(
                "hqk,qhd->khd",
                probabilities.astype(jnp.bfloat16),
                grad_attended,
                preferred_element_type=jnp.float32,
            ).reshape(row_count, model_width)
            grad_probs = jnp.einsum(
                "qhd,khd->hqk", grad_attended, value_block, preferred_element_type=jnp.float32
            )
            grad_scores = (probabilities * (grad_probs - row_delta[..., None])).astype(jnp.bfloat16)
            grad_query_acc = grad_query_acc + jnp.einsum(
                "hqk,khd->qhd", grad_scores, key_block, preferred_element_type=jnp.float32
            )
            grad_key_acc = grad_key_acc + jnp.einsum(
                "hqk,qhd->khd", grad_scores, queries, preferred_element_type=jnp.float32
            ).reshape(row_count, model_width)
            return (grad_query_acc, grad_key_acc, grad_value_acc)

        return lax.cond(source <= ctx_place, compute, keep_state, grad_parts)

    def back_compute(turn_index, loop_state):
        key_block, value_block, grad_parts = loop_state
        grad_parts = attend_back(grad_parts, key_block, value_block, turn_index)
        grad_key_acc, grad_value_acc = pass_grads(grad_parts[1], grad_parts[2])
        return (key_block, value_block, (grad_parts[0], grad_key_acc, grad_value_acc))

    def back_turn(turn_index, loop_state):
        key_block, value_block, grad_parts = back_compute(turn_index, loop_state)
        key_block, value_block = shifted((key_block, value_block), "ctx", 1)
        return (key_block, value_block, grad_parts)

    zero_heads = jnp.zeros((row_count, H, HD), jnp.float32)
    zero_flat = jnp.zeros((row_count, model_width), jnp.float32)
    back_state = lax.fori_loop(
        0, ctx_count - 1, back_turn, (key_rows, value_rows, (zero_heads, zero_flat, zero_flat))
    )
    back_state = back_compute(jnp.int32(ctx_count - 1), back_state)
    grad_query_acc, grad_key_acc, grad_value_acc = back_state[2]
    grad_query_flat = grad_query_acc.reshape(row_count, model_width)
    grad_key_low = grad_key_acc.astype(jnp.bfloat16)
    grad_value_low = grad_value_acc.astype(jnp.bfloat16)
    grad_query_raw = (grad_query_flat * scale_vec).astype(jnp.bfloat16)
    grad_scale = jnp.sum(
        (grad_query_flat * query_raw).reshape(row_count, H, HD), axis=(0, 1)
    ) / math.sqrt(HD)
    grad_qw = jnp.dot(hidden_one.T, grad_query_raw, preferred_element_type=jnp.float32)
    grad_kw = jnp.dot(hidden_one.T, grad_key_low, preferred_element_type=jnp.float32)
    grad_vw = jnp.dot(hidden_one.T, grad_value_low, preferred_element_type=jnp.float32)
    grad_hidden_one = (
        jnp.dot(grad_query_raw, query_full.T, preferred_element_type=jnp.float32)
        + jnp.dot(grad_key_low, key_full.T, preferred_element_type=jnp.float32)
        + jnp.dot(grad_value_low, value_full.T, preferred_element_type=jnp.float32)
    )
    grad_gain_one = jnp.sum(grad_hidden_one * normed_one, axis=0)
    grad_tokens = grad_resid_low.astype(jnp.float32) + norm_back(
        grad_hidden_one * gain_one, normed_one, scale_one
    )
    shard_count = lax.axis_size("fs")
    scale_rows = jnp.broadcast_to(grad_scale[None, :], (shard_count, grad_scale.shape[0]))
    shares = (
        lax.psum_scatter(
            grad_qw.astype(jnp.bfloat16), "fs", scatter_dimension=0, tiled=True
        ).astype(jnp.float32),
        lax.psum_scatter(
            grad_kw.astype(jnp.bfloat16), "fs", scatter_dimension=0, tiled=True
        ).astype(jnp.float32),
        lax.psum_scatter(
            grad_vw.astype(jnp.bfloat16), "fs", scatter_dimension=0, tiled=True
        ).astype(jnp.float32),
        lax.psum_scatter(
            grad_outw.astype(jnp.bfloat16), "fs", scatter_dimension=0, tiled=True
        ).astype(jnp.float32),
        lax.psum_scatter(
            grad_inner.astype(jnp.bfloat16), "fs", scatter_dimension=0, tiled=True
        ).astype(jnp.float32),
        lax.psum_scatter(
            grad_outer.astype(jnp.bfloat16), "fs", scatter_dimension=0, tiled=True
        ).astype(jnp.float32),
        lax.psum_scatter(
            grad_gain_one.astype(jnp.bfloat16), "fs", scatter_dimension=0, tiled=True
        ).astype(jnp.float32),
        lax.psum_scatter(
            grad_gain_two.astype(jnp.bfloat16), "fs", scatter_dimension=0, tiled=True
        ).astype(jnp.float32),
        lax.psum_scatter(
            scale_rows.astype(jnp.bfloat16), "fs", scatter_dimension=0, tiled=True
        ).astype(jnp.float32),
    )
    totals = (
        lax.psum(shares[0].astype(jnp.bfloat16), "ctx").astype(jnp.float32),
        lax.psum(shares[1].astype(jnp.bfloat16), "ctx").astype(jnp.float32),
        lax.psum(shares[2].astype(jnp.bfloat16), "ctx").astype(jnp.float32),
        lax.psum(shares[3].astype(jnp.bfloat16), "ctx").astype(jnp.float32),
        lax.psum(shares[4].astype(jnp.bfloat16), "ctx").astype(jnp.float32),
        lax.psum(shares[5].astype(jnp.bfloat16), "ctx").astype(jnp.float32),
        lax.psum(shares[6].astype(jnp.bfloat16), "ctx").astype(jnp.float32),
        lax.psum(shares[7].astype(jnp.bfloat16), "ctx").astype(jnp.float32),
        lax.psum(shares[8].astype(jnp.bfloat16), "ctx").astype(jnp.float32),
    )
    return (
        result[None].astype(jnp.bfloat16),
        grad_tokens[None].astype(jnp.bfloat16),
        totals[0],
        totals[1],
        totals[2],
        totals[3],
        totals[4],
        totals[5],
        totals[6],
        totals[7],
        totals[8][0],
    )


MESH = pl.DeviceIdType.MESH
ANY = pl.BlockSpec(memory_space=pl.ANY)
VMEM = pl.BlockSpec(memory_space=pltpu.VMEM)
BF = jnp.bfloat16
F32 = jnp.float32


def fast_fits(mesh):
    return mesh.shape["ctx"] == H and mesh.shape["fs"] == 2


def remote(src, dst, ssem, rsem, target):
    return pltpu.make_async_remote_copy(
        src_ref=src, dst_ref=dst, send_sem=ssem, recv_sem=rsem, device_id=target, device_id_type=MESH
    )


def signal(target):
    pl.semaphore_signal(
        pltpu.get_barrier_semaphore(), inc=1, device_id=target, device_id_type=MESH
    )


def place():
    me = lax.axis_index("ctx")
    return me, lax.axis_index("fs"), me // 4, lax.rem(me // 2, 2), lax.rem(me, 2)


def dot(a, b, dims=((1,), (0,))):
    return lax.dot_general(a, b, (dims, ((), ())), preferred_element_type=F32)


NT = ((1,), (1,))
TN = ((0,), (0,))


LOG2E = math.log2(math.e)
N_SHARED = 0
PULL = (1, 0)
UNITS = H // 2


def weight_pull(own, other, k, fs, me, ssem, rsem):
    half = own[0].shape[0] // 2
    rows = pl.ds(pl.multiple_of(k * half, 64), half)
    yn = (me, 1 - fs)
    sib = (me + 1 - 2 * k, fs)
    n = len(own)

    def first(i):
        return remote(own[i].at[rows], other[i].at[rows], ssem.at[i], rsem.at[i], yn)

    def second(i):
        return remote(other[i].at[rows], other[i].at[rows], ssem.at[n + i], rsem.at[n + i], sib)

    return first, second


def weight_share(own, other, k, x, fs, me, ssem, rsem):
    quarter = own[0].shape[0] // 4 if own else 32
    yn, sib, xn = (me, 1 - fs), (me + 1 - 2 * k, fs), (me + 2 - 4 * x, fs)

    def rows(c, a):
        return pl.ds(pl.multiple_of((c * 2 + a) * quarter, 32), quarter)

    def over_y(i):
        r = rows(k, x)
        return remote(own[i].at[r], other[i].at[r], ssem.at[i, 0], rsem.at[i, 0], yn)

    def over_x(i, a):
        r = rows(k, a)
        return remote(other[i].at[r], other[i].at[r], ssem.at[i, 1], rsem.at[i, 1], xn)

    def over_core(i, c, a, n):
        r = rows(c, a)
        return remote(other[i].at[r], other[i].at[r], ssem.at[i, 2 + n], rsem.at[i, 2 + n], sib)

    return over_y, over_x, over_core


def visible(j, i, rows, first_key):
    kpos = j * rows + lax.broadcasted_iota(jnp.int32, (rows, rows), 0)
    qpos = i * rows + lax.broadcasted_iota(jnp.int32, (rows, rows), 1)
    return (kpos <= qpos) & (kpos >= first_key)


def forward_kernel(n_w, n_x, tok_ref, gain_ref, wt_ref, scale_ref, first_ref, *rest):
    own = rest[:n_w]
    at = n_w
    gain_full, attn_ref = rest[at : at + 2]
    kept = rest[at + 2 : at + 11]
    other = rest[at + 11 : at + 11 + n_w]
    (
        wt_all, gain_own, gain_other, o_sc, vt_sc, m_sc, l_sc, acc_sc,
        h_all, o32_ref, lse_ref, qt_ref, q_ref, kt_ref, k_ref, v_ref, raw_ref,
        ssem, rsem, osend, orecv, wssem, wrsem, xssem, xrsem, ysem, lsem, ksem,
    ) = rest[at + 11 + n_w :]
    me, fs, z, x, k = place()
    sib, xn, yn = (me + 1 - 2 * k, fs), (me + 2 - 4 * x, fs), (me, 1 - fs)
    up, dn = (me + 4, fs), (me - 4, fs)
    rows = tok_ref.shape[0]
    here = (h_all, o32_ref, lse_ref, qt_ref, q_ref, kt_ref, k_ref, v_ref, raw_ref)

    def keep(i, u):
        return pltpu.make_async_copy(here[i].at[u], kept[i].at[u], ksem.at[i, u])

    unit_rows = 2 * rows
    bar = pltpu.get_barrier_semaphore()
    for i in range(1, H):
        signal((lax.rem(me + i, H), fs))
    signal(yn)
    gain_own[...] = gain_ref[...]
    tokens = tok_ref[...].astype(F32)
    normed = tokens * lax.rsqrt(jnp.mean(tokens * tokens, axis=-1, keepdims=True) + epsilon)
    pl.semaphore_wait(bar, H)

    gain_copy = remote(gain_own, gain_other, ysem.at[0], ysem.at[1], yn)
    gain_copy.start()
    half = wt_ref.shape[1]
    columns = pl.ds(pl.multiple_of(fs * half, 128), half)
    wt_copy = remote(wt_ref, wt_all.at[:, columns], ysem.at[2], ysem.at[3], yn)
    wt_copy.start()
    wt_here = pltpu.make_async_copy(wt_ref, wt_all.at[:, columns], lsem.at[0])
    wt_here.start()
    n_y = n_w - n_x
    first, second = weight_pull(own[:n_y], other[:n_y], k, fs, me, wssem, wrsem)
    over_y, over_x, over_core = weight_share(own[n_y:], other[n_y:], k, x, fs, me, xssem, xrsem)
    gain_copy.wait()
    g_here = gain_own[...].astype(F32)
    g_there = gain_other[...].astype(F32)
    gains = jnp.where(
        fs == 0,
        jnp.concatenate([g_here, g_there], axis=1),
        jnp.concatenate([g_there, g_here], axis=1),
    )
    gain_full[...] = gains
    my_rows = pl.ds(pl.multiple_of(k * rows, rows), rows)
    h_all[me // 2, my_rows, :] = (normed * gains[0:1]).astype(BF)

    def slot(s):
        return h_all.at[s // 2, pl.ds(pl.multiple_of(lax.rem(s, 2) * rows, rows), rows)]

    def cp(s, t, si):
        return remote(slot(s), slot(s), ssem.at[si], rsem.at[s], t)

    cp(me, xn, 0).start()

    @pl.when(z < 3)
    def _():
        cp(me, up, 1).start()

    @pl.when(z > 0)
    def _():
        cp(me, dn, 2).start()

    cp(me, sib, 3).start()
    for i in range(n_y):
        first(i).start()
    for i in range(n_x):
        over_y(i).start()
    wt_here.wait()
    wt_copy.wait()

    def project(u):
        qkv = dot(wt_all[...], h_all[u], NT)
        raw = qkv[:HD]
        raw_ref[u] = raw
        q32 = raw * scale_ref[...]
        qt_ref[u] = (q32 * LOG2E).astype(BF)
        q_ref[u] = q32.T.astype(BF)
        kt = qkv[HD : 2 * HD]
        vt = qkv[2 * HD :]
        kt_ref[u] = kt.astype(BF)
        k_ref[u] = kt.T.astype(BF)
        v_ref[u] = vt.T.astype(BF)
        vt_sc[u] = vt.astype(BF)
        m_sc[u] = jnp.full((1, unit_rows), neg_big, F32)
        l_sc[u] = jnp.zeros((1, unit_rows), F32)
        acc_sc[u] = jnp.zeros((HD, unit_rows), F32)

    def pair(j, i):
        s = dot(k_ref[j], qt_ref[i])
        s = jnp.where(visible(j, i, unit_rows, first_ref[i]), s, neg_big)
        run_max = m_sc[i]
        new_max = jnp.maximum(run_max, jnp.max(s, axis=0, keepdims=True))
        p = jnp.exp2(s - new_max)
        factor = jnp.exp2(run_max - new_max)
        l_sc[i] = l_sc[i] * factor + jnp.sum(p, axis=0, keepdims=True)
        acc_sc[i] = acc_sc[i] * factor + dot(vt_sc[j], p.astype(BF))
        m_sc[i] = new_max

    def when_here(uz, ux):
        return 4 * jnp.maximum(uz - z, z - uz) + 2 * jnp.maximum(ux - x, x - ux) + (uz + 4 - z) // 5

    def process(uz, ux):
        u = uz * 2 + ux
        cp(u * 2 + 1 - k, sib, 0).wait_recv()
        project(u)
        for i in (0, 3, 4, 5, 6, 7, 8):
            keep(i, u).start()
        pair(u, u)
        mine = when_here(uz, ux)

        def earlier(e, c):
            @pl.when(when_here(e // 2, lax.rem(e, 2)) < mine)
            def _():
                pair(jnp.minimum(e, u), jnp.maximum(e, u))

            return c

        lax.fori_loop(0, UNITS, earlier, 0)

    xo = me + 2 - 4 * x

    def column_arrival(d):
        a = 4 + (d - 1) * 6

        @pl.when(z >= d)
        def _():
            s = me - 4 * d
            cp(s, dn, a).wait_recv()

            @pl.when(z < 3)
            def _():
                cp(s, up, a).start()

            cp(s, xn, a + 1).start()
            cp(s, sib, a + 2).start()

        @pl.when(z + d <= 3)
        def _():
            s = me + 4 * d
            cp(s, up, a + 3).wait_recv()

            @pl.when(z > 0)
            def _():
                cp(s, dn, a + 3).start()

            cp(s, xn, a + 4).start()
            cp(s, sib, a + 5).start()

    def across_arrival(d):
        @pl.when(z >= d)
        def _():
            s = xo - 4 * d
            cp(s, xn, 0).wait_recv()
            cp(s, sib, 22 + z - d).start()

        @pl.when((z + d <= 3) & (d > 0))
        def _():
            s = xo + 4 * d
            cp(s, xn, 0).wait_recv()
            cp(s, sib, 22 + z + d).start()

    def step(d, c):
        @pl.when((d >= 1) & (d <= 3))
        def _():
            column_arrival(d)

        @pl.when(d >= 1)
        def _():
            across_arrival(d - 1)

        for i in range(1):

            @pl.when(d == i + 2)
            def _(i=i):
                first(i).wait_recv()
                second(i).start()

        def compute(n, c2):
            across = 1 - n // 2
            dd = d - across
            uz = z + dd * (2 * lax.rem(n, 2) - 1)
            ux = x + across * (1 - 2 * x)
            ok = (dd >= 0) & (dd <= 3) & (uz >= 0) & (uz <= 3)
            ok = ok & ((dd > 0) | (lax.rem(n, 2) == 0))

            @pl.when(ok)
            def _():
                process(uz, ux)

            return c2

        lax.fori_loop(0, 4, compute, 0)
        return c

    lax.fori_loop(0, 5, step, 0)

    def out_copy(b):
        u = b // 2
        lanes = pl.ds(pl.multiple_of(lax.rem(b, 2) * rows, 128), rows)
        return o_sc.at[u, :, lanes]

    def finish(n, c):
        u = lax.rem(me // 2 + n, UNITS)
        out = acc_sc[u] / l_sc[u]
        o32_ref[u] = out
        o_sc[u] = out.astype(BF)
        lse_ref[u] = m_sc[u] + jnp.log2(l_sc[u])
        keep(1, u).start()
        keep(2, u).start()

        def send(e, c2):
            b = u * 2 + e

            @pl.when(b != me)
            def _():
                remote(out_copy(b), attn_ref.at[me], osend.at[b], orecv.at[me], (b, fs)).start()

            @pl.when(b == me)
            def _():
                pltpu.make_async_copy(out_copy(b), attn_ref.at[me], lsem.at[1]).start()

            return c2

        return lax.fori_loop(0, 2, send, c)

    lax.fori_loop(0, UNITS, finish, 0)
    for i in range(1, n_y):
        first(i).wait_recv()
        second(i).start()
    for i in range(n_x):
        over_y(i).wait_recv()
        over_x(i, x).start()
        over_core(i, k, x, 0).start()

    def taken(b, c):
        @pl.when(b != me)
        def _():
            remote(out_copy(b), attn_ref.at[b], osend.at[b], orecv.at[b], (b, fs)).wait()

        return c

    lax.fori_loop(0, H, taken, 0)
    pltpu.make_async_copy(out_copy(me), attn_ref.at[me], lsem.at[1]).wait()

    def all_kept(u, c):
        for i in range(9):
            keep(i, u).wait()
        return c

    lax.fori_loop(0, UNITS, all_kept, 0)
    cp(me, xn, 0).wait_send()

    @pl.when(z < 3)
    def _():
        cp(me, up, 1).wait_send()

    @pl.when(z > 0)
    def _():
        cp(me, dn, 2).wait_send()

    cp(me, sib, 3).wait_send()

    def sent(d, c):
        a = 4 + (d - 1) * 6

        @pl.when(z >= d)
        def _():
            s = me - 4 * d

            @pl.when(z < 3)
            def _():
                cp(s, up, a).wait_send()

            cp(s, xn, a + 1).wait_send()
            cp(s, sib, a + 2).wait_send()

        @pl.when(z + d <= 3)
        def _():
            s = me + 4 * d

            @pl.when(z > 0)
            def _():
                cp(s, dn, a + 3).wait_send()

            cp(s, xn, a + 4).wait_send()
            cp(s, sib, a + 5).wait_send()

        return c

    lax.fori_loop(1, 4, sent, 0)

    def sent_across(zz, c):
        cp(xo + 4 * (zz - z), sib, 22 + zz).wait_send()
        return c

    lax.fori_loop(0, 4, sent_across, 0)
    for i in range(n_x):
        over_x(i, 1 - x).wait_recv()
        over_core(i, k, 1 - x, 1).start()
    for i in range(n_y):
        first(i).wait_send()
        second(i).wait()
    for i in range(n_x):
        over_y(i).wait_send()
        over_x(i, x).wait_send()
        over_core(i, k, x, 0).wait_send()
        over_core(i, k, 1 - x, 1).wait_send()
        over_core(i, 1 - k, x, 0).wait_recv()
        over_core(i, 1 - k, 1 - x, 1).wait_recv()


def forward_call(tok, gains, wt, scale_col, first_key, weights, n_x):
    n_w = len(weights)
    rows, width = tok.shape
    ur = 2 * rows

    def out(dtype, *shape):
        return jax.ShapeDtypeStruct((UNITS, *shape), dtype)

    kept = [
        out(BF, ur, width), out(F32, HD, ur), out(F32, 1, ur), out(BF, HD, ur), out(BF, ur, HD),
        out(BF, HD, ur), out(BF, ur, HD), out(BF, ur, HD), out(F32, HD, ur),
    ]
    shapes = [
        jax.ShapeDtypeStruct((gains.shape[0], 2 * gains.shape[1]), F32),
        jax.ShapeDtypeStruct((H, HD, rows), BF),
        *kept,
    ] + [jax.ShapeDtypeStruct(w.shape, BF) for w in weights]
    return pl.pallas_call(
        functools.partial(forward_kernel, n_w, n_x),
        out_shape=shapes,
        in_specs=[VMEM] * 5 + [ANY] * n_w,
        out_specs=[VMEM] + [ANY] * (10 + n_w),
        scratch_shapes=[
            pltpu.VMEM((wt.shape[0], 2 * wt.shape[1]), BF),
            pltpu.VMEM(gains.shape, BF),
            pltpu.VMEM(gains.shape, BF),
            pltpu.VMEM((UNITS, HD, ur), BF),
            pltpu.VMEM((UNITS, HD, ur), BF),
            pltpu.VMEM((UNITS, 1, ur), F32),
            pltpu.VMEM((UNITS, 1, ur), F32),
            pltpu.VMEM((UNITS, HD, ur), F32),
            *[pltpu.VMEM(a.shape, a.dtype) for a in kept],
            pltpu.SemaphoreType.DMA((26,)),
            pltpu.SemaphoreType.DMA((H,)),
            pltpu.SemaphoreType.DMA((H,)),
            pltpu.SemaphoreType.DMA((H,)),
            pltpu.SemaphoreType.DMA((2 * n_w,)),
            pltpu.SemaphoreType.DMA((2 * n_w,)),
            pltpu.SemaphoreType.DMA((max(1, n_x), 4)),
            pltpu.SemaphoreType.DMA((max(1, n_x), 4)),
            pltpu.SemaphoreType.DMA((4,)),
            pltpu.SemaphoreType.DMA((2,)),
            pltpu.SemaphoreType.DMA((9, UNITS)),
        ],
        compiler_params=pltpu.CompilerParams(
            collective_id=1, has_side_effects=True, vmem_limit_bytes=56 * 2**20
        ),
        name="forward",
    )(tok, gains, wt, scale_col, first_key, *weights)


def half_rows(start, size, align):
    return pl.ds(pl.multiple_of(start, align), size)


def tail_kernel(*rest):
    own = rest[:3]
    n_w = len(PULL)
    held = rest[3 : 6 - n_w]
    at = 6 - n_w
    mats = rest[at : at + 6]
    attn_ref, cot_ref, tok_ref, gain_ref, scale_ref, first_ref = rest[at + 6 : at + 12]
    kept = rest[at + 12 : at + 21]
    at += 21
    all_ref, tg_ref, sums_ref, scale_out, out_ref = rest[at : at + 5]
    pulled = rest[at + 5 : at + 5 + n_w]
    (
        h_ref, o_ref, lse_ref, qt_ref, q_ref, kt_ref, k_ref, v_ref, raw_ref,
        g_in, g_sc, delta_sc, scale_sc, dk_sc, dv_sc, d_sc, got, dw_sc, dw_out, dw_got, piece,
        ws, r0, ra, rb, r2, rz, small_out, small_in, small_z,
        gsend, grecv, qsend, qrecv, ksend, krecv, dsend, drecv, psend, precv,
        asend, arecv, vsend, vrecv, lsem, wsem, ksem, wssem, wrsem,
        gt_ref, gr_ref, hid_ref, gip_ref, act_ref, g2_ref, msem,
    ) = rest[at + 5 + n_w :]
    me, fs, z, x, k = place()
    sib, xn, yn = (me + 1 - 2 * k, fs), (me + 2 - 4 * x, fs), (me, 1 - fs)
    up, dn = (me + 4, fs), (me - 4, fs)
    units, rows = h_ref.shape[:2]
    block = rows // 2
    n_g = 3
    part, width = ws.shape[2:]
    so, s1 = ws.at[:, pl.ds(0, 2)], ws.at[:, pl.ds(2, 2)]
    cols = width // 2
    bar = pltpu.get_barrier_semaphore()
    for i in range(1, H):
        signal((lax.rem(me + i, H), fs))
    signal(yn)
    dq_sc = o_ref
    here = (h_ref, o_ref, lse_ref, qt_ref, q_ref, kt_ref, k_ref, v_ref, raw_ref)
    back = [pltpu.make_async_copy(kept[i], here[i], ksem.at[i]) for i in range(9)]
    for c in back[1:]:
        c.start()
    back[0].start()
    loads = []
    for n in range(3):
        for o in range(2):
            for f in range(2):
                to = ws.at[n, 2 * (fs if o == 0 else 1 - fs) + f]
                src = mats[2 * n + o].at[pl.ds(f * part, part)]
                loads.append(pltpu.make_async_copy(src, to, msem.at[n, 2 * o + f]))
                loads[-1].start()

    def mat(n):
        return ws[n].reshape(4 * part, width)

    pl.semaphore_wait(bar, H)
    first, second = weight_pull([own[w] for w in PULL], pulled, k, fs, me, wssem, wrsem)
    for i in range(EARLY):
        first(i).start()
    gain = gain_ref[1:2, :]
    for c in loads[:4]:
        c.wait()
    resid = tok_ref[...].astype(F32) + dot(attn_ref[...], mat(0), TN)
    scale_two = lax.rsqrt(jnp.mean(resid * resid, axis=-1, keepdims=True) + epsilon)
    normed_two = resid * scale_two
    hidden32 = normed_two * gain
    for c in loads[4:8]:
        c.wait()
    pre = dot(hidden32.astype(BF), mat(1))
    sig = 1.0 / (1.0 + jnp.exp(-pre))
    active32 = pre * sig
    for c in loads[8:]:
        c.wait()
    grad_active = dot(cot_ref[...], mat(2), NT)
    gip_ref[...] = (grad_active * sig * (1.0 + pre * (1.0 - sig))).astype(BF)
    grad_two = dot(gip_ref[...], mat(1), NT)
    g2_ref[...] = jnp.sum(grad_two * normed_two, axis=0, keepdims=True)
    g = grad_two * gain
    gr_ref[...] = (
        cot_ref[...].astype(F32)
        + scale_two * (g - normed_two * jnp.mean(g * normed_two, axis=-1, keepdims=True))
    ).astype(BF)
    gt_ref[...] = dot(mat(0), gr_ref[...], NT).astype(BF)

    def lanes(b):
        return half_rows(lax.rem(b, 2) * block, block, 128)

    def g_copy(b, t):
        return remote(
            gt_ref.at[half_rows(b * HD, HD, 16)], g_in.at[t // 2, :, lanes(t)],
            gsend.at[b], grecv.at[t], (b, fs),
        )

    def g_start(n, c):
        g_copy(lax.rem(me + n, H), me).start()
        return c

    lax.fori_loop(1, H, g_start, 0)
    g_here = pltpu.make_async_copy(
        gt_ref.at[half_rows(me * HD, HD, 16)], g_in.at[me // 2, :, lanes(me)], lsem.at[0]
    )
    g_here.start()
    hid_ref[...] = hidden32.T.astype(BF)
    act_ref[...] = active32.T.astype(BF)
    out_ref[...] = (resid + dot(active32.astype(BF), mat(2))).astype(BF)

    def theirs(g):
        return remote(so.at[g], r0.at[g], dsend.at[g], drecv.at[g], sib)

    def dense_rows(g, start):
        r = half_rows(start, part, 64)
        if g == 0:
            return dot(attn_ref[r, :], gr_ref[...])
        a, b = ((hid_ref, gip_ref), (act_ref, cot_ref))[g - 1]
        return dot(a[r, :], b[...])

    for g in range(n_g):
        for f in range(2):
            so[g, f] = dense_rows(g, f * 2 * part + (1 - k) * part).astype(BF)
        theirs(g).start()
    for g in range(n_g):
        for f in range(2):
            s1[g, f] = dense_rows(g, f * 2 * part + k * part).astype(BF)

    top, bottom = slice(0, part // 2), slice(part // 2, part)
    x_here = half_rows(x * cols, cols, 128)
    x_there = half_rows((1 - x) * cols, cols, 128)

    def stage(g, i):
        ends = (
            (s1.at[g, 1 - fs, top, :], ra.at[g], yn),
            (s1.at[g, :, bottom, x_there], rb.at[g], xn),
            (s1.at[g, fs, top, x_there], r2.at[g, top], xn),
            (s1.at[g, 1 - fs, bottom, x_here], r2.at[g, bottom], yn),
        )[i]
        return remote(ends[0], ends[1], psend.at[i, g], precv.at[i, g], ends[2])

    slab = part // 4

    zb = lax.rem(z, 2)
    near, far = (me + 4 - 8 * zb, fs), (me + 8 - 16 * (z // 2), fs)

    def z_rows(t):
        return s1.at[:, fs, half_rows(t * slab, slab, 16), x_here]

    def z_near(i):
        return remote(z_rows(1 - zb + 2 * i), rz.at[i], psend.at[4, i], precv.at[4, i], near)

    def z_far():
        return remote(
            z_rows(zb + 2 * (1 - z // 2)), rz.at[2], psend.at[4, 2], precv.at[4, 2], far
        )

    for g in range(n_g):
        theirs(g).wait()

        def add(i, c, g=g):
            r = half_rows(i * 32, 32, 32)
            for f in range(2):
                s1[g, f, r, :] += r0[g, f, r, :]
            return c

        lax.fori_loop(0, part // 32, add, 0)
        stage(g, 0).start()
        stage(g, 1).start()

    loads = []
    for w in range(3):
        for f in range(2):
            loads.append(
                pltpu.make_async_copy(own[w].at[pl.ds(f * part, part)], r0.at[w, f], wsem.at[w * 2 + f])
            )
            loads[-1].start()


    def load_other(src, w, f):
        return pltpu.make_async_copy(
            src.at[pl.ds(f * part, part)], so.at[w, f], wsem.at[6 + w * 2 + f]
        )

    for i, w in enumerate(w for w in range(3) if w not in PULL):
        for f in range(2):
            loads.append(load_other(held[i], w, f))
            loads[-1].start()

    def after_one():
        for g in range(n_g):
            stage(g, 0).wait()
            stage(g, 1).wait()

            def add(i, c, g=g):
                r = half_rows(i * 32, 32, 32)
                s1[g, fs, r, :] += ra[g, r, :]
                low = half_rows(part // 2 + i * 32, 32, 32)
                for f in range(2):
                    s1[g, f, low, x_here] += rb[g, f, r, :]
                return c

            lax.fori_loop(0, part // 64, add, 0)
            stage(g, 2).start()
            stage(g, 3).start()
        for i in range(EARLY, n_w):
            first(i).start()

    def after_two():
        for g in range(n_g):
            stage(g, 2).wait()
            stage(g, 3).wait()

            def add(i, c, g=g):
                r = half_rows(i * 32, 32, 32)
                s1[g, fs, r, x_here] += r2[g, r, :]
                return c

            lax.fori_loop(0, part // 32, add, 0)
        for i in range(2):
            z_near(i).start()

    def after_near():
        for i in range(2):
            z_near(i).wait()
            r = half_rows((zb + 2 * i) * slab, slab, 16)
            for g in range(n_g):
                s1[g, fs, r, x_here] += rz[i, g]
        z_far().start()

    def after_far():
        z_far().wait()
        r = half_rows(z * slab, slab, 16)
        for g in range(n_g):
            piece[g] = s1[g, fs, r, x_here] + rz[2, g]

    scale_sc[...] = jnp.zeros_like(scale_sc)
    dw_sc[...] = jnp.zeros_like(dw_sc)

    def g_taken(n, c):
        b = lax.rem(me + n, H)
        g_copy(b, b).wait()
        return c

    for c in back[1:]:
        c.wait()
    g_here.wait()
    lax.fori_loop(1, H, g_taken, 0)

    def prepare(i, c):
        g = g_in[i].astype(F32)
        g_sc[i] = g.T.astype(BF)
        delta_sc[i] = jnp.sum(g * o_ref[i], axis=0, keepdims=True)
        dq_sc[i] = jnp.zeros((HD, rows), F32)
        return c

    lax.fori_loop(0, units, prepare, 0)

    back[0].wait()

    def pair(masked, j, i):
        s = dot(k_ref[j], qt_ref[i])
        if masked:
            s = jnp.where(visible(j, i, rows, first_ref[i]), s, neg_big)
        p = jnp.exp2(s - lse_ref[i])
        dv_sc[...] += dot(p.astype(BF), g_sc[i])
        dp = dot(v_ref[j], g_in[i])
        ds = (p * (dp - delta_sc[i])).astype(BF)
        dk_sc[...] += dot(ds, q_ref[i])
        dq_sc[i] += dot(kt_ref[j], ds)

    def out(b, lo, n):
        return d_sc.at[b // 2, pl.ds(lo, n), :, lanes(b)]

    def to(t, lo, n):
        return got.at[pl.ds(lo, n), half_rows(t * HD, HD, 16)]

    def kv_copy(b, t):
        return remote(out(b, 1, 2), to(t, 1, 2), ksend.at[b], krecv.at[t], (b, fs))

    def q_copy(b, t):
        return remote(out(b, 0, 1), to(t, 0, 1), qsend.at[b], qrecv.at[t], (b, fs))

    kv_here = pltpu.make_async_copy(out(me, 1, 2), to(me, 1, 2), lsem.at[1])
    q_here = pltpu.make_async_copy(out(me, 0, 1), to(me, 0, 1), lsem.at[2])

    def column(n, c):
        j = lax.rem(me // 2 + n, units)
        dk_sc[...] = jnp.zeros_like(dk_sc)
        dv_sc[...] = jnp.zeros_like(dv_sc)
        pair(True, j, j)

        def plain(i, c2):
            pair(False, j, i)
            return c2

        def edge(i, c2):
            pair(True, j, i)
            return c2

        end = jnp.where(j == 0, 1, units - 1)
        lax.fori_loop(j + 1, end, plain, 0)
        lax.fori_loop(jnp.maximum(j + 1, end), units, edge, 0)
        d_sc[j, 1] = dk_sc[...].T.astype(BF)
        d_sc[j, 2] = dv_sc[...].T.astype(BF)

        def send(e, c2):
            b = 2 * j + e

            @pl.when(b != me)
            def _():
                kv_copy(b, me).start()

            @pl.when(b == me)
            def _():
                kv_here.start()

            return c2

        lax.fori_loop(0, 2, send, 0)
        for e in range(2):
            dw_sc[1 + e] += dot(d_sc[j, 1 + e], h_ref[j])

        @pl.when(n == ONE_AT)
        def _():
            after_one()

        @pl.when(n == TWO_AT)
        def _():
            after_two()

        return c

    lax.fori_loop(0, units, column, 0)
    half = dw_out.shape[2]

    def dw_copy(n, lo, size):
        return remote(
            dw_out.at[pl.ds(lo, size)], dw_got.at[pl.ds(lo, size)], vsend.at[6 + n], vrecv.at[6 + n], yn
        )

    def dw_send(n, lo, size):
        away = half_rows((1 - fs) * half, half, 128)
        dw_out[lo : lo + size] = dw_sc[lo : lo + size, :, away].astype(BF)
        dw_copy(n, lo, size).start()

    def dw_take(n, lo, size):
        dw_copy(n, lo, size).wait()
        keep = half_rows(fs * half, half, 128)
        total = dw_sc[lo : lo + size, :, keep] + dw_got[lo : lo + size].astype(F32)
        piece[3 + lo : 3 + lo + size] = total.astype(BF)

    dw_send(0, 1, 2)

    def queries(n, c):
        i = lax.rem(me // 2 + n, units)
        dq = dq_sc[i]
        scale_sc[...] += dq * raw_ref[i]
        d_sc[i, 0] = (dq * scale_ref[...]).astype(BF)

        def send(e, c2):
            b = 2 * i + e

            @pl.when(b != me)
            def _():
                q_copy(b, me).start()

            @pl.when(b == me)
            def _():
                q_here.start()

            return c2

        lax.fori_loop(0, 2, send, 0)
        return c

    lax.fori_loop(0, units, queries, 0)
    def query_weight(i, c):
        dw_sc[0] += dot(d_sc[i, 0], h_ref[i])
        return c

    lax.fori_loop(0, units, query_weight, 0)
    dw_send(1, 0, 1)
    small_out[...] = jnp.zeros_like(small_out)
    small_out[1:2, :] = g2_ref[...]
    small_out[2:3, :HD] = jnp.sum(scale_sc[...].T, axis=0, keepdims=True)

    spans = (pl.ds(0, 3), pl.ds(4, 2), pl.ds(3, 1))

    def cp(p, s, t, si, mine=False):
        here = all_ref.at[s, spans[p]]
        return remote(piece.at[spans[p]] if mine else here, here, asend.at[p, si], arecv.at[p, s], t)

    def keep(p):
        return pltpu.make_async_copy(
            piece.at[spans[p]], all_ref.at[me, spans[p]], lsem.at[3 + p]
        )

    def begin(p):
        keep(p).start()
        cp(p, me, xn, 0, True).start()

        @pl.when(z < 3)
        def _():
            cp(p, me, up, 1, True).start()

        @pl.when(z > 0)
        def _():
            cp(p, me, dn, 2, True).start()

        cp(p, me, sib, 3, True).start()

    def column_arrival(p, d):
        a = 4 + (d - 1) * 6

        @pl.when(z >= d)
        def _():
            s = me - 4 * d
            cp(p, s, dn, a).wait_recv()

            @pl.when(z < 3)
            def _():
                cp(p, s, up, a).start()

            cp(p, s, xn, a + 1).start()
            cp(p, s, sib, a + 2).start()

        @pl.when(z + d <= 3)
        def _():
            s = me + 4 * d
            cp(p, s, up, a + 3).wait_recv()

            @pl.when(z > 0)
            def _():
                cp(p, s, dn, a + 3).start()

            cp(p, s, xn, a + 4).start()
            cp(p, s, sib, a + 5).start()

    xo = me + 2 - 4 * x

    def across_arrival(p, d):
        @pl.when(z >= d)
        def _():
            s = xo - 4 * d
            cp(p, s, xn, 0).wait_recv()
            cp(p, s, sib, 22 + z - d).start()

        if d > 0:

            @pl.when(z + d <= 3)
            def _():
                s = xo + 4 * d
                cp(p, s, xn, 0).wait_recv()
                cp(p, s, sib, 22 + z + d).start()


    def kv_taken(n, c):
        b = lax.rem(me + n, H)
        kv_copy(b, b).wait()
        return c

    def q_taken(n, c):
        b = lax.rem(me + n, H)
        q_copy(b, b).wait()
        return c

    def input_grad(w, start):
        for r, m in ((fs, r0), (1 - fs, so)):
            for f in range(2):
                side = half_rows(r * block, block, 128)
                term = dot(m[w, f], got[w]).reshape(units // 2, HD, block)
                span = pl.ds(f * (units // 2), units // 2)
                if start:
                    raw_ref[span, :, side] = term
                else:
                    raw_ref[span, :, side] += term

    def pass_on(i):
        first(i).wait_recv()
        second(i).start()

    def load_pulled(i):
        second(i).wait()
        first(i).wait_send()
        late = [load_other(pulled[i], PULL[i], f) for f in range(2)]
        for c in late:
            c.start()
        for c in late:
            c.wait()

    def v_copy(i, t):
        n = (0, 1, 8)[i]
        return remote(small_out, small_in.at[i], vsend.at[n], vrecv.at[n], t)

    def v_column(d):
        t = lax.rem(z + d, 4)
        return t, remote(
            small_z.at[z], small_z.at[z], vsend.at[2 + d], vrecv.at[2 + z], (me + 4 * (t - z), fs)
        )

    dw_take(0, 1, 2)
    begin(1)
    after_near()
    dw_take(1, 0, 1)
    begin(2)
    pass_on(0)
    column_arrival(1, 1)
    column_arrival(2, 1)
    lax.fori_loop(1, H, kv_taken, 0)
    kv_here.wait()
    for c in loads:
        c.wait()
    input_grad(2, True)
    load_pulled(0)
    input_grad(1, False)
    across_arrival(1, 0)
    across_arrival(2, 0)
    after_far()
    begin(0)
    column_arrival(1, 2)
    column_arrival(2, 2)
    column_arrival(0, 1)
    across_arrival(0, 0)
    across_arrival(1, 1)
    across_arrival(2, 1)
    pass_on(1)
    lax.fori_loop(1, H, q_taken, 0)
    q_here.wait()
    load_pulled(1)
    input_grad(0, False)
    column_arrival(1, 3)
    column_arrival(2, 3)
    grad_hidden = jnp.concatenate(
        [raw_ref[:, :, r * block : (r + 1) * block].reshape(width // 2, block).T for r in range(2)],
        axis=1,
    )
    tokens = tok_ref[...].astype(F32)
    scale = lax.rsqrt(jnp.mean(tokens * tokens, axis=-1, keepdims=True) + epsilon)
    normed = tokens * scale
    small_out[0:1, :] = jnp.sum(grad_hidden * normed, axis=0, keepdims=True)
    v_copy(0, sib).start()
    column_arrival(0, 2)
    across_arrival(1, 2)
    across_arrival(2, 2)
    e = grad_hidden * gain_ref[0:1, :]
    tg_ref[...] = (
        gr_ref[...].astype(F32) + scale * (e - normed * jnp.mean(e * normed, axis=-1, keepdims=True))
    ).astype(BF)
    v_copy(0, sib).wait()
    small_out[...] += small_in[0]
    v_copy(1, xn).start()
    across_arrival(0, 1)
    v_copy(1, xn).wait()
    small_z[z] = small_out[...] + small_in[1]
    for d in range(1, 4):
        v_column(d)[1].start()
    column_arrival(0, 3)
    across_arrival(1, 3)
    across_arrival(2, 3)
    for d in range(1, 4):
        t, c = v_column(d)
        c.wait_send()
        remote(small_z.at[t], small_z.at[t], vsend.at[2 + d], vrecv.at[2 + t], xn).wait_recv()
    small_out[...] = (small_z[0] + small_z[1]) + (small_z[2] + small_z[3])
    v_copy(2, yn).start()
    across_arrival(0, 2)
    v_copy(2, yn).wait()
    small_out[...] += small_in[2]
    sums_ref[...] = small_out[0:2, half_rows(fs * cols, cols, 128)]
    scale_out[...] = small_out[2:3, :HD] * (1.0 / math.sqrt(HD))
    across_arrival(0, 3)

    for p in (1, 2, 0):

        def from_sib(n, c, p=p):
            cp(p, n * 2 + 1 - k, sib, 0).wait_recv()
            return c

        lax.fori_loop(0, UNITS, from_sib, 0)
        keep(p).wait()
        cp(p, me, xn, 0, True).wait_send()

        @pl.when(z < 3)
        def _(p=p):
            cp(p, me, up, 1, True).wait_send()

        @pl.when(z > 0)
        def _(p=p):
            cp(p, me, dn, 2, True).wait_send()

        cp(p, me, sib, 3, True).wait_send()

        def sent(d, c, p=p):
            a = 4 + (d - 1) * 6

            @pl.when(z >= d)
            def _():
                s = me - 4 * d

                @pl.when(z < 3)
                def _():
                    cp(p, s, up, a).wait_send()

                cp(p, s, xn, a + 1).wait_send()
                cp(p, s, sib, a + 2).wait_send()

            @pl.when(z + d <= 3)
            def _():
                s = me + 4 * d

                @pl.when(z > 0)
                def _():
                    cp(p, s, dn, a + 3).wait_send()

                cp(p, s, xn, a + 4).wait_send()
                cp(p, s, sib, a + 5).wait_send()

            return c

        lax.fori_loop(1, 4, sent, 0)

        def sent_across(zz, c, p=p):
            cp(p, xo + 4 * (zz - z), sib, 22 + zz).wait_send()
            return c

        lax.fori_loop(0, 4, sent_across, 0)


EARLY = 1
ONE_AT = 4
TWO_AT = 7


def tail_call(own, held, mats, vm, kept):
    n_w = len(PULL)
    rows, width = vm[2].shape
    n, ur = kept[0].shape[:2]
    half = width // 2
    part = width // 4
    sem = pltpu.SemaphoreType.DMA
    return pl.pallas_call(
        tail_kernel,
        out_shape=[
            jax.ShapeDtypeStruct((H, 6, part // 4, half), BF),
            jax.ShapeDtypeStruct((rows, width), BF),
            jax.ShapeDtypeStruct((2, half), F32),
            jax.ShapeDtypeStruct((1, HD), F32),
            jax.ShapeDtypeStruct((rows, width), BF),
        ]
        + [jax.ShapeDtypeStruct(own[0].shape, BF)] * n_w,
        in_specs=[ANY] * (9 + len(held)) + [VMEM] * len(vm) + [ANY] * len(kept),
        out_specs=[ANY, VMEM, VMEM, VMEM, VMEM] + [ANY] * n_w,
        scratch_shapes=[
            *[pltpu.VMEM(a.shape, a.dtype) for a in kept],
            pltpu.VMEM((n, HD, ur), BF),
            pltpu.VMEM((n, ur, HD), BF),
            pltpu.VMEM((n, 1, ur), F32),
            pltpu.VMEM((HD, ur), F32),
            pltpu.VMEM((ur, HD), F32),
            pltpu.VMEM((ur, HD), F32),
            pltpu.VMEM((n, 3, HD, ur), BF),
            pltpu.VMEM((3, H * HD, rows), BF),
            pltpu.VMEM((3, HD, width), F32),
            pltpu.VMEM((3, HD, half), BF),
            pltpu.VMEM((3, HD, half), BF),
            pltpu.VMEM((6, part // 4, half), BF),
            pltpu.VMEM((3, 4, part, width), BF),
            pltpu.VMEM((3, 2, part, width), BF),
            pltpu.VMEM((3, part // 2, width), BF),
            pltpu.VMEM((3, 2, part // 2, half), BF),
            pltpu.VMEM((3, part, half), BF),
            pltpu.VMEM((3, 3, part // 4, half), BF),
            pltpu.VMEM((8, width), F32),
            pltpu.VMEM((3, 8, width), F32),
            pltpu.VMEM((4, 8, width), F32),
            sem((H,)), sem((H,)), sem((H,)), sem((H,)), sem((H,)), sem((H,)),
            sem((3,)), sem((3,)), sem((5, 4)), sem((5, 4)),
            sem((3, 26)), sem((3, H)), sem((9,)), sem((9,)), sem((6,)), sem((12,)),
            sem((9,)), sem((max(1, 2 * n_w),)), sem((max(1, 2 * n_w),)),
            pltpu.VMEM((H * HD, rows), BF), pltpu.VMEM((rows, width), BF), pltpu.VMEM((width, rows), BF),
            pltpu.VMEM((rows, width), BF), pltpu.VMEM((width, rows), BF), pltpu.VMEM((1, width), F32),
            sem((3, 4)),
        ],
        compiler_params=pltpu.CompilerParams(
            collective_id=2, has_side_effects=True, vmem_limit_bytes=63 * 2**20
        ),
        name="tail",
    )(*own, *held, *mats, *vm, *kept)


def spread_kernel(dense_ref, heads_ref, *outs):
    slab, cols = dense_ref.shape[-2:]
    n, _, hd, _ = heads_ref.shape
    for w in range(3):

        @pl.when(pl.program_id(0) // 2 == w)
        def _(w=w):
            for zz in range(4):
                for xx in range(2):
                    outs[w][zz * slab : (zz + 1) * slab, xx * cols : (xx + 1) * cols] = dense_ref[
                        zz, xx, 0, 0
                    ].astype(F32)
            outs[3 + w][...] = heads_ref[...].reshape(n * hd, cols).astype(F32).T


def spread_call(pieces):
    n, parts, slab, cols = pieces.shape
    split = pieces.reshape(4, 2, 2, parts, slab, cols)

    def half(w):
        return lambda i: jnp.clip(i - 2 * w, 0, 1)

    def dense_spec(w):
        return pl.BlockSpec((4 * slab, 2 * cols), lambda i: (half(w)(i), 0))

    def heads_spec(w):
        return pl.BlockSpec((cols, n * slab // 2), lambda i: (0, half(w)(i)))

    return pl.pallas_call(
        spread_kernel,
        grid=(6,),
        out_shape=[jax.ShapeDtypeStruct((8 * slab, 2 * cols), F32)] * 3
        + [jax.ShapeDtypeStruct((cols, n * slab), F32)] * 3,
        in_specs=[
            pl.BlockSpec((4, 2, 1, 1, slab, cols), lambda i: (0, 0, lax.rem(i, 2), i // 2, 0, 0)),
            pl.BlockSpec((n // 2, 1, slab, cols), lambda i: (lax.rem(i, 2), 3 + i // 2, 0, 0)),
        ],
        out_specs=[dense_spec(w) for w in range(3)] + [heads_spec(w) for w in range(3)],
        compiler_params=pltpu.CompilerParams(vmem_limit_bytes=48 * 2**20),
        name="spread",
    )(split, pieces)


def fast_local(
    tokens, query_weight, key_weight, value_weight, out_weight, inner_weight, outer_weight,
    attn_gain, mlp_gain, query_scale, doc_starts, cotangent,
):
    me, fs = lax.axis_index("ctx"), lax.axis_index("fs")
    rows, width = tokens.shape[1:]
    tok = tokens[0]
    cot = cotangent[0]

    def head_columns(w):
        return lax.dynamic_slice(w, (0, me * HD), (w.shape[0], HD)).T

    wt = jnp.concatenate([head_columns(w) for w in (query_weight, key_weight, value_weight)], axis=0)
    gains = jnp.stack([attn_gain, mlp_gain])
    positions = jnp.arange(H * rows, dtype=jnp.int32)
    starts = doc_starts[0]
    first_key = jnp.max(
        jnp.where(starts[None, :] <= positions[:, None], starts[None, :], 0), axis=1
    ).reshape(UNITS, 1, 2 * rows)
    scale_col = (query_scale / math.sqrt(HD))[:, None]

    (
        gain_full, attn_t, h_all, o32, lse, qt, q, kt, k, v, raw,
        out_o, inner_o, outer_o, value_o,
    ) = forward_call(
        tok, gains, wt, scale_col, first_key,
        (out_weight, inner_weight, outer_weight, value_weight), N_SHARED,
    )
    attn_t = attn_t.reshape(width, rows)

    pieces, grad_tokens, gain_sums, scale_sum, result, *_ = tail_call(
        (query_weight, key_weight, value_weight), (value_o,),
        (out_weight, out_o, inner_weight, inner_o, outer_weight, outer_o),
        (attn_t, cot, tok, gain_full, scale_col, first_key),
        (h_all, o32, lse, qt, q, kt, k, v, raw),
    )
    out_g, inner_g, outer_g, query_g, key_g, value_g = spread_call(pieces)
    return (
        result[None], grad_tokens[None], query_g, key_g, value_g, out_g, inner_g, outer_g,
        gain_sums[0], gain_sums[1], scale_sum[0],
    )


def solution(mesh):
    placed = (
        P("fs", "ctx", None),
        P("fs", None),
        P("fs", None),
        P("fs", None),
        P("fs", None),
        P("fs", None),
        P("fs", None),
        P("fs"),
        P("fs"),
        P(),
        P("fs", None),
        P("fs", "ctx", None),
    )
    return jax.shard_map(
        fast_local if fast_fits(mesh) else general_local,
        mesh=mesh,
        in_specs=placed,
        out_specs=(
            P("fs", "ctx", None),
            P("fs", "ctx", None),
            P("fs", None),
            P("fs", None),
            P("fs", None),
            P("fs", None),
            P("fs", None),
            P("fs", None),
            P("fs"),
            P("fs"),
            P(),
        ),
        check_vma=False,
    )
```
